32 devices in a mesh: narrow: 4 (over y, x), wide: 2 (over core), tensor: 4 (over z).
Axes of the slice: x: 2, y: 2, z: 4, core: 2. Of those that a mesh axis runs over, the one named last changes fastest.
Arguments:
- frames: bfloat16 [4, 8, 4, 32, 1152], P('narrow', None, 'wide'), may hold values from -6 to 6
- cotangent: bfloat16 [4, 8, 4, 32, 1152], P('narrow', None, 'wide'), may hold values from -6 to 6
- prompt: bfloat16 [4, 120, 4096], P('narrow'), may hold values from -6 to 6
- timestep: int32 [4], P('narrow'), may hold values from 0 to 999
- clip_lengths: int32 [4], P('narrow'), may hold values from 1 to 8, as said below
- text_lengths: int32 [4], P('narrow'), may hold values from 1 to 120, as said below
- modulation_weight: bfloat16 [1152, 6912], P('wide', 'tensor'), may hold values from -0.1875 to 0.1875
- modulation_bias: float32 [6912], replicated, may hold values from -0.5 to 0.5
- space_query: bfloat16 [1152, 1152], P('wide', 'tensor'), may hold values from -0.1875 to 0.1875
- space_key: bfloat16 [1152, 1152], P('wide', 'tensor'), may hold values from -0.1875 to 0.1875
- space_value: bfloat16 [1152, 1152], P('wide', 'tensor'), may hold values from -0.1875 to 0.1875
- space_out: bfloat16 [1152, 1152], P('wide', 'tensor'), may hold values from -1 to 1
- time_gain: float32 [1152], replicated, may hold values from 0.5 to 1.5
- time_query: bfloat16 [1152, 1152], P('wide', 'tensor'), may hold values from -0.1875 to 0.1875
- time_key: bfloat16 [1152, 1152], P('wide', 'tensor'), may hold values from -0.1875 to 0.1875
- time_value: bfloat16 [1152, 1152], P('wide', 'tensor'), may hold values from -0.1875 to 0.1875
- time_out: bfloat16 [1152, 1152], P('wide', 'tensor'), may hold values from -0.375 to 0.375
- time_gate: float32 [1152], replicated, may hold values from 0.3 to 1.5
- cross_gain: float32 [1152], replicated, may hold values from 0.5 to 1.5
- cross_query: bfloat16 [1152, 1152], P('wide', 'tensor'), may hold values from -0.1875 to 0.1875
- prompt_key: bfloat16 [4096, 1152], P('wide', 'tensor'), may hold values from -0.09375 to 0.09375
- prompt_value: bfloat16 [4096, 1152], P('wide', 'tensor'), may hold values from -0.09375 to 0.09375
- cross_out: bfloat16 [1152, 1152], P('wide', 'tensor'), may hold values from -0.75 to 0.75
- feed_up: bfloat16 [1152, 4608], P('wide', 'tensor'), may hold values from -0.1875 to 0.1875
- feed_down: bfloat16 [1152, 4608], P('wide', 'tensor'), may hold values from -0.09375 to 0.09375
Outputs:
- output: bfloat16 [4, 8, 4, 32, 1152], P('narrow', None, 'wide')
- frames_grad: bfloat16 [4, 8, 4, 32, 1152], P('narrow', None, 'wide')
- modulation_weight_grad: float32 [1152, 6912], P(('narrow', 'wide'), 'tensor')
- modulation_bias_grad: float32 [6912], P(('narrow', 'wide'))
- space_query_grad: float32 [1152, 1152], P(('narrow', 'wide'), 'tensor')
- space_key_grad: float32 [1152, 1152], P(('narrow', 'wide'), 'tensor')
- space_value_grad: float32 [1152, 1152], P(('narrow', 'wide'), 'tensor')
- space_out_grad: float32 [1152, 1152], P(('narrow', 'wide'), 'tensor')
- time_gain_grad: float32 [1152], P(('narrow', 'wide'))
- time_query_grad: float32 [1152, 1152], P(('narrow', 'wide'), 'tensor')
- time_key_grad: float32 [1152, 1152], P(('narrow', 'wide'), 'tensor')
- time_value_grad: float32 [1152, 1152], P(('narrow', 'wide'), 'tensor')
- time_out_grad: float32 [1152, 1152], P(('narrow', 'wide'), 'tensor')
- time_gate_grad: float32 [1152], P(('narrow', 'wide'))
- cross_gain_grad: float32 [1152], P(('narrow', 'wide'))
- cross_query_grad: float32 [1152, 1152], P(('narrow', 'wide'), 'tensor')
- prompt_key_grad: float32 [4096, 1152], P(('narrow', 'wide'), 'tensor')
- prompt_value_grad: float32 [4096, 1152], P(('narrow', 'wide'), 'tensor')
- cross_out_grad: float32 [1152, 1152], P(('narrow', 'wide'), 'tensor')
- feed_up_grad: float32 [1152, 4608], P(('narrow', 'wide'), 'tensor')
- feed_down_grad: float32 [1152, 4608], P(('narrow', 'wide'), 'tensor')
The draws below stay inside these ranges and needn't reach their ends.
Inputs may be any that keep to these rules, and one draw needn't show every extreme that they name: `clip_lengths`: some clip has exactly 8 frames. `text_lengths`: some clip uses all 120 prompt tokens.
All inputs are finite; a program needn't handle non-finite values.
Results may differ from the reference program's by a relative error of at most 0.04.
Values may be sent and summed in bfloat16 or wider, within the bound.
A program may use at most 256 MiB of HBM per device.

```python
import math
import jax
import jax.numpy as jnp
from jax import lax

D = 1152
HEADS = 16
HEAD_DIM = 72
MLP = 4608
TW = 4096
TEXT = 120
FRAMES = 8
COLS = 32
GRID = 4
CLIPS = 4


def draw_text_lengths(key, part):
    key = jax.random.fold_in(key, 7)
    first_key, second_key = jax.random.split(key)
    counts = jax.random.randint(first_key, (CLIPS,), 1, TEXT + 1)
    chosen = jax.random.randint(second_key, (), 0, CLIPS)
    return jnp.where(jnp.arange(CLIPS) == chosen, TEXT, counts).astype(jnp.int32)


def draw_clip_lengths(key, part):
    key = jax.random.fold_in(key, 11)
    first_key, second_key = jax.random.split(key)
    counts = jax.random.randint(first_key, (CLIPS,), 1, FRAMES + 1)
    chosen = jax.random.randint(second_key, (), 0, CLIPS)
    return jnp.where(jnp.arange(CLIPS) == chosen, FRAMES, counts).astype(jnp.int32)


def touch_ends(entries, key, least, largest):
    longest = entries.shape.index(max(entries.shape))
    spots = []
    for shift in (0, 1):
        where = [jax.random.randint(jax.random.fold_in(key, axis), (), 0, length) for axis, length in enumerate(entries.shape)]
        where[longest] = (where[longest] + shift) % entries.shape[longest]
        spots.append(tuple(where))
    return entries.at[spots[0]].set(least).at[spots[1]].set(largest)


def levels(stream_key, dims, cuts, least, largest):
    def one(dim, blocks):
        steps = jax.random.uniform(jax.random.fold_in(jax.random.fold_in(stream_key, 6), dim), (blocks,), jnp.float32, least / len(cuts), largest / len(cuts))
        return jnp.repeat(jnp.exp(steps), dims[dim] // blocks).reshape((-1,) + (1,) * (len(dims) - dim - 1))

    level = one(*cuts[0])
    for cut in cuts[1:]:
        level = level * one(*cut)
    return level


def scatter_about(key, shape, scale, bound, cuts=(), kind=jnp.bfloat16):
    drawn = jax.random.normal(key, shape, jnp.float32) * scale
    if len(cuts) > 0:
        drawn = levels(key, shape, cuts, -0.22, 0.18) * drawn
    return jnp.clip(drawn, min=-bound, max=bound).astype(kind)


def setup_inputs(seed: int = 0) -> dict:
    seeds = jax.random.split(jax.random.key(seed), 26)
    frames = scatter_about(seeds[0], (CLIPS, FRAMES, GRID, COLS, D), 1.0, 6.0, ((0, 4), (2, 2)))
    cotangent = scatter_about(seeds[1], (CLIPS, FRAMES, GRID, COLS, D), 1.0, 6.0, ((0, 4), (2, 2)))
    prompt = scatter_about(seeds[2], (CLIPS, TEXT, TW), 1.0, 6.0, ((0, 4),))
    timestep = touch_ends(jax.random.randint(seeds[3], (CLIPS,), 0, 1000), jax.random.fold_in(seeds[3], 1), 0, 999).astype(jnp.int32)
    clip_lengths = draw_clip_lengths(jax.random.fold_in(seeds[25], 71), 0)
    text_lengths = draw_text_lengths(jax.random.fold_in(seeds[25], 71), 0)
    modulation_weight = scatter_about(seeds[6], (D, 6 * D), D ** -0.5, 0.1875, ((0, 2), (1, 4)))
    modulation_bias = jnp.clip(jax.random.uniform(seeds[7], (6 * D,), jnp.float32, -0.5, 0.5), -0.5, 0.5)
    space_query = scatter_about(seeds[8], (D, D), D ** -0.5, 0.1875, ((0, 2), (1, 4)))
    space_key = scatter_about(seeds[9], (D, D), D ** -0.5, 0.1875, ((0, 2), (1, 4)))
    space_value = scatter_about(seeds[10], (D, D), D ** -0.5, 0.1875, ((0, 2), (1, 4)))
    space_out = scatter_about(seeds[11], (D, D), (max(1, 4 * D // (GRID * COLS))) ** -0.5, 1.0, ((0, 2), (1, 4)))
    time_gain = jnp.clip(1.0 + 0.1 * jax.random.normal(seeds[12], (D,), jnp.float32), 0.5, 1.5)
    time_query = scatter_about(seeds[13], (D, D), D ** -0.5, 0.1875, ((0, 2), (1, 4)))
    time_key = scatter_about(seeds[14], (D, D), D ** -0.5, 0.1875, ((0, 2), (1, 4)))
    time_value = scatter_about(seeds[15], (D, D), D ** -0.5, 0.1875, ((0, 2), (1, 4)))
    time_out = scatter_about(seeds[16], (D, D), (D // 4) ** -0.5, 0.375, ((0, 2), (1, 4)))
    time_gate = jnp.clip(jax.random.uniform(seeds[17], (D,), jnp.float32, 0.3, 1.5), 0.3, 1.5)
    cross_gain = jnp.clip(1.0 + 0.1 * jax.random.normal(seeds[18], (D,), jnp.float32), 0.5, 1.5)
    cross_query = scatter_about(seeds[19], (D, D), D ** -0.5, 0.1875, ((0, 2), (1, 4)))
    prompt_key = scatter_about(seeds[20], (TW, D), TW ** -0.5, 0.09375, ((0, 2), (1, 4)))
    prompt_value = scatter_about(seeds[21], (TW, D), TW ** -0.5, 0.09375, ((0, 2), (1, 4)))
    cross_out = scatter_about(seeds[22], (D, D), (D // 16) ** -0.5, 0.75, ((0, 2), (1, 4)))
    feed_up = scatter_about(seeds[23], (D, MLP), D ** -0.5, 0.1875, ((0, 2), (1, 4)))
    feed_down = scatter_about(seeds[24], (D, MLP), MLP ** -0.5, 0.09375, ((0, 2), (1, 4)))
    return {"frames": frames, "cotangent": cotangent, "prompt": prompt, "timestep": timestep, "clip_lengths": clip_lengths, "text_lengths": text_lengths, "modulation_weight": modulation_weight, "modulation_bias": modulation_bias, "space_query": space_query, "space_key": space_key, "space_value": space_value, "space_out": space_out, "time_gain": time_gain, "time_query": time_query, "time_key": time_key, "time_value": time_value, "time_out": time_out, "time_gate": time_gate, "cross_gain": cross_gain, "cross_query": cross_query, "prompt_key": prompt_key, "prompt_value": prompt_value, "cross_out": cross_out, "feed_up": feed_up, "feed_down": feed_down}


@jax.custom_vjp
def low(v):
    return lax.optimization_barrier(v.astype(jnp.bfloat16)).astype(jnp.float32)

@jax.custom_vjp
def low_back(v):
    return v

def low_keep(v):
    return (low(v), None)

def low_pass(kept, grad):
    return (grad,)

def back_keep(v):
    return (v, None)

def back_low(kept, grad):
    return (low(grad),)
low.defvjp(low_keep, low_pass)
low_back.defvjp(back_keep, back_low)
EPSILON = 1e-06
NEGATIVE = -1e+30
HIGHEST = lax.Precision.HIGHEST

def rounded(values):
    return low(low_back(values))

def norm_rows(values):
    center = values - lax.optimization_barrier(jnp.mean(values, -1, keepdims=True))
    return center * lax.rsqrt(lax.optimization_barrier(jnp.mean(center * center, -1, keepdims=True)) + EPSILON)

def embed_time(instant):
    half_width = D // 2
    frequency = jnp.exp(-math.log(10000.0) * jnp.arange(half_width, dtype=jnp.float32) / half_width)
    angles = instant.astype(jnp.float32) * frequency
    return jax.nn.silu(jnp.concatenate([jnp.cos(angles), jnp.sin(angles)]))

def frame_attention(pieces):
    queries, key_rows, values = pieces
    score_scale = 1.0 / math.sqrt(HEAD_DIM)
    scores = low_back(jnp.einsum('phe,khe->hpk', queries, key_rows, precision=HIGHEST) * score_scale)
    attend = low(jax.nn.softmax(scores, axis=-1))
    return jnp.einsum('hpk,khe->phe', attend, values, precision=HIGHEST)

def block(inputs, weights, condition, frame_live, prompt_rows, word_live):
    modulation_weight, modulation_bias, space_query, space_key, space_value, space_out, time_gain, time_query, time_key, time_value, time_out, time_gate, cross_gain, cross_query, prompt_key, prompt_value, cross_out, feed_up, feed_down = weights
    score_scale = 1.0 / math.sqrt(HEAD_DIM)
    frame_count = inputs.shape[0]
    patch_count = inputs.shape[1]
    split_heads = (frame_count, patch_count, HEADS, HEAD_DIM)
    joined = (frame_count, patch_count, D)
    modulation = jnp.dot(low(condition), modulation_weight, precision=HIGHEST) + modulation_bias
    shift_one, scale_one, gate_one, shift_two, scale_two, gate_two = jnp.split(modulation, 6)
    input_one = low(norm_rows(inputs) * (1.0 + scale_one) + shift_one)
    query_one = rounded(jnp.dot(input_one, space_query, precision=HIGHEST)).reshape(split_heads)
    key_one = rounded(jnp.dot(input_one, space_key, precision=HIGHEST)).reshape(split_heads)
    value_one = rounded(jnp.dot(input_one, space_value, precision=HIGHEST)).reshape(split_heads)
    context_one = lax.map(jax.checkpoint(frame_attention), (query_one, key_one, value_one))
    context_one = rounded(context_one.reshape(joined))
    branch_one = low_back(jnp.einsum('fpj,mj->fpm', context_one, space_out, precision=HIGHEST))
    after_one = inputs + gate_one * branch_one
    input_two = low(norm_rows(after_one) * time_gain)
    query_two = rounded(jnp.dot(input_two, time_query, precision=HIGHEST)).reshape(split_heads)
    key_two = rounded(jnp.dot(input_two, time_key, precision=HIGHEST)).reshape(split_heads)
    value_two = rounded(jnp.dot(input_two, time_value, precision=HIGHEST)).reshape(split_heads)
    scores_two = low_back(jnp.einsum('fphe,gphe->phfg', query_two, key_two, precision=HIGHEST) * score_scale)
    scores_two = jnp.where(frame_live, scores_two, NEGATIVE)
    attend_two = low(jax.nn.softmax(scores_two, axis=-1))
    context_two = jnp.einsum('phfg,gphe->fphe', attend_two, value_two, precision=HIGHEST)
    context_two = rounded(context_two.reshape(joined))
    branch_two = low_back(jnp.einsum('fpj,mj->fpm', context_two, time_out, precision=HIGHEST))
    after_two = after_one + jnp.tanh(time_gate) * branch_two
    input_three = low(norm_rows(after_two) * cross_gain)
    query_three = rounded(jnp.dot(input_three, cross_query, precision=HIGHEST)).reshape(split_heads)
    word_keys = rounded(jnp.dot(prompt_rows, prompt_key, precision=HIGHEST)).reshape(-1, HEADS, HEAD_DIM)
    word_values = rounded(jnp.dot(prompt_rows, prompt_value, precision=HIGHEST)).reshape(-1, HEADS, HEAD_DIM)
    scores_three = low_back(jnp.einsum('fphe,jhe->fphj', query_three, word_keys, precision=HIGHEST) * score_scale)
    scores_three = jnp.where(word_live, scores_three, NEGATIVE)
    attend_three = low(jax.nn.softmax(scores_three, axis=-1))
    context_three = jnp.einsum('fphj,jhe->fphe', attend_three, word_values, precision=HIGHEST)
    context_three = rounded(context_three.reshape(joined))
    branch_three = low_back(jnp.einsum('fpj,mj->fpm', context_three, cross_out, precision=HIGHEST))
    after_three = after_two + branch_three
    input_four = low(norm_rows(after_three) * (1.0 + scale_two) + shift_two)
    pre_act = low_back(jnp.dot(input_four, feed_up, precision=HIGHEST))
    hidden = low(jax.nn.gelu(pre_act, approximate=True))
    branch_four = low_back(jnp.einsum('fpj,mj->fpm', hidden, feed_down, precision=HIGHEST))
    after_four = after_three + gate_two * branch_four
    return jnp.where(frame_live[:, None, None], after_four, 0.0)

def reference(frames, cotangent, prompt, timestep, clip_lengths, text_lengths, modulation_weight, modulation_bias, space_query, space_key, space_value, space_out, time_gain, time_query, time_key, time_value, time_out, time_gate, cross_gain, cross_query, prompt_key, prompt_value, cross_out, feed_up, feed_down):
    weights = tuple((element.astype(jnp.float32) for element in (modulation_weight, modulation_bias, space_query, space_key, space_value, space_out, time_gain, time_query, time_key, time_value, time_out, time_gate, cross_gain, cross_query, prompt_key, prompt_value, cross_out, feed_up, feed_down)))
    shaped = (CLIPS, FRAMES, GRID * COLS, D)
    inputs_all = frames.astype(jnp.float32).reshape(shaped)
    upstream_all = cotangent.astype(jnp.float32).reshape(shaped)
    prompt_all = prompt.astype(jnp.float32)

    def per_clip(running, pieces):
        clip_inputs, clip_upstream, clip_prompt, instant, frame_total, word_total = pieces
        frame_live = jnp.arange(FRAMES) < frame_total
        word_live = jnp.arange(TEXT) < word_total
        condition = embed_time(instant)

        def forward(clip_values, *params):
            return block(clip_values, params, condition, frame_live, clip_prompt, word_live)
        result, pullback = jax.vjp(forward, clip_inputs, *weights)
        gradients = pullback(clip_upstream)
        running = tuple((former + gradient for former, gradient in zip(running, gradients[1:])))
        return (running, (result.astype(jnp.bfloat16), gradients[0].astype(jnp.bfloat16)))
    initial = tuple((jnp.zeros_like(element) for element in weights))
    totals, (results, input_grads) = lax.scan(per_clip, initial, (inputs_all, upstream_all, prompt_all, timestep, clip_lengths, text_lengths))
    full_shape = (CLIPS, FRAMES, GRID, COLS, D)
    return (results.reshape(full_shape), input_grads.reshape(full_shape), totals[0], totals[1], totals[2], totals[3], totals[4], totals[5], totals[6], totals[7], totals[8], totals[9], totals[10], totals[11], totals[12], totals[13], totals[14], totals[15], totals[16], totals[17], totals[18])
```

```python
import functools
import math

import jax
import jax.numpy as jnp
from jax import lax
from jax.experimental import pallas as pl
from jax.experimental.pallas import tpu as pltpu
from jax.sharding import PartitionSpec as P

HEAD_DIM = 72
LANES = 128
EPSILON = 1e-06
NEGATIVE = -1e30
NARROW, WIDE, TENSOR = "narrow", "wide", "tensor"
COLS = "cols"
MESH_ID = pl.DeviceIdType.MESH
F32 = jnp.float32
BF16 = jnp.bfloat16
VMEM = pltpu.VMEM
VM = pl.BlockSpec(memory_space=pltpu.VMEM)
ANY = pl.BlockSpec(memory_space=pl.ANY)
DMA = pltpu.SemaphoreType.DMA


def dot(left, right):
    return jnp.dot(left, right, preferred_element_type=F32)


def dot_tr(left, right):
    return lax.dot_general(left, right, (((1,), (1,)), ((), ())), preferred_element_type=F32)


def dot_outer(left, right):
    return lax.dot_general(left, right, (((0,), (0,)), ((), ())), preferred_element_type=F32)


def norm_tile(values):
    center = values - jnp.mean(values, -1, keepdims=True)
    inverse = lax.rsqrt(jnp.mean(center * center, -1, keepdims=True) + EPSILON)
    return center * inverse, inverse


def norm_pull(normed, inverse, incoming):
    return inverse * (
        incoming
        - jnp.mean(incoming, -1, keepdims=True)
        - normed * jnp.mean(incoming * normed, -1, keepdims=True)
    )


def softmax_tile(scores):
    exponent = jnp.exp(scores - jnp.max(scores, -1, keepdims=True))
    return exponent / jnp.sum(exponent, -1, keepdims=True)


class Place:
    def __init__(self, sizes):
        self.sizes = sizes
        self.n = lax.axis_index(NARROW)
        self.w = lax.axis_index(WIDE)
        self.t = lax.axis_index(TENSOR)

    def tensor_peer(self, step):
        return lax.rem(self.t + step, self.sizes[TENSOR])

    def over_tensor(self, step):
        return (self.n, self.w, self.tensor_peer(step))

    def sibling(self):
        return (self.n, 1 - self.w, self.t)

    def over_narrow(self, peer):
        return (peer, self.w, self.t)


def greet(partners):
    barrier = pltpu.get_barrier_semaphore()
    for partner in partners:
        pl.semaphore_signal(barrier, inc=1, device_id=partner, device_id_type=MESH_ID)
    pl.semaphore_wait(barrier, len(partners))


def send(source, target, send_sem, recv_sem, partner):
    copy = pltpu.make_async_remote_copy(
        src_ref=source,
        dst_ref=target,
        send_sem=send_sem,
        recv_sem=recv_sem,
        device_id=partner,
        device_id_type=MESH_ID,
    )
    copy.start()
    return copy


class Ring:
    def __init__(self, place, quarter, send_sems, recv_sems):
        self.place, self.quarter = place, quarter
        self.send_sems, self.recv_sems = send_sems, recv_sems
        self.peers = place.sizes[TENSOR] - 1
        self.used = 0

    def take(self):
        self.used += 1
        return self.used - 1

    def scatter(self, partial, landing):
        slot = self.take()
        copies = []
        for step in (2, 1, 3) if self.peers == 3 else range(1, self.peers + 1):
            rows = pl.ds(
                pl.multiple_of(self.place.tensor_peer(step) * self.quarter, self.quarter),
                self.quarter,
            )
            copies.append(
                send(
                    partial.at[rows],
                    landing.at[step - 1],
                    self.send_sems.at[slot, step - 1],
                    self.recv_sems.at[slot, step - 1],
                    self.place.over_tensor(step),
                )
            )
        return copies

    def gather(self, own):
        slot = self.take()
        return [
            send(
                own,
                own,
                self.send_sems.at[slot, step - 1],
                self.recv_sems.at[slot, step - 1],
                self.place.over_tensor(step),
            )
            for step in ((2, 1, 3) if self.peers == 3 else range(1, self.peers + 1))
        ]


def wait_all(copies):
    for copy in copies:
        copy.wait()


def summed(partial, landing, rows, peers):
    total = partial[rows].astype(F32)
    for peer in range(peers):
        total = total + landing[peer].astype(F32)
    return total


def modulation_kernel(sizes, condition, weight, shared, mine, landing, send_sems, recv_sems):
    place = Place(sizes)
    partners = []
    for dw in range(sizes[WIDE]):
        for dt in range(sizes[TENSOR]):
            if dw or dt:
                partners.append(
                    (
                        place.n,
                        lax.rem(place.w + dw, sizes[WIDE]),
                        lax.rem(place.t + dt, sizes[TENSOR]),
                    )
                )
    greet(partners)
    mine[0] = dot(condition[...], weight[...])[0:1]
    slot = place.w * sizes[TENSOR] + place.t
    copies = [
        send(mine.at[0], landing.at[slot], send_sems.at[i], recv_sems.at[i], partner)
        for i, partner in enumerate(partners)
    ]
    landing[slot] = mine[0]
    wait_all(copies)
    shared[...] = landing[...]


def modulation_call(sizes, condition, weight):
    group = sizes[WIDE] * sizes[TENSOR]
    width = weight.shape[1]
    return pl.pallas_call(
        functools.partial(modulation_kernel, sizes),
        name="modulation",
        out_shape=jax.ShapeDtypeStruct((group, 1, width), F32),
        in_specs=[VM, VM],
        out_specs=VM,
        scratch_shapes=[
            VMEM((1, 1, width), F32),
            VMEM((group, 1, width), F32),
            DMA((group - 1,)),
            DMA((group - 1,)),
        ],
        compiler_params=pltpu.CompilerParams(collective_id=0, has_side_effects=True),
    )(condition, weight)


def forward_kernel(
    sizes,
    frames,
    vectors,
    key_live,
    word_live,
    spread,
    prompt,
    *refs,
):
    weights = refs[:12]
    (
        h1, q1, side, o1, h2, q2, o2, h3, q3, kv3, o3, h4,
        a1_own, a2_own, x3_own, n2_own, n3_own, n4_own, inverses,
    ) = refs[12:31]
    (
        full, full_prompt, wide_context, partial, landing, residual, group_mask,
        local_sems, side_send, side_recv, kv_send, kv_recv, ring_send, ring_recv,
    ) = refs[31:]
    place = Place(sizes)
    peers = sizes[TENSOR] - 1
    frame_count, chunks, cols, width = frames.shape
    rows = frame_count * cols
    quarter = rows // sizes[TENSOR]
    own_frames = frame_count // sizes[TENSOR]
    heads = spread.shape[1] // LANES
    scale = 1.0 / math.sqrt(HEAD_DIM)
    ring = Ring(place, quarter, ring_send, ring_recv)
    greet([place.sibling()] + [place.over_tensor(step) for step in range(1, peers + 1)])

    def fetch(i):
        half = weights[i].shape[0]
        spot = pl.ds(pl.multiple_of(place.w * half, half), half)
        target = full.at[i, spot] if i < 10 else full_prompt.at[i - 10, spot]
        local = pltpu.make_async_copy(weights[i], target, local_sems.at[i])
        local.start()
        return [local, send(weights[i], target, side_send.at[i], side_recv.at[i], place.sibling())]

    pending = {i: fetch(i) for i in (0, 1, 2, 3)}

    def ready(*which):
        for i in which:
            wait_all(pending.pop(i))

    @pl.loop(0, frame_count)
    def _(f):
        for r in range(chunks):
            normed, _ = norm_tile(frames[f, r].astype(F32))
            h1[pl.ds(pl.multiple_of(r * rows + f * cols, cols), cols)] = (
                normed * vectors[1:2] + vectors[0:1]
            ).astype(BF16)

    row_id = lax.broadcasted_iota(jnp.int32, (rows, rows), 0)
    col_id = lax.broadcasted_iota(jnp.int32, (rows, rows), 1)
    group_mask[...] = jnp.where(
        lax.rem(row_id, cols) == lax.rem(col_id, cols),
        jnp.broadcast_to(key_live[0:1], (rows, rows)),
        0.0,
    )

    def project(source, spot, weight, out, index):
        narrow = dot(source[spot], full[weight]).astype(BF16)
        out[index, spot] = dot(narrow, spread[...]).astype(BF16)

    def chunk_rows(r):
        return pl.ds(r * rows, rows)

    ready(0, 1, 2)

    @pl.loop(0, 3)
    def _(i):
        for r in range(chunks):
            project(h1, chunk_rows(r), i, q1, i)

    kv_copies = [
        send(q1.at[1 + j], side.at[j], kv_send.at[j], kv_recv.at[j], place.sibling())
        for j in range(2)
    ]
    for i in (4, 5, 6, 7, 10, 11, 8, 9):
        pending[i] = fetch(i)
    wait_all(kv_copies)

    @pl.loop(0, frame_count)
    def _(f):
        spots = [
            pl.ds(pl.multiple_of(r * rows + f * cols, cols), cols) for r in range(chunks)
        ]
        queries = jnp.concatenate([q1[0, spot] for spot in spots], 0)
        keys = jnp.concatenate(
            [q1[1, spot] for spot in spots] + [side[0, spot] for spot in spots], 0
        )
        values = jnp.concatenate(
            [q1[2, spot] for spot in spots] + [side[1, spot] for spot in spots], 0
        )
        for h in range(heads):
            lanes = slice(h * LANES, (h + 1) * LANES)
            attend = softmax_tile(dot_tr(queries[:, lanes], keys[:, lanes]) * scale)
            context = dot(attend.astype(BF16), values[:, lanes]).astype(BF16)
            for r in range(chunks):
                wide_context[spots[r], lanes] = context[r * cols : (r + 1) * cols]

    def emit(r, out, weight):
        spot = chunk_rows(r)
        out[spot] = dot_tr(wide_context[spot], spread[...]).astype(BF16)
        partial[r] = dot_tr(out[spot], full[weight]).astype(BF16)
        return ring.scatter(partial.at[r], landing.at[ring.used])

    own = pl.ds(pl.multiple_of(place.t * quarter, quarter), quarter)

    def own_rows(r):
        return pl.ds(pl.multiple_of(r * rows + place.t * quarter, quarter), quarter)

    def kept(r):
        return pl.ds(r * quarter, quarter)

    def branch(r, stage):
        return summed(partial.at[r], landing.at[stage], own, peers)

    ready(3)
    scatters = []
    for r in range(chunks):
        scatters.append((ring.used, emit(r, o1, 3)))

    ready(10, 11)
    kv3[...] = jnp.zeros_like(kv3)
    for j in range(2):
        narrow = dot(prompt[...], full_prompt[j]).astype(BF16)
        kv3[j, 0 : prompt.shape[0]] = dot(narrow, spread[...]).astype(BF16)

    gathers = []
    for r in range(chunks):
        stage, copies = scatters[r]
        wait_all(copies)
        branch_one = branch(r, stage)
        a1_own[kept(r)] = branch_one
        x_own = frames[pl.ds(place.t * own_frames, own_frames), r].reshape(quarter, width)
        after = x_own.astype(F32) + vectors[2:3] * branch_one
        normed, inverse = norm_tile(after)
        residual[kept(r)] = after
        n2_own[kept(r)] = normed
        inverses[0, kept(r)] = jnp.broadcast_to(inverse, (quarter, LANES))
        h2[own_rows(r)] = (normed * vectors[6:7]).astype(BF16)
        gathers.append(ring.gather(h2.at[own_rows(r)]))

    ready(4, 5, 6, 7)
    scatters = []
    for r in range(chunks):
        wait_all(gathers[r])
        spot = chunk_rows(r)

        @pl.loop(0, 3)
        def _(i):
            project(h2, spot, 4 + i, q2, i)

        @pl.loop(0, heads)
        def _(h):
            lanes = pl.ds(pl.multiple_of(h * LANES, LANES), LANES)
            scores = dot_tr(q2[0, spot, lanes], q2[1, spot, lanes]) * scale
            attend = softmax_tile(jnp.where(group_mask[...] > 0.5, scores, NEGATIVE))
            wide_context[spot, lanes] = dot(attend.astype(BF16), q2[2, spot, lanes]).astype(BF16)

        scatters.append((ring.used, emit(r, o2, 7)))

    gathers = []
    for r in range(chunks):
        stage, copies = scatters[r]
        wait_all(copies)
        branch_two = branch(r, stage)
        a2_own[kept(r)] = branch_two
        after = residual[kept(r)] + vectors[7:8] * branch_two
        normed, inverse = norm_tile(after)
        residual[kept(r)] = after
        n3_own[kept(r)] = normed
        inverses[1, kept(r)] = jnp.broadcast_to(inverse, (quarter, LANES))
        h3[own_rows(r)] = (normed * vectors[8:9]).astype(BF16)
        gathers.append(ring.gather(h3.at[own_rows(r)]))

    ready(8, 9)
    scatters = []
    for r in range(chunks):
        wait_all(gathers[r])
        spot = chunk_rows(r)
        narrow = dot(h3[spot], full[8]).astype(BF16)
        q3[spot] = dot(narrow, spread[...]).astype(BF16)

        @pl.loop(0, heads)
        def _(h):
            lanes = pl.ds(pl.multiple_of(h * LANES, LANES), LANES)
            scores = dot_tr(q3[spot, lanes], kv3[0, :, lanes]) * scale
            attend = softmax_tile(jnp.where(word_live[0:1] > 0.5, scores, NEGATIVE))
            wide_context[spot, lanes] = dot(attend.astype(BF16), kv3[1, :, lanes]).astype(BF16)

        scatters.append((ring.used, emit(r, o3, 9)))

    gathers = []
    for r in range(chunks):
        stage, copies = scatters[r]
        wait_all(copies)
        after = residual[kept(r)] + branch(r, stage)
        normed, inverse = norm_tile(after)
        x3_own[kept(r)] = after
        n4_own[kept(r)] = normed
        inverses[2, kept(r)] = jnp.broadcast_to(inverse, (quarter, LANES))
        h4[own_rows(r)] = (normed * vectors[4:5] + vectors[3:4]).astype(BF16)
        gathers.append(ring.gather(h4.at[own_rows(r)]))
    for copies in gathers:
        wait_all(copies)


def forward_call(sizes, frames, vectors, key_live, word_live, spread, prompt, weights):
    frame_count, chunks, cols, width = frames.shape
    rows = frame_count * cols
    tokens = rows * chunks
    head_width, padded = spread.shape
    quarter = rows // sizes[TENSOR]
    peers = sizes[TENSOR] - 1
    kept = quarter * chunks
    full_rows = weights[0].shape[0] * sizes[WIDE]
    prompt_width = weights[10].shape[0] * sizes[WIDE]
    stages = 6 * chunks
    s = jax.ShapeDtypeStruct
    wide_act, heads_act = s((tokens, width), BF16), s((tokens, head_width), BF16)
    triple, own = s((3, tokens, padded), BF16), s((kept, width), F32)
    outs = [
        wide_act, triple, s((2, tokens, padded), BF16), heads_act,
        wide_act, triple, heads_act,
        wide_act, s((tokens, padded), BF16), s((2, LANES, padded), BF16), heads_act,
        wide_act, own, own, own, own, own, own, s((3, kept, LANES), F32),
    ]
    return pl.pallas_call(
        functools.partial(forward_kernel, sizes),
        name="forward",
        out_shape=outs,
        in_specs=[VM] * 6 + [ANY] * 12,
        out_specs=[VM] * len(outs),
        scratch_shapes=[
            VMEM((10, full_rows, head_width), BF16),
            VMEM((2, prompt_width, head_width), BF16),
            VMEM((tokens, padded), BF16),
            VMEM((chunks, rows, width), BF16),
            VMEM((stages, peers, quarter, width), BF16),
            VMEM((kept, width), F32),
            VMEM((rows, rows), F32),
            DMA((12,)), DMA((12,)), DMA((12,)), DMA((2,)), DMA((2,)),
            DMA((stages, peers)), DMA((stages, peers)),
        ],
        compiler_params=pltpu.CompilerParams(
            collective_id=1, has_side_effects=True, vmem_limit_bytes=60 << 20
        ),
    )(frames, vectors, key_live, word_live, spread, prompt, *weights)


def prepare(sizes, frames, timestep, clip_lengths, text_lengths, modulation_weight,
            modulation_bias, time_gain, time_gate, cross_gain, head_width):
    frame_count, width = frames.shape[1], frames.shape[4]
    cols = frames.shape[3]
    half_width = width // 2
    frequency = jnp.exp(-math.log(10000.0) * jnp.arange(half_width, dtype=F32) / half_width)
    angles = timestep[0].astype(F32) * frequency
    condition = jax.nn.silu(jnp.concatenate([jnp.cos(angles), jnp.sin(angles)])).astype(BF16)
    mine = lax.dynamic_slice_in_dim(
        condition, lax.axis_index(WIDE) * modulation_weight.shape[0], modulation_weight.shape[0]
    )
    parts = modulation_call(
        sizes, jnp.broadcast_to(mine[None], (16, mine.shape[0])), modulation_weight
    )
    parts = parts.reshape(sizes[WIDE], -1)
    modulation = (jnp.sum(parts, 0) + modulation_bias).reshape(6, width)
    vectors = jnp.stack(
        [
            modulation[0], 1.0 + modulation[1], modulation[2],
            modulation[3], 1.0 + modulation[4], modulation[5],
            time_gain, jnp.tanh(time_gate), cross_gain,
        ]
    )
    live = jnp.arange(frame_count) < clip_lengths[0]
    key_live = jnp.repeat(live, cols).astype(F32)[None]
    word_live = (jnp.arange(LANES) < text_lengths[0]).astype(F32)[None]
    heads = head_width // HEAD_DIM
    padded = jnp.arange(heads * LANES)
    source = jnp.where(
        padded % LANES < HEAD_DIM, padded // LANES * HEAD_DIM + padded % LANES, -1
    )
    spread = (jnp.arange(head_width)[:, None] == source[None]).astype(BF16)
    return condition, vectors, live, key_live, word_live, spread


def over_columns(width, tile, body):
    whole = width // tile

    @pl.loop(0, whole)
    def _(j):
        body(pl.ds(pl.multiple_of(j * tile, tile), tile))

    if width % tile:
        body(pl.ds(whole * tile, width % tile))


GELU_C = math.sqrt(2.0 / math.pi)


def mlp_kernel(
    sizes,
    h4, cotangent, vectors, live, n4_own, inverses, x3_own, up_half, down_half,
    output, e3, g3_own, up_grad, down_grad, sums,
    up, down, e4, hidden, pre_grad, partial, landing,
    local_sems, side_send, side_recv, ring_send, ring_recv,
):
    place = Place(sizes)
    peers = sizes[TENSOR] - 1
    frame_count, chunks, cols, width = cotangent.shape
    rows = frame_count * cols
    quarter = rows // sizes[TENSOR]
    own_frames = frame_count // sizes[TENSOR]
    ring = Ring(place, quarter, ring_send, ring_recv)
    greet([place.sibling()] + [place.over_tensor(step) for step in range(1, peers + 1)])
    copies = []
    for i, (source, target) in enumerate(((up_half, up), (down_half, down))):
        half = source.shape[0]
        spot = pl.ds(pl.multiple_of(place.w * half, half), half)
        local = pltpu.make_async_copy(source, target.at[spot], local_sems.at[i])
        local.start()
        copies += [
            local,
            send(source, target.at[spot], side_send.at[i], side_recv.at[i], place.sibling()),
        ]

    @pl.loop(0, frame_count)
    def _(f):
        for r in range(chunks):
            e4[pl.ds(pl.multiple_of(r * rows + f * cols, cols), cols)] = (
                vectors[5:6] * (cotangent[f, r].astype(F32) * live[f, 0:1, 0:1])
            ).astype(BF16)

    wait_all(copies)
    scatters = []
    for r in range(chunks):
        spot = pl.ds(r * rows, rows)

        def act(lanes):
            pre = dot(h4[spot], up[:, lanes])
            grad = dot(e4[spot], down[:, lanes])
            inner = jnp.tanh(GELU_C * (pre + 0.044715 * pre * pre * pre))
            gate = 0.5 * (1.0 + inner)
            hidden[spot, lanes] = (pre * gate).astype(BF16)
            slope = gate + 0.5 * pre * (1.0 - inner * inner) * (
                GELU_C * (1.0 + 3.0 * 0.044715 * pre * pre)
            )
            pre_grad[spot, lanes] = (grad * slope).astype(BF16)

        over_columns(up.shape[1], 256, act)
        partial[r] = dot_tr(pre_grad[spot], up[...]).astype(BF16)
        scatters.append((ring.used, ring.scatter(partial.at[r], landing.at[ring.used])))

    for r in range(chunks):
        spot = pl.ds(r * rows, rows)
        partial[chunks + r] = dot_tr(hidden[spot], down[...]).astype(BF16)

    def down_tile(lanes):
        down_grad[:, lanes] = dot_outer(e4[...], hidden[:, lanes]).astype(BF16)

    def up_tile(lanes):
        up_grad[:, lanes] = dot_outer(h4[...], pre_grad[:, lanes]).astype(BF16)

    over_columns(up.shape[1], 256, down_tile)

    own = pl.ds(pl.multiple_of(place.t * quarter, quarter), quarter)
    own_spot = pl.ds(place.t * own_frames, own_frames)
    shift_sum = jnp.zeros((1, width), F32)
    scale_sum = jnp.zeros((1, width), F32)
    gate_sum = jnp.zeros((1, width), F32)

    def own_live(r):
        pieces = []
        for f in range(own_frames):
            pieces.append(
                jnp.broadcast_to(live[place.t * own_frames + f, 0:1, 0:1], (cols, 1))
            )
        return jnp.concatenate(pieces, 0)

    def own_upstream(r):
        return cotangent[own_spot, r].reshape(quarter, width).astype(F32) * own_live(r)

    gathers = []
    for r in range(chunks):
        kept = pl.ds(r * quarter, quarter)
        stage, copies = scatters[r]
        wait_all(copies)
        grad = summed(partial.at[r], landing.at[stage], own, peers)
        normed = n4_own[kept]
        shift_sum = shift_sum + jnp.sum(grad, 0, keepdims=True)
        scale_sum = scale_sum + jnp.sum(grad * normed, 0, keepdims=True)
        upstream = own_upstream(r) + norm_pull(
            normed, inverses[2, kept][:, 0:1], grad * vectors[4:5]
        )
        g3_own[kept] = upstream
        rows_own = pl.ds(pl.multiple_of(r * rows + place.t * quarter, quarter), quarter)
        e3[rows_own] = upstream.astype(BF16)
        gathers.append(ring.gather(e3.at[rows_own]))
    scatters = []
    for r in range(chunks):
        scatters.append((ring.used, ring.scatter(partial.at[chunks + r], landing.at[ring.used])))

    over_columns(up.shape[1], 256, up_tile)

    for r in range(chunks):
        kept = pl.ds(r * quarter, quarter)
        stage, copies = scatters[r]
        wait_all(copies)
        branch = summed(partial.at[chunks + r], landing.at[stage], own, peers)
        gate_sum = gate_sum + jnp.sum(own_upstream(r) * branch, 0, keepdims=True)
        after = (x3_own[kept] + vectors[5:6] * branch) * own_live(r)
        output[own_spot, r] = after.astype(BF16).reshape(own_frames, cols, width)
        gathers.append(ring.gather(output.at[own_spot, r]))
    sums[...] = jnp.concatenate(
        [shift_sum, scale_sum, gate_sum, jnp.zeros((5, width), F32)], 0
    )
    for copies in gathers:
        wait_all(copies)


def mlp_call(sizes, h4, cotangent, vectors, live, n4_own, inverses, x3_own, up_half, down_half):
    frame_count, chunks, cols, width = cotangent.shape
    rows = frame_count * cols
    tokens = rows * chunks
    quarter = rows // sizes[TENSOR]
    peers = sizes[TENSOR] - 1
    hidden = up_half.shape[1]
    s = jax.ShapeDtypeStruct
    stages = 4 * chunks
    live = jnp.broadcast_to(live.astype(F32)[:, None, None], (frame_count, 8, LANES))
    outs = [
        s(cotangent.shape, BF16), s((tokens, width), BF16), s((quarter * chunks, width), F32),
        s((width, hidden), BF16), s((width, hidden), BF16), s((8, width), F32),
    ]
    return pl.pallas_call(
        functools.partial(mlp_kernel, sizes),
        name="mlp",
        out_shape=outs,
        in_specs=[VM] * 7 + [ANY] * 2,
        out_specs=[VM] * len(outs),
        scratch_shapes=[
            VMEM((width, hidden), BF16), VMEM((width, hidden), BF16),
            VMEM((tokens, width), BF16), VMEM((tokens, hidden), BF16),
            VMEM((tokens, hidden), BF16),
            VMEM((2 * chunks, rows, width), BF16),
            VMEM((stages, peers, quarter, width), BF16),
            DMA((2,)), DMA((2,)), DMA((2,)), DMA((stages, peers)), DMA((stages, peers)),
        ],
        compiler_params=pltpu.CompilerParams(
            collective_id=2, has_side_effects=True, vmem_limit_bytes=60 << 20
        ),
    )(h4, cotangent, vectors, live, n4_own, inverses, x3_own, up_half, down_half)


class Reducer:
    def __init__(self, place, source, mine, merged, received, sems):
        self.place, self.source = place, source
        self.mine, self.merged, self.received = mine, merged, received
        self.local, self.side_send, self.side_recv, self.far_send, self.far_recv = sems
        self.clips = place.sizes[NARROW]
        self.block = mine.shape[1]

    def rows(self, clip, core):
        start = (clip * self.place.sizes[WIDE] + core) * self.block
        return pl.ds(pl.multiple_of(start, self.block), self.block)

    def split(self):
        self.copies = []
        for clip in range(self.clips):
            local = pltpu.make_async_copy(
                self.source.at[self.rows(clip, self.place.w)],
                self.mine.at[clip],
                self.local.at[clip],
            )
            local.start()
            self.copies += [
                local,
                send(
                    self.source.at[self.rows(clip, 1 - self.place.w)],
                    self.merged.at[clip],
                    self.side_send.at[clip],
                    self.side_recv.at[clip],
                    self.place.sibling(),
                ),
            ]

    def spread(self):
        wait_all(self.copies)
        self.copies = []

        @pl.loop(0, self.clips)
        def _(clip):
            self.merged[clip] = (
                self.merged[clip].astype(F32) + self.mine[clip].astype(F32)
            ).astype(BF16)

        for step in (3, 1, 2) if self.clips == 4 else range(1, self.clips):
            peer = lax.rem(self.place.n + step, self.clips)
            self.copies.append(
                send(
                    self.merged.at[peer],
                    self.received.at[step - 1],
                    self.far_send.at[step - 1],
                    self.far_recv.at[step - 1],
                    self.place.over_narrow(peer),
                )
            )

    def finish(self, out):
        wait_all(self.copies)
        total = self.merged[self.place.n].astype(F32)
        for step in range(self.clips - 1):
            total = total + self.received[step].astype(F32)
        out[...] = total


def reducer_scratch(sizes, jobs, block, width):
    clips = sizes[NARROW]
    return [
        VMEM((jobs, clips, block, width), BF16),
        VMEM((jobs, clips, block, width), BF16),
        VMEM((jobs, clips - 1, block, width), BF16),
        DMA((jobs, clips)), DMA((jobs, clips)), DMA((jobs, clips)),
        DMA((jobs, clips - 1)), DMA((jobs, clips - 1)),
    ]


def reducers(place, sources, scratch):
    mine, merged, received, *sems = scratch
    return [
        Reducer(
            place, source, mine.at[i], merged.at[i], received.at[i], [sem.at[i] for sem in sems]
        )
        for i, source in enumerate(sources)
    ]


def all_partners(place):
    sizes = place.sizes
    return (
        [place.sibling()]
        + [place.over_tensor(step) for step in range(1, sizes[TENSOR])]
        + [
            place.over_narrow(lax.rem(place.n + step, sizes[NARROW]))
            for step in range(1, sizes[NARROW])
        ]
    )


def fetch_weights(place, halves, full, local_sems, side_send, side_recv):
    pending = []
    for i, half_ref in enumerate(halves):
        half = half_ref.shape[0]
        spot = pl.ds(pl.multiple_of(place.w * half, half), half)
        local = pltpu.make_async_copy(half_ref, full.at[i, spot], local_sems.at[i])
        local.start()
        pending.append(
            [
                local,
                send(half_ref, full.at[i, spot], side_send.at[i], side_recv.at[i], place.sibling()),
            ]
        )
    return pending


def attention_pull(queries, keys, values, context_grad, mask, scale):
    scores = dot_tr(queries, keys) * scale
    if mask is not None:
        scores = jnp.where(mask, scores, NEGATIVE)
    attend = softmax_tile(scores)
    attend_grad = dot_tr(context_grad, values)
    score_grad = (
        attend * (attend_grad - jnp.sum(attend * attend_grad, -1, keepdims=True))
    ).astype(BF16)
    return (
        dot(score_grad, keys) * scale,
        dot_outer(score_grad, queries) * scale,
        dot_outer(attend.astype(BF16), context_grad),
    )


def back_kernel(
    sizes,
    e3, g3_own, n3_own, n2_own, inverses, a2_own, vectors, key_live, word_live, spread,
    h3, q3, kv3, o3, h2, q2, o2,
    *refs,
):
    halves, gradients = refs[:6], refs[6:8]
    g1_own, e1, query_out, value_out, word_grads, up_out, down_out, sums = refs[8:16]
    (
        full, wide_grad, wide_parts, narrow_parts, word_sums, word_side, e2, partial, landing,
        group_mask, local_sems, side_send, side_recv, word_send, word_recv, ring_send, ring_recv,
    ) = refs[16:33]
    place = Place(sizes)
    peers = sizes[TENSOR] - 1
    tokens, width = e3.shape
    chunks = tokens // group_mask.shape[0]
    rows = tokens // chunks
    cols = sizes[COLS]
    quarter = rows // sizes[TENSOR]
    heads = spread.shape[1] // LANES
    scale = 1.0 / math.sqrt(HEAD_DIM)
    ring = Ring(place, quarter, ring_send, ring_recv)
    greet(all_partners(place))
    pending = fetch_weights(place, halves, full, local_sems, side_send, side_recv)
    feed = reducers(place, gradients, refs[33:])
    for job in feed:
        job.split()

    row_id = lax.broadcasted_iota(jnp.int32, (rows, rows), 0)
    col_id = lax.broadcasted_iota(jnp.int32, (rows, rows), 1)
    group_mask[...] = jnp.where(
        lax.rem(row_id, cols) == lax.rem(col_id, cols),
        jnp.broadcast_to(key_live[0:1], (rows, rows)),
        0.0,
    )
    own = pl.ds(pl.multiple_of(place.t * quarter, quarter), quarter)

    def chunk_rows(r):
        return pl.ds(r * rows, rows)

    def own_rows(r):
        return pl.ds(pl.multiple_of(r * rows + place.t * quarter, quarter), quarter)

    def kept(r):
        return pl.ds(r * quarter, quarter)

    def head_lanes(h):
        return pl.ds(pl.multiple_of(h * LANES, LANES), LANES)

    def context_grad(source, spot, weight):
        narrow = dot(source[spot], full[weight]).astype(BF16)
        wide_grad[spot] = dot(narrow, spread[...]).astype(BF16)

    word_sums[...] = jnp.zeros_like(word_sums)
    wait_all(pending[0])
    wait_all(pending[1])
    scatters = []
    for r in range(chunks):
        spot = chunk_rows(r)
        context_grad(e3, spot, 0)

        @pl.loop(0, heads)
        def _(h):
            lanes = head_lanes(h)
            query_grad, key_grad, value_grad = attention_pull(
                q3[spot, lanes], kv3[0, :, lanes], kv3[1, :, lanes], wide_grad[spot, lanes],
                word_live[0:1] > 0.5, scale,
            )
            wide_parts[0, spot, lanes] = query_grad.astype(BF16)
            word_sums[0, :, lanes] += key_grad
            word_sums[1, :, lanes] += value_grad

        narrow_parts[0, spot] = dot_tr(wide_parts[0, spot], spread[...]).astype(BF16)
        partial[r] = dot_tr(narrow_parts[0, spot], full[1]).astype(BF16)
        scatters.append((ring.used, ring.scatter(partial.at[r], landing.at[ring.used])))
    word_copy = send(word_sums, word_side, word_send, word_recv, place.sibling())
    value_out[0] = dot_outer(e3[...], o3[...]).astype(BF16)
    query_out[0] = dot_outer(h3[...], narrow_parts[0]).astype(BF16)
    for job in feed:
        job.spread()

    gain_sum = jnp.zeros((1, width), F32)
    gate_sum = jnp.zeros((1, width), F32)
    time_sum = jnp.zeros((1, width), F32)
    gathers = []
    for r in range(chunks):
        stage, copies = scatters[r]
        wait_all(copies)
        grad = summed(partial.at[r], landing.at[stage], own, peers)
        normed = n3_own[kept(r)]
        gain_sum = gain_sum + jnp.sum(grad * normed, 0, keepdims=True)
        upstream = g3_own[kept(r)] + norm_pull(
            normed, inverses[1, kept(r)][:, 0:1], grad * vectors[8:9]
        )
        g1_own[kept(r)] = upstream
        gate_sum = gate_sum + jnp.sum(upstream * a2_own[kept(r)], 0, keepdims=True)
        e2[own_rows(r)] = (vectors[7:8] * upstream).astype(BF16)
        gathers.append(ring.gather(e2.at[own_rows(r)]))
    word_copy.wait()
    for j in range(2):
        word_grads[j] = dot_tr(
            (word_sums[j] + word_side[j]).astype(BF16), spread[...]
        ).astype(BF16)

    for copies in pending[2:]:
        wait_all(copies)
    scatters = []
    for r in range(chunks):
        spot = chunk_rows(r)
        wait_all(gathers[r])
        context_grad(e2, spot, 2)

        @pl.loop(0, heads)
        def _(h):
            lanes = head_lanes(h)
            parts = attention_pull(
                q2[0, spot, lanes], q2[1, spot, lanes], q2[2, spot, lanes],
                wide_grad[spot, lanes], group_mask[...] > 0.5, scale,
            )
            for i in range(3):
                wide_parts[i, spot, lanes] = parts[i].astype(BF16)

        @pl.loop(0, 3)
        def _(i):
            narrow_parts[i, spot] = dot_tr(wide_parts[i, spot], spread[...]).astype(BF16)

        total = dot_tr(narrow_parts[0, spot], full[3])
        for i in (1, 2):
            total = total + dot_tr(narrow_parts[i, spot], full[3 + i])
        partial[r] = total.astype(BF16)
        scatters.append((ring.used, ring.scatter(partial.at[r], landing.at[ring.used])))
    value_out[1] = dot_outer(e2[...], o2[...]).astype(BF16)

    @pl.loop(0, 3)
    def _(i):
        query_out[1 + i] = dot_outer(h2[...], narrow_parts[i]).astype(BF16)

    gathers = []
    for r in range(chunks):
        stage, copies = scatters[r]
        wait_all(copies)
        grad = summed(partial.at[r], landing.at[stage], own, peers)
        normed = n2_own[kept(r)]
        time_sum = time_sum + jnp.sum(grad * normed, 0, keepdims=True)
        upstream = g1_own[kept(r)] + norm_pull(
            normed, inverses[0, kept(r)][:, 0:1], grad * vectors[6:7]
        )
        g1_own[kept(r)] = upstream
        e1[own_rows(r)] = (vectors[2:3] * upstream).astype(BF16)
        gathers.append(ring.gather(e1.at[own_rows(r)]))
    feed[0].finish(up_out)
    feed[1].finish(down_out)
    sums[...] = jnp.concatenate([gain_sum, gate_sum, time_sum, jnp.zeros((5, width), F32)], 0)
    for copies in gathers:
        wait_all(copies)


def back_call(sizes, cols, acts, halves, gradients):
    e3, spread = acts[0], acts[9]
    tokens, width = e3.shape
    key_live = acts[7]
    rows = key_live.shape[1]
    chunks = tokens // rows
    quarter = rows // sizes[TENSOR]
    peers = sizes[TENSOR] - 1
    head_width, padded = spread.shape
    full_rows = halves[0].shape[0] * sizes[WIDE]
    hidden = gradients[0].shape[1]
    block = width // (sizes[NARROW] * sizes[WIDE])
    s = jax.ShapeDtypeStruct
    stages = 4 * chunks
    outs = [
        s((quarter * chunks, width), F32), s((tokens, width), BF16),
        s((4, width, head_width), BF16), s((2, width, head_width), BF16),
        s((2, LANES, head_width), BF16),
        s((block, hidden), F32), s((block, hidden), F32), s((8, width), F32),
    ]
    return pl.pallas_call(
        functools.partial(back_kernel, {**sizes, COLS: cols}),
        name="back",
        out_shape=outs,
        in_specs=[VM] * len(acts) + [ANY] * 8,
        out_specs=[VM] * len(outs),
        scratch_shapes=[
            VMEM((6, full_rows, head_width), BF16),
            VMEM((tokens, padded), BF16),
            VMEM((3, tokens, padded), BF16),
            VMEM((3, tokens, head_width), BF16),
            VMEM((2, LANES, padded), F32), VMEM((2, LANES, padded), F32),
            VMEM((tokens, width), BF16),
            VMEM((chunks, rows, width), BF16),
            VMEM((stages, peers, quarter, width), BF16),
            VMEM((rows, rows), F32),
            DMA((6,)), DMA((6,)), DMA((6,)), DMA(()), DMA(()),
            DMA((stages, peers)), DMA((stages, peers)),
        ]
        + reducer_scratch(sizes, 2, block, hidden),
        compiler_params=pltpu.CompilerParams(
            collective_id=3, has_side_effects=True, vmem_limit_bytes=60 << 20
        ),
    )(*acts, *halves, *gradients)


def space_kernel(
    sizes,
    e1, g1_own, frames, a1_own, vectors, spread, h1, q1, side, o1, prompt, word_grads,
    *refs,
):
    halves, early_value, early_query = refs[:4], refs[4], refs[5]
    frames_grad, early_out, space_out, prompt_out, sums = refs[6:11]
    (
        full, wide_grad, wide_parts, narrow_parts, key_sums, side_out, side_in, space_grads,
        words, word_parts, partial, landing,
        local_sems, side_send, side_recv, key_send, key_recv, word_send, word_recv,
        ring_send, ring_recv,
    ) = refs[11:32]
    place = Place(sizes)
    peers = sizes[TENSOR] - 1
    clips = sizes[NARROW]
    frame_count, chunks, cols, width = frames.shape
    rows = frame_count * cols
    tokens = rows * chunks
    quarter = rows // sizes[TENSOR]
    own_frames = frame_count // sizes[TENSOR]
    heads = spread.shape[1] // LANES
    half = chunks * cols
    scale = 1.0 / math.sqrt(HEAD_DIM)
    ring = Ring(place, quarter, ring_send, ring_recv)
    greet(all_partners(place))
    pending = fetch_weights(place, halves, full, local_sems, side_send, side_recv)
    early_scratch, late_scratch = refs[32:40], refs[40:48]
    sources = [early_value.at[0], early_query.at[0], early_value.at[1]] + [
        early_query.at[1 + i] for i in range(3)
    ]
    early = reducers(place, sources, early_scratch)
    late = reducers(place, [space_grads.at[i] for i in range(4)], late_scratch)
    block = words.shape[2]
    word_copies = []
    for step in range(1, clips):
        peer = lax.rem(place.n + step, clips)
        lanes = pl.ds(
            pl.multiple_of((peer * sizes[WIDE] + place.w) * block, block), block
        )
        for j, (source, target) in enumerate(
            ((prompt.at[:, lanes], words.at[step]), (word_grads, word_parts.at[step]))
        ):
            word_copies.append(
                send(
                    source, target, word_send.at[step - 1, j], word_recv.at[step - 1, j],
                    place.over_narrow(peer),
                )
            )
    for job in early:
        job.split()
    mine = pl.ds(pl.multiple_of((place.n * sizes[WIDE] + place.w) * block, block), block)
    words[0] = prompt[:, mine]
    word_parts[0] = word_grads[...]
    own = pl.ds(pl.multiple_of(place.t * quarter, quarter), quarter)
    own_spot = pl.ds(place.t * own_frames, own_frames)

    for copies in pending:
        wait_all(copies)
    for r in range(chunks):
        spot = pl.ds(r * rows, rows)
        narrow = dot(e1[spot], full[0]).astype(BF16)
        wide_grad[spot] = dot(narrow, spread[...]).astype(BF16)

    @pl.loop(0, frame_count)
    def _(f):
        spots = [
            pl.ds(pl.multiple_of(r * rows + f * cols, cols), cols) for r in range(chunks)
        ]
        queries = jnp.concatenate([q1[0, spot] for spot in spots], 0)
        grads = jnp.concatenate([wide_grad[spot] for spot in spots], 0)
        keys = jnp.concatenate(
            [q1[1, spot] for spot in spots] + [side[0, spot] for spot in spots], 0
        )
        values = jnp.concatenate(
            [q1[2, spot] for spot in spots] + [side[1, spot] for spot in spots], 0
        )
        for h in range(heads):
            lanes = slice(h * LANES, (h + 1) * LANES)
            parts = attention_pull(
                queries[:, lanes], keys[:, lanes], values[:, lanes], grads[:, lanes], None, scale
            )
            for r in range(chunks):
                here = slice(r * cols, (r + 1) * cols)
                there = slice(half + r * cols, half + (r + 1) * cols)
                wide_parts[0, spots[r], lanes] = parts[0][here].astype(BF16)
                for j in range(2):
                    key_sums[j, spots[r], lanes] = parts[1 + j][here]
                    side_out[j, spots[r], lanes] = parts[1 + j][there].astype(BF16)

    key_copy = send(side_out, side_in, key_send, key_recv, place.sibling())
    for job in early:
        job.spread()
    space_grads[0] = dot_outer(e1[...], o1[...]).astype(BF16)
    narrow_parts[0] = dot_tr(wide_parts[0], spread[...]).astype(BF16)
    key_copy.wait()
    for j in range(2):
        wide_parts[1 + j] = (key_sums[j] + side_in[j].astype(F32)).astype(BF16)
        narrow_parts[1 + j] = dot_tr(wide_parts[1 + j], spread[...]).astype(BF16)
    scatters = []
    for r in range(chunks):
        spot = pl.ds(r * rows, rows)
        total = dot_tr(narrow_parts[0, spot], full[1])
        for i in (1, 2):
            total = total + dot_tr(narrow_parts[i, spot], full[1 + i])
        partial[r] = total.astype(BF16)
        scatters.append((ring.used, ring.scatter(partial.at[r], landing.at[ring.used])))

    @pl.loop(0, 3)
    def _(i):
        space_grads[1 + i] = dot_outer(h1[...], narrow_parts[i]).astype(BF16)

    for job in late:
        job.split()
    wait_all(word_copies)
    for j in range(2):
        total = dot_outer(words[0], word_parts[0, j, 0 : prompt.shape[0]])
        for step in range(1, clips):
            total = total + dot_outer(words[step], word_parts[step, j, 0 : prompt.shape[0]])
        prompt_out[j] = total
    for job in late:
        job.spread()

    gate_sum = jnp.zeros((1, width), F32)
    shift_sum = jnp.zeros((1, width), F32)
    scale_sum = jnp.zeros((1, width), F32)
    gathers = []
    for r in range(chunks):
        kept = pl.ds(r * quarter, quarter)
        stage, copies = scatters[r]
        wait_all(copies)
        grad = summed(partial.at[r], landing.at[stage], own, peers)
        x_own = frames[own_spot, r].reshape(quarter, width).astype(F32)
        normed, inverse = norm_tile(x_own)
        gate_sum = gate_sum + jnp.sum(g1_own[kept] * a1_own[kept], 0, keepdims=True)
        shift_sum = shift_sum + jnp.sum(grad, 0, keepdims=True)
        scale_sum = scale_sum + jnp.sum(grad * normed, 0, keepdims=True)
        upstream = g1_own[kept] + norm_pull(normed, inverse, grad * vectors[1:2])
        frames_grad[own_spot, r] = upstream.astype(BF16).reshape(own_frames, cols, width)
        gathers.append(ring.gather(frames_grad.at[own_spot, r]))
    sums[...] = jnp.concatenate(
        [shift_sum, scale_sum, gate_sum, jnp.zeros((5, width), F32)], 0
    )
    for i, job in enumerate(early):
        job.finish(early_out.at[i])
    for i, job in enumerate(late):
        job.finish(space_out.at[i])
    for copies in gathers:
        wait_all(copies)


def space_call(sizes, acts, halves, gradients):
    frames, spread, prompt = acts[2], acts[5], acts[10]
    frame_count, chunks, cols, width = frames.shape
    rows = frame_count * cols
    tokens = rows * chunks
    quarter = rows // sizes[TENSOR]
    peers = sizes[TENSOR] - 1
    head_width, padded = spread.shape
    full_rows = halves[0].shape[0] * sizes[WIDE]
    parts = sizes[NARROW] * sizes[WIDE]
    block, word_block = width // parts, prompt.shape[1] // parts
    clips = sizes[NARROW]
    s = jax.ShapeDtypeStruct
    stages = 2 * chunks
    outs = [
        s(frames.shape, BF16), s((6, block, head_width), F32), s((4, block, head_width), F32),
        s((2, word_block, head_width), F32), s((8, width), F32),
    ]
    return pl.pallas_call(
        functools.partial(space_kernel, sizes),
        name="space",
        out_shape=outs,
        in_specs=[VM] * len(acts) + [ANY] * 6,
        out_specs=[VM] * len(outs),
        scratch_shapes=[
            VMEM((4, full_rows, head_width), BF16),
            VMEM((tokens, padded), BF16),
            VMEM((3, tokens, padded), BF16),
            VMEM((3, tokens, head_width), BF16),
            VMEM((2, tokens, padded), F32),
            VMEM((2, tokens, padded), BF16), VMEM((2, tokens, padded), BF16),
            VMEM((4, width, head_width), BF16),
            VMEM((clips, prompt.shape[0], word_block), BF16),
            VMEM((clips, 2, LANES, head_width), BF16),
            VMEM((chunks, rows, width), BF16),
            VMEM((stages, peers, quarter, width), BF16),
            DMA((4,)), DMA((4,)), DMA((4,)), DMA(()), DMA(()),
            DMA((clips - 1, 2)), DMA((clips - 1, 2)),
            DMA((stages, peers)), DMA((stages, peers)),
        ]
        + reducer_scratch(sizes, 6, block, head_width)
        + reducer_scratch(sizes, 4, block, head_width),
        compiler_params=pltpu.CompilerParams(
            collective_id=4, has_side_effects=True, vmem_limit_bytes=61 << 20
        ),
    )(*acts, *halves, *gradients)


def tail_kernel(sizes, rows, condition, merged, conditions, landing, total, send_sems, recv_sems,
                far_send, far_recv):
    place = Place(sizes)
    partners = []
    for dw in range(sizes[WIDE]):
        for dt in range(sizes[TENSOR]):
            if dw or dt:
                partners.append(
                    (
                        place.n,
                        lax.rem(place.w + dw, sizes[WIDE]),
                        lax.rem(place.t + dt, sizes[TENSOR]),
                    )
                )
    far = [
        place.over_narrow(lax.rem(place.n + step, sizes[NARROW]))
        for step in range(1, sizes[NARROW])
    ]
    greet(partners + far)
    copies = [
        send(rows, landing.at[i], send_sems.at[i], recv_sems.at[i], partner)
        for i, partner in enumerate(partners)
    ]
    cond_copies = [
        send(condition, conditions.at[place.n], far_send.at[i, 1], far_recv.at[i, 1], partner)
        for i, partner in enumerate(far)
    ]
    conditions[place.n] = condition[...]
    wait_all(copies)
    value = rows[...]
    for i in range(len(partners)):
        value = value + landing[i]
    total[...] = value
    far_copies = [
        send(total, merged.at[place.n], far_send.at[i, 0], far_recv.at[i, 0], partner)
        for i, partner in enumerate(far)
    ]
    merged[place.n] = value
    wait_all(cond_copies + far_copies)


def tail_call(sizes, rows, condition):
    clips = sizes[NARROW]
    group = sizes[WIDE] * sizes[TENSOR] - 1
    s = jax.ShapeDtypeStruct
    return pl.pallas_call(
        functools.partial(tail_kernel, sizes),
        name="tail",
        out_shape=[s((clips,) + rows.shape, F32), s((clips,) + condition.shape, F32)],
        in_specs=[VM, VM],
        out_specs=[VM, VM],
        scratch_shapes=[
            VMEM((group,) + rows.shape, F32), VMEM(rows.shape, F32),
            DMA((group,)), DMA((group,)), DMA((clips - 1, 2)), DMA((clips - 1, 2)),
        ],
        compiler_params=pltpu.CompilerParams(collective_id=5, has_side_effects=True),
    )(rows, condition)


def fused_on_device(
    sizes,
    frames, cotangent, prompt, timestep, clip_lengths, text_lengths,
    modulation_weight, modulation_bias, space_query, space_key, space_value, space_out,
    time_gain, time_query, time_key, time_value, time_out, time_gate, cross_gain, cross_query,
    prompt_key, prompt_value, cross_out, feed_up, feed_down,
):
    width = frames.shape[4]
    cols = frames.shape[3]
    head_width = space_query.shape[1]
    condition, vectors, live, key_live, word_live, spread = prepare(
        sizes, frames, timestep, clip_lengths, text_lengths, modulation_weight, modulation_bias,
        time_gain, time_gate, cross_gain, head_width,
    )
    (
        h1, q1, side, o1, h2, q2, o2, h3, q3, kv3, o3, h4,
        a1_own, a2_own, x3_own, n2_own, n3_own, n4_own, inverses,
    ) = forward_call(
        sizes, frames[0], vectors, key_live, word_live, spread, prompt[0],
        [space_query, space_key, space_value, space_out, time_query, time_key, time_value,
         time_out, cross_query, cross_out, prompt_key, prompt_value],
    )
    output, e3, g3_own, up_grad, down_grad, sums_four = mlp_call(
        sizes, h4, cotangent[0], vectors, live, n4_own, inverses, x3_own, feed_up, feed_down
    )
    g1_own, e1, query_out, value_out, word_grads, up_out, down_out, sums_two = back_call(
        sizes, cols,
        [e3, g3_own, n3_own, n2_own, inverses, a2_own, vectors, key_live, word_live, spread,
         h3, q3, kv3, o3, h2, q2, o2],
        [cross_out, cross_query, time_out, time_query, time_key, time_value],
        [up_grad, down_grad],
    )
    frames_grad, early_out, late_out, prompt_out, sums_one = space_call(
        sizes,
        [e1, g1_own, frames[0], a1_own, vectors, spread, h1, q1, side, o1, prompt[0], word_grads],
        [space_out, space_query, space_key, space_value],
        [value_out, query_out],
    )
    merged, conditions = tail_call(
        sizes,
        jnp.concatenate([sums_one[:3], sums_four[:3], sums_two[:3], jnp.zeros((7, width), F32)]),
        condition.astype(F32)[None],
    )
    part = lax.axis_index(NARROW) * sizes[WIDE] + lax.axis_index(WIDE)
    block = width // (sizes[NARROW] * sizes[WIDE])
    slice_width = modulation_weight.shape[1]
    pulled = merged[:, :6].reshape(sizes[NARROW], 6 * width)
    own_pulled = lax.dynamic_slice_in_dim(
        pulled, lax.axis_index(TENSOR) * slice_width, slice_width, 1
    )
    own_condition = lax.dynamic_slice_in_dim(conditions[:, 0], part * block, block, 1)
    modulation_weight_grad = jnp.sum(own_condition[:, :, None] * own_pulled[:, None], 0)
    summed_rows = jnp.sum(merged, 0)
    bias_block = 6 * block
    modulation_bias_grad = lax.dynamic_slice_in_dim(
        summed_rows[:6].reshape(6 * width), part * bias_block, bias_block
    )
    cross_gain_grad, gate_rows, time_gain_grad = (
        lax.dynamic_slice_in_dim(summed_rows[i], part * block, block) for i in (6, 7, 8)
    )
    own_gate = jnp.tanh(lax.dynamic_slice_in_dim(time_gate, part * block, block))
    time_gate_grad = gate_rows * (1.0 - own_gate * own_gate)
    return (
        output[None], frames_grad[None], modulation_weight_grad, modulation_bias_grad,
        late_out[1], late_out[2], late_out[3], late_out[0],
        time_gain_grad, early_out[3], early_out[4], early_out[5], early_out[2], time_gate_grad,
        cross_gain_grad, early_out[1], prompt_out[0], prompt_out[1], early_out[0],
        up_out, down_out,
    )


CONTRACT_LAST = (((1,), (1,)), ((), ()))
CONTRACT_FIRST = (((0,), (0,)), ((), ()))


def matmul(left, right):
    return jnp.dot(left, right, preferred_element_type=jnp.float32)


def matmul_tr(left, right):
    return lax.dot_general(left, right, CONTRACT_LAST, preferred_element_type=jnp.float32)


def outer_sum(left, right):
    return lax.dot_general(left, right, CONTRACT_FIRST, preferred_element_type=jnp.float32)


def norm_rows(values):
    center = values - jnp.mean(values, -1, keepdims=True)
    inverse = lax.rsqrt(jnp.mean(center * center, -1, keepdims=True) + EPSILON)
    return (center * inverse, inverse)


def norm_back(normed, inverse, incoming):
    return inverse * (
        incoming
        - jnp.mean(incoming, -1, keepdims=True)
        - normed * jnp.mean(incoming * normed, -1, keepdims=True)
    )


def over_heads(partial_sum):
    return lax.psum(partial_sum.astype(jnp.bfloat16), TENSOR).astype(jnp.float32)


def attend_forward(queries, key_rows, values, allowed, pattern, score_scale):
    scores = jnp.where(
        allowed,
        jnp.einsum(pattern[0], queries, key_rows, preferred_element_type=jnp.float32) * score_scale,
        NEGATIVE,
    )
    row_max = jnp.max(scores, -1, keepdims=True)
    exponent = jnp.exp(scores - row_max)
    row_total = jnp.sum(exponent, -1, keepdims=True)
    attend = (exponent / row_total).astype(jnp.bfloat16)
    context = jnp.einsum(pattern[1], attend, values, preferred_element_type=jnp.float32)
    return (context.astype(jnp.bfloat16), row_max + jnp.log(row_total))


def attend_back(queries, key_rows, values, allowed, log_total, context_grad, pattern, score_scale):
    scores = jnp.where(
        allowed,
        jnp.einsum(pattern[0], queries, key_rows, preferred_element_type=jnp.float32) * score_scale,
        NEGATIVE,
    )
    attend = jnp.exp(scores - log_total)
    attend_grad = jnp.einsum(pattern[0], context_grad, values, preferred_element_type=jnp.float32)
    score_grad = (attend * (attend_grad - jnp.sum(attend * attend_grad, -1, keepdims=True))).astype(
        jnp.bfloat16
    )
    query_grad = (
        jnp.einsum(pattern[1], score_grad, key_rows, preferred_element_type=jnp.float32)
        * score_scale
    )
    key_grad = (
        jnp.einsum(pattern[2], score_grad, queries, preferred_element_type=jnp.float32)
        * score_scale
    )
    value_grad = jnp.einsum(
        pattern[2], attend.astype(jnp.bfloat16), context_grad, preferred_element_type=jnp.float32
    )
    return (query_grad, key_grad, value_grad)


def on_device(
    frames,
    cotangent,
    prompt,
    timestep,
    clip_lengths,
    text_lengths,
    modulation_weight,
    modulation_bias,
    space_query,
    space_key,
    space_value,
    space_out,
    time_gain,
    time_query,
    time_key,
    time_value,
    time_out,
    time_gate,
    cross_gain,
    cross_query,
    prompt_key,
    prompt_value,
    cross_out,
    feed_up,
    feed_down,
):
    frame_count = frames.shape[1]
    patch_count = frames.shape[2] * frames.shape[3]
    model_width = frames.shape[4]
    token_count = frame_count * patch_count
    score_scale = 1.0 / math.sqrt(HEAD_DIM)
    residual = frames.reshape(token_count, model_width).astype(jnp.float32)
    frame_live = jnp.arange(frame_count) < clip_lengths[0]
    token_live = jnp.repeat(frame_live, patch_count)[:, None]
    prompt_rows = prompt[0]
    word_live = jnp.arange(prompt_rows.shape[0]) < text_lengths[0]
    (
        modulation_weight,
        space_query,
        space_key,
        space_value,
        space_out,
        time_query,
        time_key,
        time_value,
        time_out,
        cross_query,
        prompt_key,
        prompt_value,
        cross_out,
        feed_up,
        feed_down,
    ) = (
        lax.all_gather(modulation_weight, WIDE, axis=0, tiled=True),
        lax.all_gather(space_query, WIDE, axis=0, tiled=True),
        lax.all_gather(space_key, WIDE, axis=0, tiled=True),
        lax.all_gather(space_value, WIDE, axis=0, tiled=True),
        lax.all_gather(space_out, WIDE, axis=0, tiled=True),
        lax.all_gather(time_query, WIDE, axis=0, tiled=True),
        lax.all_gather(time_key, WIDE, axis=0, tiled=True),
        lax.all_gather(time_value, WIDE, axis=0, tiled=True),
        lax.all_gather(time_out, WIDE, axis=0, tiled=True),
        lax.all_gather(cross_query, WIDE, axis=0, tiled=True),
        lax.all_gather(prompt_key, WIDE, axis=0, tiled=True),
        lax.all_gather(prompt_value, WIDE, axis=0, tiled=True),
        lax.all_gather(cross_out, WIDE, axis=0, tiled=True),
        lax.all_gather(feed_up, WIDE, axis=0, tiled=True),
        lax.all_gather(feed_down, WIDE, axis=0, tiled=True),
    )
    head_width = space_query.shape[1]
    head_count = head_width // HEAD_DIM
    split_heads = (frame_count, patch_count, head_count, HEAD_DIM)
    half_width = model_width // 2
    frequency = jnp.exp(-math.log(10000.0) * jnp.arange(half_width, dtype=jnp.float32) / half_width)
    angles = timestep[0].astype(jnp.float32) * frequency
    condition = jax.nn.silu(jnp.concatenate([jnp.cos(angles), jnp.sin(angles)])).astype(
        jnp.bfloat16
    )
    slice_width = modulation_weight.shape[1]
    slice_start = lax.axis_index(TENSOR) * slice_width
    own_modulation = matmul(condition[None, :], modulation_weight)[0] + lax.dynamic_slice_in_dim(
        modulation_bias, slice_start, slice_width
    )
    modulation = lax.all_gather(own_modulation, TENSOR, axis=0, tiled=True)
    shift_one, scale_one, gate_one, shift_two, scale_two, gate_two = jnp.split(modulation, 6)
    normed_one, inverse_one = norm_rows(residual)
    input_one = (normed_one * (1.0 + scale_one) + shift_one).astype(jnp.bfloat16)
    query_one = matmul(input_one, space_query).astype(jnp.bfloat16).reshape(split_heads)
    key_one = matmul(input_one, space_key).astype(jnp.bfloat16).reshape(split_heads)
    value_one = matmul(input_one, space_value).astype(jnp.bfloat16).reshape(split_heads)
    key_frame, value_frame = (
        lax.all_gather(key_one, WIDE, axis=1, tiled=True),
        lax.all_gather(value_one, WIDE, axis=1, tiled=True),
    )
    space_pattern = ("fphe,fkhe->fhpk", "fhpk,fkhe->fphe", "fhpk,fphe->fkhe")
    every_patch = jnp.ones((key_frame.shape[1],), jnp.bool_)
    context_one, log_one = attend_forward(
        query_one, key_frame, value_frame, every_patch, space_pattern, score_scale
    )
    context_one = context_one.reshape(token_count, head_width)
    branch_one = over_heads(matmul_tr(context_one, space_out))
    after_one = residual + gate_one * branch_one
    normed_two, inverse_two = norm_rows(after_one)
    input_two = (normed_two * time_gain).astype(jnp.bfloat16)
    query_two = matmul(input_two, time_query).astype(jnp.bfloat16).reshape(split_heads)
    key_two = matmul(input_two, time_key).astype(jnp.bfloat16).reshape(split_heads)
    value_two = matmul(input_two, time_value).astype(jnp.bfloat16).reshape(split_heads)
    time_pattern = ("fphe,gphe->phfg", "phfg,gphe->fphe", "phfg,fphe->gphe")
    context_two, log_two = attend_forward(
        query_two, key_two, value_two, frame_live, time_pattern, score_scale
    )
    context_two = context_two.reshape(token_count, head_width)
    branch_two = over_heads(matmul_tr(context_two, time_out))
    gate_time = jnp.tanh(time_gate)
    after_two = after_one + gate_time * branch_two
    normed_three, inverse_three = norm_rows(after_two)
    input_three = (normed_three * cross_gain).astype(jnp.bfloat16)
    query_three = (
        matmul(input_three, cross_query)
        .astype(jnp.bfloat16)
        .reshape(token_count, head_count, HEAD_DIM)
    )
    word_keys = (
        matmul(prompt_rows, prompt_key).astype(jnp.bfloat16).reshape(-1, head_count, HEAD_DIM)
    )
    word_values = (
        matmul(prompt_rows, prompt_value).astype(jnp.bfloat16).reshape(-1, head_count, HEAD_DIM)
    )
    cross_pattern = ("nhe,jhe->nhj", "nhj,jhe->nhe", "nhj,nhe->jhe")
    context_three, log_three = attend_forward(
        query_three, word_keys, word_values, word_live, cross_pattern, score_scale
    )
    context_three = context_three.reshape(token_count, head_width)
    branch_three = over_heads(matmul_tr(context_three, cross_out))
    after_three = after_two + branch_three
    normed_four, inverse_four = norm_rows(after_three)
    input_four = (normed_four * (1.0 + scale_two) + shift_two).astype(jnp.bfloat16)
    pre_act = matmul(input_four, feed_up)
    hidden, gelu_pull = jax.vjp(lambda inner: jax.nn.gelu(inner, approximate=True), pre_act)
    hidden = hidden.astype(jnp.bfloat16)
    branch_four = over_heads(matmul_tr(hidden, feed_down))
    after_four = after_three + gate_two * branch_four
    output = jnp.where(token_live, after_four, 0.0).astype(jnp.bfloat16).reshape(frames.shape)
    upstream = jnp.where(
        token_live, cotangent.reshape(token_count, model_width).astype(jnp.float32), 0.0
    )
    feed_grad = (gate_two * upstream).astype(jnp.bfloat16)
    gate_two_grad = jnp.sum(upstream * branch_four, 0)
    feed_down_grad = outer_sum(feed_grad, hidden)
    pre_grad = gelu_pull(matmul(feed_grad, feed_down))[0].astype(jnp.bfloat16)
    feed_up_grad = outer_sum(input_four, pre_grad)
    input_four_grad = over_heads(matmul_tr(pre_grad, feed_up))
    shift_two_grad = jnp.sum(input_four_grad, 0)
    scale_two_grad = jnp.sum(input_four_grad * normed_four, 0)
    upstream = upstream + norm_back(normed_four, inverse_four, input_four_grad * (1.0 + scale_two))
    cross_grad = upstream.astype(jnp.bfloat16)
    cross_out_grad = outer_sum(cross_grad, context_three)
    context_grad = (
        matmul(cross_grad, cross_out)
        .astype(jnp.bfloat16)
        .reshape(token_count, head_count, HEAD_DIM)
    )
    query_grad, key_grad, value_grad = attend_back(
        query_three,
        word_keys,
        word_values,
        word_live,
        log_three,
        context_grad,
        cross_pattern,
        score_scale,
    )
    query_grad = query_grad.astype(jnp.bfloat16).reshape(token_count, head_width)
    cross_query_grad = outer_sum(input_three, query_grad)
    word_key_grad = key_grad.astype(jnp.bfloat16).reshape(-1, head_width)
    word_value_grad = value_grad.astype(jnp.bfloat16).reshape(-1, head_width)
    prompt_key_grad = outer_sum(prompt_rows, word_key_grad)
    prompt_value_grad = outer_sum(prompt_rows, word_value_grad)
    input_three_grad = over_heads(matmul_tr(query_grad, cross_query))
    cross_gain_grad = jnp.sum(input_three_grad * normed_three, 0)
    upstream = upstream + norm_back(normed_three, inverse_three, input_three_grad * cross_gain)
    time_grad = (gate_time * upstream).astype(jnp.bfloat16)
    time_gate_grad = jnp.sum(upstream * branch_two, 0) * (1.0 - gate_time * gate_time)
    time_out_grad = outer_sum(time_grad, context_two)
    context_grad = matmul(time_grad, time_out).astype(jnp.bfloat16).reshape(split_heads)
    query_grad, key_grad, value_grad = attend_back(
        query_two, key_two, value_two, frame_live, log_two, context_grad, time_pattern, score_scale
    )
    query_grad = query_grad.astype(jnp.bfloat16).reshape(token_count, head_width)
    key_grad = key_grad.astype(jnp.bfloat16).reshape(token_count, head_width)
    value_grad = value_grad.astype(jnp.bfloat16).reshape(token_count, head_width)
    time_query_grad = outer_sum(input_two, query_grad)
    time_key_grad = outer_sum(input_two, key_grad)
    time_value_grad = outer_sum(input_two, value_grad)
    input_two_grad = over_heads(
        matmul_tr(query_grad, time_query)
        + matmul_tr(key_grad, time_key)
        + matmul_tr(value_grad, time_value)
    )
    time_gain_grad = jnp.sum(input_two_grad * normed_two, 0)
    upstream = upstream + norm_back(normed_two, inverse_two, input_two_grad * time_gain)
    space_grad = (gate_one * upstream).astype(jnp.bfloat16)
    gate_one_grad = jnp.sum(upstream * branch_one, 0)
    space_out_grad = outer_sum(space_grad, context_one)
    context_grad = matmul(space_grad, space_out).astype(jnp.bfloat16).reshape(split_heads)
    key_frame, value_frame = (
        lax.all_gather(key_one, WIDE, axis=1, tiled=True),
        lax.all_gather(value_one, WIDE, axis=1, tiled=True),
    )
    query_grad, key_grad, value_grad = attend_back(
        query_one,
        key_frame,
        value_frame,
        every_patch,
        log_one,
        context_grad,
        space_pattern,
        score_scale,
    )
    key_grad, value_grad = (
        lax.psum_scatter(
            key_grad.astype(jnp.bfloat16), WIDE, scatter_dimension=1, tiled=True
        ).astype(jnp.float32),
        lax.psum_scatter(
            value_grad.astype(jnp.bfloat16), WIDE, scatter_dimension=1, tiled=True
        ).astype(jnp.float32),
    )
    query_grad = query_grad.astype(jnp.bfloat16).reshape(token_count, head_width)
    key_grad = key_grad.astype(jnp.bfloat16).reshape(token_count, head_width)
    value_grad = value_grad.astype(jnp.bfloat16).reshape(token_count, head_width)
    space_query_grad = outer_sum(input_one, query_grad)
    space_key_grad = outer_sum(input_one, key_grad)
    space_value_grad = outer_sum(input_one, value_grad)
    input_one_grad = over_heads(
        matmul_tr(query_grad, space_query)
        + matmul_tr(key_grad, space_key)
        + matmul_tr(value_grad, space_value)
    )
    shift_one_grad = jnp.sum(input_one_grad, 0)
    scale_one_grad = jnp.sum(input_one_grad * normed_one, 0)
    upstream = upstream + norm_back(normed_one, inverse_one, input_one_grad * (1.0 + scale_one))
    frames_grad = upstream.astype(jnp.bfloat16).reshape(frames.shape)
    modulation_bias_grad = jnp.concatenate(
        [
            shift_one_grad,
            scale_one_grad,
            gate_one_grad,
            shift_two_grad,
            scale_two_grad,
            gate_two_grad,
        ]
    )
    own_grad = lax.dynamic_slice_in_dim(modulation_bias_grad, slice_start, slice_width)
    modulation_weight_grad = condition.astype(jnp.float32)[:, None] * own_grad[None, :]
    (
        modulation_weight_grad,
        modulation_bias_grad,
        space_query_grad,
        space_key_grad,
        space_value_grad,
        space_out_grad,
        time_gain_grad,
        time_query_grad,
        time_key_grad,
        time_value_grad,
        time_out_grad,
        time_gate_grad,
        cross_gain_grad,
        cross_query_grad,
        prompt_key_grad,
        prompt_value_grad,
        cross_out_grad,
        feed_up_grad,
        feed_down_grad,
    ) = (
        lax.psum_scatter(
            modulation_weight_grad, (NARROW, WIDE), scatter_dimension=0, tiled=True
        ),
        lax.psum_scatter(modulation_bias_grad, (NARROW, WIDE), scatter_dimension=0, tiled=True),
        lax.psum_scatter(space_query_grad, (NARROW, WIDE), scatter_dimension=0, tiled=True),
        lax.psum_scatter(space_key_grad, (NARROW, WIDE), scatter_dimension=0, tiled=True),
        lax.psum_scatter(space_value_grad, (NARROW, WIDE), scatter_dimension=0, tiled=True),
        lax.psum_scatter(space_out_grad, (NARROW, WIDE), scatter_dimension=0, tiled=True),
        lax.psum_scatter(time_gain_grad, (NARROW, WIDE), scatter_dimension=0, tiled=True),
        lax.psum_scatter(time_query_grad, (NARROW, WIDE), scatter_dimension=0, tiled=True),
        lax.psum_scatter(time_key_grad, (NARROW, WIDE), scatter_dimension=0, tiled=True),
        lax.psum_scatter(time_value_grad, (NARROW, WIDE), scatter_dimension=0, tiled=True),
        lax.psum_scatter(time_out_grad, (NARROW, WIDE), scatter_dimension=0, tiled=True),
        lax.psum_scatter(time_gate_grad, (NARROW, WIDE), scatter_dimension=0, tiled=True),
        lax.psum_scatter(cross_gain_grad, (NARROW, WIDE), scatter_dimension=0, tiled=True),
        lax.psum_scatter(cross_query_grad, (NARROW, WIDE), scatter_dimension=0, tiled=True),
        lax.psum_scatter(prompt_key_grad, (NARROW, WIDE), scatter_dimension=0, tiled=True),
        lax.psum_scatter(prompt_value_grad, (NARROW, WIDE), scatter_dimension=0, tiled=True),
        lax.psum_scatter(cross_out_grad, (NARROW, WIDE), scatter_dimension=0, tiled=True),
        lax.psum_scatter(feed_up_grad, (NARROW, WIDE), scatter_dimension=0, tiled=True),
        lax.psum_scatter(feed_down_grad, (NARROW, WIDE), scatter_dimension=0, tiled=True),
    )
    return (
        output,
        frames_grad,
        modulation_weight_grad,
        modulation_bias_grad,
        space_query_grad,
        space_key_grad,
        space_value_grad,
        space_out_grad,
        time_gain_grad,
        time_query_grad,
        time_key_grad,
        time_value_grad,
        time_out_grad,
        time_gate_grad,
        cross_gain_grad,
        cross_query_grad,
        prompt_key_grad,
        prompt_value_grad,
        cross_out_grad,
        feed_up_grad,
        feed_down_grad,
    )


WEIGHT = P(WIDE, TENSOR)
OWNED = P((NARROW, WIDE), TENSOR)
ROWS = P((NARROW, WIDE))
PATCHES = P(NARROW, None, WIDE, None, None)
CLIP = P(NARROW)
COPIED = P()


def fits(sizes):
    return sizes[WIDE] == 2 and sizes[TENSOR] == 4 and sizes[NARROW] == 4


def solution(mesh):
    sizes = {name: mesh.shape[name] for name in mesh.axis_names}
    return jax.shard_map(
        functools.partial(fused_on_device, sizes) if fits(sizes) else on_device,
        mesh=mesh,
        in_specs=(
            (PATCHES, PATCHES, P(NARROW, None, None), CLIP, CLIP, CLIP)
            + (WEIGHT, COPIED, WEIGHT, WEIGHT, WEIGHT, WEIGHT)
            + (COPIED, WEIGHT, WEIGHT, WEIGHT, WEIGHT, COPIED)
            + (COPIED, WEIGHT, WEIGHT, WEIGHT, WEIGHT, WEIGHT, WEIGHT)
        ),
        out_specs=(
            (PATCHES, PATCHES, OWNED, ROWS, OWNED, OWNED, OWNED, OWNED)
            + (ROWS, OWNED, OWNED, OWNED, OWNED, ROWS)
            + (ROWS, OWNED, OWNED, OWNED, OWNED, OWNED, OWNED)
        ),
        check_vma=False,
    )
```

```python
import functools
import math

import jax
import jax.numpy as jnp
from jax import lax
from jax.experimental import pallas as pl
from jax.experimental.pallas import tpu as pltpu
from jax.sharding import PartitionSpec as P

HEAD_DIM = 72
LANES = 128
GRANULES = 2
WHOLE = 256
CHUNKS = 2
EPSILON = 1e-06
NEGATIVE = -1e30
NARROW, WIDE, TENSOR = "narrow", "wide", "tensor"
COLS = "cols"
MESH_ID = pl.DeviceIdType.MESH
F32 = jnp.float32
BF16 = jnp.bfloat16
VMEM = pltpu.VMEM
VM = pl.BlockSpec(memory_space=pltpu.VMEM)
ANY = pl.BlockSpec(memory_space=pl.ANY)
DMA = pltpu.SemaphoreType.DMA


def dot(left, right):
    return jnp.dot(left, right, preferred_element_type=F32)


def dot_tr(left, right):
    return lax.dot_general(left, right, (((1,), (1,)), ((), ())), preferred_element_type=F32)


def dot_outer(left, right):
    return lax.dot_general(left, right, (((0,), (0,)), ((), ())), preferred_element_type=F32)


def norm_tile(values):
    center = values - jnp.mean(values, -1, keepdims=True)
    inverse = lax.rsqrt(jnp.mean(center * center, -1, keepdims=True) + EPSILON)
    return center * inverse, inverse


def norm_pull(normed, inverse, incoming):
    return inverse * (
        incoming
        - jnp.mean(incoming, -1, keepdims=True)
        - normed * jnp.mean(incoming * normed, -1, keepdims=True)
    )


def softmax_tile(scores):
    exponent = jnp.exp(scores - jnp.max(scores, -1, keepdims=True))
    return exponent / jnp.sum(exponent, -1, keepdims=True)


class Place:
    def __init__(self, sizes):
        self.sizes = sizes
        self.n = lax.axis_index(NARROW)
        self.w = lax.axis_index(WIDE)
        self.t = lax.axis_index(TENSOR)

    def tensor_peer(self, step):
        return lax.rem(self.t + step, self.sizes[TENSOR])

    def over_tensor(self, step):
        return (self.n, self.w, self.tensor_peer(step))

    def sibling(self):
        return (self.n, 1 - self.w, self.t)

    def over_narrow(self, peer):
        return (peer, self.w, self.t)


def greet(partners):
    barrier = pltpu.get_barrier_semaphore()
    for partner in partners:
        pl.semaphore_signal(barrier, inc=1, device_id=partner, device_id_type=MESH_ID)
    pl.semaphore_wait(barrier, len(partners))


def send(source, target, send_sem, recv_sem, partner):
    copy = pltpu.make_async_remote_copy(
        src_ref=source,
        dst_ref=target,
        send_sem=send_sem,
        recv_sem=recv_sem,
        device_id=partner,
        device_id_type=MESH_ID,
    )
    copy.start()
    return copy


class Transfer:
    def __init__(self, slot, scatter, view, landing, born):
        self.slot, self.scatter, self.view, self.landing = slot, scatter, view, landing
        self.step, self.born = 0, born


class Line:
    def __init__(self, place, send_sems, recv_sems):
        self.place, self.send_sems, self.recv_sems = place, send_sems, recv_sems
        self.open, self.slots, self.clock = [], 0, 0

    def at(self, index, body):
        pl.when(self.place.t == index)(body)

    def hop(self, move, source, target, sent, received, g, peer):
        return pltpu.make_async_remote_copy(
            src_ref=source,
            dst_ref=target,
            send_sem=self.send_sems.at[move.slot, sent, g],
            recv_sem=self.recv_sems.at[move.slot, received, g],
            device_id=(self.place.n, self.place.w, peer),
            device_id_type=MESH_ID,
        )

    def reduce_hop(self, move, owner, lands, g, peer):
        return self.hop(
            move, move.view(owner, g), move.landing(lands, g), owner, lands, g, peer
        )

    def copy_hop(self, move, owner, sent, g, peer):
        block = move.view(owner, g)
        return self.hop(move, block, block, sent, owner, g, peer)

    def start(self, scatter, view, landing=None):
        move = Transfer(self.slots, scatter, view, landing, self.clock)
        self.slots += 1
        if scatter:
            plan = {
                0: [(3, 3, 1), (2, 2, 1), (1, 1, 1)],
                1: [(0, 0, 0)],
                2: [(3, 3, 3)],
                3: [(0, 0, 2), (1, 1, 2), (2, 2, 2)],
            }
            make = self.reduce_hop
        else:
            plan = {
                0: [(0, 0, 2), (0, 1, 1)],
                1: [(1, 0, 2), (1, 1, 0)],
                2: [(2, 0, 1), (2, 1, 3)],
                3: [(3, 0, 1), (3, 1, 2)],
            }
            make = self.copy_hop
        for device, hops in plan.items():

            def begin(hops=hops):
                for owner, index, peer in hops:
                    for g in range(GRANULES):
                        make(move, owner, index, g, peer).start()

            self.at(device, begin)
        self.open.append(move)
        return move

    def pending_block(self, move, index, g):
        block = move.landing(index, g) if move.scatter else move.view(index, g)
        return self.hop(move, block, block, 0, index, g, 0)

    def relay(self, move, index, g, lands, sent, peer):
        self.pending_block(move, index, g).wait_recv()
        if move.scatter:
            block = move.landing(index, g)
            block[...] = (block[...].astype(F32) + move.view(index, g)[...].astype(F32)).astype(
                BF16
            )
            self.hop(move, block, move.landing(lands, g), index, lands, g, peer).start()
        else:
            self.copy_hop(move, index, sent, g, peer).start()

    def steps(self):
        return 2 * GRANULES

    def advance(self, move):
        late, g = divmod(move.step, GRANULES)
        move.step += 1
        if move.scatter:
            plan = {1: ((3, 2, 0, 3), (2, 3, 0, 2)), 2: ((0, 1, 0, 0), (1, 0, 0, 1))}
        else:
            plan = {1: ((2, 0, 2, 0), (3, 0, 3, 0)), 2: ((1, 0, 2, 3), (0, 0, 3, 3))}
        for device, pair in plan.items():
            index, lands, sent, peer = pair[late]

            def body(index=index, lands=lands, sent=sent, peer=peer):
                self.relay(move, index, g, lands, sent, peer)

            self.at(device, body)

    def tick(self, count=1, lag=2):
        self.clock += 1
        for _ in range(count):
            for move in self.open:
                if move.step < self.steps() and move.born + lag <= self.clock:
                    self.advance(move)
                    break

    def drain(self, move):
        while move.step < self.steps():
            self.advance(move)

    def finish(self, move):
        while move.step < self.steps():
            self.advance(move)
            for other in self.open:
                if other is not move and other.step < self.steps() and not other.scatter:
                    self.advance(other)
                    break
        self.open.remove(move)
        if move.scatter:
            plan = {0: (0, 1), 1: (1, 0), 2: (2, 3), 3: (3, 2)}
        else:
            plan = {0: (1, 2, 3), 1: (0,), 2: (3,), 3: (2, 1, 0)}
        for device, blocks in plan.items():

            def body(blocks=blocks):
                for index in blocks:
                    for g in range(GRANULES):
                        self.pending_block(move, index, g).wait_recv()

            self.at(device, body)

    def release(self, move):
        for device in range(4):
            if move.scatter:
                sent = [d for d in range(4) if d != device]
            else:
                sent = range(4) if device in (1, 2) else range(2)

            def body(sent=sent):
                for index in sent:
                    for g in range(GRANULES):
                        block = move.view(0, g)
                        self.hop(move, block, block, index, 0, g, 0).wait_send()

            self.at(device, body)


def wait_all(copies):
    for copy in copies:
        copy.wait()


def modulation_kernel(sizes, condition, weight, shared, mine, landing, send_sems, recv_sems):
    place = Place(sizes)
    partners = []
    for dw in range(sizes[WIDE]):
        for dt in range(sizes[TENSOR]):
            if dw or dt:
                partners.append(
                    (
                        place.n,
                        lax.rem(place.w + dw, sizes[WIDE]),
                        lax.rem(place.t + dt, sizes[TENSOR]),
                    )
                )
    greet(partners)
    mine[0] = dot(condition[...], weight[...])[0:1]
    slot = place.w * sizes[TENSOR] + place.t
    copies = [
        send(mine.at[0], landing.at[slot], send_sems.at[i], recv_sems.at[i], partner)
        for i, partner in enumerate(partners)
    ]
    landing[slot] = mine[0]
    wait_all(copies)
    shared[...] = landing[...]


def modulation_call(sizes, condition, weight):
    group = sizes[WIDE] * sizes[TENSOR]
    width = weight.shape[1]
    return pl.pallas_call(
        functools.partial(modulation_kernel, sizes),
        name="modulation",
        out_shape=jax.ShapeDtypeStruct((group, 1, width), F32),
        in_specs=[VM, VM],
        out_specs=VM,
        scratch_shapes=[
            VMEM((1, 1, width), F32),
            VMEM((group, 1, width), F32),
            DMA((group - 1,)),
            DMA((group - 1,)),
        ],
        compiler_params=pltpu.CompilerParams(collective_id=0, has_side_effects=True),
    )(condition, weight)


class Split:
    def __init__(self, place, frame_count, chunks, cols):
        parts = place.sizes[TENSOR]
        self.frame_count, self.chunks, self.cols = frame_count, chunks, cols
        self.rows = frame_count * cols
        self.quarter = self.rows // parts
        self.place = place
        self.frames = frame_count // parts

    def chunk(self, r):
        return pl.ds(r * self.rows, self.rows)

    def kept(self, r):
        return pl.ds(r * self.quarter, self.quarter)

    def own(self, r):
        start = r * self.rows + self.place.t * self.quarter
        return pl.ds(pl.multiple_of(start, self.quarter), self.quarter)

    def own_frames(self):
        return pl.ds(self.place.t * self.frames, self.frames)

    def rows_view(self, ref, r):
        size = self.quarter // GRANULES

        def view(s, g):
            return ref.at[pl.ds(r * self.rows + s * self.quarter + g * size, size)]

        return view

    def frames_view(self, ref, r):
        size = self.frames // GRANULES

        def view(s, g):
            return ref.at[pl.ds(s * self.frames + g * size, size), r]

        return view

    def landing_view(self, ref):
        size = self.quarter // GRANULES

        def view(s, g):
            return ref.at[s, pl.ds(g * size, size)]

        return view

    def total(self, partial, landing, r):
        t = self.place.t
        beside = t + 1 - 2 * lax.rem(t, 2)
        return (
            partial[self.own(r)].astype(F32)
            + landing[t].astype(F32)
            + landing[beside].astype(F32)
        )

    def spots(self, f):
        return [
            pl.ds(pl.multiple_of(r * self.rows + f * self.cols, self.cols), self.cols)
            for r in range(self.chunks)
        ]


def neighbours(place):
    steps = range(1, place.sizes[TENSOR])
    return [place.sibling()] + [place.over_tensor(step) for step in steps]


def write_group_mask(group_mask, key_live, cols):
    shape = group_mask.shape
    row_id = lax.broadcasted_iota(jnp.int32, shape, 0)
    col_id = lax.broadcasted_iota(jnp.int32, shape, 1)
    group_mask[...] = jnp.where(
        lax.rem(row_id, cols) == lax.rem(col_id, cols),
        jnp.broadcast_to(key_live[0:1], shape),
        0.0,
    )


def forward_kernel(
    sizes,
    frames,
    vectors,
    key_live,
    word_live,
    spread,
    prompt,
    *refs,
):
    weights = refs[:12]
    (
        h1, q1, side, o1, h2, q2, o2, h3, q3, kv3, o3, h4,
        a1_own, a2_own, x3_own, n2_own, n3_own, n4_own, inverses,
    ) = refs[12:31]
    (
        full, full_prompt, wide_context, partial, landing, residual, group_mask,
        local_sems, side_send, side_recv, kv_send, kv_recv, ring_send, ring_recv,
    ) = refs[31:]
    place = Place(sizes)
    frame_count, chunks, cols, width = frames.shape
    split = Split(place, frame_count, chunks, cols)
    rows, half = split.rows, split.quarter
    heads = spread.shape[1] // LANES
    scale = 1.0 / math.sqrt(HEAD_DIM)
    chain = Line(place, ring_send, ring_recv)
    greet(neighbours(place))

    def fetch(i):
        weight_half = weights[i].shape[0]
        spot = pl.ds(pl.multiple_of(place.w * weight_half, weight_half), weight_half)
        target = full.at[i, spot] if i < 10 else full_prompt.at[i - 10, spot]
        local = pltpu.make_async_copy(weights[i], target, local_sems.at[i])
        local.start()
        return [local, send(weights[i], target, side_send.at[i], side_recv.at[i], place.sibling())]

    pending = {i: fetch(i) for i in (0, 1, 2, 3)}

    def ready(*which):
        for i in which:
            wait_all(pending.pop(i))

    @pl.loop(0, frame_count)
    def _(f):
        for r in range(chunks):
            normed, _ = norm_tile(frames[f, r].astype(F32))
            h1[pl.ds(pl.multiple_of(r * rows + f * cols, cols), cols)] = (
                normed * vectors[1:2] + vectors[0:1]
            ).astype(BF16)

    write_group_mask(group_mask, key_live, cols)

    def project(source, spot, weight, out, index):
        narrow = dot(source[spot], full[weight]).astype(BF16)
        out[index, spot] = dot(narrow, spread[...]).astype(BF16)

    ready(0, 1, 2)

    @pl.loop(0, 3)
    def _(i):
        for r in range(0, chunks * rows, WHOLE):
            project(h1, pl.ds(r, WHOLE), i, q1, i)

    kv_copies = [
        send(q1.at[1 + j], side.at[j], kv_send.at[j], kv_recv.at[j], place.sibling())
        for j in range(2)
    ]
    for i in (4, 5, 6, 7, 10, 11, 8, 9):
        pending[i] = fetch(i)
    wait_all(kv_copies)

    @pl.loop(0, frame_count)
    def _(f):
        spots = split.spots(f)
        queries = jnp.concatenate([q1[0, spot] for spot in spots], 0)
        keys = jnp.concatenate(
            [q1[1, spot] for spot in spots] + [side[0, spot] for spot in spots], 0
        )
        values = jnp.concatenate(
            [q1[2, spot] for spot in spots] + [side[1, spot] for spot in spots], 0
        )
        for h in range(heads):
            lanes = slice(h * LANES, (h + 1) * LANES)
            attend = softmax_tile(dot_tr(queries[:, lanes], keys[:, lanes]) * scale)
            context = dot(attend.astype(BF16), values[:, lanes]).astype(BF16)
            for r in range(chunks):
                wide_context[spots[r], lanes] = context[r * cols : (r + 1) * cols]

    sent = [None] * chunks

    def emit(r, out, weight, stage):
        spot = split.chunk(r)
        out[spot] = dot_tr(wide_context[spot], spread[...]).astype(BF16)
        if sent[r] is not None:
            chain.release(sent[r])
        partial[spot] = dot_tr(out[spot], full[weight]).astype(BF16)
        sent[r] = chain.start(
            True, split.rows_view(partial, r), split.landing_view(landing.at[stage * chunks + r])
        )
        return sent[r]

    def branch(r, stage):
        return split.total(partial, landing.at[stage * chunks + r], r)

    def settle(scatters, body, target):
        gathers = []
        for r in range(chunks):
            chain.finish(scatters[r])
            body(r)
            gathers.append(chain.start(False, split.rows_view(target, r)))
        return gathers

    ready(3)
    scatters = []
    for r in range(chunks):
        scatters.append(emit(r, o1, 3, 0))
        chain.tick(0)

    ready(10, 11)
    kv3[...] = jnp.zeros_like(kv3)
    for j in range(2):
        narrow = dot(prompt[...], full_prompt[j]).astype(BF16)
        kv3[j, 0 : prompt.shape[0]] = dot(narrow, spread[...]).astype(BF16)
        chain.tick(4)

    def body_one(r):
        kept = split.kept(r)
        branch_one = branch(r, 0)
        a1_own[kept] = branch_one
        x_own = frames[split.own_frames(), r].reshape(half, width)
        after = x_own.astype(F32) + vectors[2:3] * branch_one
        normed, inverse = norm_tile(after)
        residual[kept] = after
        n2_own[kept] = normed
        inverses[0, kept] = jnp.broadcast_to(inverse, (half, LANES))
        h2[split.own(r)] = (normed * vectors[6:7]).astype(BF16)

    gathers = settle(scatters, body_one, h2)
    released = list(gathers)
    ready(4, 5, 6, 7)
    scatters = []
    for r in range(chunks):
        chain.finish(gathers[r])
        spot = split.chunk(r)
        for i in range(3):
            project(h2, spot, 4 + i, q2, i)
            chain.tick()
        for h in range(heads):
            lanes = slice(h * LANES, (h + 1) * LANES)
            scores = dot_tr(q2[0, spot, lanes], q2[1, spot, lanes]) * scale
            attend = softmax_tile(jnp.where(group_mask[...] > 0.5, scores, NEGATIVE))
            wide_context[spot, lanes] = dot(attend.astype(BF16), q2[2, spot, lanes]).astype(BF16)
        chain.tick()
        scatters.append(emit(r, o2, 7, 1))

    def body_two(r):
        kept = split.kept(r)
        branch_two = branch(r, 1)
        a2_own[kept] = branch_two
        after = residual[kept] + vectors[7:8] * branch_two
        normed, inverse = norm_tile(after)
        residual[kept] = after
        n3_own[kept] = normed
        inverses[1, kept] = jnp.broadcast_to(inverse, (half, LANES))
        h3[split.own(r)] = (normed * vectors[8:9]).astype(BF16)

    gathers = settle(scatters, body_two, h3)
    released += gathers
    ready(8, 9)
    scatters = []
    for r in range(chunks):
        chain.finish(gathers[r])
        spot = split.chunk(r)
        narrow = dot(h3[spot], full[8]).astype(BF16)
        q3[spot] = dot(narrow, spread[...]).astype(BF16)
        chain.tick()
        for h in range(heads):
            lanes = slice(h * LANES, (h + 1) * LANES)
            scores = dot_tr(q3[spot, lanes], kv3[0, :, lanes]) * scale
            attend = softmax_tile(jnp.where(word_live[0:1] > 0.5, scores, NEGATIVE))
            wide_context[spot, lanes] = dot(attend.astype(BF16), kv3[1, :, lanes]).astype(BF16)
        chain.tick()
        scatters.append(emit(r, o3, 9, 2))

    def body_three(r):
        kept = split.kept(r)
        after = residual[kept] + branch(r, 2)
        normed, inverse = norm_tile(after)
        x3_own[kept] = after
        n4_own[kept] = normed
        inverses[2, kept] = jnp.broadcast_to(inverse, (half, LANES))
        h4[split.own(r)] = (normed * vectors[4:5] + vectors[3:4]).astype(BF16)

    gathers = settle(scatters, body_three, h4)
    for move in gathers:
        chain.finish(move)
    for move in sent + released + gathers:
        chain.release(move)


def forward_call(sizes, frames, vectors, key_live, word_live, spread, prompt, weights):
    frame_count, chunks, cols, width = frames.shape
    rows = frame_count * cols
    tokens = rows * chunks
    head_width, padded = spread.shape
    half = rows // sizes[TENSOR]
    kept = half * chunks
    full_rows = weights[0].shape[0] * sizes[WIDE]
    prompt_width = weights[10].shape[0] * sizes[WIDE]
    moves = 6 * chunks
    s = jax.ShapeDtypeStruct
    wide_act, heads_act = s((tokens, width), BF16), s((tokens, head_width), BF16)
    triple, own = s((3, tokens, padded), BF16), s((kept, width), F32)
    outs = [
        wide_act, triple, s((2, tokens, padded), BF16), heads_act,
        wide_act, triple, heads_act,
        wide_act, s((tokens, padded), BF16), s((2, LANES, padded), BF16), heads_act,
        wide_act, own, own, own, own, own, own, s((3, kept, LANES), F32),
    ]
    return pl.pallas_call(
        functools.partial(forward_kernel, sizes),
        name="forward",
        out_shape=outs,
        in_specs=[VM] * 6 + [ANY] * 12,
        out_specs=[VM] * len(outs),
        scratch_shapes=[
            VMEM((10, full_rows, head_width), BF16),
            VMEM((2, prompt_width, head_width), BF16),
            VMEM((tokens, padded), BF16),
            VMEM((tokens, width), BF16),
            VMEM((3 * chunks, 4, half, width), BF16),
            VMEM((kept, width), F32),
            VMEM((rows, rows), F32),
            DMA((12,)), DMA((12,)), DMA((12,)), DMA((2,)), DMA((2,)),
            DMA((moves, 4, GRANULES)), DMA((moves, 4, GRANULES)),
        ],
        compiler_params=pltpu.CompilerParams(
            collective_id=1, has_side_effects=True, vmem_limit_bytes=60 << 20
        ),
    )(frames, vectors, key_live, word_live, spread, prompt, *weights)


def prepare(sizes, frames, timestep, clip_lengths, text_lengths, modulation_weight,
            modulation_bias, time_gain, time_gate, cross_gain, head_width):
    frame_count, width = frames.shape[1], frames.shape[4]
    cols = frames.shape[2] * frames.shape[3] // CHUNKS
    half_width = width // 2
    frequency = jnp.exp(-math.log(10000.0) * jnp.arange(half_width, dtype=F32) / half_width)
    angles = timestep[0].astype(F32) * frequency
    condition = jax.nn.silu(jnp.concatenate([jnp.cos(angles), jnp.sin(angles)])).astype(BF16)
    mine = lax.dynamic_slice_in_dim(
        condition, lax.axis_index(WIDE) * modulation_weight.shape[0], modulation_weight.shape[0]
    )
    parts = modulation_call(
        sizes, jnp.broadcast_to(mine[None], (16, mine.shape[0])), modulation_weight
    )
    parts = parts.reshape(sizes[WIDE], -1)
    modulation = (jnp.sum(parts, 0) + modulation_bias).reshape(6, width)
    vectors = jnp.stack(
        [
            modulation[0], 1.0 + modulation[1], modulation[2],
            modulation[3], 1.0 + modulation[4], modulation[5],
            time_gain, jnp.tanh(time_gate), cross_gain,
        ]
    )
    live = jnp.arange(frame_count) < clip_lengths[0]
    key_live = jnp.repeat(live, cols).astype(F32)[None]
    word_live = (jnp.arange(LANES) < text_lengths[0]).astype(F32)[None]
    heads = head_width // HEAD_DIM
    padded = jnp.arange(heads * LANES)
    source = jnp.where(
        padded % LANES < HEAD_DIM, padded // LANES * HEAD_DIM + padded % LANES, -1
    )
    spread = (jnp.arange(head_width)[:, None] == source[None]).astype(BF16)
    return condition, vectors, live, key_live, word_live, spread


def over_columns(width, tile, body):
    whole = width // tile

    @pl.loop(0, whole)
    def _(j):
        body(pl.ds(pl.multiple_of(j * tile, tile), tile))

    if width % tile:
        body(pl.ds(whole * tile, width % tile))


GELU_C = math.sqrt(2.0 / math.pi)


def live_rows(live, split):
    pieces = [
        jnp.broadcast_to(
            live[split.place.t * split.frames + f, 0:1, 0:1], (split.cols, 1)
        )
        for f in range(split.frames)
    ]
    return jnp.concatenate(pieces, 0)


def own_cotangent(cotangent, live, split, r):
    width = cotangent.shape[3]
    rows = cotangent[split.own_frames(), r].reshape(split.quarter, width)
    return rows.astype(F32) * live_rows(live, split)


def mlp_kernel(
    sizes,
    h4, cotangent, vectors, live, n4_own, inverses, up_half, down_half,
    branch_part, e3, g3_own, up_grad, down_grad, sums,
    up, down, e4, hidden, pre_grad, partial, landing,
    local_sems, side_send, side_recv, ring_send, ring_recv,
):
    place = Place(sizes)
    frame_count, chunks, cols, width = cotangent.shape
    split = Split(place, frame_count, chunks, cols)
    line = Line(place, ring_send, ring_recv)
    greet(neighbours(place))
    copies = []
    for i, (source, target) in enumerate(((up_half, up), (down_half, down))):
        half = source.shape[0]
        spot = pl.ds(pl.multiple_of(place.w * half, half), half)
        local = pltpu.make_async_copy(source, target.at[spot], local_sems.at[i])
        local.start()
        copies += [
            local,
            send(source, target.at[spot], side_send.at[i], side_recv.at[i], place.sibling()),
        ]

    @pl.loop(0, frame_count)
    def _(f):
        for r, spot in enumerate(split.spots(f)):
            e4[spot] = (
                vectors[5:6] * (cotangent[f, r].astype(F32) * live[f, 0:1, 0:1])
            ).astype(BF16)

    sums[...] = jnp.zeros_like(sums)
    wait_all(copies)
    scatters = []
    for r in range(chunks):
        spot = split.chunk(r)

        def act(lanes):
            pre = dot(h4[spot], up[:, lanes])
            grad = dot(e4[spot], down[:, lanes])
            inner = jnp.tanh(GELU_C * (pre + 0.044715 * pre * pre * pre))
            gate = 0.5 * (1.0 + inner)
            hidden[spot, lanes] = (pre * gate).astype(BF16)
            slope = gate + 0.5 * pre * (1.0 - inner * inner) * (
                GELU_C * (1.0 + 3.0 * 0.044715 * pre * pre)
            )
            pre_grad[spot, lanes] = (grad * slope).astype(BF16)

        over_columns(up.shape[1], 256, act)
        line.tick(1, 1)
        partial[spot] = dot_tr(pre_grad[spot], up[...]).astype(BF16)
        line.tick(1, 1)
        scatters.append(
            line.start(True, split.rows_view(partial, r), split.landing_view(landing.at[r]))
        )

    for r in range(chunks):
        spot = split.chunk(r)
        branch_part[spot] = dot_tr(hidden[spot], down[...]).astype(BF16)
        line.tick(1, 1)

    def down_tile(lanes):
        down_grad[:, lanes] = dot_outer(e4[...], hidden[:, lanes]).astype(BF16)

    def up_tile(lanes):
        up_grad[:, lanes] = dot_outer(h4[...], pre_grad[:, lanes]).astype(BF16)

    gathers = []
    for r in range(chunks):
        kept = split.kept(r)
        line.finish(scatters[r])
        grad = split.total(partial, landing.at[r], r)
        normed = n4_own[kept]
        sums[0:1] += jnp.sum(grad, 0, keepdims=True)
        sums[1:2] += jnp.sum(grad * normed, 0, keepdims=True)
        upstream = own_cotangent(cotangent, live, split, r) + norm_pull(
            normed, inverses[2, kept][:, 0:1], grad * vectors[4:5]
        )
        g3_own[kept] = upstream
        e3[split.own(r)] = upstream.astype(BF16)
        gathers.append(line.start(False, split.rows_view(e3, r)))
        if r == 0:
            over_columns(up.shape[1], 256, down_tile)
            line.tick(2, 1)

    over_columns(up.shape[1], 256, up_tile)
    for move in gathers:
        line.finish(move)
    for move in scatters + gathers:
        line.release(move)


def mlp_call(sizes, h4, cotangent, vectors, live, n4_own, inverses, up_half, down_half):
    frame_count, chunks, cols, width = cotangent.shape
    rows = frame_count * cols
    tokens = rows * chunks
    quarter = rows // sizes[TENSOR]
    hidden = up_half.shape[1]
    s = jax.ShapeDtypeStruct
    moves = 2 * chunks
    outs = [
        s((tokens, width), BF16), s((tokens, width), BF16), s((quarter * chunks, width), F32),
        s((width, hidden), BF16), s((width, hidden), BF16), s((8, width), F32),
    ]
    return pl.pallas_call(
        functools.partial(mlp_kernel, sizes),
        name="mlp",
        out_shape=outs,
        in_specs=[VM] * 6 + [ANY] * 2,
        out_specs=[VM] * len(outs),
        scratch_shapes=[
            VMEM((width, hidden), BF16), VMEM((width, hidden), BF16),
            VMEM((tokens, width), BF16), VMEM((tokens, hidden), BF16),
            VMEM((tokens, hidden), BF16),
            VMEM((tokens, width), BF16),
            VMEM((chunks, 4, quarter, width), BF16),
            DMA((2,)), DMA((2,)), DMA((2,)),
            DMA((moves, 4, GRANULES)), DMA((moves, 4, GRANULES)),
        ],
        compiler_params=pltpu.CompilerParams(
            collective_id=2, has_side_effects=True, vmem_limit_bytes=60 << 20
        ),
    )(h4, cotangent, vectors, live, n4_own, inverses, up_half, down_half)


class Reducer:
    def __init__(self, place, source, mine, merged, received, sems):
        self.place, self.source = place, source
        self.mine, self.merged, self.received = mine, merged, received
        self.local, self.side_send, self.side_recv, self.far_send, self.far_recv = sems
        self.clips = place.sizes[NARROW]
        self.block = mine.shape[1]

    def rows(self, clip, core):
        start = (clip * self.place.sizes[WIDE] + core) * self.block
        return pl.ds(pl.multiple_of(start, self.block), self.block)

    def split(self):
        self.copies = []
        for clip in range(self.clips):
            local = pltpu.make_async_copy(
                self.source.at[self.rows(clip, self.place.w)],
                self.mine.at[clip],
                self.local.at[clip],
            )
            local.start()
            self.copies += [
                local,
                send(
                    self.source.at[self.rows(clip, 1 - self.place.w)],
                    self.merged.at[clip],
                    self.side_send.at[clip],
                    self.side_recv.at[clip],
                    self.place.sibling(),
                ),
            ]

    def spread(self):
        wait_all(self.copies)
        self.copies = []

        @pl.loop(0, self.clips)
        def _(clip):
            self.merged[clip] = (
                self.merged[clip].astype(F32) + self.mine[clip].astype(F32)
            ).astype(BF16)

        for step in (3, 1, 2) if self.clips == 4 else range(1, self.clips):
            peer = lax.rem(self.place.n + step, self.clips)
            self.copies.append(
                send(
                    self.merged.at[peer],
                    self.received.at[step - 1],
                    self.far_send.at[step - 1],
                    self.far_recv.at[step - 1],
                    self.place.over_narrow(peer),
                )
            )

    def finish(self, out):
        wait_all(self.copies)
        total = self.merged[self.place.n].astype(F32)
        for step in range(self.clips - 1):
            total = total + self.received[step].astype(F32)
        out[...] = total


def reducer_scratch(sizes, jobs, block, width):
    clips = sizes[NARROW]
    return [
        VMEM((jobs, clips, block, width), BF16),
        VMEM((jobs, clips, block, width), BF16),
        VMEM((jobs, clips - 1, block, width), BF16),
        DMA((jobs, clips)), DMA((jobs, clips)), DMA((jobs, clips)),
        DMA((jobs, clips - 1)), DMA((jobs, clips - 1)),
    ]


def reducers(place, sources, scratch):
    mine, merged, received, *sems = scratch
    return [
        Reducer(
            place, source, mine.at[i], merged.at[i], received.at[i], [sem.at[i] for sem in sems]
        )
        for i, source in enumerate(sources)
    ]


def all_partners(place):
    sizes = place.sizes
    return (
        [place.sibling()]
        + [place.over_tensor(step) for step in range(1, sizes[TENSOR])]
        + [
            place.over_narrow(lax.rem(place.n + step, sizes[NARROW]))
            for step in range(1, sizes[NARROW])
        ]
    )


def fetch_weights(place, halves, full, local_sems, side_send, side_recv):
    pending = []
    for i, half_ref in enumerate(halves):
        half = half_ref.shape[0]
        spot = pl.ds(pl.multiple_of(place.w * half, half), half)
        local = pltpu.make_async_copy(half_ref, full.at[i, spot], local_sems.at[i])
        local.start()
        pending.append(
            [
                local,
                send(half_ref, full.at[i, spot], side_send.at[i], side_recv.at[i], place.sibling()),
            ]
        )
    return pending


def attention_pull(queries, keys, values, context_grad, mask, scale):
    scores = dot_tr(queries, keys) * scale
    if mask is not None:
        scores = jnp.where(mask, scores, NEGATIVE)
    attend = softmax_tile(scores)
    attend_grad = dot_tr(context_grad, values)
    score_grad = (
        attend * (attend_grad - jnp.sum(attend * attend_grad, -1, keepdims=True))
    ).astype(BF16)
    return (
        dot(score_grad, keys) * scale,
        dot_outer(score_grad, queries) * scale,
        dot_outer(attend.astype(BF16), context_grad),
    )


def back_kernel(
    sizes,
    e3, g3_own, n3_own, n2_own, inverses, a2_own, vectors, key_live, word_live, spread,
    h3, q3, kv3, o3, h2, q2, o2,
    *refs,
):
    halves, gradients = refs[:6], refs[6:8]
    g1_own, e1, time_grads, word_grads, up_out, down_out, cross_out, sums = refs[8:16]
    (
        full, wide_grad, wide_parts, narrow_parts, word_sums, word_side, e2, partial, landing,
        group_mask, cross_grads,
        local_sems, side_send, side_recv, word_send, word_recv, ring_send, ring_recv,
    ) = refs[16:34]
    place = Place(sizes)
    tokens, width = e3.shape
    rows, cols = group_mask.shape[0], sizes[COLS]
    chunks = tokens // rows
    split = Split(place, rows // cols, chunks, cols)
    heads = spread.shape[1] // LANES
    scale = 1.0 / math.sqrt(HEAD_DIM)
    line = Line(place, ring_send, ring_recv)
    greet(all_partners(place))
    pending = fetch_weights(place, halves, full, local_sems, side_send, side_recv)
    feed = reducers(place, gradients, refs[34:42])
    cross = reducers(place, [cross_grads.at[0], cross_grads.at[1]], refs[42:50])
    for job in feed:
        job.split()
    write_group_mask(group_mask, key_live, cols)
    sums[...] = jnp.zeros_like(sums)
    word_sums[...] = jnp.zeros_like(word_sums)

    def context_grad(source, spot, weight):
        narrow = dot(source[spot], full[weight]).astype(BF16)
        wide_grad[spot] = dot(narrow, spread[...]).astype(BF16)

    def scatter(r, stage):
        return line.start(
            True,
            split.rows_view(partial, r),
            split.landing_view(landing.at[stage * chunks + r]),
        )

    wait_all(pending[0])
    wait_all(pending[1])
    scatters = []
    for r in range(chunks):
        spot = split.chunk(r)
        context_grad(e3, spot, 0)
        line.tick()
        for h in range(heads):
            lanes = slice(h * LANES, (h + 1) * LANES)
            query_grad, key_grad, value_grad = attention_pull(
                q3[spot, lanes], kv3[0, :, lanes], kv3[1, :, lanes], wide_grad[spot, lanes],
                word_live[0:1] > 0.5, scale,
            )
            wide_parts[0, spot, lanes] = query_grad.astype(BF16)
            word_sums[0, :, lanes] += key_grad
            word_sums[1, :, lanes] += value_grad
        line.tick()
        narrow_parts[0, spot] = dot_tr(wide_parts[0, spot], spread[...]).astype(BF16)
        partial[spot] = dot_tr(narrow_parts[0, spot], full[1]).astype(BF16)
        scatters.append(scatter(r, 0))
    word_copy = send(word_sums, word_side, word_send, word_recv, place.sibling())
    cross_grads[0] = dot_outer(e3[...], o3[...]).astype(BF16)
    line.tick(2)
    cross_grads[1] = dot_outer(h3[...], narrow_parts[0]).astype(BF16)
    line.tick(2)
    for job in cross:
        job.split()
    gathers = []
    for r in range(chunks):
        kept = split.kept(r)
        line.finish(scatters[r])
        grad = split.total(partial, landing.at[r], r)
        normed = n3_own[kept]
        sums[0:1] += jnp.sum(grad * normed, 0, keepdims=True)
        upstream = g3_own[kept] + norm_pull(
            normed, inverses[1, kept][:, 0:1], grad * vectors[8:9]
        )
        g1_own[kept] = upstream
        sums[1:2] += jnp.sum(upstream * a2_own[kept], 0, keepdims=True)
        e2[split.own(r)] = (vectors[7:8] * upstream).astype(BF16)
        gathers.append(line.start(False, split.rows_view(e2, r)))
        if r == 0:
            for job in feed:
                job.spread()
    for job in cross:
        job.spread()
    word_copy.wait()
    for j in range(2):
        word_grads[j] = dot_tr(
            (word_sums[j] + word_side[j]).astype(BF16), spread[...]
        ).astype(BF16)
    sent = scatters + gathers

    for copies in pending[2:]:
        wait_all(copies)
    former, scatters = scatters, []
    for r in range(chunks):
        spot = split.chunk(r)
        line.finish(gathers[r])
        context_grad(e2, spot, 2)
        line.tick()
        for h in range(heads):
            lanes = slice(h * LANES, (h + 1) * LANES)
            parts = attention_pull(
                q2[0, spot, lanes], q2[1, spot, lanes], q2[2, spot, lanes],
                wide_grad[spot, lanes], group_mask[...] > 0.5, scale,
            )
            for i in range(3):
                wide_parts[i, spot, lanes] = parts[i].astype(BF16)
            if h % 2:
                line.tick()
        total = None
        for i in range(3):
            narrow_parts[i, spot] = dot_tr(wide_parts[i, spot], spread[...]).astype(BF16)
            part = dot_tr(narrow_parts[i, spot], full[3 + i])
            total = part if total is None else total + part
        line.tick()
        line.release(former[r])
        sent.remove(former[r])
        partial[spot] = total.astype(BF16)
        scatters.append(scatter(r, 1))
    sent += scatters
    time_grads[0] = dot_outer(e2[...], o2[...]).astype(BF16)
    line.tick(2)
    for i in range(3):
        time_grads[1 + i] = dot_outer(h2[...], narrow_parts[i]).astype(BF16)
        line.tick(1)

    gathers = []
    for r in range(chunks):
        kept = split.kept(r)
        line.finish(scatters[r])
        grad = split.total(partial, landing.at[chunks + r], r)
        normed = n2_own[kept]
        sums[2:3] += jnp.sum(grad * normed, 0, keepdims=True)
        upstream = g1_own[kept] + norm_pull(
            normed, inverses[0, kept][:, 0:1], grad * vectors[6:7]
        )
        g1_own[kept] = upstream
        e1[split.own(r)] = (vectors[2:3] * upstream).astype(BF16)
        gathers.append(line.start(False, split.rows_view(e1, r)))
    for r in range(chunks):
        line.drain(gathers[r])
    feed[0].finish(up_out)
    feed[1].finish(down_out)
    cross[0].finish(cross_out.at[0])
    cross[1].finish(cross_out.at[1])
    for move in gathers:
        line.finish(move)
    for move in sent + gathers:
        line.release(move)


def back_call(sizes, cols, acts, halves, gradients):
    e3, spread = acts[0], acts[9]
    tokens, width = e3.shape
    rows = acts[7].shape[1]
    chunks = tokens // rows
    quarter = rows // sizes[TENSOR]
    head_width, padded = spread.shape
    full_rows = halves[0].shape[0] * sizes[WIDE]
    hidden = gradients[0].shape[1]
    block = width // (sizes[NARROW] * sizes[WIDE])
    s = jax.ShapeDtypeStruct
    moves = 4 * chunks
    outs = [
        s((quarter * chunks, width), F32), s((tokens, width), BF16),
        s((4, width, head_width), BF16), s((2, LANES, head_width), BF16),
        s((block, hidden), F32), s((block, hidden), F32), s((2, block, head_width), F32),
        s((8, width), F32),
    ]
    return pl.pallas_call(
        functools.partial(back_kernel, {**sizes, COLS: cols}),
        name="back",
        out_shape=outs,
        in_specs=[VM] * len(acts) + [ANY] * 8,
        out_specs=[VM] * len(outs),
        scratch_shapes=[
            VMEM((6, full_rows, head_width), BF16),
            VMEM((tokens, padded), BF16),
            VMEM((3, tokens, padded), BF16),
            VMEM((3, tokens, head_width), BF16),
            VMEM((2, LANES, padded), F32), VMEM((2, LANES, padded), F32),
            VMEM((tokens, width), BF16),
            VMEM((tokens, width), BF16),
            VMEM((2 * chunks, 4, quarter, width), BF16),
            VMEM((rows, rows), F32),
            VMEM((2, width, head_width), BF16),
            DMA((6,)), DMA((6,)), DMA((6,)), DMA(()), DMA(()),
            DMA((moves, 4, GRANULES)), DMA((moves, 4, GRANULES)),
        ]
        + reducer_scratch(sizes, 2, block, hidden)
        + reducer_scratch(sizes, 2, block, head_width),
        compiler_params=pltpu.CompilerParams(
            collective_id=3, has_side_effects=True, vmem_limit_bytes=60 << 20
        ),
    )(*acts, *halves, *gradients)


def space_kernel(
    sizes,
    e1, g1_own, frames, a1_own, vectors, spread, h1, q1, side, o1, prompt, word_grads,
    branch_part, x3_own, cotangent, live, mlp_sums, back_sums, condition,
    *refs,
):
    halves, gradients = refs[:4], refs[4]
    frames_grad, output, early_out, space_out, prompt_out, merged, conditions = refs[5:12]
    (
        full, wide_grad, wide_parts, narrow_parts, key_sums, side_out, side_in, space_grads,
        words, word_parts, partial, landing, tally, tally_side, tally_peers,
        local_sems, side_send, side_recv, key_send, key_recv, word_send, word_recv,
        tally_send, tally_recv, ring_send, ring_recv,
    ) = refs[12:38]
    early_scratch, late_scratch = refs[38:46], refs[46:54]
    place = Place(sizes)
    clips = sizes[NARROW]
    frame_count, chunks, cols, width = frames.shape
    split = Split(place, frame_count, chunks, cols)
    quarter = split.quarter
    heads = spread.shape[1] // LANES
    scale = 1.0 / math.sqrt(HEAD_DIM)
    line = Line(place, ring_send, ring_recv)
    greet(all_partners(place))

    def scatter(source, r, stage):
        return line.start(
            True,
            split.rows_view(source, r),
            split.landing_view(landing.at[stage * chunks + r]),
        )

    feed_scatters = [scatter(branch_part, r, 1) for r in range(chunks)]
    pending = fetch_weights(place, halves, full, local_sems, side_send, side_recv)
    early = reducers(place, [gradients.at[i] for i in range(4)], early_scratch)
    late = reducers(place, [space_grads.at[i] for i in range(4)], late_scratch)
    for job in early:
        job.split()
    block = words.shape[2]
    far = [lax.rem(place.n + step, clips) for step in range(1, clips)]
    word_copies = []
    for i, peer in enumerate(far):
        lanes = pl.ds(pl.multiple_of((peer * sizes[WIDE] + place.w) * block, block), block)
        for j, (source, target) in enumerate(
            (
                (prompt.at[:, lanes], words.at[i + 1]),
                (word_grads, word_parts.at[i + 1]),
                (condition, conditions.at[place.n]),
            )
        ):
            word_copies.append(
                send(
                    source, target, word_send.at[i, j], word_recv.at[i, j],
                    place.over_narrow(peer),
                )
            )
    mine = pl.ds(pl.multiple_of((place.n * sizes[WIDE] + place.w) * block, block), block)
    words[0] = prompt[:, mine]
    word_parts[0] = word_grads[...]
    conditions[place.n] = condition[...]
    tally[...] = jnp.zeros_like(tally)
    tally[2:3] = jnp.sum(g1_own[...] * a1_own[...], 0, keepdims=True)
    tally[3:5] = mlp_sums[0:2]
    tally[6:9] = back_sums[0:3]

    wait_all(pending[0])
    for r in range(chunks):
        spot = split.chunk(r)
        narrow = dot(e1[spot], full[0]).astype(BF16)
        wide_grad[spot] = dot(narrow, spread[...]).astype(BF16)
        line.tick()

    def attend(first, stop):
        @pl.loop(first, stop)
        def _(f):
            spots = split.spots(f)
            queries = jnp.concatenate([q1[0, spot] for spot in spots], 0)
            grads = jnp.concatenate([wide_grad[spot] for spot in spots], 0)
            keys = jnp.concatenate(
                [q1[1, spot] for spot in spots] + [side[0, spot] for spot in spots], 0
            )
            values = jnp.concatenate(
                [q1[2, spot] for spot in spots] + [side[1, spot] for spot in spots], 0
            )
            for h in range(heads):
                lanes = slice(h * LANES, (h + 1) * LANES)
                parts = attention_pull(
                    queries[:, lanes], keys[:, lanes], values[:, lanes], grads[:, lanes],
                    None, scale,
                )
                for r in range(chunks):
                    here = slice(r * cols, (r + 1) * cols)
                    there = slice((chunks + r) * cols, (chunks + r + 1) * cols)
                    wide_parts[0, spots[r], lanes] = parts[0][here].astype(BF16)
                    for j in range(2):
                        key_sums[j, spots[r], lanes] = parts[1 + j][here]
                        side_out[j, spots[r], lanes] = parts[1 + j][there].astype(BF16)

    outputs = []

    def finish_feed(r):
        kept = split.kept(r)
        line.finish(feed_scatters[r])
        branch = split.total(branch_part, landing.at[chunks + r], r)
        tally[5:6] += jnp.sum(
            own_cotangent(cotangent, live, split, r) * branch, 0, keepdims=True
        )
        after = (x3_own[kept] + vectors[5:6] * branch) * live_rows(live, split)
        output[split.own_frames(), r] = after.astype(BF16).reshape(split.frames, cols, width)
        outputs.append(line.start(False, split.frames_view(output, r)))

    quarters = frame_count // 4
    for part in range(4):
        attend(part * quarters, (part + 1) * quarters)
        line.tick(2)
        if part >= 2 and part - 2 < chunks:
            finish_feed(part - 2)
    for r in range(2, chunks):
        finish_feed(r)
    key_copy = send(side_out, side_in, key_send, key_recv, place.sibling())
    for job in early:
        job.spread()
    narrow_parts[0] = dot_tr(wide_parts[0], spread[...]).astype(BF16)
    line.tick(2)
    for copies in pending[1:]:
        wait_all(copies)
    key_copy.wait()
    for j in range(2):
        wide_parts[1 + j] = (key_sums[j] + side_in[j].astype(F32)).astype(BF16)
        narrow_parts[1 + j] = dot_tr(wide_parts[1 + j], spread[...]).astype(BF16)
    line.tick(2)
    scatters = []
    for r in range(chunks):
        spot = split.chunk(r)
        total = dot_tr(narrow_parts[0, spot], full[1])
        for i in (1, 2):
            total = total + dot_tr(narrow_parts[i, spot], full[1 + i])
        partial[spot] = total.astype(BF16)
        scatters.append(scatter(partial, r, 0))
        line.tick(2)

    space_grads[0] = dot_outer(e1[...], o1[...]).astype(BF16)
    late[0].split()
    for i in range(3):
        space_grads[1 + i] = dot_outer(h1[...], narrow_parts[i]).astype(BF16)
        late[1 + i].split()
        line.tick(2)
    for job in late:
        job.spread()
    gathers = []
    for r in range(chunks):
        kept = split.kept(r)
        line.finish(scatters[r])
        grad = split.total(partial, landing.at[r], r)
        x_own = frames[split.own_frames(), r].reshape(quarter, width).astype(F32)
        normed, inverse = norm_tile(x_own)
        tally[0:1] += jnp.sum(grad, 0, keepdims=True)
        tally[1:2] += jnp.sum(grad * normed, 0, keepdims=True)
        upstream = g1_own[kept] + norm_pull(normed, inverse, grad * vectors[1:2])
        frames_grad[split.own_frames(), r] = upstream.astype(BF16).reshape(
            split.frames, cols, width
        )
        gathers.append(line.start(False, split.frames_view(frames_grad, r)))

    tally_copy = send(tally, tally_side, tally_send.at[0], tally_recv.at[0], place.sibling())
    wait_all(word_copies)
    for j in range(2):
        total = dot_outer(words[0], word_parts[0, j, 0 : prompt.shape[0]])
        for step in range(1, clips):
            total = total + dot_outer(words[step], word_parts[step, j, 0 : prompt.shape[0]])
        prompt_out[j] = total
    tally_copy.wait()
    tally_side[...] = tally_side[...] + tally[...]
    peer_copies = [
        send(
            tally_side, tally_peers.at[step - 1], tally_send.at[step], tally_recv.at[step],
            place.over_tensor(step),
        )
        for step in range(1, sizes[TENSOR])
    ]
    for move in gathers:
        line.drain(move)
    for i, job in enumerate(early):
        job.finish(early_out.at[i])
    wait_all(peer_copies)
    total = tally_side[...]
    for step in range(sizes[TENSOR] - 1):
        total = total + tally_peers[step]
    merged[place.n] = total
    base = sizes[TENSOR]
    far_copies = [
        send(
            merged.at[place.n], merged.at[place.n],
            tally_send.at[base + i], tally_recv.at[base + i], place.over_narrow(peer),
        )
        for i, peer in enumerate(far)
    ]
    for i, job in enumerate(late):
        job.finish(space_out.at[i])
    for move in outputs + gathers:
        line.finish(move)
    wait_all(far_copies)
    for move in feed_scatters + outputs + scatters + gathers:
        line.release(move)


def space_call(sizes, acts, halves, gradients):
    frames, spread, prompt, condition = acts[2], acts[5], acts[10], acts[18]
    frame_count, chunks, cols, width = frames.shape
    rows = frame_count * cols
    tokens = rows * chunks
    quarter = rows // sizes[TENSOR]
    head_width, padded = spread.shape
    full_rows = halves[0].shape[0] * sizes[WIDE]
    parts = sizes[NARROW] * sizes[WIDE]
    block, word_block = width // parts, prompt.shape[1] // parts
    clips, peers = sizes[NARROW], sizes[TENSOR] - 1
    s = jax.ShapeDtypeStruct
    moves = 4 * chunks
    outs = [
        s(frames.shape, BF16), s(frames.shape, BF16),
        s((4, block, head_width), F32), s((4, block, head_width), F32),
        s((2, word_block, head_width), F32), s((clips, 16, width), F32),
        s((clips,) + condition.shape, F32),
    ]
    return pl.pallas_call(
        functools.partial(space_kernel, sizes),
        name="space",
        out_shape=outs,
        in_specs=[VM] * len(acts) + [ANY] * 5,
        out_specs=[VM] * len(outs),
        scratch_shapes=[
            VMEM((4, full_rows, head_width), BF16),
            VMEM((tokens, padded), BF16),
            VMEM((3, tokens, padded), BF16),
            VMEM((3, tokens, head_width), BF16),
            VMEM((2, tokens, padded), F32),
            VMEM((2, tokens, padded), BF16), VMEM((2, tokens, padded), BF16),
            VMEM((4, width, head_width), BF16),
            VMEM((clips, prompt.shape[0], word_block), BF16),
            VMEM((clips, 2, LANES, head_width), BF16),
            VMEM((tokens, width), BF16),
            VMEM((2 * chunks, 4, quarter, width), BF16),
            VMEM((16, width), F32), VMEM((16, width), F32), VMEM((peers, 16, width), F32),
            DMA((4,)), DMA((4,)), DMA((4,)), DMA(()), DMA(()),
            DMA((clips - 1, 3)), DMA((clips - 1, 3)),
            DMA((peers + clips,)), DMA((peers + clips,)),
            DMA((moves, 4, GRANULES)), DMA((moves, 4, GRANULES)),
        ]
        + reducer_scratch(sizes, 4, block, head_width)
        + reducer_scratch(sizes, 4, block, head_width),
        compiler_params=pltpu.CompilerParams(
            collective_id=4, has_side_effects=True, vmem_limit_bytes=61 << 20
        ),
    )(*acts, *halves, gradients)


def fused_on_device(
    sizes,
    frames, cotangent, prompt, timestep, clip_lengths, text_lengths,
    modulation_weight, modulation_bias, space_query, space_key, space_value, space_out,
    time_gain, time_query, time_key, time_value, time_out, time_gate, cross_gain, cross_query,
    prompt_key, prompt_value, cross_out, feed_up, feed_down,
):
    frame_count, width = frames.shape[1], frames.shape[4]
    cols = frames.shape[2] * frames.shape[3] // CHUNKS
    head_width = space_query.shape[1]
    condition, vectors, live, key_live, word_live, spread = prepare(
        sizes, frames, timestep, clip_lengths, text_lengths, modulation_weight, modulation_bias,
        time_gain, time_gate, cross_gain, head_width,
    )
    tiles = frames.reshape(frame_count, CHUNKS, cols, width)
    pulls = cotangent.reshape(frame_count, CHUNKS, cols, width)
    live = jnp.broadcast_to(live.astype(F32)[:, None, None], (frame_count, 8, LANES))
    (
        h1, q1, side, o1, h2, q2, o2, h3, q3, kv3, o3, h4,
        a1_own, a2_own, x3_own, n2_own, n3_own, n4_own, inverses,
    ) = forward_call(
        sizes, tiles, vectors, key_live, word_live, spread, prompt[0],
        [space_query, space_key, space_value, space_out, time_query, time_key, time_value,
         time_out, cross_query, cross_out, prompt_key, prompt_value],
    )
    branch_part, e3, g3_own, up_grad, down_grad, mlp_sums = mlp_call(
        sizes, h4, pulls, vectors, live, n4_own, inverses, feed_up, feed_down
    )
    g1_own, e1, time_grads, word_grads, up_out, down_out, cross_grads, back_sums = back_call(
        sizes, cols,
        [e3, g3_own, n3_own, n2_own, inverses, a2_own, vectors, key_live, word_live, spread,
         h3, q3, kv3, o3, h2, q2, o2],
        [cross_out, cross_query, time_out, time_query, time_key, time_value],
        [up_grad, down_grad],
    )
    frames_grad, output, early_out, late_out, prompt_out, merged, conditions = space_call(
        sizes,
        [e1, g1_own, tiles, a1_own, vectors, spread, h1, q1, side, o1, prompt[0], word_grads,
         branch_part, x3_own, pulls, live, mlp_sums, back_sums, condition.astype(F32)[None]],
        [space_out, space_query, space_key, space_value],
        time_grads,
    )
    part = lax.axis_index(NARROW) * sizes[WIDE] + lax.axis_index(WIDE)
    block = width // (sizes[NARROW] * sizes[WIDE])
    slice_width = modulation_weight.shape[1]
    pulled = merged[:, :6].reshape(sizes[NARROW], 6 * width)
    own_pulled = lax.dynamic_slice_in_dim(
        pulled, lax.axis_index(TENSOR) * slice_width, slice_width, 1
    )
    own_condition = lax.dynamic_slice_in_dim(conditions[:, 0], part * block, block, 1)
    modulation_weight_grad = jnp.sum(own_condition[:, :, None] * own_pulled[:, None], 0)
    summed_rows = jnp.sum(merged, 0)
    bias_block = 6 * block
    modulation_bias_grad = lax.dynamic_slice_in_dim(
        summed_rows[:6].reshape(6 * width), part * bias_block, bias_block
    )
    cross_gain_grad, gate_rows, time_gain_grad = (
        lax.dynamic_slice_in_dim(summed_rows[i], part * block, block) for i in (6, 7, 8)
    )
    own_gate = jnp.tanh(lax.dynamic_slice_in_dim(time_gate, part * block, block))
    time_gate_grad = gate_rows * (1.0 - own_gate * own_gate)
    return (
        output.reshape(frames.shape), frames_grad.reshape(frames.shape),
        modulation_weight_grad, modulation_bias_grad,
        late_out[1], late_out[2], late_out[3], late_out[0],
        time_gain_grad, early_out[1], early_out[2], early_out[3], early_out[0], time_gate_grad,
        cross_gain_grad, cross_grads[1], prompt_out[0], prompt_out[1], cross_grads[0],
        up_out, down_out,
    )


CONTRACT_LAST = (((1,), (1,)), ((), ()))
CONTRACT_FIRST = (((0,), (0,)), ((), ()))


def matmul(left, right):
    return jnp.dot(left, right, preferred_element_type=jnp.float32)


def matmul_tr(left, right):
    return lax.dot_general(left, right, CONTRACT_LAST, preferred_element_type=jnp.float32)


def outer_sum(left, right):
    return lax.dot_general(left, right, CONTRACT_FIRST, preferred_element_type=jnp.float32)


def norm_rows(values):
    center = values - jnp.mean(values, -1, keepdims=True)
    inverse = lax.rsqrt(jnp.mean(center * center, -1, keepdims=True) + EPSILON)
    return (center * inverse, inverse)


def norm_back(normed, inverse, incoming):
    return inverse * (
        incoming
        - jnp.mean(incoming, -1, keepdims=True)
        - normed * jnp.mean(incoming * normed, -1, keepdims=True)
    )


def over_heads(partial_sum):
    return lax.psum(partial_sum.astype(jnp.bfloat16), TENSOR).astype(jnp.float32)


def attend_forward(queries, key_rows, values, allowed, pattern, score_scale):
    scores = jnp.where(
        allowed,
        jnp.einsum(pattern[0], queries, key_rows, preferred_element_type=jnp.float32) * score_scale,
        NEGATIVE,
    )
    row_max = jnp.max(scores, -1, keepdims=True)
    exponent = jnp.exp(scores - row_max)
    row_total = jnp.sum(exponent, -1, keepdims=True)
    attend = (exponent / row_total).astype(jnp.bfloat16)
    context = jnp.einsum(pattern[1], attend, values, preferred_element_type=jnp.float32)
    return (context.astype(jnp.bfloat16), row_max + jnp.log(row_total))


def attend_back(queries, key_rows, values, allowed, log_total, context_grad, pattern, score_scale):
    scores = jnp.where(
        allowed,
        jnp.einsum(pattern[0], queries, key_rows, preferred_element_type=jnp.float32) * score_scale,
        NEGATIVE,
    )
    attend = jnp.exp(scores - log_total)
    attend_grad = jnp.einsum(pattern[0], context_grad, values, preferred_element_type=jnp.float32)
    score_grad = (attend * (attend_grad - jnp.sum(attend * attend_grad, -1, keepdims=True))).astype(
        jnp.bfloat16
    )
    query_grad = (
        jnp.einsum(pattern[1], score_grad, key_rows, preferred_element_type=jnp.float32)
        * score_scale
    )
    key_grad = (
        jnp.einsum(pattern[2], score_grad, queries, preferred_element_type=jnp.float32)
        * score_scale
    )
    value_grad = jnp.einsum(
        pattern[2], attend.astype(jnp.bfloat16), context_grad, preferred_element_type=jnp.float32
    )
    return (query_grad, key_grad, value_grad)


def on_device(
    frames,
    cotangent,
    prompt,
    timestep,
    clip_lengths,
    text_lengths,
    modulation_weight,
    modulation_bias,
    space_query,
    space_key,
    space_value,
    space_out,
    time_gain,
    time_query,
    time_key,
    time_value,
    time_out,
    time_gate,
    cross_gain,
    cross_query,
    prompt_key,
    prompt_value,
    cross_out,
    feed_up,
    feed_down,
):
    frame_count = frames.shape[1]
    patch_count = frames.shape[2] * frames.shape[3]
    model_width = frames.shape[4]
    token_count = frame_count * patch_count
    score_scale = 1.0 / math.sqrt(HEAD_DIM)
    residual = frames.reshape(token_count, model_width).astype(jnp.float32)
    frame_live = jnp.arange(frame_count) < clip_lengths[0]
    token_live = jnp.repeat(frame_live, patch_count)[:, None]
    prompt_rows = prompt[0]
    word_live = jnp.arange(prompt_rows.shape[0]) < text_lengths[0]
    (
        modulation_weight,
        space_query,
        space_key,
        space_value,
        space_out,
        time_query,
        time_key,
        time_value,
        time_out,
        cross_query,
        prompt_key,
        prompt_value,
        cross_out,
        feed_up,
        feed_down,
    ) = (
        lax.all_gather(modulation_weight, WIDE, axis=0, tiled=True),
        lax.all_gather(space_query, WIDE, axis=0, tiled=True),
        lax.all_gather(space_key, WIDE, axis=0, tiled=True),
        lax.all_gather(space_value, WIDE, axis=0, tiled=True),
        lax.all_gather(space_out, WIDE, axis=0, tiled=True),
        lax.all_gather(time_query, WIDE, axis=0, tiled=True),
        lax.all_gather(time_key, WIDE, axis=0, tiled=True),
        lax.all_gather(time_value, WIDE, axis=0, tiled=True),
        lax.all_gather(time_out, WIDE, axis=0, tiled=True),
        lax.all_gather(cross_query, WIDE, axis=0, tiled=True),
        lax.all_gather(prompt_key, WIDE, axis=0, tiled=True),
        lax.all_gather(prompt_value, WIDE, axis=0, tiled=True),
        lax.all_gather(cross_out, WIDE, axis=0, tiled=True),
        lax.all_gather(feed_up, WIDE, axis=0, tiled=True),
        lax.all_gather(feed_down, WIDE, axis=0, tiled=True),
    )
    head_width = space_query.shape[1]
    head_count = head_width // HEAD_DIM
    split_heads = (frame_count, patch_count, head_count, HEAD_DIM)
    half_width = model_width // 2
    frequency = jnp.exp(-math.log(10000.0) * jnp.arange(half_width, dtype=jnp.float32) / half_width)
    angles = timestep[0].astype(jnp.float32) * frequency
    condition = jax.nn.silu(jnp.concatenate([jnp.cos(angles), jnp.sin(angles)])).astype(
        jnp.bfloat16
    )
    slice_width = modulation_weight.shape[1]
    slice_start = lax.axis_index(TENSOR) * slice_width
    own_modulation = matmul(condition[None, :], modulation_weight)[0] + lax.dynamic_slice_in_dim(
        modulation_bias, slice_start, slice_width
    )
    modulation = lax.all_gather(own_modulation, TENSOR, axis=0, tiled=True)
    shift_one, scale_one, gate_one, shift_two, scale_two, gate_two = jnp.split(modulation, 6)
    normed_one, inverse_one = norm_rows(residual)
    input_one = (normed_one * (1.0 + scale_one) + shift_one).astype(jnp.bfloat16)
    query_one = matmul(input_one, space_query).astype(jnp.bfloat16).reshape(split_heads)
    key_one = matmul(input_one, space_key).astype(jnp.bfloat16).reshape(split_heads)
    value_one = matmul(input_one, space_value).astype(jnp.bfloat16).reshape(split_heads)
    key_frame, value_frame = (
        lax.all_gather(key_one, WIDE, axis=1, tiled=True),
        lax.all_gather(value_one, WIDE, axis=1, tiled=True),
    )
    space_pattern = ("fphe,fkhe->fhpk", "fhpk,fkhe->fphe", "fhpk,fphe->fkhe")
    every_patch = jnp.ones((key_frame.shape[1],), jnp.bool_)
    context_one, log_one = attend_forward(
        query_one, key_frame, value_frame, every_patch, space_pattern, score_scale
    )
    context_one = context_one.reshape(token_count, head_width)
    branch_one = over_heads(matmul_tr(context_one, space_out))
    after_one = residual + gate_one * branch_one
    normed_two, inverse_two = norm_rows(after_one)
    input_two = (normed_two * time_gain).astype(jnp.bfloat16)
    query_two = matmul(input_two, time_query).astype(jnp.bfloat16).reshape(split_heads)
    key_two = matmul(input_two, time_key).astype(jnp.bfloat16).reshape(split_heads)
    value_two = matmul(input_two, time_value).astype(jnp.bfloat16).reshape(split_heads)
    time_pattern = ("fphe,gphe->phfg", "phfg,gphe->fphe", "phfg,fphe->gphe")
    context_two, log_two = attend_forward(
        query_two, key_two, value_two, frame_live, time_pattern, score_scale
    )
    context_two = context_two.reshape(token_count, head_width)
    branch_two = over_heads(matmul_tr(context_two, time_out))
    gate_time = jnp.tanh(time_gate)
    after_two = after_one + gate_time * branch_two
    normed_three, inverse_three = norm_rows(after_two)
    input_three = (normed_three * cross_gain).astype(jnp.bfloat16)
    query_three = (
        matmul(input_three, cross_query)
        .astype(jnp.bfloat16)
        .reshape(token_count, head_count, HEAD_DIM)
    )
    word_keys = (
        matmul(prompt_rows, prompt_key).astype(jnp.bfloat16).reshape(-1, head_count, HEAD_DIM)
    )
    word_values = (
        matmul(prompt_rows, prompt_value).astype(jnp.bfloat16).reshape(-1, head_count, HEAD_DIM)
    )
    cross_pattern = ("nhe,jhe->nhj", "nhj,jhe->nhe", "nhj,nhe->jhe")
    context_three, log_three = attend_forward(
        query_three, word_keys, word_values, word_live, cross_pattern, score_scale
    )
    context_three = context_three.reshape(token_count, head_width)
    branch_three = over_heads(matmul_tr(context_three, cross_out))
    after_three = after_two + branch_three
    normed_four, inverse_four = norm_rows(after_three)
    input_four = (normed_four * (1.0 + scale_two) + shift_two).astype(jnp.bfloat16)
    pre_act = matmul(input_four, feed_up)
    hidden, gelu_pull = jax.vjp(lambda inner: jax.nn.gelu(inner, approximate=True), pre_act)
    hidden = hidden.astype(jnp.bfloat16)
    branch_four = over_heads(matmul_tr(hidden, feed_down))
    after_four = after_three + gate_two * branch_four
    output = jnp.where(token_live, after_four, 0.0).astype(jnp.bfloat16).reshape(frames.shape)
    upstream = jnp.where(
        token_live, cotangent.reshape(token_count, model_width).astype(jnp.float32), 0.0
    )
    feed_grad = (gate_two * upstream).astype(jnp.bfloat16)
    gate_two_grad = jnp.sum(upstream * branch_four, 0)
    feed_down_grad = outer_sum(feed_grad, hidden)
    pre_grad = gelu_pull(matmul(feed_grad, feed_down))[0].astype(jnp.bfloat16)
    feed_up_grad = outer_sum(input_four, pre_grad)
    input_four_grad = over_heads(matmul_tr(pre_grad, feed_up))
    shift_two_grad = jnp.sum(input_four_grad, 0)
    scale_two_grad = jnp.sum(input_four_grad * normed_four, 0)
    upstream = upstream + norm_back(normed_four, inverse_four, input_four_grad * (1.0 + scale_two))
    cross_grad = upstream.astype(jnp.bfloat16)
    cross_out_grad = outer_sum(cross_grad, context_three)
    context_grad = (
        matmul(cross_grad, cross_out)
        .astype(jnp.bfloat16)
        .reshape(token_count, head_count, HEAD_DIM)
    )
    query_grad, key_grad, value_grad = attend_back(
        query_three,
        word_keys,
        word_values,
        word_live,
        log_three,
        context_grad,
        cross_pattern,
        score_scale,
    )
    query_grad = query_grad.astype(jnp.bfloat16).reshape(token_count, head_width)
    cross_query_grad = outer_sum(input_three, query_grad)
    word_key_grad = key_grad.astype(jnp.bfloat16).reshape(-1, head_width)
    word_value_grad = value_grad.astype(jnp.bfloat16).reshape(-1, head_width)
    prompt_key_grad = outer_sum(prompt_rows, word_key_grad)
    prompt_value_grad = outer_sum(prompt_rows, word_value_grad)
    input_three_grad = over_heads(matmul_tr(query_grad, cross_query))
    cross_gain_grad = jnp.sum(input_three_grad * normed_three, 0)
    upstream = upstream + norm_back(normed_three, inverse_three, input_three_grad * cross_gain)
    time_grad = (gate_time * upstream).astype(jnp.bfloat16)
    time_gate_grad = jnp.sum(upstream * branch_two, 0) * (1.0 - gate_time * gate_time)
    time_out_grad = outer_sum(time_grad, context_two)
    context_grad = matmul(time_grad, time_out).astype(jnp.bfloat16).reshape(split_heads)
    query_grad, key_grad, value_grad = attend_back(
        query_two, key_two, value_two, frame_live, log_two, context_grad, time_pattern, score_scale
    )
    query_grad = query_grad.astype(jnp.bfloat16).reshape(token_count, head_width)
    key_grad = key_grad.astype(jnp.bfloat16).reshape(token_count, head_width)
    value_grad = value_grad.astype(jnp.bfloat16).reshape(token_count, head_width)
    time_query_grad = outer_sum(input_two, query_grad)
    time_key_grad = outer_sum(input_two, key_grad)
    time_value_grad = outer_sum(input_two, value_grad)
    input_two_grad = over_heads(
        matmul_tr(query_grad, time_query)
        + matmul_tr(key_grad, time_key)
        + matmul_tr(value_grad, time_value)
    )
    time_gain_grad = jnp.sum(input_two_grad * normed_two, 0)
    upstream = upstream + norm_back(normed_two, inverse_two, input_two_grad * time_gain)
    space_grad = (gate_one * upstream).astype(jnp.bfloat16)
    gate_one_grad = jnp.sum(upstream * branch_one, 0)
    space_out_grad = outer_sum(space_grad, context_one)
    context_grad = matmul(space_grad, space_out).astype(jnp.bfloat16).reshape(split_heads)
    key_frame, value_frame = (
        lax.all_gather(key_one, WIDE, axis=1, tiled=True),
        lax.all_gather(value_one, WIDE, axis=1, tiled=True),
    )
    query_grad, key_grad, value_grad = attend_back(
        query_one,
        key_frame,
        value_frame,
        every_patch,
        log_one,
        context_grad,
        space_pattern,
        score_scale,
    )
    key_grad, value_grad = (
        lax.psum_scatter(
            key_grad.astype(jnp.bfloat16), WIDE, scatter_dimension=1, tiled=True
        ).astype(jnp.float32),
        lax.psum_scatter(
            value_grad.astype(jnp.bfloat16), WIDE, scatter_dimension=1, tiled=True
        ).astype(jnp.float32),
    )
    query_grad = query_grad.astype(jnp.bfloat16).reshape(token_count, head_width)
    key_grad = key_grad.astype(jnp.bfloat16).reshape(token_count, head_width)
    value_grad = value_grad.astype(jnp.bfloat16).reshape(token_count, head_width)
    space_query_grad = outer_sum(input_one, query_grad)
    space_key_grad = outer_sum(input_one, key_grad)
    space_value_grad = outer_sum(input_one, value_grad)
    input_one_grad = over_heads(
        matmul_tr(query_grad, space_query)
        + matmul_tr(key_grad, space_key)
        + matmul_tr(value_grad, space_value)
    )
    shift_one_grad = jnp.sum(input_one_grad, 0)
    scale_one_grad = jnp.sum(input_one_grad * normed_one, 0)
    upstream = upstream + norm_back(normed_one, inverse_one, input_one_grad * (1.0 + scale_one))
    frames_grad = upstream.astype(jnp.bfloat16).reshape(frames.shape)
    modulation_bias_grad = jnp.concatenate(
        [
            shift_one_grad,
            scale_one_grad,
            gate_one_grad,
            shift_two_grad,
            scale_two_grad,
            gate_two_grad,
        ]
    )
    own_grad = lax.dynamic_slice_in_dim(modulation_bias_grad, slice_start, slice_width)
    modulation_weight_grad = condition.astype(jnp.float32)[:, None] * own_grad[None, :]
    (
        modulation_weight_grad,
        modulation_bias_grad,
        space_query_grad,
        space_key_grad,
        space_value_grad,
        space_out_grad,
        time_gain_grad,
        time_query_grad,
        time_key_grad,
        time_value_grad,
        time_out_grad,
        time_gate_grad,
        cross_gain_grad,
        cross_query_grad,
        prompt_key_grad,
        prompt_value_grad,
        cross_out_grad,
        feed_up_grad,
        feed_down_grad,
    ) = (
        lax.psum_scatter(
            modulation_weight_grad, (NARROW, WIDE), scatter_dimension=0, tiled=True
        ),
        lax.psum_scatter(modulation_bias_grad, (NARROW, WIDE), scatter_dimension=0, tiled=True),
        lax.psum_scatter(space_query_grad, (NARROW, WIDE), scatter_dimension=0, tiled=True),
        lax.psum_scatter(space_key_grad, (NARROW, WIDE), scatter_dimension=0, tiled=True),
        lax.psum_scatter(space_value_grad, (NARROW, WIDE), scatter_dimension=0, tiled=True),
        lax.psum_scatter(space_out_grad, (NARROW, WIDE), scatter_dimension=0, tiled=True),
        lax.psum_scatter(time_gain_grad, (NARROW, WIDE), scatter_dimension=0, tiled=True),
        lax.psum_scatter(time_query_grad, (NARROW, WIDE), scatter_dimension=0, tiled=True),
        lax.psum_scatter(time_key_grad, (NARROW, WIDE), scatter_dimension=0, tiled=True),
        lax.psum_scatter(time_value_grad, (NARROW, WIDE), scatter_dimension=0, tiled=True),
        lax.psum_scatter(time_out_grad, (NARROW, WIDE), scatter_dimension=0, tiled=True),
        lax.psum_scatter(time_gate_grad, (NARROW, WIDE), scatter_dimension=0, tiled=True),
        lax.psum_scatter(cross_gain_grad, (NARROW, WIDE), scatter_dimension=0, tiled=True),
        lax.psum_scatter(cross_query_grad, (NARROW, WIDE), scatter_dimension=0, tiled=True),
        lax.psum_scatter(prompt_key_grad, (NARROW, WIDE), scatter_dimension=0, tiled=True),
        lax.psum_scatter(prompt_value_grad, (NARROW, WIDE), scatter_dimension=0, tiled=True),
        lax.psum_scatter(cross_out_grad, (NARROW, WIDE), scatter_dimension=0, tiled=True),
        lax.psum_scatter(feed_up_grad, (NARROW, WIDE), scatter_dimension=0, tiled=True),
        lax.psum_scatter(feed_down_grad, (NARROW, WIDE), scatter_dimension=0, tiled=True),
    )
    return (
        output,
        frames_grad,
        modulation_weight_grad,
        modulation_bias_grad,
        space_query_grad,
        space_key_grad,
        space_value_grad,
        space_out_grad,
        time_gain_grad,
        time_query_grad,
        time_key_grad,
        time_value_grad,
        time_out_grad,
        time_gate_grad,
        cross_gain_grad,
        cross_query_grad,
        prompt_key_grad,
        prompt_value_grad,
        cross_out_grad,
        feed_up_grad,
        feed_down_grad,
    )


WEIGHT = P(WIDE, TENSOR)
OWNED = P((NARROW, WIDE), TENSOR)
ROWS = P((NARROW, WIDE))
PATCHES = P(NARROW, None, WIDE, None, None)
CLIP = P(NARROW)
COPIED = P()


def fits(sizes):
    return sizes[WIDE] == 2 and sizes[TENSOR] == 4 and sizes[NARROW] == 4


def solution(mesh):
    sizes = {name: mesh.shape[name] for name in mesh.axis_names}
    return jax.shard_map(
        functools.partial(fused_on_device, sizes) if fits(sizes) else on_device,
        mesh=mesh,
        in_specs=(
            (PATCHES, PATCHES, P(NARROW, None, None), CLIP, CLIP, CLIP)
            + (WEIGHT, COPIED, WEIGHT, WEIGHT, WEIGHT, WEIGHT)
            + (COPIED, WEIGHT, WEIGHT, WEIGHT, WEIGHT, COPIED)
            + (COPIED, WEIGHT, WEIGHT, WEIGHT, WEIGHT, WEIGHT, WEIGHT)
        ),
        out_specs=(
            (PATCHES, PATCHES, OWNED, ROWS, OWNED, OWNED, OWNED, OWNED)
            + (ROWS, OWNED, OWNED, OWNED, OWNED, ROWS)
            + (ROWS, OWNED, OWNED, OWNED, OWNED, OWNED, OWNED)
        ),
        check_vma=False,
    )
```

```python
import functools
import math

import jax
import jax.numpy as jnp
from jax import lax
from jax.experimental import pallas as pl
from jax.experimental.pallas import tpu as pltpu
from jax.sharding import PartitionSpec as P

HEAD_DIM = 72
LANES = 128
WHOLE = 256
CHUNKS = 4
EPSILON = 1e-06
NEGATIVE = -1e30
NARROW, WIDE, TENSOR = "narrow", "wide", "tensor"
COLS = "cols"
MESH_ID = pl.DeviceIdType.MESH
F32 = jnp.float32
BF16 = jnp.bfloat16
VMEM = pltpu.VMEM
VM = pl.BlockSpec(memory_space=pltpu.VMEM)
ANY = pl.BlockSpec(memory_space=pl.ANY)
DMA = pltpu.SemaphoreType.DMA


def dot(left, right):
    return jnp.dot(left, right, preferred_element_type=F32)


def dot_tr(left, right):
    return lax.dot_general(left, right, (((1,), (1,)), ((), ())), preferred_element_type=F32)


def dot_outer(left, right):
    return lax.dot_general(left, right, (((0,), (0,)), ((), ())), preferred_element_type=F32)


def norm_tile(values):
    center = values - jnp.mean(values, -1, keepdims=True)
    inverse = lax.rsqrt(jnp.mean(center * center, -1, keepdims=True) + EPSILON)
    return center * inverse, inverse


def norm_pull(normed, inverse, incoming):
    return inverse * (
        incoming
        - jnp.mean(incoming, -1, keepdims=True)
        - normed * jnp.mean(incoming * normed, -1, keepdims=True)
    )


def softmax_tile(scores):
    exponent = jnp.exp(scores - jnp.max(scores, -1, keepdims=True))
    return exponent / jnp.sum(exponent, -1, keepdims=True)


class Place:
    def __init__(self, sizes):
        self.sizes = sizes
        self.n = lax.axis_index(NARROW)
        self.w = lax.axis_index(WIDE)
        self.t = lax.axis_index(TENSOR)

    def tensor_peer(self, step):
        return lax.rem(self.t + step, self.sizes[TENSOR])

    def over_tensor(self, step):
        return (self.n, self.w, self.tensor_peer(step))

    def sibling(self):
        return (self.n, 1 - self.w, self.t)

    def over_narrow(self, peer):
        return (peer, self.w, self.t)


def greet(partners):
    barrier = pltpu.get_barrier_semaphore()
    for partner in partners:
        pl.semaphore_signal(barrier, inc=1, device_id=partner, device_id_type=MESH_ID)
    pl.semaphore_wait(barrier, len(partners))


def send(source, target, send_sem, recv_sem, partner):
    copy = pltpu.make_async_remote_copy(
        src_ref=source,
        dst_ref=target,
        send_sem=send_sem,
        recv_sem=recv_sem,
        device_id=partner,
        device_id_type=MESH_ID,
    )
    copy.start()
    return copy


class Transfer:
    def __init__(self, slot, scatter, view, landing, born):
        self.slot, self.scatter, self.view, self.landing = slot, scatter, view, landing
        self.step, self.born = 0, born


class Line:
    def __init__(self, place, send_sems, recv_sems):
        self.place, self.send_sems, self.recv_sems = place, send_sems, recv_sems
        self.granules = send_sems.shape[2]
        self.open, self.slots, self.clock = [], 0, 0

    def at(self, index, body):
        pl.when(self.place.t == index)(body)

    def hop(self, move, source, target, sent, received, g, peer):
        return pltpu.make_async_remote_copy(
            src_ref=source,
            dst_ref=target,
            send_sem=self.send_sems.at[move.slot, sent, g],
            recv_sem=self.recv_sems.at[move.slot, received, g],
            device_id=(self.place.n, self.place.w, peer),
            device_id_type=MESH_ID,
        )

    def reduce_hop(self, move, owner, lands, g, peer):
        return self.hop(
            move, move.view(owner, g), move.landing(lands, g), owner, lands, g, peer
        )

    def copy_hop(self, move, owner, sent, g, peer):
        block = move.view(owner, g)
        return self.hop(move, block, block, sent, owner, g, peer)

    def start(self, scatter, view, landing=None):
        move = Transfer(self.slots, scatter, view, landing, self.clock)
        self.slots += 1
        if scatter:
            plan = {
                0: [(3, 3, 1), (2, 2, 1), (1, 1, 1)],
                1: [(0, 0, 0)],
                2: [(3, 3, 3)],
                3: [(0, 0, 2), (1, 1, 2), (2, 2, 2)],
            }
            make = self.reduce_hop
        else:
            plan = {
                0: [(0, 0, 2), (0, 1, 1)],
                1: [(1, 0, 2), (1, 1, 0)],
                2: [(2, 0, 1), (2, 1, 3)],
                3: [(3, 0, 1), (3, 1, 2)],
            }
            make = self.copy_hop
        for device, hops in plan.items():

            def begin(hops=hops):
                for owner, index, peer in hops:
                    for g in range(self.granules):
                        make(move, owner, index, g, peer).start()

            self.at(device, begin)
        self.open.append(move)
        return move

    def pending_block(self, move, index, g):
        block = move.landing(index, g) if move.scatter else move.view(index, g)
        return self.hop(move, block, block, 0, index, g, 0)

    def relay(self, move, index, g, lands, sent, peer):
        self.pending_block(move, index, g).wait_recv()
        if move.scatter:
            block = move.landing(index, g)
            block[...] = (block[...].astype(F32) + move.view(index, g)[...].astype(F32)).astype(
                BF16
            )
            self.hop(move, block, move.landing(lands, g), index, lands, g, peer).start()
        else:
            self.copy_hop(move, index, sent, g, peer).start()

    def steps(self):
        return 2 * self.granules

    def advance(self, move):
        late, g = divmod(move.step, self.granules)
        move.step += 1
        if move.scatter:
            plan = {1: ((3, 2, 0, 3), (2, 3, 0, 2)), 2: ((0, 1, 0, 0), (1, 0, 0, 1))}
        else:
            plan = {1: ((2, 0, 2, 0), (3, 0, 3, 0)), 2: ((1, 0, 2, 3), (0, 0, 3, 3))}
        for device, pair in plan.items():
            index, lands, sent, peer = pair[late]

            def body(index=index, lands=lands, sent=sent, peer=peer):
                self.relay(move, index, g, lands, sent, peer)

            self.at(device, body)

    def tick(self, count=1, lag=2):
        self.clock += 1
        for _ in range(count):
            for move in self.open:
                if move.step < self.steps() and move.born + lag <= self.clock:
                    self.advance(move)
                    break

    def drain(self, move):
        while move.step < self.steps():
            self.advance(move)

    def finish(self, move):
        while move.step < self.steps():
            self.advance(move)
            for other in self.open:
                if other is not move and other.step < self.steps() and not other.scatter:
                    self.advance(other)
                    break
        self.open.remove(move)
        if move.scatter:
            plan = {0: (0, 1), 1: (1, 0), 2: (2, 3), 3: (3, 2)}
        else:
            plan = {0: (1, 2, 3), 1: (0,), 2: (3,), 3: (2, 1, 0)}
        for device, blocks in plan.items():

            def body(blocks=blocks):
                for index in blocks:
                    for g in range(self.granules):
                        self.pending_block(move, index, g).wait_recv()

            self.at(device, body)

    def release(self, move):
        for device in range(4):
            if move.scatter:
                sent = [d for d in range(4) if d != device]
            else:
                sent = range(4) if device in (1, 2) else range(2)

            def body(sent=sent):
                for index in sent:
                    for g in range(self.granules):
                        block = move.view(0, g)
                        self.hop(move, block, block, index, 0, g, 0).wait_send()

            self.at(device, body)


class Mover:
    def __init__(self, sems):
        self.sems, self.used, self.loads, self.saves = sems, 0, {}, []

    def go(self, source, target):
        copy = pltpu.make_async_copy(source, target, self.sems.at[self.used])
        self.used += 1
        copy.start()
        return copy

    def load(self, sources, targets):
        for source, target in zip(sources, targets):
            self.loads[id(target)] = self.go(source, target)

    def need(self, *targets):
        for target in targets:
            copy = self.loads.pop(id(target), None)
            if copy is not None:
                copy.wait()

    def keep(self, source, target):
        self.saves.append(self.go(source, target))

    def settle(self):
        wait_all(self.saves)


def stage_scratch(shapes):
    return [VMEM(shape.shape, shape.dtype) for shape in shapes] + [DMA((len(shapes) + 5,))]


def wait_all(copies):
    for copy in copies:
        copy.wait()


class Split:
    def __init__(self, place, frame_count, chunks, cols, group=1):
        parts = place.sizes[TENSOR]
        self.frame_count, self.chunks, self.cols = frame_count, chunks, cols
        self.rows = frame_count * cols
        self.quarter = self.rows // parts
        self.place, self.group = place, group
        self.frames = frame_count // parts

    def chunk(self, r):
        return pl.ds(r * self.rows * self.group, self.rows * self.group)

    def kept(self, r):
        return pl.ds(r * self.quarter, self.quarter)

    def own(self, r):
        start = r * self.rows + self.place.t * self.quarter
        return pl.ds(pl.multiple_of(start, self.quarter), self.quarter)

    def own_frames(self):
        return pl.ds(self.place.t * self.frames, self.frames)

    def rows_view(self, ref, r):
        def view(s, g):
            start = (r * self.group + g) * self.rows + s * self.quarter
            return ref.at[pl.ds(start, self.quarter)]

        return view

    def frames_view(self, ref, r):
        def view(s, g):
            return ref.at[pl.ds(s * self.frames, self.frames), r * self.group + g]

        return view

    def landing_view(self, ref):
        def view(s, g):
            return ref.at[s, g]

        return view

    def total(self, partial, landing, r):
        t = self.place.t
        beside = t + 1 - 2 * lax.rem(t, 2)
        return (
            partial[self.own(r)].astype(F32)
            + landing[t, r % self.group].astype(F32)
            + landing[beside, r % self.group].astype(F32)
        )

    def spots(self, f):
        return [
            pl.ds(pl.multiple_of(r * self.rows + f * self.cols, self.cols), self.cols)
            for r in range(self.chunks)
        ]


def neighbours(place):
    steps = range(1, place.sizes[TENSOR])
    return [place.sibling()] + [place.over_tensor(step) for step in steps]


def write_group_mask(group_mask, key_live, cols):
    shape = group_mask.shape
    row_id = lax.broadcasted_iota(jnp.int32, shape, 0)
    col_id = lax.broadcasted_iota(jnp.int32, shape, 1)
    group_mask[...] = jnp.where(
        lax.rem(row_id, cols) == lax.rem(col_id, cols),
        jnp.broadcast_to(key_live[0:1], shape),
        0.0,
    )


def group_partners(place):
    wide, tensor = place.sizes[WIDE], place.sizes[TENSOR]
    return [
        (place.n, lax.rem(place.w + dw, wide), lax.rem(place.t + dt, tensor))
        for dw in range(wide)
        for dt in range(tensor)
        if dw or dt
    ]


def forward_kernel(
    sizes,
    frames,
    condition,
    params,
    key_live,
    word_live,
    spread,
    prompt,
    *refs,
):
    weights, feed, modulation_weight = refs[:12], refs[12:14], refs[14]
    kept_out, full_out, feed_out, vectors_out = refs[15:34], refs[34], refs[35:37], refs[37]
    (
        h1, q1, side, o1, h2, q2, o2, h3, q3, kv3, o3, h4,
        a1_own, a2_own, x3_own, n2_own, n3_own, n4_own, inverses,
    ) = kept_refs = refs[38:57]
    (
        save_sems, turned, turned_prompt, full, full_prompt, feed_full, modulation_full,
        mine, shared, flat, vectors,
        wide_context, partial, landing, residual, group_mask,
        local_sems, side_send, side_recv, share_send, share_recv, kv_send, kv_recv,
        ring_send, ring_recv,
    ) = refs[57:]
    mover = Mover(save_sems)

    def keep(*sources):
        for source in sources:
            for kept_ref, out in zip(kept_refs, kept_out):
                if kept_ref is source:
                    mover.keep(source, out)

    place = Place(sizes)
    frame_count, chunks, cols, width = frames.shape
    split = Split(place, frame_count, chunks, cols)
    rows, half = split.rows, split.quarter
    heads = spread.shape[1] // LANES
    scale = 1.0 / math.sqrt(HEAD_DIM)
    chain = Line(place, ring_send, ring_recv)
    order = (0, 1, 2, 3, 4, 5, 6, 7, 8, 9, 10, 11)
    loads = {}

    def begin(i):
        target = turned.at[i] if i < 10 else turned_prompt.at[i - 10]
        loads[i] = pltpu.make_async_copy(weights[i], target, local_sems.at[i])
        loads[i].start()

    for i in order[:4]:
        begin(i)
    modulation_load = pltpu.make_async_copy(modulation_weight, modulation_full, local_sems.at[14])
    modulation_load.start()
    for i in order[4:]:
        begin(i)
    feed_spots, feed_loads = [], []
    for i in range(2):
        feed_half = feed[i].shape[0]
        feed_spots.append(pl.ds(pl.multiple_of(place.w * feed_half, feed_half), feed_half))
        feed_loads.append(
            pltpu.make_async_copy(
                feed[i], feed_full.at[i, feed_spots[i]], local_sems.at[12 + i]
            )
        )
        feed_loads[i].start()
    partners = group_partners(place)
    greet(partners)
    modulation_load.wait()
    slice_width = modulation_weight.shape[1]
    mine[...] = jnp.zeros_like(mine)
    mine[:, 0:slice_width] = dot(condition[...], modulation_full[...])[0:8]
    shifted = pltpu.roll(mine[...], slice_width % LANES, 1)
    mine[...] = jnp.where(lax.rem(place.t, 2) == 1, shifted, mine[...])
    slot = place.w * sizes[TENSOR] + place.t
    shared[slot] = mine[0:1]
    share_copies = [
        send(shared.at[slot], shared.at[slot], share_send.at[i], share_recv.at[i], partner)
        for i, partner in enumerate(partners)
    ]
    pending = {}

    def turn(*which):
        for i in which:
            loads[i].wait()
            half_rows = weights[i].shape[1]
            spot = pl.ds(pl.multiple_of(place.w * half_rows, half_rows), half_rows)
            if i < 10:
                full[i, spot] = turned[i].T
                target = full.at[i, spot]
            else:
                full_prompt[i - 10, spot] = turned_prompt[i - 10].T
                target = full_prompt.at[i - 10, spot]
            pending[i] = [
                send(target, target, side_send.at[i], side_recv.at[i], place.sibling())
            ]

    def ready(*which):
        for i in which:
            wait_all(pending.pop(i))

    turn(0, 1, 2)
    write_group_mask(group_mask, key_live, cols)
    wait_all(share_copies)
    flat[...] = params[:, 0 : flat.shape[1]]
    for slot in range(shared.shape[0]):
        start = slot % sizes[TENSOR] * slice_width // LANES * LANES
        flat[:, start : start + shared.shape[2]] += shared[slot]
    for j in range(6):
        row = flat[:, j * width : (j + 1) * width]
        vectors[j : j + 1] = 1.0 + row if j in (1, 4) else row
    for j in range(6, 9):
        row = params[:, j * width : (j + 1) * width]
        vectors[j : j + 1] = jnp.tanh(row) if j == 7 else row
    mover.keep(vectors, vectors_out)

    @pl.loop(0, frame_count)
    def _(f):
        for r in range(chunks):
            normed, _ = norm_tile(frames[f, r].astype(F32))
            h1[pl.ds(pl.multiple_of(r * rows + f * cols, cols), cols)] = (
                normed * vectors[1:2] + vectors[0:1]
            ).astype(BF16)

    keep(h1)

    def project(source, spot, weight, out, index):
        narrow = dot(source[spot], full[weight]).astype(BF16)
        out[index, spot] = dot(narrow, spread[...]).astype(BF16)

    ready(0, 1, 2)

    @pl.loop(0, 3)
    def _(i):
        for r in range(0, chunks * rows, WHOLE):
            project(h1, pl.ds(r, WHOLE), i, q1, i)

    kv_copies = [
        send(q1.at[1 + j], side.at[j], kv_send.at[j], kv_recv.at[j], place.sibling())
        for j in range(2)
    ]
    turn(3)
    wait_all(kv_copies)
    keep(q1, side)

    @pl.loop(0, frame_count)
    def _(f):
        spots = split.spots(f)
        queries = jnp.concatenate([q1[0, spot] for spot in spots], 0)
        keys = jnp.concatenate(
            [q1[1, spot] for spot in spots] + [side[0, spot] for spot in spots], 0
        )
        values = jnp.concatenate(
            [q1[2, spot] for spot in spots] + [side[1, spot] for spot in spots], 0
        )
        for h in range(heads):
            lanes = slice(h * LANES, (h + 1) * LANES)
            attend = softmax_tile(dot_tr(queries[:, lanes], keys[:, lanes]) * scale)
            context = dot(attend.astype(BF16), values[:, lanes]).astype(BF16)
            for r in range(chunks):
                wide_context[spots[r], lanes] = context[r * cols : (r + 1) * cols]

    sent = [None] * chunks

    def emit(r, out, weight, stage):
        spot = split.chunk(r)
        out[spot] = dot_tr(wide_context[spot], spread[...]).astype(BF16)
        if sent[r] is not None:
            chain.release(sent[r])
        partial[spot] = dot_tr(out[spot], full[weight]).astype(BF16)
        sent[r] = chain.start(
            True, split.rows_view(partial, r), split.landing_view(landing.at[stage * chunks + r])
        )
        return sent[r]

    def branch(r, stage):
        return split.total(partial, landing.at[stage * chunks + r], r)

    def settle(scatters, body, target):
        gathers = []
        for r in range(chunks):
            chain.finish(scatters[r])
            body(r)
            gathers.append(chain.start(False, split.rows_view(target, r)))
        return gathers

    ready(3)
    scatters = []
    for r in range(chunks):
        scatters.append(emit(r, o1, 3, 0))
        chain.tick(0)

    keep(o1)
    turn(4, 5, 6, 7)
    chain.tick(4)
    turn(10, 11)
    chain.tick(4)
    ready(10, 11)
    kv3[...] = jnp.zeros_like(kv3)
    for j in range(2):
        narrow = dot(prompt[...], full_prompt[j]).astype(BF16)
        kv3[j, 0 : prompt.shape[0]] = dot(narrow, spread[...]).astype(BF16)
        chain.tick(4)
    keep(kv3)

    def body_one(r):
        kept = split.kept(r)
        branch_one = branch(r, 0)
        a1_own[kept] = branch_one
        x_own = frames[split.own_frames(), r].reshape(half, width)
        after = x_own.astype(F32) + vectors[2:3] * branch_one
        normed, inverse = norm_tile(after)
        residual[kept] = after
        n2_own[kept] = normed
        inverses[0, kept] = jnp.broadcast_to(inverse, (half, LANES))
        h2[split.own(r)] = (normed * vectors[6:7]).astype(BF16)

    gathers = settle(scatters, body_one, h2)
    released = list(gathers)
    keep(a1_own, n2_own)
    turn(8, 9)
    feed_copies = []
    for i in range(2):
        feed_loads[i].wait()
        target = feed_full.at[i, feed_spots[i]]
        feed_copies.append(
            send(target, target, side_send.at[12 + i], side_recv.at[12 + i], place.sibling())
        )
    ready(4, 5, 6, 7)
    scatters = []
    for r in range(chunks):
        chain.finish(gathers[r])
        spot = split.chunk(r)
        for i in range(3):
            project(h2, spot, 4 + i, q2, i)
            chain.tick()
        for h in range(heads):
            lanes = slice(h * LANES, (h + 1) * LANES)
            scores = dot_tr(q2[0, spot, lanes], q2[1, spot, lanes]) * scale
            attend = softmax_tile(jnp.where(group_mask[...] > 0.5, scores, NEGATIVE))
            wide_context[spot, lanes] = dot(attend.astype(BF16), q2[2, spot, lanes]).astype(BF16)
        chain.tick()
        scatters.append(emit(r, o2, 7, 1))

    def body_two(r):
        kept = split.kept(r)
        branch_two = branch(r, 1)
        a2_own[kept] = branch_two
        after = residual[kept] + vectors[7:8] * branch_two
        normed, inverse = norm_tile(after)
        residual[kept] = after
        n3_own[kept] = normed
        inverses[1, kept] = jnp.broadcast_to(inverse, (half, LANES))
        h3[split.own(r)] = (normed * vectors[8:9]).astype(BF16)

    gathers = settle(scatters, body_two, h3)
    released += gathers
    keep(h2, q2, o2, a2_own, n3_own)
    ready(8, 9)
    mover.keep(full, full_out)
    scatters = []
    for r in range(chunks):
        chain.finish(gathers[r])
        spot = split.chunk(r)
        narrow = dot(h3[spot], full[8]).astype(BF16)
        q3[spot] = dot(narrow, spread[...]).astype(BF16)
        chain.tick()
        for h in range(heads):
            lanes = slice(h * LANES, (h + 1) * LANES)
            scores = dot_tr(q3[spot, lanes], kv3[0, :, lanes]) * scale
            attend = softmax_tile(jnp.where(word_live[0:1] > 0.5, scores, NEGATIVE))
            wide_context[spot, lanes] = dot(attend.astype(BF16), kv3[1, :, lanes]).astype(BF16)
        chain.tick()
        scatters.append(emit(r, o3, 9, 2))

    def body_three(r):
        kept = split.kept(r)
        after = residual[kept] + branch(r, 2)
        normed, inverse = norm_tile(after)
        x3_own[kept] = after
        n4_own[kept] = normed
        inverses[2, kept] = jnp.broadcast_to(inverse, (half, LANES))
        h4[split.own(r)] = (normed * vectors[4:5] + vectors[3:4]).astype(BF16)

    gathers = settle(scatters, body_three, h4)
    keep(h3, q3, o3, x3_own, n4_own, inverses)
    wait_all(feed_copies)
    for i in range(2):
        mover.keep(feed_full.at[i], feed_out[i])
    for move in gathers:
        chain.finish(move)
    keep(h4)
    for move in sent + released + gathers:
        chain.release(move)
    mover.settle()


def forward_call(
    sizes, frames, condition, params, key_live, word_live, spread, prompt, weights, feed,
    modulation_weight,
):
    frame_count, chunks, cols, width = frames.shape
    rows = frame_count * cols
    tokens = rows * chunks
    head_width, padded = spread.shape
    half = rows // sizes[TENSOR]
    kept = half * chunks
    full_rows = weights[0].shape[1] * sizes[WIDE]
    prompt_width = weights[10].shape[1] * sizes[WIDE]
    slice_width = modulation_weight.shape[1]
    group = sizes[WIDE] * sizes[TENSOR]
    placed = slice_width + slice_width % LANES
    moves = 6 * chunks
    s = jax.ShapeDtypeStruct
    wide_act, heads_act = s((tokens, width), BF16), s((tokens, head_width), BF16)
    triple, own = s((3, tokens, padded), BF16), s((kept, width), F32)
    outs = [
        wide_act, triple, s((2, tokens, padded), BF16), heads_act,
        wide_act, triple, heads_act,
        wide_act, s((tokens, padded), BF16), s((2, LANES, padded), BF16), heads_act,
        wide_act, own, own, own, own, own, own, s((3, kept, LANES), F32),
    ]
    return pl.pallas_call(
        functools.partial(forward_kernel, sizes),
        name="forward",
        out_shape=outs
        + [s((10, full_rows, head_width), BF16)]
        + [s((ref.shape[0] * sizes[WIDE], ref.shape[1]), BF16) for ref in feed]
        + [s((16, width), F32)],
        in_specs=[VM] * 7 + [ANY] * 15,
        out_specs=[ANY] * (len(outs) + 4),
        scratch_shapes=stage_scratch(outs)
        + [
            VMEM((10,) + weights[0].shape, BF16), VMEM((2,) + weights[10].shape, BF16),
            VMEM((10, full_rows, head_width), BF16),
            VMEM((2, prompt_width, head_width), BF16),
            VMEM((2, feed[0].shape[0] * sizes[WIDE], feed[0].shape[1]), BF16),
            VMEM(modulation_weight.shape, BF16),
            VMEM((8, placed), F32), VMEM((group, 1, placed), F32),
            VMEM((1, 6 * width), F32), VMEM((16, width), F32),
            VMEM((tokens, padded), BF16),
            VMEM((tokens, width), BF16),
            VMEM((3 * chunks, 4, 1, half, width), BF16),
            VMEM((kept, width), F32),
            VMEM((rows, rows), F32),
            DMA((15,)), DMA((14,)), DMA((14,)), DMA((group - 1,)), DMA((group - 1,)),
            DMA((2,)), DMA((2,)),
            DMA((moves, 4, 1)), DMA((moves, 4, 1)),
        ],
        compiler_params=pltpu.CompilerParams(
            collective_id=1, has_side_effects=True, vmem_limit_bytes=60 << 20
        ),
    )(
        frames, condition, params, key_live, word_live, spread, prompt, *weights, *feed,
        modulation_weight,
    )


def prepare(frames, timestep, clip_lengths, text_lengths, head_width):
    frame_count, width = frames.shape[1], frames.shape[4]
    cols = frames.shape[2] * frames.shape[3] // CHUNKS
    half_width = width // 2
    frequency = jnp.exp(-math.log(10000.0) * jnp.arange(half_width, dtype=F32) / half_width)
    angles = timestep[0].astype(F32) * frequency
    condition = jax.nn.silu(jnp.concatenate([jnp.cos(angles), jnp.sin(angles)])).astype(BF16)
    live = jnp.arange(frame_count) < clip_lengths[0]
    key_live = jnp.repeat(live, cols).astype(F32)[None]
    word_live = (jnp.arange(LANES) < text_lengths[0]).astype(F32)[None]
    heads = head_width // HEAD_DIM
    padded = jnp.arange(heads * LANES)
    source = jnp.where(
        padded % LANES < HEAD_DIM, padded // LANES * HEAD_DIM + padded % LANES, -1
    )
    spread = (jnp.arange(head_width)[:, None] == source[None]).astype(BF16)
    return condition, live, key_live, word_live, spread


def over_columns(width, tile, body):
    whole = width // tile

    @pl.loop(0, whole)
    def _(j):
        body(pl.ds(pl.multiple_of(j * tile, tile), tile))

    if width % tile:
        body(pl.ds(whole * tile, width % tile))


GELU_C = math.sqrt(2.0 / math.pi)


def live_rows(live, split):
    pieces = [
        jnp.broadcast_to(
            live[split.place.t * split.frames + f, 0:1, 0:1], (split.cols, 1)
        )
        for f in range(split.frames)
    ]
    return jnp.concatenate(pieces, 0)


def own_cotangent(cotangent, live, split, r):
    width = cotangent.shape[3]
    rows = cotangent[split.own_frames(), r].reshape(split.quarter, width)
    return rows.astype(F32) * live_rows(live, split)


def mlp_kernel(
    sizes,
    vectors, live, *refs,
):
    ins, outs = refs[:6], refs[6:12]
    h4, cotangent, n4_own, inverses, up, down = loaded = refs[12:18]
    branch_part, e3, g3_own, up_grad, down_grad, sums = made = refs[18:24]
    (
        move_sems, e4, hidden, pre_grad, partial, landing, ring_send, ring_recv,
    ) = refs[24:]
    place = Place(sizes)
    frame_count, chunks, cols, width = cotangent.shape
    group = landing.shape[2]
    split = Split(place, frame_count, chunks, cols, group)
    line = Line(place, ring_send, ring_recv)
    mover = Mover(move_sems)
    mover.load(
        [ins[i] for i in (1, 4, 5, 0, 2, 3)], [loaded[i] for i in (1, 4, 5, 0, 2, 3)]
    )
    greet(neighbours(place))
    mover.need(cotangent)

    @pl.loop(0, frame_count)
    def _(f):
        for r, spot in enumerate(split.spots(f)):
            e4[spot] = (
                vectors[5:6] * (cotangent[f, r].astype(F32) * live[f, 0:1, 0:1])
            ).astype(BF16)

    sums[...] = jnp.zeros_like(sums)
    mover.need(up, down, h4)
    scatters = []
    for r in range(chunks // group):
        spot = split.chunk(r)

        def act(lanes):
            pre = dot(h4[spot], up[:, lanes])
            grad = dot(e4[spot], down[:, lanes])
            inner = jnp.tanh(GELU_C * (pre + 0.044715 * pre * pre * pre))
            gate = 0.5 * (1.0 + inner)
            hidden[spot, lanes] = (pre * gate).astype(BF16)
            slope = gate + 0.5 * pre * (1.0 - inner * inner) * (
                GELU_C * (1.0 + 3.0 * 0.044715 * pre * pre)
            )
            pre_grad[spot, lanes] = (grad * slope).astype(BF16)

        over_columns(up.shape[1], 256, act)
        line.tick(1, 1)
        partial[spot] = dot_tr(pre_grad[spot], up[...]).astype(BF16)
        line.tick(1, 1)
        scatters.append(
            line.start(True, split.rows_view(partial, r), split.landing_view(landing.at[r]))
        )

    for r in range(chunks // group):
        spot = split.chunk(r)
        branch_part[spot] = dot_tr(hidden[spot], down[...]).astype(BF16)
        line.tick(1, 1)

    mover.keep(branch_part, outs[0])

    def down_tile(lanes):
        down_grad[:, lanes] = dot_outer(e4[...], hidden[:, lanes]).astype(BF16)

    def up_tile(lanes):
        up_grad[:, lanes] = dot_outer(h4[...], pre_grad[:, lanes]).astype(BF16)

    mover.need(n4_own, inverses)
    gathers = []
    for r in range(chunks // group):
        line.finish(scatters[r])
        for c in range(r * group, (r + 1) * group):
            kept = split.kept(c)
            grad = split.total(partial, landing.at[r], c)
            normed = n4_own[kept]
            sums[0:1] += jnp.sum(grad, 0, keepdims=True)
            sums[1:2] += jnp.sum(grad * normed, 0, keepdims=True)
            upstream = own_cotangent(cotangent, live, split, c) + norm_pull(
                normed, inverses[2, kept][:, 0:1], grad * vectors[4:5]
            )
            g3_own[kept] = upstream
            e3[split.own(c)] = upstream.astype(BF16)
        gathers.append(line.start(False, split.rows_view(e3, r)))
        if r == 0:
            over_columns(up.shape[1], 256, down_tile)
            line.tick(2, 1)

    mover.keep(g3_own, outs[2])
    mover.keep(sums, outs[5])
    mover.keep(down_grad, outs[4])
    over_columns(up.shape[1], 256, up_tile)
    mover.keep(up_grad, outs[3])
    for move in gathers:
        line.finish(move)
    mover.keep(e3, outs[1])
    for move in scatters + gathers:
        line.release(move)
    mover.settle()


def mlp_call(sizes, vectors, live, acts):
    frame_count, chunks, cols, width = acts[1].shape
    rows = frame_count * cols
    tokens = rows * chunks
    quarter = rows // sizes[TENSOR]
    hidden = acts[4].shape[1]
    s = jax.ShapeDtypeStruct
    group = max(1, chunks // 2)
    moves = 2 * chunks // group
    outs = [
        s((tokens, width), BF16), s((tokens, width), BF16), s((quarter * chunks, width), F32),
        s((width, hidden), BF16), s((width, hidden), BF16), s((8, width), F32),
    ]
    return pl.pallas_call(
        functools.partial(mlp_kernel, sizes),
        name="mlp",
        out_shape=outs,
        in_specs=[VM] * 2 + [ANY] * len(acts),
        out_specs=[ANY] * len(outs),
        scratch_shapes=stage_scratch(list(acts) + outs)
        + [
            VMEM((tokens, width), BF16), VMEM((tokens, hidden), BF16),
            VMEM((tokens, hidden), BF16),
            VMEM((tokens, width), BF16),
            VMEM((chunks // group, 4, group, quarter, width), BF16),
            DMA((moves, 4, group)), DMA((moves, 4, group)),
        ],
        compiler_params=pltpu.CompilerParams(
            collective_id=2, has_side_effects=True, vmem_limit_bytes=60 << 20
        ),
    )(vectors, live, *acts)


class Reducer:
    def __init__(self, place, source, mine, merged, received, sems):
        self.place, self.source = place, source
        self.mine, self.merged, self.received = mine, merged, received
        self.local, self.side_send, self.side_recv, self.far_send, self.far_recv = sems
        self.clips = place.sizes[NARROW]
        self.block = mine.shape[1]

    def rows(self, clip, core):
        start = (clip * self.place.sizes[WIDE] + core) * self.block
        return pl.ds(pl.multiple_of(start, self.block), self.block)

    def split(self):
        self.copies = []
        for clip in range(self.clips):
            local = pltpu.make_async_copy(
                self.source.at[self.rows(clip, self.place.w)],
                self.mine.at[clip],
                self.local.at[clip],
            )
            local.start()
            self.copies += [
                local,
                send(
                    self.source.at[self.rows(clip, 1 - self.place.w)],
                    self.merged.at[clip],
                    self.side_send.at[clip],
                    self.side_recv.at[clip],
                    self.place.sibling(),
                ),
            ]

    def spread(self):
        wait_all(self.copies)
        self.copies = []

        @pl.loop(0, self.clips)
        def _(clip):
            self.merged[clip] = (
                self.merged[clip].astype(F32) + self.mine[clip].astype(F32)
            ).astype(BF16)

        for step in (3, 1, 2) if self.clips == 4 else range(1, self.clips):
            peer = lax.rem(self.place.n + step, self.clips)
            self.copies.append(
                send(
                    self.merged.at[peer],
                    self.received.at[step - 1],
                    self.far_send.at[step - 1],
                    self.far_recv.at[step - 1],
                    self.place.over_narrow(peer),
                )
            )

    def finish(self, out):
        wait_all(self.copies)
        total = self.merged[self.place.n].astype(F32)
        for step in range(self.clips - 1):
            total = total + self.received[step].astype(F32)
        out[...] = total


def reducer_scratch(sizes, jobs, block, width):
    clips = sizes[NARROW]
    return [
        VMEM((jobs, clips, block, width), BF16),
        VMEM((jobs, clips, block, width), BF16),
        VMEM((jobs, clips - 1, block, width), BF16),
        DMA((jobs, clips)), DMA((jobs, clips)), DMA((jobs, clips)),
        DMA((jobs, clips - 1)), DMA((jobs, clips - 1)),
    ]


def reducers(place, sources, scratch):
    mine, merged, received, *sems = scratch
    return [
        Reducer(
            place, source, mine.at[i], merged.at[i], received.at[i], [sem.at[i] for sem in sems]
        )
        for i, source in enumerate(sources)
    ]


def all_partners(place):
    sizes = place.sizes
    return (
        [place.sibling()]
        + [place.over_tensor(step) for step in range(1, sizes[TENSOR])]
        + [
            place.over_narrow(lax.rem(place.n + step, sizes[NARROW]))
            for step in range(1, sizes[NARROW])
        ]
    )


def attention_pull(queries, keys, values, context_grad, mask, scale):
    scores = dot_tr(queries, keys) * scale
    if mask is not None:
        scores = jnp.where(mask, scores, NEGATIVE)
    attend = softmax_tile(scores)
    attend_grad = dot_tr(context_grad, values)
    score_grad = (
        attend * (attend_grad - jnp.sum(attend * attend_grad, -1, keepdims=True))
    ).astype(BF16)
    return (
        dot(score_grad, keys) * scale,
        dot_outer(score_grad, queries) * scale,
        dot_outer(attend.astype(BF16), context_grad),
    )


def back_kernel(
    sizes,
    vectors, key_live, word_live, spread, *refs,
):
    ins, full_in, gradients = refs[:13], refs[13], refs[14:16]
    outs = refs[16:24]
    (
        e3, g3_own, n3_own, n2_own, inverses, a2_own, h3, q3, kv3, o3, h2, q2, o2,
    ) = loaded = refs[24:37]
    g1_own, e1, time_grads, word_grads, up_out, down_out, cross_out, sums = refs[37:45]
    (
        move_sems, cross_full, time_full, wide_grad, wide_parts, narrow_parts, word_sums,
        word_side, e2, partial, landing, group_mask, cross_grads,
        full_sems, word_send, word_recv, ring_send, ring_recv,
    ) = refs[45:63]
    place = Place(sizes)
    tokens, width = e3.shape
    rows, cols = group_mask.shape[0], sizes[COLS]
    chunks = tokens // rows
    split = Split(place, rows // cols, chunks, cols)
    heads = spread.shape[1] // LANES
    scale = 1.0 / math.sqrt(HEAD_DIM)
    line = Line(place, ring_send, ring_recv)
    mover = Mover(move_sems)
    weights = []
    for i, (source, target) in enumerate(
        ((full_in.at[pl.ds(8, 2)], cross_full), (full_in.at[pl.ds(4, 4)], time_full))
    ):
        weights.append(pltpu.make_async_copy(source, target, full_sems.at[i]))
    weights[0].start()
    first = (0, 7, 8)
    order = first + tuple(i for i in range(13) if i not in first)
    mover.load([ins[i] for i in order], [loaded[i] for i in order])
    weights[1].start()
    greet(all_partners(place))
    feed = reducers(place, gradients, refs[63:71])
    cross = reducers(place, [cross_grads.at[0], cross_grads.at[1]], refs[71:79])
    for job in feed:
        job.split()
    write_group_mask(group_mask, key_live, cols)
    sums[...] = jnp.zeros_like(sums)
    word_sums[...] = jnp.zeros_like(word_sums)

    def context_grad(source, spot, weight):
        narrow = dot(source[spot], weight).astype(BF16)
        wide_grad[spot] = dot(narrow, spread[...]).astype(BF16)

    def scatter(r, stage):
        return line.start(
            True,
            split.rows_view(partial, r),
            split.landing_view(landing.at[stage * chunks + r]),
        )

    weights[0].wait()
    mover.need(e3, q3, kv3)
    scatters = []
    for r in range(chunks):
        spot = split.chunk(r)
        context_grad(e3, spot, cross_full[1])
        line.tick()
        for h in range(heads):
            lanes = slice(h * LANES, (h + 1) * LANES)
            query_grad, key_grad, value_grad = attention_pull(
                q3[spot, lanes], kv3[0, :, lanes], kv3[1, :, lanes], wide_grad[spot, lanes],
                word_live[0:1] > 0.5, scale,
            )
            wide_parts[0, spot, lanes] = query_grad.astype(BF16)
            word_sums[0, :, lanes] += key_grad
            word_sums[1, :, lanes] += value_grad
        line.tick()
        narrow_parts[0, spot] = dot_tr(wide_parts[0, spot], spread[...]).astype(BF16)
        partial[spot] = dot_tr(narrow_parts[0, spot], cross_full[0]).astype(BF16)
        scatters.append(scatter(r, 0))
    word_copy = send(word_sums, word_side, word_send, word_recv, place.sibling())
    mover.need(o3, h3)
    cross_grads[0] = dot_outer(e3[...], o3[...]).astype(BF16)
    line.tick(2)
    cross_grads[1] = dot_outer(h3[...], narrow_parts[0]).astype(BF16)
    line.tick(2)
    for job in cross:
        job.split()
    mover.need(*loaded)
    gathers = []
    for r in range(chunks):
        kept = split.kept(r)
        line.finish(scatters[r])
        grad = split.total(partial, landing.at[r], r)
        normed = n3_own[kept]
        sums[0:1] += jnp.sum(grad * normed, 0, keepdims=True)
        upstream = g3_own[kept] + norm_pull(
            normed, inverses[1, kept][:, 0:1], grad * vectors[8:9]
        )
        g1_own[kept] = upstream
        sums[1:2] += jnp.sum(upstream * a2_own[kept], 0, keepdims=True)
        e2[split.own(r)] = (vectors[7:8] * upstream).astype(BF16)
        gathers.append(line.start(False, split.rows_view(e2, r)))
        if r == 0:
            for job in feed:
                job.spread()
    for job in cross:
        job.spread()
    word_copy.wait()
    for j in range(2):
        word_grads[j] = dot_tr(
            (word_sums[j] + word_side[j]).astype(BF16), spread[...]
        ).astype(BF16)
    mover.keep(word_grads, outs[3])
    sent = scatters + gathers

    weights[1].wait()
    former, scatters = scatters, []
    for r in range(chunks):
        spot = split.chunk(r)
        line.finish(gathers[r])
        context_grad(e2, spot, time_full[3])
        line.tick()
        for h in range(heads):
            lanes = slice(h * LANES, (h + 1) * LANES)
            parts = attention_pull(
                q2[0, spot, lanes], q2[1, spot, lanes], q2[2, spot, lanes],
                wide_grad[spot, lanes], group_mask[...] > 0.5, scale,
            )
            for i in range(3):
                wide_parts[i, spot, lanes] = parts[i].astype(BF16)
            if h % 2:
                line.tick()
        total = None
        for i in range(3):
            narrow_parts[i, spot] = dot_tr(wide_parts[i, spot], spread[...]).astype(BF16)
            part = dot_tr(narrow_parts[i, spot], time_full[i])
            total = part if total is None else total + part
        line.tick()
        line.release(former[r])
        sent.remove(former[r])
        partial[spot] = total.astype(BF16)
        scatters.append(scatter(r, 1))
    sent += scatters
    time_grads[0] = dot_outer(e2[...], o2[...]).astype(BF16)
    line.tick(2)
    for i in range(3):
        time_grads[1 + i] = dot_outer(h2[...], narrow_parts[i]).astype(BF16)
        line.tick(1)
    mover.keep(time_grads, outs[2])

    gathers = []
    for r in range(chunks):
        kept = split.kept(r)
        line.finish(scatters[r])
        grad = split.total(partial, landing.at[chunks + r], r)
        normed = n2_own[kept]
        sums[2:3] += jnp.sum(grad * normed, 0, keepdims=True)
        upstream = g1_own[kept] + norm_pull(
            normed, inverses[0, kept][:, 0:1], grad * vectors[6:7]
        )
        g1_own[kept] = upstream
        e1[split.own(r)] = (vectors[2:3] * upstream).astype(BF16)
        gathers.append(line.start(False, split.rows_view(e1, r)))
    mover.keep(g1_own, outs[0])
    mover.keep(sums, outs[7])
    feed[0].finish(up_out)
    mover.keep(up_out, outs[4])
    line.drain(gathers[0])
    feed[1].finish(down_out)
    mover.keep(down_out, outs[5])
    for r in range(1, chunks):
        line.drain(gathers[r])
    cross[0].finish(cross_out.at[0])
    cross[1].finish(cross_out.at[1])
    mover.keep(cross_out, outs[6])
    for move in gathers:
        line.finish(move)
    mover.keep(e1, outs[1])
    for move in sent + gathers:
        line.release(move)
    mover.settle()


def back_call(sizes, cols, small, acts, full, gradients):
    spread = small[3]
    tokens, width = acts[0].shape
    rows = small[1].shape[1]
    chunks = tokens // rows
    quarter = rows // sizes[TENSOR]
    head_width, padded = spread.shape
    full_rows = full.shape[1]
    hidden = gradients[0].shape[1]
    block = width // (sizes[NARROW] * sizes[WIDE])
    s = jax.ShapeDtypeStruct
    moves = 4 * chunks
    outs = [
        s((quarter * chunks, width), F32), s((tokens, width), BF16),
        s((4, width, head_width), BF16), s((2, LANES, head_width), BF16),
        s((block, hidden), F32), s((block, hidden), F32), s((2, block, head_width), F32),
        s((8, width), F32),
    ]
    return pl.pallas_call(
        functools.partial(back_kernel, {**sizes, COLS: cols}),
        name="back",
        out_shape=outs,
        in_specs=[VM] * 4 + [ANY] * (len(acts) + 3),
        out_specs=[ANY] * len(outs),
        scratch_shapes=stage_scratch(list(acts) + outs)
        + [
            VMEM((2, full_rows, head_width), BF16), VMEM((4, full_rows, head_width), BF16),
            VMEM((tokens, padded), BF16),
            VMEM((3, tokens, padded), BF16),
            VMEM((3, tokens, head_width), BF16),
            VMEM((2, LANES, padded), F32), VMEM((2, LANES, padded), F32),
            VMEM((tokens, width), BF16),
            VMEM((tokens, width), BF16),
            VMEM((2 * chunks, 4, 1, quarter, width), BF16),
            VMEM((rows, rows), F32),
            VMEM((2, width, head_width), BF16),
            DMA((2,)), DMA(()), DMA(()),
            DMA((moves, 4, 1)), DMA((moves, 4, 1)),
        ]
        + reducer_scratch(sizes, 2, block, hidden)
        + reducer_scratch(sizes, 2, block, head_width),
        compiler_params=pltpu.CompilerParams(
            collective_id=3, has_side_effects=True, vmem_limit_bytes=60 << 20
        ),
    )(*small, *acts, full, *gradients)


def space_kernel(
    sizes,
    vectors, spread, live, mlp_sums, back_sums, condition, *refs,
):
    ins, full_in, gradients, outs = refs[:13], refs[13], refs[14], refs[15:22]
    (
        e1, g1_own, frames, a1_own, h1, q1, side, o1, prompt, word_grads, branch_part, x3_own,
        cotangent,
    ) = loaded = refs[22:35]
    frames_grad, output, early_out, space_out, prompt_out, merged, conditions = refs[35:42]
    (
        move_sems, query_full, out_full, wide_grad, wide_parts, narrow_parts, key_sums, side_out,
        side_in, space_grads, words, word_parts, partial, landing, tally, tally_side, tally_peers,
        full_sems, key_send, key_recv, word_send, word_recv,
        tally_send, tally_recv, ring_send, ring_recv,
    ) = refs[42:68]
    early_scratch, late_scratch = refs[68:76], refs[76:84]
    place = Place(sizes)
    clips = sizes[NARROW]
    frame_count, chunks, cols, width = frames.shape
    split = Split(place, frame_count, chunks, cols)
    quarter = split.quarter
    heads = spread.shape[1] // LANES
    scale = 1.0 / math.sqrt(HEAD_DIM)
    line = Line(place, ring_send, ring_recv)
    mover = Mover(move_sems)
    weights = [
        pltpu.make_async_copy(full_in.at[pl.ds(3, 1)], out_full, full_sems.at[0]),
        pltpu.make_async_copy(full_in.at[pl.ds(0, 3)], query_full, full_sems.at[1]),
    ]
    weights[0].start()
    first = (10, 8, 9, 0, 5, 6)
    order = first + tuple(i for i in range(13) if i not in first)
    mover.load([ins[i] for i in order], [loaded[i] for i in order])
    weights[1].start()
    greet(all_partners(place))
    mover.need(branch_part)

    def scatter(source, r, stage):
        return line.start(
            True,
            split.rows_view(source, r),
            split.landing_view(landing.at[stage * chunks + r]),
        )

    feed_scatters = [scatter(branch_part, r, 1) for r in range(chunks)]
    mover.need(prompt, word_grads)
    early = reducers(place, [gradients.at[i] for i in range(4)], early_scratch)
    late = reducers(place, [space_grads.at[i] for i in range(4)], late_scratch)
    for job in early:
        job.split()
    block = words.shape[2]
    far = [lax.rem(place.n + step, clips) for step in range(1, clips)]
    word_copies = []
    for i, peer in enumerate(far):
        lanes = pl.ds(pl.multiple_of((peer * sizes[WIDE] + place.w) * block, block), block)
        for j, (source, target) in enumerate(
            (
                (prompt.at[:, lanes], words.at[i + 1]),
                (word_grads, word_parts.at[i + 1]),
                (condition, conditions.at[place.n]),
            )
        ):
            word_copies.append(
                send(
                    source, target, word_send.at[i, j], word_recv.at[i, j],
                    place.over_narrow(peer),
                )
            )
    mine = pl.ds(pl.multiple_of((place.n * sizes[WIDE] + place.w) * block, block), block)
    words[0] = prompt[:, mine]
    word_parts[0] = word_grads[...]
    conditions[place.n] = condition[...]
    tally[...] = jnp.zeros_like(tally)
    tally[3:5] = mlp_sums[0:2]
    tally[6:9] = back_sums[0:3]

    weights[0].wait()
    mover.need(e1)
    for r in range(chunks):
        spot = split.chunk(r)
        narrow = dot(e1[spot], out_full[0]).astype(BF16)
        wide_grad[spot] = dot(narrow, spread[...]).astype(BF16)
        line.tick()

    mover.need(*loaded)
    weights[1].wait()
    tally[2:3] = jnp.sum(g1_own[...] * a1_own[...], 0, keepdims=True)

    def attend(first, stop):
        @pl.loop(first, stop)
        def _(f):
            spots = split.spots(f)
            queries = jnp.concatenate([q1[0, spot] for spot in spots], 0)
            grads = jnp.concatenate([wide_grad[spot] for spot in spots], 0)
            keys = jnp.concatenate(
                [q1[1, spot] for spot in spots] + [side[0, spot] for spot in spots], 0
            )
            values = jnp.concatenate(
                [q1[2, spot] for spot in spots] + [side[1, spot] for spot in spots], 0
            )
            for h in range(heads):
                lanes = slice(h * LANES, (h + 1) * LANES)
                parts = attention_pull(
                    queries[:, lanes], keys[:, lanes], values[:, lanes], grads[:, lanes],
                    None, scale,
                )
                for r in range(chunks):
                    here = slice(r * cols, (r + 1) * cols)
                    there = slice((chunks + r) * cols, (chunks + r + 1) * cols)
                    wide_parts[0, spots[r], lanes] = parts[0][here].astype(BF16)
                    for j in range(2):
                        key_sums[j, spots[r], lanes] = parts[1 + j][here]
                        side_out[j, spots[r], lanes] = parts[1 + j][there].astype(BF16)

    outputs = []

    def finish_feed(r):
        kept = split.kept(r)
        line.finish(feed_scatters[r])
        branch = split.total(branch_part, landing.at[chunks + r], r)
        tally[5:6] += jnp.sum(
            own_cotangent(cotangent, live, split, r) * branch, 0, keepdims=True
        )
        after = (x3_own[kept] + vectors[5:6] * branch) * live_rows(live, split)
        output[split.own_frames(), r] = after.astype(BF16).reshape(split.frames, cols, width)
        outputs.append(line.start(False, split.frames_view(output, r)))

    quarters = frame_count // 4
    for part in range(4):
        attend(part * quarters, (part + 1) * quarters)
        line.tick(2)
        if part >= 2 and part - 2 < chunks:
            finish_feed(part - 2)
    for r in range(2, chunks):
        finish_feed(r)
    key_copy = send(side_out, side_in, key_send, key_recv, place.sibling())
    for job in early:
        job.spread()
    narrow_parts[0] = dot_tr(wide_parts[0], spread[...]).astype(BF16)
    line.tick(2)
    key_copy.wait()
    for j in range(2):
        wide_parts[1 + j] = (key_sums[j] + side_in[j].astype(F32)).astype(BF16)
        narrow_parts[1 + j] = dot_tr(wide_parts[1 + j], spread[...]).astype(BF16)
    line.tick(2)
    scatters = []
    for r in range(chunks):
        spot = split.chunk(r)
        total = dot_tr(narrow_parts[0, spot], query_full[0])
        for i in (1, 2):
            total = total + dot_tr(narrow_parts[i, spot], query_full[i])
        partial[spot] = total.astype(BF16)
        scatters.append(scatter(partial, r, 0))
        line.tick(2)

    space_grads[0] = dot_outer(e1[...], o1[...]).astype(BF16)
    late[0].split()
    for i in range(3):
        space_grads[1 + i] = dot_outer(h1[...], narrow_parts[i]).astype(BF16)
        late[1 + i].split()
        line.tick(2)
    for job in late:
        job.spread()
    gathers = []
    for r in range(chunks):
        kept = split.kept(r)
        line.finish(scatters[r])
        grad = split.total(partial, landing.at[r], r)
        x_own = frames[split.own_frames(), r].reshape(quarter, width).astype(F32)
        normed, inverse = norm_tile(x_own)
        tally[0:1] += jnp.sum(grad, 0, keepdims=True)
        tally[1:2] += jnp.sum(grad * normed, 0, keepdims=True)
        upstream = g1_own[kept] + norm_pull(normed, inverse, grad * vectors[1:2])
        frames_grad[split.own_frames(), r] = upstream.astype(BF16).reshape(
            split.frames, cols, width
        )
        gathers.append(line.start(False, split.frames_view(frames_grad, r)))

    tally_copy = send(tally, tally_side, tally_send.at[0], tally_recv.at[0], place.sibling())
    wait_all(word_copies)
    for j in range(2):
        total = dot_outer(words[0], word_parts[0, j, 0 : prompt.shape[0]])
        for step in range(1, clips):
            total = total + dot_outer(words[step], word_parts[step, j, 0 : prompt.shape[0]])
        prompt_out[j] = total
    mover.keep(prompt_out, outs[4])
    mover.keep(conditions, outs[6])
    tally_copy.wait()
    tally_side[...] = tally_side[...] + tally[...]
    peer_copies = [
        send(
            tally_side, tally_peers.at[step - 1], tally_send.at[step], tally_recv.at[step],
            place.over_tensor(step),
        )
        for step in range(1, sizes[TENSOR])
    ]
    for move in gathers:
        line.drain(move)
    for i, job in enumerate(early):
        job.finish(early_out.at[i])
    mover.keep(early_out, outs[2])
    wait_all(peer_copies)
    total = tally_side[...]
    for step in range(sizes[TENSOR] - 1):
        total = total + tally_peers[step]
    merged[place.n] = total
    base = sizes[TENSOR]
    far_copies = [
        send(
            merged.at[place.n], merged.at[place.n],
            tally_send.at[base + i], tally_recv.at[base + i], place.over_narrow(peer),
        )
        for i, peer in enumerate(far)
    ]
    for i, job in enumerate(late):
        job.finish(space_out.at[i])
    mover.keep(space_out, outs[3])
    for move in outputs:
        line.finish(move)
    mover.keep(output, outs[1])
    for move in gathers:
        line.finish(move)
    mover.keep(frames_grad, outs[0])
    wait_all(far_copies)
    mover.keep(merged, outs[5])
    for move in feed_scatters + outputs + scatters + gathers:
        line.release(move)
    mover.settle()


def space_call(sizes, small, acts, full, gradients):
    frames, spread, prompt, condition = acts[2], small[1], acts[8], small[5]
    frame_count, chunks, cols, width = frames.shape
    rows = frame_count * cols
    tokens = rows * chunks
    quarter = rows // sizes[TENSOR]
    head_width, padded = spread.shape
    full_rows = full.shape[1]
    parts = sizes[NARROW] * sizes[WIDE]
    block, word_block = width // parts, prompt.shape[1] // parts
    clips, peers = sizes[NARROW], sizes[TENSOR] - 1
    s = jax.ShapeDtypeStruct
    moves = 4 * chunks
    outs = [
        s(frames.shape, BF16), s(frames.shape, BF16),
        s((4, block, head_width), F32), s((4, block, head_width), F32),
        s((2, word_block, head_width), F32), s((clips, 16, width), F32),
        s((clips,) + condition.shape, F32),
    ]
    return pl.pallas_call(
        functools.partial(space_kernel, sizes),
        name="space",
        out_shape=outs,
        in_specs=[VM] * 6 + [ANY] * (len(acts) + 2),
        out_specs=[ANY] * len(outs),
        scratch_shapes=stage_scratch(list(acts) + outs)
        + [
            VMEM((3, full_rows, head_width), BF16), VMEM((1, full_rows, head_width), BF16),
            VMEM((tokens, padded), BF16),
            VMEM((3, tokens, padded), BF16),
            VMEM((3, tokens, head_width), BF16),
            VMEM((2, tokens, padded), F32),
            VMEM((2, tokens, padded), BF16), VMEM((2, tokens, padded), BF16),
            VMEM((4, width, head_width), BF16),
            VMEM((clips, prompt.shape[0], word_block), BF16),
            VMEM((clips, 2, LANES, head_width), BF16),
            VMEM((tokens, width), BF16),
            VMEM((2 * chunks, 4, 1, quarter, width), BF16),
            VMEM((16, width), F32), VMEM((16, width), F32), VMEM((peers, 16, width), F32),
            DMA((2,)), DMA(()), DMA(()),
            DMA((clips - 1, 3)), DMA((clips - 1, 3)),
            DMA((peers + clips,)), DMA((peers + clips,)),
            DMA((moves, 4, 1)), DMA((moves, 4, 1)),
        ]
        + reducer_scratch(sizes, 4, block, head_width)
        + reducer_scratch(sizes, 4, block, head_width),
        compiler_params=pltpu.CompilerParams(
            collective_id=4, has_side_effects=True, vmem_limit_bytes=61 << 20
        ),
    )(*small, *acts, full, gradients)


def fused_on_device(
    sizes,
    frames, cotangent, prompt, timestep, clip_lengths, text_lengths,
    modulation_weight, modulation_bias, space_query, space_key, space_value, space_out,
    time_gain, time_query, time_key, time_value, time_out, time_gate, cross_gain, cross_query,
    prompt_key, prompt_value, cross_out, feed_up, feed_down,
):
    frame_count, width = frames.shape[1], frames.shape[4]
    cols = frames.shape[2] * frames.shape[3] // CHUNKS
    head_width = space_query.shape[1]
    condition, live, key_live, word_live, spread = prepare(
        frames, timestep, clip_lengths, text_lengths, head_width
    )
    half_condition = lax.dynamic_slice_in_dim(
        condition, lax.axis_index(WIDE) * modulation_weight.shape[0], modulation_weight.shape[0]
    )
    params = jnp.concatenate([modulation_bias, time_gain, time_gate, cross_gain])[None]
    tiles = frames.reshape(frame_count, CHUNKS, cols, width)
    pulls = cotangent.reshape(frame_count, CHUNKS, cols, width)
    live = jnp.broadcast_to(live.astype(F32)[:, None, None], (frame_count, 8, LANES))
    (
        h1, q1, side, o1, h2, q2, o2, h3, q3, kv3, o3, h4,
        a1_own, a2_own, x3_own, n2_own, n3_own, n4_own, inverses, full, up, down, vectors,
    ) = forward_call(
        sizes, tiles, jnp.broadcast_to(half_condition[None], (16, half_condition.shape[0])),
        params, key_live, word_live, spread, prompt[0],
        [
            weight.T
            for weight in (
                space_query, space_key, space_value, space_out, time_query, time_key,
                time_value, time_out, cross_query, cross_out, prompt_key, prompt_value,
            )
        ],
        [feed_up, feed_down], modulation_weight,
    )
    branch_part, e3, g3_own, up_grad, down_grad, mlp_sums = mlp_call(
        sizes, vectors, live, [h4, pulls, n4_own, inverses, up, down]
    )
    g1_own, e1, time_grads, word_grads, up_out, down_out, cross_grads, back_sums = back_call(
        sizes, cols, [vectors, key_live, word_live, spread],
        [e3, g3_own, n3_own, n2_own, inverses, a2_own, h3, q3, kv3, o3, h2, q2, o2],
        full, [up_grad, down_grad],
    )
    frames_grad, output, early_out, late_out, prompt_out, merged, conditions = space_call(
        sizes,
        [vectors, spread, live, mlp_sums, back_sums, condition.astype(F32)[None]],
        [e1, g1_own, tiles, a1_own, h1, q1, side, o1, prompt[0], word_grads, branch_part, x3_own,
         pulls],
        full, time_grads,
    )
    part = lax.axis_index(NARROW) * sizes[WIDE] + lax.axis_index(WIDE)
    block = width // (sizes[NARROW] * sizes[WIDE])
    slice_width = modulation_weight.shape[1]
    pulled = merged[:, :6].reshape(sizes[NARROW], 6 * width)
    own_pulled = lax.dynamic_slice_in_dim(
        pulled, lax.axis_index(TENSOR) * slice_width, slice_width, 1
    )
    own_condition = lax.dynamic_slice_in_dim(conditions[:, 0], part * block, block, 1)
    modulation_weight_grad = jnp.sum(own_condition[:, :, None] * own_pulled[:, None], 0)
    summed_rows = jnp.sum(merged, 0)
    bias_block = 6 * block
    modulation_bias_grad = lax.dynamic_slice_in_dim(
        summed_rows[:6].reshape(6 * width), part * bias_block, bias_block
    )
    cross_gain_grad, gate_rows, time_gain_grad = (
        lax.dynamic_slice_in_dim(summed_rows[i], part * block, block) for i in (6, 7, 8)
    )
    own_gate = jnp.tanh(lax.dynamic_slice_in_dim(time_gate, part * block, block))
    time_gate_grad = gate_rows * (1.0 - own_gate * own_gate)
    return (
        output.reshape(frames.shape), frames_grad.reshape(frames.shape),
        modulation_weight_grad, modulation_bias_grad,
        late_out[1], late_out[2], late_out[3], late_out[0],
        time_gain_grad, early_out[1], early_out[2], early_out[3], early_out[0], time_gate_grad,
        cross_gain_grad, cross_grads[1], prompt_out[0], prompt_out[1], cross_grads[0],
        up_out, down_out,
    )


CONTRACT_LAST = (((1,), (1,)), ((), ()))
CONTRACT_FIRST = (((0,), (0,)), ((), ()))


def matmul(left, right):
    return jnp.dot(left, right, preferred_element_type=jnp.float32)


def matmul_tr(left, right):
    return lax.dot_general(left, right, CONTRACT_LAST, preferred_element_type=jnp.float32)


def outer_sum(left, right):
    return lax.dot_general(left, right, CONTRACT_FIRST, preferred_element_type=jnp.float32)


def norm_rows(values):
    center = values - jnp.mean(values, -1, keepdims=True)
    inverse = lax.rsqrt(jnp.mean(center * center, -1, keepdims=True) + EPSILON)
    return (center * inverse, inverse)


def norm_back(normed, inverse, incoming):
    return inverse * (
        incoming
        - jnp.mean(incoming, -1, keepdims=True)
        - normed * jnp.mean(incoming * normed, -1, keepdims=True)
    )


def over_heads(partial_sum):
    return lax.psum(partial_sum.astype(jnp.bfloat16), TENSOR).astype(jnp.float32)


def attend_forward(queries, key_rows, values, allowed, pattern, score_scale):
    scores = jnp.where(
        allowed,
        jnp.einsum(pattern[0], queries, key_rows, preferred_element_type=jnp.float32) * score_scale,
        NEGATIVE,
    )
    row_max = jnp.max(scores, -1, keepdims=True)
    exponent = jnp.exp(scores - row_max)
    row_total = jnp.sum(exponent, -1, keepdims=True)
    attend = (exponent / row_total).astype(jnp.bfloat16)
    context = jnp.einsum(pattern[1], attend, values, preferred_element_type=jnp.float32)
    return (context.astype(jnp.bfloat16), row_max + jnp.log(row_total))


def attend_back(queries, key_rows, values, allowed, log_total, context_grad, pattern, score_scale):
    scores = jnp.where(
        allowed,
        jnp.einsum(pattern[0], queries, key_rows, preferred_element_type=jnp.float32) * score_scale,
        NEGATIVE,
    )
    attend = jnp.exp(scores - log_total)
    attend_grad = jnp.einsum(pattern[0], context_grad, values, preferred_element_type=jnp.float32)
    score_grad = (attend * (attend_grad - jnp.sum(attend * attend_grad, -1, keepdims=True))).astype(
        jnp.bfloat16
    )
    query_grad = (
        jnp.einsum(pattern[1], score_grad, key_rows, preferred_element_type=jnp.float32)
        * score_scale
    )
    key_grad = (
        jnp.einsum(pattern[2], score_grad, queries, preferred_element_type=jnp.float32)
        * score_scale
    )
    value_grad = jnp.einsum(
        pattern[2], attend.astype(jnp.bfloat16), context_grad, preferred_element_type=jnp.float32
    )
    return (query_grad, key_grad, value_grad)


def on_device(
    frames,
    cotangent,
    prompt,
    timestep,
    clip_lengths,
    text_lengths,
    modulation_weight,
    modulation_bias,
    space_query,
    space_key,
    space_value,
    space_out,
    time_gain,
    time_query,
    time_key,
    time_value,
    time_out,
    time_gate,
    cross_gain,
    cross_query,
    prompt_key,
    prompt_value,
    cross_out,
    feed_up,
    feed_down,
):
    frame_count = frames.shape[1]
    patch_count = frames.shape[2] * frames.shape[3]
    model_width = frames.shape[4]
    token_count = frame_count * patch_count
    score_scale = 1.0 / math.sqrt(HEAD_DIM)
    residual = frames.reshape(token_count, model_width).astype(jnp.float32)
    frame_live = jnp.arange(frame_count) < clip_lengths[0]
    token_live = jnp.repeat(frame_live, patch_count)[:, None]
    prompt_rows = prompt[0]
    word_live = jnp.arange(prompt_rows.shape[0]) < text_lengths[0]
    (
        modulation_weight,
        space_query,
        space_key,
        space_value,
        space_out,
        time_query,
        time_key,
        time_value,
        time_out,
        cross_query,
        prompt_key,
        prompt_value,
        cross_out,
        feed_up,
        feed_down,
    ) = (
        lax.all_gather(modulation_weight, WIDE, axis=0, tiled=True),
        lax.all_gather(space_query, WIDE, axis=0, tiled=True),
        lax.all_gather(space_key, WIDE, axis=0, tiled=True),
        lax.all_gather(space_value, WIDE, axis=0, tiled=True),
        lax.all_gather(space_out, WIDE, axis=0, tiled=True),
        lax.all_gather(time_query, WIDE, axis=0, tiled=True),
        lax.all_gather(time_key, WIDE, axis=0, tiled=True),
        lax.all_gather(time_value, WIDE, axis=0, tiled=True),
        lax.all_gather(time_out, WIDE, axis=0, tiled=True),
        lax.all_gather(cross_query, WIDE, axis=0, tiled=True),
        lax.all_gather(prompt_key, WIDE, axis=0, tiled=True),
        lax.all_gather(prompt_value, WIDE, axis=0, tiled=True),
        lax.all_gather(cross_out, WIDE, axis=0, tiled=True),
        lax.all_gather(feed_up, WIDE, axis=0, tiled=True),
        lax.all_gather(feed_down, WIDE, axis=0, tiled=True),
    )
    head_width = space_query.shape[1]
    head_count = head_width // HEAD_DIM
    split_heads = (frame_count, patch_count, head_count, HEAD_DIM)
    half_width = model_width // 2
    frequency = jnp.exp(-math.log(10000.0) * jnp.arange(half_width, dtype=jnp.float32) / half_width)
    angles = timestep[0].astype(jnp.float32) * frequency
    condition = jax.nn.silu(jnp.concatenate([jnp.cos(angles), jnp.sin(angles)])).astype(
        jnp.bfloat16
    )
    slice_width = modulation_weight.shape[1]
    slice_start = lax.axis_index(TENSOR) * slice_width
    own_modulation = matmul(condition[None, :], modulation_weight)[0] + lax.dynamic_slice_in_dim(
        modulation_bias, slice_start, slice_width
    )
    modulation = lax.all_gather(own_modulation, TENSOR, axis=0, tiled=True)
    shift_one, scale_one, gate_one, shift_two, scale_two, gate_two = jnp.split(modulation, 6)
    normed_one, inverse_one = norm_rows(residual)
    input_one = (normed_one * (1.0 + scale_one) + shift_one).astype(jnp.bfloat16)
    query_one = matmul(input_one, space_query).astype(jnp.bfloat16).reshape(split_heads)
    key_one = matmul(input_one, space_key).astype(jnp.bfloat16).reshape(split_heads)
    value_one = matmul(input_one, space_value).astype(jnp.bfloat16).reshape(split_heads)
    key_frame, value_frame = (
        lax.all_gather(key_one, WIDE, axis=1, tiled=True),
        lax.all_gather(value_one, WIDE, axis=1, tiled=True),
    )
    space_pattern = ("fphe,fkhe->fhpk", "fhpk,fkhe->fphe", "fhpk,fphe->fkhe")
    every_patch = jnp.ones((key_frame.shape[1],), jnp.bool_)
    context_one, log_one = attend_forward(
        query_one, key_frame, value_frame, every_patch, space_pattern, score_scale
    )
    context_one = context_one.reshape(token_count, head_width)
    branch_one = over_heads(matmul_tr(context_one, space_out))
    after_one = residual + gate_one * branch_one
    normed_two, inverse_two = norm_rows(after_one)
    input_two = (normed_two * time_gain).astype(jnp.bfloat16)
    query_two = matmul(input_two, time_query).astype(jnp.bfloat16).reshape(split_heads)
    key_two = matmul(input_two, time_key).astype(jnp.bfloat16).reshape(split_heads)
    value_two = matmul(input_two, time_value).astype(jnp.bfloat16).reshape(split_heads)
    time_pattern = ("fphe,gphe->phfg", "phfg,gphe->fphe", "phfg,fphe->gphe")
    context_two, log_two = attend_forward(
        query_two, key_two, value_two, frame_live, time_pattern, score_scale
    )
    context_two = context_two.reshape(token_count, head_width)
    branch_two = over_heads(matmul_tr(context_two, time_out))
    gate_time = jnp.tanh(time_gate)
    after_two = after_one + gate_time * branch_two
    normed_three, inverse_three = norm_rows(after_two)
    input_three = (normed_three * cross_gain).astype(jnp.bfloat16)
    query_three = (
        matmul(input_three, cross_query)
        .astype(jnp.bfloat16)
        .reshape(token_count, head_count, HEAD_DIM)
    )
    word_keys = (
        matmul(prompt_rows, prompt_key).astype(jnp.bfloat16).reshape(-1, head_count, HEAD_DIM)
    )
    word_values = (
        matmul(prompt_rows, prompt_value).astype(jnp.bfloat16).reshape(-1, head_count, HEAD_DIM)
    )
    cross_pattern = ("nhe,jhe->nhj", "nhj,jhe->nhe", "nhj,nhe->jhe")
    context_three, log_three = attend_forward(
        query_three, word_keys, word_values, word_live, cross_pattern, score_scale
    )
    context_three = context_three.reshape(token_count, head_width)
    branch_three = over_heads(matmul_tr(context_three, cross_out))
    after_three = after_two + branch_three
    normed_four, inverse_four = norm_rows(after_three)
    input_four = (normed_four * (1.0 + scale_two) + shift_two).astype(jnp.bfloat16)
    pre_act = matmul(input_four, feed_up)
    hidden, gelu_pull = jax.vjp(lambda inner: jax.nn.gelu(inner, approximate=True), pre_act)
    hidden = hidden.astype(jnp.bfloat16)
    branch_four = over_heads(matmul_tr(hidden, feed_down))
    after_four = after_three + gate_two * branch_four
    output = jnp.where(token_live, after_four, 0.0).astype(jnp.bfloat16).reshape(frames.shape)
    upstream = jnp.where(
        token_live, cotangent.reshape(token_count, model_width).astype(jnp.float32), 0.0
    )
    feed_grad = (gate_two * upstream).astype(jnp.bfloat16)
    gate_two_grad = jnp.sum(upstream * branch_four, 0)
    feed_down_grad = outer_sum(feed_grad, hidden)
    pre_grad = gelu_pull(matmul(feed_grad, feed_down))[0].astype(jnp.bfloat16)
    feed_up_grad = outer_sum(input_four, pre_grad)
    input_four_grad = over_heads(matmul_tr(pre_grad, feed_up))
    shift_two_grad = jnp.sum(input_four_grad, 0)
    scale_two_grad = jnp.sum(input_four_grad * normed_four, 0)
    upstream = upstream + norm_back(normed_four, inverse_four, input_four_grad * (1.0 + scale_two))
    cross_grad = upstream.astype(jnp.bfloat16)
    cross_out_grad = outer_sum(cross_grad, context_three)
    context_grad = (
        matmul(cross_grad, cross_out)
        .astype(jnp.bfloat16)
        .reshape(token_count, head_count, HEAD_DIM)
    )
    query_grad, key_grad, value_grad = attend_back(
        query_three,
        word_keys,
        word_values,
        word_live,
        log_three,
        context_grad,
        cross_pattern,
        score_scale,
    )
    query_grad = query_grad.astype(jnp.bfloat16).reshape(token_count, head_width)
    cross_query_grad = outer_sum(input_three, query_grad)
    word_key_grad = key_grad.astype(jnp.bfloat16).reshape(-1, head_width)
    word_value_grad = value_grad.astype(jnp.bfloat16).reshape(-1, head_width)
    prompt_key_grad = outer_sum(prompt_rows, word_key_grad)
    prompt_value_grad = outer_sum(prompt_rows, word_value_grad)
    input_three_grad = over_heads(matmul_tr(query_grad, cross_query))
    cross_gain_grad = jnp.sum(input_three_grad * normed_three, 0)
    upstream = upstream + norm_back(normed_three, inverse_three, input_three_grad * cross_gain)
    time_grad = (gate_time * upstream).astype(jnp.bfloat16)
    time_gate_grad = jnp.sum(upstream * branch_two, 0) * (1.0 - gate_time * gate_time)
    time_out_grad = outer_sum(time_grad, context_two)
    context_grad = matmul(time_grad, time_out).astype(jnp.bfloat16).reshape(split_heads)
    query_grad, key_grad, value_grad = attend_back(
        query_two, key_two, value_two, frame_live, log_two, context_grad, time_pattern, score_scale
    )
    query_grad = query_grad.astype(jnp.bfloat16).reshape(token_count, head_width)
    key_grad = key_grad.astype(jnp.bfloat16).reshape(token_count, head_width)
    value_grad = value_grad.astype(jnp.bfloat16).reshape(token_count, head_width)
    time_query_grad = outer_sum(input_two, query_grad)
    time_key_grad = outer_sum(input_two, key_grad)
    time_value_grad = outer_sum(input_two, value_grad)
    input_two_grad = over_heads(
        matmul_tr(query_grad, time_query)
        + matmul_tr(key_grad, time_key)
        + matmul_tr(value_grad, time_value)
    )
    time_gain_grad = jnp.sum(input_two_grad * normed_two, 0)
    upstream = upstream + norm_back(normed_two, inverse_two, input_two_grad * time_gain)
    space_grad = (gate_one * upstream).astype(jnp.bfloat16)
    gate_one_grad = jnp.sum(upstream * branch_one, 0)
    space_out_grad = outer_sum(space_grad, context_one)
    context_grad = matmul(space_grad, space_out).astype(jnp.bfloat16).reshape(split_heads)
    key_frame, value_frame = (
        lax.all_gather(key_one, WIDE, axis=1, tiled=True),
        lax.all_gather(value_one, WIDE, axis=1, tiled=True),
    )
    query_grad, key_grad, value_grad = attend_back(
        query_one,
        key_frame,
        value_frame,
        every_patch,
        log_one,
        context_grad,
        space_pattern,
        score_scale,
    )
    key_grad, value_grad = (
        lax.psum_scatter(
            key_grad.astype(jnp.bfloat16), WIDE, scatter_dimension=1, tiled=True
        ).astype(jnp.float32),
        lax.psum_scatter(
            value_grad.astype(jnp.bfloat16), WIDE, scatter_dimension=1, tiled=True
        ).astype(jnp.float32),
    )
    query_grad = query_grad.astype(jnp.bfloat16).reshape(token_count, head_width)
    key_grad = key_grad.astype(jnp.bfloat16).reshape(token_count, head_width)
    value_grad = value_grad.astype(jnp.bfloat16).reshape(token_count, head_width)
    space_query_grad = outer_sum(input_one, query_grad)
    space_key_grad = outer_sum(input_one, key_grad)
    space_value_grad = outer_sum(input_one, value_grad)
    input_one_grad = over_heads(
        matmul_tr(query_grad, space_query)
        + matmul_tr(key_grad, space_key)
        + matmul_tr(value_grad, space_value)
    )
    shift_one_grad = jnp.sum(input_one_grad, 0)
    scale_one_grad = jnp.sum(input_one_grad * normed_one, 0)
    upstream = upstream + norm_back(normed_one, inverse_one, input_one_grad * (1.0 + scale_one))
    frames_grad = upstream.astype(jnp.bfloat16).reshape(frames.shape)
    modulation_bias_grad = jnp.concatenate(
        [
            shift_one_grad,
            scale_one_grad,
            gate_one_grad,
            shift_two_grad,
            scale_two_grad,
            gate_two_grad,
        ]
    )
    own_grad = lax.dynamic_slice_in_dim(modulation_bias_grad, slice_start, slice_width)
    modulation_weight_grad = condition.astype(jnp.float32)[:, None] * own_grad[None, :]
    (
        modulation_weight_grad,
        modulation_bias_grad,
        space_query_grad,
        space_key_grad,
        space_value_grad,
        space_out_grad,
        time_gain_grad,
        time_query_grad,
        time_key_grad,
        time_value_grad,
        time_out_grad,
        time_gate_grad,
        cross_gain_grad,
        cross_query_grad,
        prompt_key_grad,
        prompt_value_grad,
        cross_out_grad,
        feed_up_grad,
        feed_down_grad,
    ) = (
        lax.psum_scatter(
            modulation_weight_grad, (NARROW, WIDE), scatter_dimension=0, tiled=True
        ),
        lax.psum_scatter(modulation_bias_grad, (NARROW, WIDE), scatter_dimension=0, tiled=True),
        lax.psum_scatter(space_query_grad, (NARROW, WIDE), scatter_dimension=0, tiled=True),
        lax.psum_scatter(space_key_grad, (NARROW, WIDE), scatter_dimension=0, tiled=True),
        lax.psum_scatter(space_value_grad, (NARROW, WIDE), scatter_dimension=0, tiled=True),
        lax.psum_scatter(space_out_grad, (NARROW, WIDE), scatter_dimension=0, tiled=True),
        lax.psum_scatter(time_gain_grad, (NARROW, WIDE), scatter_dimension=0, tiled=True),
        lax.psum_scatter(time_query_grad, (NARROW, WIDE), scatter_dimension=0, tiled=True),
        lax.psum_scatter(time_key_grad, (NARROW, WIDE), scatter_dimension=0, tiled=True),
        lax.psum_scatter(time_value_grad, (NARROW, WIDE), scatter_dimension=0, tiled=True),
        lax.psum_scatter(time_out_grad, (NARROW, WIDE), scatter_dimension=0, tiled=True),
        lax.psum_scatter(time_gate_grad, (NARROW, WIDE), scatter_dimension=0, tiled=True),
        lax.psum_scatter(cross_gain_grad, (NARROW, WIDE), scatter_dimension=0, tiled=True),
        lax.psum_scatter(cross_query_grad, (NARROW, WIDE), scatter_dimension=0, tiled=True),
        lax.psum_scatter(prompt_key_grad, (NARROW, WIDE), scatter_dimension=0, tiled=True),
        lax.psum_scatter(prompt_value_grad, (NARROW, WIDE), scatter_dimension=0, tiled=True),
        lax.psum_scatter(cross_out_grad, (NARROW, WIDE), scatter_dimension=0, tiled=True),
        lax.psum_scatter(feed_up_grad, (NARROW, WIDE), scatter_dimension=0, tiled=True),
        lax.psum_scatter(feed_down_grad, (NARROW, WIDE), scatter_dimension=0, tiled=True),
    )
    return (
        output,
        frames_grad,
        modulation_weight_grad,
        modulation_bias_grad,
        space_query_grad,
        space_key_grad,
        space_value_grad,
        space_out_grad,
        time_gain_grad,
        time_query_grad,
        time_key_grad,
        time_value_grad,
        time_out_grad,
        time_gate_grad,
        cross_gain_grad,
        cross_query_grad,
        prompt_key_grad,
        prompt_value_grad,
        cross_out_grad,
        feed_up_grad,
        feed_down_grad,
    )


WEIGHT = P(WIDE, TENSOR)
OWNED = P((NARROW, WIDE), TENSOR)
ROWS = P((NARROW, WIDE))
PATCHES = P(NARROW, None, WIDE, None, None)
CLIP = P(NARROW)
COPIED = P()


def fits(sizes):
    return sizes[WIDE] == 2 and sizes[TENSOR] == 4 and sizes[NARROW] == 4


def solution(mesh):
    sizes = {name: mesh.shape[name] for name in mesh.axis_names}
    return jax.shard_map(
        functools.partial(fused_on_device, sizes) if fits(sizes) else on_device,
        mesh=mesh,
        in_specs=(
            (PATCHES, PATCHES, P(NARROW, None, None), CLIP, CLIP, CLIP)
            + (WEIGHT, COPIED, WEIGHT, WEIGHT, WEIGHT, WEIGHT)
            + (COPIED, WEIGHT, WEIGHT, WEIGHT, WEIGHT, COPIED)
            + (COPIED, WEIGHT, WEIGHT, WEIGHT, WEIGHT, WEIGHT, WEIGHT)
        ),
        out_specs=(
            (PATCHES, PATCHES, OWNED, ROWS, OWNED, OWNED, OWNED, OWNED)
            + (ROWS, OWNED, OWNED, OWNED, OWNED, ROWS)
            + (ROWS, OWNED, OWNED, OWNED, OWNED, OWNED, OWNED)
        ),
        check_vma=False,
    )
```

```python
import functools
import math

import jax
import jax.numpy as jnp
import numpy as np
from jax import lax
from jax.experimental import pallas as pl
from jax.experimental.pallas import tpu as pltpu
from jax.sharding import PartitionSpec as P

HEAD_DIM = 72
LANES = 128
WHOLE = 256
CHUNKS = 4
EPSILON = 1e-06
NEGATIVE = -1e30
NARROW, WIDE, TENSOR = "narrow", "wide", "tensor"
COLS = "cols"
MESH_ID = pl.DeviceIdType.MESH
F32 = jnp.float32
BF16 = jnp.bfloat16
VMEM = pltpu.VMEM
VM = pl.BlockSpec(memory_space=pltpu.VMEM)
ANY = pl.BlockSpec(memory_space=pl.ANY)
DMA = pltpu.SemaphoreType.DMA


def dot(left, right):
    return jnp.dot(left, right, preferred_element_type=F32)


def dot_tr(left, right):
    return lax.dot_general(left, right, (((1,), (1,)), ((), ())), preferred_element_type=F32)


def dot_outer(left, right):
    return lax.dot_general(left, right, (((0,), (0,)), ((), ())), preferred_element_type=F32)


def norm_tile(values):
    center = values - jnp.mean(values, -1, keepdims=True)
    inverse = lax.rsqrt(jnp.mean(center * center, -1, keepdims=True) + EPSILON)
    return center * inverse, inverse


def norm_pull(normed, inverse, incoming):
    return inverse * (
        incoming
        - jnp.mean(incoming, -1, keepdims=True)
        - normed * jnp.mean(incoming * normed, -1, keepdims=True)
    )


def softmax_tile(scores):
    exponent = jnp.exp(scores - jnp.max(scores, -1, keepdims=True))
    return exponent / jnp.sum(exponent, -1, keepdims=True)


class Place:
    def __init__(self, sizes):
        self.sizes = sizes
        self.n = lax.axis_index(NARROW)
        self.w = lax.axis_index(WIDE)
        self.t = lax.axis_index(TENSOR)

    def tensor_peer(self, step):
        return lax.rem(self.t + step, self.sizes[TENSOR])

    def over_tensor(self, step):
        return (self.n, self.w, self.tensor_peer(step))

    def sibling(self):
        return (self.n, 1 - self.w, self.t)

    def over_narrow(self, peer):
        return (peer, self.w, self.t)


def greet(partners):
    barrier = pltpu.get_barrier_semaphore()
    for partner in partners:
        pl.semaphore_signal(barrier, inc=1, device_id=partner, device_id_type=MESH_ID)
    pl.semaphore_wait(barrier, len(partners))


def send(source, target, send_sem, recv_sem, partner):
    copy = pltpu.make_async_remote_copy(
        src_ref=source,
        dst_ref=target,
        send_sem=send_sem,
        recv_sem=recv_sem,
        device_id=partner,
        device_id_type=MESH_ID,
    )
    copy.start()
    return copy


class Transfer:
    def __init__(self, slot, scatter, view, landing, born):
        self.slot, self.scatter, self.view, self.landing = slot, scatter, view, landing
        self.step, self.born = 0, born


class Line:
    def __init__(self, place, send_sems, recv_sems):
        self.place, self.send_sems, self.recv_sems = place, send_sems, recv_sems
        self.granules = send_sems.shape[2]
        self.open, self.slots, self.clock = [], 0, 0

    def at(self, index, body):
        pl.when(self.place.t == index)(body)

    def hop(self, move, source, target, sent, received, g, peer):
        return pltpu.make_async_remote_copy(
            src_ref=source,
            dst_ref=target,
            send_sem=self.send_sems.at[move.slot, sent, g],
            recv_sem=self.recv_sems.at[move.slot, received, g],
            device_id=(self.place.n, self.place.w, peer),
            device_id_type=MESH_ID,
        )

    def reduce_hop(self, move, owner, lands, g, peer):
        return self.hop(
            move, move.view(owner, g), move.landing(lands, g), owner, lands, g, peer
        )

    def copy_hop(self, move, owner, sent, g, peer):
        block = move.view(owner, g)
        return self.hop(move, block, block, sent, owner, g, peer)

    def start(self, scatter, view, landing=None):
        move = Transfer(self.slots, scatter, view, landing, self.clock)
        self.slots += 1
        if scatter:
            plan = {
                0: [(3, 3, 1), (2, 2, 1), (1, 1, 1)],
                1: [(0, 0, 0)],
                2: [(3, 3, 3)],
                3: [(0, 0, 2), (1, 1, 2), (2, 2, 2)],
            }
            make = self.reduce_hop
        else:
            plan = {
                0: [(0, 0, 2), (0, 1, 1)],
                1: [(1, 0, 2), (1, 1, 0)],
                2: [(2, 0, 1), (2, 1, 3)],
                3: [(3, 0, 1), (3, 1, 2)],
            }
            make = self.copy_hop
        for device, hops in plan.items():

            def begin(hops=hops):
                for owner, index, peer in hops:
                    for g in range(self.granules):
                        make(move, owner, index, g, peer).start()

            self.at(device, begin)
        self.open.append(move)
        return move

    def pending_block(self, move, index, g):
        block = move.landing(index, g) if move.scatter else move.view(index, g)
        return self.hop(move, block, block, 0, index, g, 0)

    def relay(self, move, index, g, lands, sent, peer):
        self.pending_block(move, index, g).wait_recv()
        if move.scatter:
            block = move.landing(index, g)
            block[...] = (block[...].astype(F32) + move.view(index, g)[...].astype(F32)).astype(
                BF16
            )
            self.hop(move, block, move.landing(lands, g), index, lands, g, peer).start()
        else:
            self.copy_hop(move, index, sent, g, peer).start()

    def steps(self):
        return 2 * self.granules

    def advance(self, move):
        late, g = divmod(move.step, self.granules)
        move.step += 1
        if move.scatter:
            plan = {1: ((3, 2, 0, 3), (2, 3, 0, 2)), 2: ((0, 1, 0, 0), (1, 0, 0, 1))}
        else:
            plan = {1: ((2, 0, 2, 0), (3, 0, 3, 0)), 2: ((1, 0, 2, 3), (0, 0, 3, 3))}
        for device, pair in plan.items():
            index, lands, sent, peer = pair[late]

            def body(index=index, lands=lands, sent=sent, peer=peer):
                self.relay(move, index, g, lands, sent, peer)

            self.at(device, body)

    def tick(self, count=1, lag=2):
        self.clock += 1
        for _ in range(count):
            for move in self.open:
                if move.step < self.steps() and move.born + lag <= self.clock:
                    self.advance(move)
                    break

    def drain(self, move):
        while move.step < self.steps():
            self.advance(move)

    def finish(self, move):
        while move.step < self.steps():
            self.advance(move)
            for other in self.open:
                if other is not move and other.step < self.steps() and not other.scatter:
                    self.advance(other)
                    break
        self.open.remove(move)
        if move.scatter:
            plan = {0: (0, 1), 1: (1, 0), 2: (2, 3), 3: (3, 2)}
        else:
            plan = {0: (1, 2, 3), 1: (0,), 2: (3,), 3: (2, 1, 0)}
        for device, blocks in plan.items():

            def body(blocks=blocks):
                for index in blocks:
                    for g in range(self.granules):
                        self.pending_block(move, index, g).wait_recv()

            self.at(device, body)

    def release(self, move):
        for device in range(4):
            if move.scatter:
                sent = [d for d in range(4) if d != device]
            else:
                sent = range(4) if device in (1, 2) else range(2)

            def body(sent=sent):
                for index in sent:
                    for g in range(self.granules):
                        block = move.view(0, g)
                        self.hop(move, block, block, index, 0, g, 0).wait_send()

            self.at(device, body)


class Mover:
    def __init__(self, sems):
        self.sems, self.used, self.loads, self.saves = sems, 0, {}, []

    def go(self, source, target):
        copy = pltpu.make_async_copy(source, target, self.sems.at[self.used])
        self.used += 1
        copy.start()
        return copy

    def load(self, sources, targets):
        for source, target in zip(sources, targets):
            self.loads[id(target)] = self.go(source, target)

    def need(self, *targets):
        for target in targets:
            copy = self.loads.pop(id(target), None)
            if copy is not None:
                copy.wait()

    def keep(self, source, target):
        self.saves.append(self.go(source, target))

    def settle(self):
        wait_all(self.saves)


def stage_scratch(shapes):
    return [VMEM(shape.shape, shape.dtype) for shape in shapes] + [DMA((len(shapes) + 5,))]


def wait_all(copies):
    for copy in copies:
        copy.wait()


class Split:
    def __init__(self, place, frame_count, chunks, cols, group=1):
        parts = place.sizes[TENSOR]
        self.frame_count, self.chunks, self.cols = frame_count, chunks, cols
        self.rows = frame_count * cols
        self.quarter = self.rows // parts
        self.place, self.group = place, group
        self.frames = frame_count // parts

    def chunk(self, r):
        return pl.ds(r * self.rows * self.group, self.rows * self.group)

    def kept(self, r):
        return pl.ds(r * self.quarter, self.quarter)

    def own(self, r):
        start = r * self.rows + self.place.t * self.quarter
        return pl.ds(pl.multiple_of(start, self.quarter), self.quarter)

    def own_frames(self):
        return pl.ds(self.place.t * self.frames, self.frames)

    def rows_view(self, ref, r):
        def view(s, g):
            start = (r * self.group + g) * self.rows + s * self.quarter
            return ref.at[pl.ds(start, self.quarter)]

        return view

    def frames_view(self, ref, r):
        def view(s, g):
            return ref.at[pl.ds(s * self.frames, self.frames), r * self.group + g]

        return view

    def landing_view(self, ref):
        def view(s, g):
            return ref.at[s, g]

        return view

    def total(self, partial, landing, r):
        t = self.place.t
        beside = t + 1 - 2 * lax.rem(t, 2)
        return (
            partial[self.own(r)].astype(F32)
            + landing[t, r % self.group].astype(F32)
            + landing[beside, r % self.group].astype(F32)
        )

    def spots(self, f):
        return [
            pl.ds(pl.multiple_of(r * self.rows + f * self.cols, self.cols), self.cols)
            for r in range(self.chunks)
        ]


def neighbours(place):
    steps = range(1, place.sizes[TENSOR])
    return [place.sibling()] + [place.over_tensor(step) for step in steps]


def write_group_mask(group_mask, lengths, cols):
    shape = group_mask.shape
    row_id = lax.broadcasted_iota(jnp.int32, shape, 0)
    col_id = lax.broadcasted_iota(jnp.int32, shape, 1)
    live = col_id.astype(F32) < lengths[0:1, 0:1] * cols
    same = lax.rem(row_id, cols) == lax.rem(col_id, cols)
    group_mask[...] = jnp.where(jnp.logical_and(same, live), 1.0, 0.0)


def live_words(lengths):
    return lax.broadcasted_iota(jnp.int32, (1, LANES), 1).astype(F32) < lengths[1:2]


def pad_heads(turned):
    rows, columns = turned.shape
    filler = jnp.zeros((LANES - HEAD_DIM, columns), F32)
    pieces = []
    for start in range(0, rows, HEAD_DIM):
        pieces += [turned[start : start + HEAD_DIM].astype(F32), filler]
    return jnp.concatenate(pieces, 0).T.astype(BF16)


def group_partners(place):
    wide, tensor = place.sizes[WIDE], place.sizes[TENSOR]
    return [
        (place.n, lax.rem(place.w + dw, wide), lax.rem(place.t + dt, tensor))
        for dw in range(wide)
        for dt in range(tensor)
        if dw or dt
    ]


def forward_kernel(
    sizes,
    frames,
    condition,
    params,
    lengths,
    spread,
    prompt,
    *refs,
):
    weights, feed, modulation_weight = refs[:12], refs[12:14], refs[14]
    kept_out, full_out, feed_out, vectors_out = refs[15:34], refs[34], refs[35:37], refs[37]
    (
        h1, q1, side, o1, h2, q2, o2, h3, q3, kv3, o3, h4,
        a1_own, a2_own, x3_own, n2_own, n3_own, n4_own, inverses,
    ) = kept_refs = refs[38:57]
    (
        save_sems, turned, turned_prompt, full, full_prompt, feed_full, modulation_full,
        mine, shared, flat, vectors,
        wide_context, partial, landing, residual, group_mask,
        local_sems, side_send, side_recv, share_send, share_recv, kv_send, kv_recv,
        ring_send, ring_recv,
    ) = refs[57:]
    mover = Mover(save_sems)

    def keep(*sources):
        for source in sources:
            for kept_ref, out in zip(kept_refs, kept_out):
                if kept_ref is source:
                    mover.keep(source, out)

    place = Place(sizes)
    frame_count, chunks, cols, width = frames.shape
    split = Split(place, frame_count, chunks, cols)
    rows, half = split.rows, split.quarter
    heads = spread.shape[1] // LANES
    scale = 1.0 / math.sqrt(HEAD_DIM)
    chain = Line(place, ring_send, ring_recv)
    order = (0, 1, 2, 3, 4, 5, 6, 7, 8, 9, 10, 11)
    loads = {}

    def begin(i):
        target = turned.at[i] if i < 10 else turned_prompt.at[i - 10]
        loads[i] = pltpu.make_async_copy(weights[i], target, local_sems.at[i])
        loads[i].start()

    for i in order[:4]:
        begin(i)
    modulation_load = pltpu.make_async_copy(modulation_weight, modulation_full, local_sems.at[14])
    modulation_load.start()
    for i in order[4:]:
        begin(i)
    feed_spots, feed_loads = [], []
    for i in range(2):
        feed_half = feed[i].shape[0]
        feed_spots.append(pl.ds(pl.multiple_of(place.w * feed_half, feed_half), feed_half))
        feed_loads.append(
            pltpu.make_async_copy(
                feed[i], feed_full.at[i, feed_spots[i]], local_sems.at[12 + i]
            )
        )
        feed_loads[i].start()
    partners = group_partners(place)
    greet(partners)
    modulation_load.wait()
    slice_width = modulation_weight.shape[1]
    mine[...] = jnp.zeros_like(mine)
    mine[:, 0:slice_width] = dot(condition[...], modulation_full[...])[0:8]
    shifted = pltpu.roll(mine[...], slice_width % LANES, 1)
    mine[...] = jnp.where(lax.rem(place.t, 2) == 1, shifted, mine[...])
    slot = place.w * sizes[TENSOR] + place.t
    shared[slot] = mine[0:1]
    share_copies = [
        send(shared.at[slot], shared.at[slot], share_send.at[i], share_recv.at[i], partner)
        for i, partner in enumerate(partners)
    ]
    pending = {}

    def turn(*which):
        for i in which:
            loads[i].wait()
            half_rows = weights[i].shape[1]
            spot = pl.ds(pl.multiple_of(place.w * half_rows, half_rows), half_rows)
            if i < 10:
                full[i, spot] = pad_heads(turned[i])
                target = full.at[i, spot]
            else:
                full_prompt[i - 10, spot] = turned_prompt[i - 10].T
                target = full_prompt.at[i - 10, spot]
            pending[i] = [
                send(target, target, side_send.at[i], side_recv.at[i], place.sibling())
            ]

    def ready(*which):
        for i in which:
            wait_all(pending.pop(i))

    turn(0, 1, 2)
    write_group_mask(group_mask, lengths, cols)
    wait_all(share_copies)
    flat[...] = params[:, 0 : flat.shape[1]]
    for slot in range(shared.shape[0]):
        start = slot % sizes[TENSOR] * slice_width // LANES * LANES
        flat[:, start : start + shared.shape[2]] += shared[slot]
    for j in range(6):
        row = flat[:, j * width : (j + 1) * width]
        vectors[j : j + 1] = 1.0 + row if j in (1, 4) else row
    for j in range(6, 9):
        row = params[:, j * width : (j + 1) * width]
        vectors[j : j + 1] = jnp.tanh(row) if j == 7 else row
    mover.keep(vectors, vectors_out)

    @pl.loop(0, frame_count)
    def _(f):
        for r in range(chunks):
            normed, _ = norm_tile(frames[f, r].astype(F32))
            h1[pl.ds(pl.multiple_of(r * rows + f * cols, cols), cols)] = (
                normed * vectors[1:2] + vectors[0:1]
            ).astype(BF16)

    keep(h1)

    def project(source, spot, weight, out, index):
        out[index, spot] = dot(source[spot], full[weight]).astype(BF16)

    ready(0, 1, 2)

    @pl.loop(0, 3)
    def _(i):
        for r in range(0, chunks * rows, WHOLE):
            project(h1, pl.ds(r, WHOLE), i, q1, i)

    kv_copies = [
        send(q1.at[1 + j], side.at[j], kv_send.at[j], kv_recv.at[j], place.sibling())
        for j in range(2)
    ]
    turn(3)
    wait_all(kv_copies)
    keep(q1, side)

    @pl.loop(0, frame_count)
    def _(f):
        spots = split.spots(f)
        queries = jnp.concatenate([q1[0, spot] for spot in spots], 0)
        keys = jnp.concatenate(
            [q1[1, spot] for spot in spots] + [side[0, spot] for spot in spots], 0
        )
        values = jnp.concatenate(
            [q1[2, spot] for spot in spots] + [side[1, spot] for spot in spots], 0
        )
        for h in range(heads):
            lanes = slice(h * LANES, (h + 1) * LANES)
            attend = softmax_tile(dot_tr(queries[:, lanes], keys[:, lanes]) * scale)
            context = dot(attend.astype(BF16), values[:, lanes]).astype(BF16)
            for r in range(chunks):
                wide_context[spots[r], lanes] = context[r * cols : (r + 1) * cols]

    sent = [None] * chunks

    def emit(r, out, weight, stage):
        spot = split.chunk(r)
        if sent[r] is not None:
            chain.release(sent[r])
        partial[spot] = dot_tr(wide_context[spot], full[weight]).astype(BF16)
        sent[r] = chain.start(
            True, split.rows_view(partial, r), split.landing_view(landing.at[stage * chunks + r])
        )
        out[spot] = dot_tr(wide_context[spot], spread[...]).astype(BF16)
        return sent[r]

    def branch(r, stage):
        return split.total(partial, landing.at[stage * chunks + r], r)

    def settle(scatters, body, target):
        gathers = []
        for r in range(chunks):
            chain.finish(scatters[r])
            body(r)
            gathers.append(chain.start(False, split.rows_view(target, r)))
            chain.tick(4, 3)
        return gathers

    ready(3)
    scatters = []
    for r in range(chunks):
        scatters.append(emit(r, o1, 3, 0))
        chain.tick(0)

    keep(o1)
    turn(4, 5, 6, 7)
    chain.tick(4)
    turn(10, 11)
    chain.tick(4)
    ready(10, 11)
    kv3[...] = jnp.zeros_like(kv3)
    for j in range(2):
        narrow = dot(prompt[...], full_prompt[j]).astype(BF16)
        kv3[j, 0 : prompt.shape[0]] = dot(narrow, spread[...]).astype(BF16)
        chain.tick(4)
    keep(kv3)

    def body_one(r):
        kept = split.kept(r)
        branch_one = branch(r, 0)
        a1_own[kept] = branch_one
        x_own = frames[split.own_frames(), r].reshape(half, width)
        after = x_own.astype(F32) + vectors[2:3] * branch_one
        normed, inverse = norm_tile(after)
        residual[kept] = after
        n2_own[kept] = normed
        inverses[0, kept] = jnp.broadcast_to(inverse, (half, LANES))
        h2[split.own(r)] = (normed * vectors[6:7]).astype(BF16)

    gathers = settle(scatters, body_one, h2)
    released = list(gathers)
    keep(a1_own, n2_own)
    turn(8, 9)
    feed_copies = []
    for i in range(2):
        feed_loads[i].wait()
        target = feed_full.at[i, feed_spots[i]]
        feed_copies.append(
            send(target, target, side_send.at[12 + i], side_recv.at[12 + i], place.sibling())
        )
    ready(4, 5, 6, 7)
    scatters = []
    for r in range(chunks):
        chain.finish(gathers[r])
        spot = split.chunk(r)
        for i in range(3):
            project(h2, spot, 4 + i, q2, i)
            chain.tick()
        for h in range(heads):
            lanes = slice(h * LANES, (h + 1) * LANES)
            scores = dot_tr(q2[0, spot, lanes], q2[1, spot, lanes]) * scale
            attend = softmax_tile(jnp.where(group_mask[...] > 0.5, scores, NEGATIVE))
            wide_context[spot, lanes] = dot(attend.astype(BF16), q2[2, spot, lanes]).astype(BF16)
        chain.tick()
        scatters.append(emit(r, o2, 7, 1))

    def body_two(r):
        kept = split.kept(r)
        branch_two = branch(r, 1)
        a2_own[kept] = branch_two
        after = residual[kept] + vectors[7:8] * branch_two
        normed, inverse = norm_tile(after)
        residual[kept] = after
        n3_own[kept] = normed
        inverses[1, kept] = jnp.broadcast_to(inverse, (half, LANES))
        h3[split.own(r)] = (normed * vectors[8:9]).astype(BF16)

    gathers = settle(scatters, body_two, h3)
    released += gathers
    keep(h2, q2, o2, a2_own, n3_own)
    ready(8, 9)
    mover.keep(full, full_out)
    scatters = []
    for r in range(chunks):
        chain.finish(gathers[r])
        spot = split.chunk(r)
        q3[spot] = dot(h3[spot], full[8]).astype(BF16)
        chain.tick()
        for h in range(heads):
            lanes = slice(h * LANES, (h + 1) * LANES)
            scores = dot_tr(q3[spot, lanes], kv3[0, :, lanes]) * scale
            attend = softmax_tile(jnp.where(live_words(lengths), scores, NEGATIVE))
            wide_context[spot, lanes] = dot(attend.astype(BF16), kv3[1, :, lanes]).astype(BF16)
        chain.tick()
        scatters.append(emit(r, o3, 9, 2))

    def body_three(r):
        kept = split.kept(r)
        after = residual[kept] + branch(r, 2)
        normed, inverse = norm_tile(after)
        x3_own[kept] = after
        n4_own[kept] = normed
        inverses[2, kept] = jnp.broadcast_to(inverse, (half, LANES))
        h4[split.own(r)] = (normed * vectors[4:5] + vectors[3:4]).astype(BF16)

    gathers = settle(scatters, body_three, h4)
    keep(h3, q3, o3, x3_own, n4_own, inverses)
    wait_all(feed_copies)
    for i in range(2):
        mover.keep(feed_full.at[i], feed_out[i])
    for move in gathers:
        chain.finish(move)
    keep(h4)
    for move in sent + released + gathers:
        chain.release(move)
    mover.settle()


def forward_call(
    sizes, frames, condition, params, lengths, spread, prompt, weights, feed,
    modulation_weight,
):
    frame_count, chunks, cols, width = frames.shape
    rows = frame_count * cols
    tokens = rows * chunks
    head_width, padded = spread.shape
    half = rows // sizes[TENSOR]
    kept = half * chunks
    full_rows = weights[0].shape[1] * sizes[WIDE]
    prompt_width = weights[10].shape[1] * sizes[WIDE]
    slice_width = modulation_weight.shape[1]
    group = sizes[WIDE] * sizes[TENSOR]
    placed = slice_width + slice_width % LANES
    moves = 6 * chunks
    s = jax.ShapeDtypeStruct
    wide_act, heads_act = s((tokens, width), BF16), s((tokens, head_width), BF16)
    triple, own = s((3, tokens, padded), BF16), s((kept, width), F32)
    outs = [
        wide_act, triple, s((2, tokens, padded), BF16), heads_act,
        wide_act, triple, heads_act,
        wide_act, s((tokens, padded), BF16), s((2, LANES, padded), BF16), heads_act,
        wide_act, own, own, own, own, own, own, s((3, kept, LANES), F32),
    ]
    return pl.pallas_call(
        functools.partial(forward_kernel, sizes),
        name="forward",
        out_shape=outs
        + [s((10, full_rows, padded), BF16)]
        + [s((ref.shape[0] * sizes[WIDE], ref.shape[1]), BF16) for ref in feed]
        + [s((16, width), F32)],
        in_specs=[VM] * 6 + [ANY] * 15,
        out_specs=[ANY] * (len(outs) + 4),
        scratch_shapes=stage_scratch(outs)
        + [
            VMEM((10,) + weights[0].shape, BF16), VMEM((2,) + weights[10].shape, BF16),
            VMEM((10, full_rows, padded), BF16),
            VMEM((2, prompt_width, head_width), BF16),
            VMEM((2, feed[0].shape[0] * sizes[WIDE], feed[0].shape[1]), BF16),
            VMEM(modulation_weight.shape, BF16),
            VMEM((8, placed), F32), VMEM((group, 1, placed), F32),
            VMEM((1, 6 * width), F32), VMEM((16, width), F32),
            VMEM((tokens, padded), BF16),
            VMEM((tokens, width), BF16),
            VMEM((3 * chunks, 4, 1, half, width), BF16),
            VMEM((kept, width), F32),
            VMEM((rows, rows), F32),
            DMA((15,)), DMA((14,)), DMA((14,)), DMA((group - 1,)), DMA((group - 1,)),
            DMA((2,)), DMA((2,)),
            DMA((moves, 4, 1)), DMA((moves, 4, 1)),
        ],
        compiler_params=pltpu.CompilerParams(
            collective_id=1, has_side_effects=True, vmem_limit_bytes=60 << 20
        ),
    )(
        frames, condition, params, lengths, spread, prompt, *weights, *feed,
        modulation_weight,
    )


def prepare(frames, timestep, head_width):
    width = frames.shape[4]
    half_width = width // 2
    frequency = jnp.exp(-math.log(10000.0) * jnp.arange(half_width, dtype=F32) / half_width)
    angles = timestep[0].astype(F32) * frequency
    condition = jax.nn.silu(jnp.concatenate([jnp.cos(angles), jnp.sin(angles)])).astype(BF16)
    heads = head_width // HEAD_DIM
    padded = np.arange(heads * LANES)
    source = np.where(
        padded % LANES < HEAD_DIM, padded // LANES * HEAD_DIM + padded % LANES, -1
    )
    spread = (np.arange(head_width)[:, None] == source[None]).astype(np.float32)
    return condition, jnp.asarray(spread, BF16)


def over_columns(width, tile, body):
    whole = width // tile

    @pl.loop(0, whole)
    def _(j):
        body(pl.ds(pl.multiple_of(j * tile, tile), tile))

    if width % tile:
        body(pl.ds(whole * tile, width % tile))


GELU_C = math.sqrt(2.0 / math.pi)


def live_rows(lengths, split):
    first = split.place.t * split.frames
    pieces = []
    for f in range(split.frames):
        live = (first + f).astype(F32) < lengths[0:1, 0:1]
        pieces.append(jnp.broadcast_to(jnp.where(live, 1.0, 0.0), (split.cols, 1)))
    return jnp.concatenate(pieces, 0)


def own_cotangent(cotangent, lengths, split, r):
    width = cotangent.shape[3]
    rows = cotangent[split.own_frames(), r].reshape(split.quarter, width)
    return rows.astype(F32) * live_rows(lengths, split)


def mlp_kernel(
    sizes,
    vectors, lengths, *refs,
):
    ins, outs = refs[:6], refs[6:12]
    h4, cotangent, n4_own, inverses, up, down = loaded = refs[12:18]
    branch_part, e3, g3_own, up_grad, down_grad, sums = made = refs[18:24]
    (
        move_sems, e4, hidden, pre_grad, partial, landing, ring_send, ring_recv,
    ) = refs[24:]
    place = Place(sizes)
    frame_count, chunks, cols, width = cotangent.shape
    group = landing.shape[2]
    split = Split(place, frame_count, chunks, cols, group)
    line = Line(place, ring_send, ring_recv)
    mover = Mover(move_sems)
    mover.load(
        [ins[i] for i in (1, 4, 5, 0, 2, 3)], [loaded[i] for i in (1, 4, 5, 0, 2, 3)]
    )
    greet(neighbours(place))
    mover.need(cotangent)

    @pl.loop(0, frame_count)
    def _(f):
        live = jnp.where(f.astype(F32) < lengths[0:1, 0:1], 1.0, 0.0)
        for r, spot in enumerate(split.spots(f)):
            e4[spot] = (
                vectors[5:6] * (cotangent[f, r].astype(F32) * live)
            ).astype(BF16)

    sums[...] = jnp.zeros_like(sums)
    mover.need(up, down, h4)
    scatters = []
    for r in range(chunks // group):
        spot = split.chunk(r)

        def act(lanes):
            pre = dot(h4[spot], up[:, lanes])
            grad = dot(e4[spot], down[:, lanes])
            inner = jnp.tanh(GELU_C * (pre + 0.044715 * pre * pre * pre))
            gate = 0.5 * (1.0 + inner)
            hidden[spot, lanes] = (pre * gate).astype(BF16)
            slope = gate + 0.5 * pre * (1.0 - inner * inner) * (
                GELU_C * (1.0 + 3.0 * 0.044715 * pre * pre)
            )
            pre_grad[spot, lanes] = (grad * slope).astype(BF16)

        over_columns(up.shape[1], 256, act)
        line.tick(1, 1)
        partial[spot] = dot_tr(pre_grad[spot], up[...]).astype(BF16)
        line.tick(1, 1)
        scatters.append(
            line.start(True, split.rows_view(partial, r), split.landing_view(landing.at[r]))
        )

    for r in range(chunks // group):
        spot = split.chunk(r)
        branch_part[spot] = dot_tr(hidden[spot], down[...]).astype(BF16)
        line.tick(1, 1)

    mover.keep(branch_part, outs[0])

    def down_tile(lanes):
        down_grad[:, lanes] = dot_outer(e4[...], hidden[:, lanes]).astype(BF16)

    def up_tile(lanes):
        up_grad[:, lanes] = dot_outer(h4[...], pre_grad[:, lanes]).astype(BF16)

    mover.need(n4_own, inverses)
    gathers = []
    for r in range(chunks // group):
        line.finish(scatters[r])
        for c in range(r * group, (r + 1) * group):
            kept = split.kept(c)
            grad = split.total(partial, landing.at[r], c)
            normed = n4_own[kept]
            sums[0:1] += jnp.sum(grad, 0, keepdims=True)
            sums[1:2] += jnp.sum(grad * normed, 0, keepdims=True)
            upstream = own_cotangent(cotangent, lengths, split, c) + norm_pull(
                normed, inverses[2, kept][:, 0:1], grad * vectors[4:5]
            )
            g3_own[kept] = upstream
            e3[split.own(c)] = upstream.astype(BF16)
        gathers.append(line.start(False, split.rows_view(e3, r)))
        if r == 0:
            over_columns(up.shape[1], 256, down_tile)
            line.tick(2, 1)

    mover.keep(g3_own, outs[2])
    mover.keep(sums, outs[5])
    mover.keep(down_grad, outs[4])
    over_columns(up.shape[1], 256, up_tile)
    mover.keep(up_grad, outs[3])
    for move in gathers:
        line.finish(move)
    mover.keep(e3, outs[1])
    for move in scatters + gathers:
        line.release(move)
    mover.settle()


def mlp_call(sizes, vectors, lengths, acts):
    frame_count, chunks, cols, width = acts[1].shape
    rows = frame_count * cols
    tokens = rows * chunks
    quarter = rows // sizes[TENSOR]
    hidden = acts[4].shape[1]
    s = jax.ShapeDtypeStruct
    group = max(1, chunks // 2)
    moves = 2 * chunks // group
    outs = [
        s((tokens, width), BF16), s((tokens, width), BF16), s((quarter * chunks, width), F32),
        s((width, hidden), BF16), s((width, hidden), BF16), s((8, width), F32),
    ]
    return pl.pallas_call(
        functools.partial(mlp_kernel, sizes),
        name="mlp",
        out_shape=outs,
        in_specs=[VM] * 2 + [ANY] * len(acts),
        out_specs=[ANY] * len(outs),
        scratch_shapes=stage_scratch(list(acts) + outs)
        + [
            VMEM((tokens, width), BF16), VMEM((tokens, hidden), BF16),
            VMEM((tokens, hidden), BF16),
            VMEM((tokens, width), BF16),
            VMEM((chunks // group, 4, group, quarter, width), BF16),
            DMA((moves, 4, group)), DMA((moves, 4, group)),
        ],
        compiler_params=pltpu.CompilerParams(
            collective_id=2, has_side_effects=True, vmem_limit_bytes=60 << 20
        ),
    )(vectors, lengths, *acts)


class Reducer:
    def __init__(self, place, source, mine, merged, received, sems):
        self.place, self.source = place, source
        self.mine, self.merged, self.received = mine, merged, received
        self.local, self.side_send, self.side_recv, self.far_send, self.far_recv = sems
        self.clips = place.sizes[NARROW]
        self.block = mine.shape[1]

    def rows(self, clip, core):
        start = (clip * self.place.sizes[WIDE] + core) * self.block
        return pl.ds(pl.multiple_of(start, self.block), self.block)

    def split(self):
        self.copies = []
        for clip in range(self.clips):
            local = pltpu.make_async_copy(
                self.source.at[self.rows(clip, self.place.w)],
                self.mine.at[clip],
                self.local.at[clip],
            )
            local.start()
            self.copies += [
                local,
                send(
                    self.source.at[self.rows(clip, 1 - self.place.w)],
                    self.merged.at[clip],
                    self.side_send.at[clip],
                    self.side_recv.at[clip],
                    self.place.sibling(),
                ),
            ]

    def spread(self):
        wait_all(self.copies)
        self.copies = []

        @pl.loop(0, self.clips)
        def _(clip):
            self.merged[clip] = (
                self.merged[clip].astype(F32) + self.mine[clip].astype(F32)
            ).astype(BF16)

        for step in (3, 1, 2) if self.clips == 4 else range(1, self.clips):
            peer = lax.rem(self.place.n + step, self.clips)
            self.copies.append(
                send(
                    self.merged.at[peer],
                    self.received.at[step - 1],
                    self.far_send.at[step - 1],
                    self.far_recv.at[step - 1],
                    self.place.over_narrow(peer),
                )
            )

    def finish(self, out):
        wait_all(self.copies)
        total = self.merged[self.place.n].astype(F32)
        for step in range(self.clips - 1):
            total = total + self.received[step].astype(F32)
        out[...] = total


def reducer_scratch(sizes, jobs, block, width):
    clips = sizes[NARROW]
    return [
        VMEM((jobs, clips, block, width), BF16),
        VMEM((jobs, clips, block, width), BF16),
        VMEM((jobs, clips - 1, block, width), BF16),
        DMA((jobs, clips)), DMA((jobs, clips)), DMA((jobs, clips)),
        DMA((jobs, clips - 1)), DMA((jobs, clips - 1)),
    ]


def reducers(place, sources, scratch):
    mine, merged, received, *sems = scratch
    return [
        Reducer(
            place, source, mine.at[i], merged.at[i], received.at[i], [sem.at[i] for sem in sems]
        )
        for i, source in enumerate(sources)
    ]


def all_partners(place):
    sizes = place.sizes
    return (
        [place.sibling()]
        + [place.over_tensor(step) for step in range(1, sizes[TENSOR])]
        + [
            place.over_narrow(lax.rem(place.n + step, sizes[NARROW]))
            for step in range(1, sizes[NARROW])
        ]
    )


def attention_pull(queries, keys, values, context_grad, mask, scale):
    scores = dot_tr(queries, keys) * scale
    if mask is not None:
        scores = jnp.where(mask, scores, NEGATIVE)
    attend = softmax_tile(scores)
    attend_grad = dot_tr(context_grad, values)
    score_grad = (
        attend * (attend_grad - jnp.sum(attend * attend_grad, -1, keepdims=True))
    ).astype(BF16)
    return (
        dot(score_grad, keys) * scale,
        dot_outer(score_grad, queries) * scale,
        dot_outer(attend.astype(BF16), context_grad),
    )


def back_kernel(
    sizes,
    vectors, lengths, spread, *refs,
):
    ins, full_in, gradients = refs[:13], refs[13], refs[14:16]
    outs = refs[16:24]
    (
        e3, g3_own, n3_own, n2_own, inverses, a2_own, h3, q3, kv3, o3, h2, q2, o2,
    ) = loaded = refs[24:37]
    g1_own, e1, time_grads, word_grads, up_out, down_out, cross_out, sums = refs[37:45]
    (
        move_sems, cross_full, time_full, wide_grad, wide_parts, narrow_parts, word_sums,
        word_side, e2, partial, landing, group_mask, cross_grads,
        full_sems, word_send, word_recv, ring_send, ring_recv,
    ) = refs[45:63]
    place = Place(sizes)
    tokens, width = e3.shape
    rows, cols = group_mask.shape[0], sizes[COLS]
    chunks = tokens // rows
    split = Split(place, rows // cols, chunks, cols)
    heads = spread.shape[1] // LANES
    scale = 1.0 / math.sqrt(HEAD_DIM)
    line = Line(place, ring_send, ring_recv)
    mover = Mover(move_sems)
    weights = []
    for i, (source, target) in enumerate(
        ((full_in.at[pl.ds(8, 2)], cross_full), (full_in.at[pl.ds(4, 4)], time_full))
    ):
        weights.append(pltpu.make_async_copy(source, target, full_sems.at[i]))
    weights[0].start()
    first = (0, 7, 8)
    order = first + tuple(i for i in range(13) if i not in first)
    mover.load([ins[i] for i in order], [loaded[i] for i in order])
    weights[1].start()
    greet(all_partners(place))
    feed = reducers(place, gradients, refs[63:71])
    cross = reducers(place, [cross_grads.at[0], cross_grads.at[1]], refs[71:79])
    for job in feed:
        job.split()
    write_group_mask(group_mask, lengths, cols)
    sums[...] = jnp.zeros_like(sums)
    word_sums[...] = jnp.zeros_like(word_sums)

    def context_grad(source, spot, weight):
        wide_grad[spot] = dot(source[spot], weight).astype(BF16)

    def scatter(r, stage):
        return line.start(
            True,
            split.rows_view(partial, r),
            split.landing_view(landing.at[stage * chunks + r]),
        )

    weights[0].wait()
    mover.need(e3, q3, kv3)
    scatters = []
    for r in range(chunks):
        spot = split.chunk(r)
        context_grad(e3, spot, cross_full[1])
        line.tick()
        for h in range(heads):
            lanes = slice(h * LANES, (h + 1) * LANES)
            query_grad, key_grad, value_grad = attention_pull(
                q3[spot, lanes], kv3[0, :, lanes], kv3[1, :, lanes], wide_grad[spot, lanes],
                live_words(lengths), scale,
            )
            wide_parts[0, spot, lanes] = query_grad.astype(BF16)
            word_sums[0, :, lanes] += key_grad
            word_sums[1, :, lanes] += value_grad
        line.tick()
        partial[spot] = dot_tr(wide_parts[0, spot], cross_full[0]).astype(BF16)
        scatters.append(scatter(r, 0))
        narrow_parts[0, spot] = dot_tr(wide_parts[0, spot], spread[...]).astype(BF16)
    word_copy = send(word_sums, word_side, word_send, word_recv, place.sibling())
    mover.need(o3, h3)
    cross_grads[0] = dot_outer(e3[...], o3[...]).astype(BF16)
    line.tick(2)
    cross_grads[1] = dot_outer(h3[...], narrow_parts[0]).astype(BF16)
    line.tick(2)
    for job in cross:
        job.split()
    mover.need(*loaded)
    gathers = []
    for r in range(chunks):
        kept = split.kept(r)
        line.finish(scatters[r])
        grad = split.total(partial, landing.at[r], r)
        normed = n3_own[kept]
        sums[0:1] += jnp.sum(grad * normed, 0, keepdims=True)
        upstream = g3_own[kept] + norm_pull(
            normed, inverses[1, kept][:, 0:1], grad * vectors[8:9]
        )
        g1_own[kept] = upstream
        sums[1:2] += jnp.sum(upstream * a2_own[kept], 0, keepdims=True)
        e2[split.own(r)] = (vectors[7:8] * upstream).astype(BF16)
        gathers.append(line.start(False, split.rows_view(e2, r)))
        line.tick(4, 3)
        if r == 0:
            for job in feed:
                job.spread()
    for job in cross:
        job.spread()
    word_copy.wait()
    for j in range(2):
        word_grads[j] = dot_tr(
            (word_sums[j] + word_side[j]).astype(BF16), spread[...]
        ).astype(BF16)
    mover.keep(word_grads, outs[3])
    sent = scatters + gathers

    weights[1].wait()
    former, scatters = scatters, []
    for r in range(chunks):
        spot = split.chunk(r)
        line.finish(gathers[r])
        context_grad(e2, spot, time_full[3])
        line.tick()
        for h in range(heads):
            lanes = slice(h * LANES, (h + 1) * LANES)
            parts = attention_pull(
                q2[0, spot, lanes], q2[1, spot, lanes], q2[2, spot, lanes],
                wide_grad[spot, lanes], group_mask[...] > 0.5, scale,
            )
            for i in range(3):
                wide_parts[i, spot, lanes] = parts[i].astype(BF16)
            if h % 2:
                line.tick()
        total = None
        for i in range(3):
            part = dot_tr(wide_parts[i, spot], time_full[i])
            total = part if total is None else total + part
        line.tick()
        line.release(former[r])
        sent.remove(former[r])
        partial[spot] = total.astype(BF16)
        scatters.append(scatter(r, 1))
        for i in range(3):
            narrow_parts[i, spot] = dot_tr(wide_parts[i, spot], spread[...]).astype(BF16)
    sent += scatters
    time_grads[0] = dot_outer(e2[...], o2[...]).astype(BF16)
    line.tick(2)
    for i in range(3):
        time_grads[1 + i] = dot_outer(h2[...], narrow_parts[i]).astype(BF16)
        line.tick(1)
    mover.keep(time_grads, outs[2])

    gathers = []
    for r in range(chunks):
        kept = split.kept(r)
        line.finish(scatters[r])
        grad = split.total(partial, landing.at[chunks + r], r)
        normed = n2_own[kept]
        sums[2:3] += jnp.sum(grad * normed, 0, keepdims=True)
        upstream = g1_own[kept] + norm_pull(
            normed, inverses[0, kept][:, 0:1], grad * vectors[6:7]
        )
        g1_own[kept] = upstream
        e1[split.own(r)] = (vectors[2:3] * upstream).astype(BF16)
        gathers.append(line.start(False, split.rows_view(e1, r)))
        line.tick(4, 3)
    mover.keep(g1_own, outs[0])
    mover.keep(sums, outs[7])
    feed[0].finish(up_out)
    mover.keep(up_out, outs[4])
    line.drain(gathers[0])
    feed[1].finish(down_out)
    mover.keep(down_out, outs[5])
    for r in range(1, chunks):
        line.drain(gathers[r])
    cross[0].finish(cross_out.at[0])
    cross[1].finish(cross_out.at[1])
    mover.keep(cross_out, outs[6])
    for move in gathers:
        line.finish(move)
    mover.keep(e1, outs[1])
    for move in sent + gathers:
        line.release(move)
    mover.settle()


def back_call(sizes, cols, small, acts, full, gradients):
    spread = small[2]
    tokens, width = acts[0].shape
    rows = tokens // CHUNKS
    chunks = tokens // rows
    quarter = rows // sizes[TENSOR]
    head_width, padded = spread.shape
    full_rows = full.shape[1]
    hidden = gradients[0].shape[1]
    block = width // (sizes[NARROW] * sizes[WIDE])
    s = jax.ShapeDtypeStruct
    moves = 4 * chunks
    outs = [
        s((quarter * chunks, width), F32), s((tokens, width), BF16),
        s((4, width, head_width), BF16), s((2, LANES, head_width), BF16),
        s((block, hidden), F32), s((block, hidden), F32), s((2, block, head_width), F32),
        s((8, width), F32),
    ]
    return pl.pallas_call(
        functools.partial(back_kernel, {**sizes, COLS: cols}),
        name="back",
        out_shape=outs,
        in_specs=[VM] * 3 + [ANY] * (len(acts) + 3),
        out_specs=[ANY] * len(outs),
        scratch_shapes=stage_scratch(list(acts) + outs)
        + [
            VMEM((2, full_rows, padded), BF16), VMEM((4, full_rows, padded), BF16),
            VMEM((tokens, padded), BF16),
            VMEM((3, tokens, padded), BF16),
            VMEM((3, tokens, head_width), BF16),
            VMEM((2, LANES, padded), F32), VMEM((2, LANES, padded), F32),
            VMEM((tokens, width), BF16),
            VMEM((tokens, width), BF16),
            VMEM((2 * chunks, 4, 1, quarter, width), BF16),
            VMEM((rows, rows), F32),
            VMEM((2, width, head_width), BF16),
            DMA((2,)), DMA(()), DMA(()),
            DMA((moves, 4, 1)), DMA((moves, 4, 1)),
        ]
        + reducer_scratch(sizes, 2, block, hidden)
        + reducer_scratch(sizes, 2, block, head_width),
        compiler_params=pltpu.CompilerParams(
            collective_id=3, has_side_effects=True, vmem_limit_bytes=60 << 20
        ),
    )(*small, *acts, full, *gradients)


def space_kernel(
    sizes,
    vectors, spread, lengths, mlp_sums, back_sums, condition, *refs,
):
    ins, full_in, gradients, outs = refs[:13], refs[13], refs[14], refs[15:22]
    (
        e1, g1_own, frames, a1_own, h1, q1, side, o1, prompt, word_grads, branch_part, x3_own,
        cotangent,
    ) = loaded = refs[22:35]
    frames_grad, output, early_out, space_out, prompt_out, merged, conditions = refs[35:42]
    (
        move_sems, query_full, out_full, wide_grad, wide_parts, narrow_parts, key_sums, side_out,
        side_in, space_grads, words, word_parts, partial, landing, tally, tally_side, tally_peers,
        full_sems, key_send, key_recv, word_send, word_recv,
        tally_send, tally_recv, ring_send, ring_recv,
    ) = refs[42:68]
    early_scratch, late_scratch = refs[68:76], refs[76:84]
    place = Place(sizes)
    clips = sizes[NARROW]
    frame_count, chunks, cols, width = frames.shape
    split = Split(place, frame_count, chunks, cols)
    quarter = split.quarter
    heads = spread.shape[1] // LANES
    scale = 1.0 / math.sqrt(HEAD_DIM)
    line = Line(place, ring_send, ring_recv)
    mover = Mover(move_sems)
    weights = [
        pltpu.make_async_copy(full_in.at[pl.ds(3, 1)], out_full, full_sems.at[0]),
        pltpu.make_async_copy(full_in.at[pl.ds(0, 3)], query_full, full_sems.at[1]),
    ]
    weights[0].start()
    first = (10, 8, 9, 0, 5, 6)
    order = first + tuple(i for i in range(13) if i not in first)
    mover.load([ins[i] for i in order], [loaded[i] for i in order])
    weights[1].start()
    greet(all_partners(place))
    mover.need(branch_part)

    def scatter(source, r, stage):
        return line.start(
            True,
            split.rows_view(source, r),
            split.landing_view(landing.at[stage * chunks + r]),
        )

    feed_scatters = [scatter(branch_part, r, 1) for r in range(chunks)]
    mover.need(prompt, word_grads)
    early = reducers(place, [gradients.at[i] for i in range(4)], early_scratch)
    late = reducers(place, [space_grads.at[i] for i in range(4)], late_scratch)
    for job in early:
        job.split()
    block = words.shape[2]
    far = [lax.rem(place.n + step, clips) for step in range(1, clips)]
    word_copies = []
    for i, peer in enumerate(far):
        lanes = pl.ds(pl.multiple_of((peer * sizes[WIDE] + place.w) * block, block), block)
        for j, (source, target) in enumerate(
            (
                (prompt.at[:, lanes], words.at[i + 1]),
                (word_grads, word_parts.at[i + 1]),
                (condition, conditions.at[place.n]),
            )
        ):
            word_copies.append(
                send(
                    source, target, word_send.at[i, j], word_recv.at[i, j],
                    place.over_narrow(peer),
                )
            )
    mine = pl.ds(pl.multiple_of((place.n * sizes[WIDE] + place.w) * block, block), block)
    words[0] = prompt[:, mine]
    word_parts[0] = word_grads[...]
    conditions[place.n] = condition[...]
    tally[...] = jnp.zeros_like(tally)
    tally[3:5] = mlp_sums[0:2]
    tally[6:9] = back_sums[0:3]

    weights[0].wait()
    mover.need(e1)
    for r in range(chunks):
        spot = split.chunk(r)
        wide_grad[spot] = dot(e1[spot], out_full[0]).astype(BF16)
        line.tick()

    mover.need(*loaded)
    weights[1].wait()
    tally[2:3] = jnp.sum(g1_own[...] * a1_own[...], 0, keepdims=True)

    def attend(first, stop):
        @pl.loop(first, stop)
        def _(f):
            spots = split.spots(f)
            queries = jnp.concatenate([q1[0, spot] for spot in spots], 0)
            grads = jnp.concatenate([wide_grad[spot] for spot in spots], 0)
            keys = jnp.concatenate(
                [q1[1, spot] for spot in spots] + [side[0, spot] for spot in spots], 0
            )
            values = jnp.concatenate(
                [q1[2, spot] for spot in spots] + [side[1, spot] for spot in spots], 0
            )
            for h in range(heads):
                lanes = slice(h * LANES, (h + 1) * LANES)
                parts = attention_pull(
                    queries[:, lanes], keys[:, lanes], values[:, lanes], grads[:, lanes],
                    None, scale,
                )
                for r in range(chunks):
                    here = slice(r * cols, (r + 1) * cols)
                    there = slice((chunks + r) * cols, (chunks + r + 1) * cols)
                    wide_parts[0, spots[r], lanes] = parts[0][here].astype(BF16)
                    for j in range(2):
                        key_sums[j, spots[r], lanes] = parts[1 + j][here]
                        side_out[j, spots[r], lanes] = parts[1 + j][there].astype(BF16)

    outputs = []

    def finish_feed(r):
        kept = split.kept(r)
        line.finish(feed_scatters[r])
        branch = split.total(branch_part, landing.at[chunks + r], r)
        tally[5:6] += jnp.sum(
            own_cotangent(cotangent, lengths, split, r) * branch, 0, keepdims=True
        )
        after = (x3_own[kept] + vectors[5:6] * branch) * live_rows(lengths, split)
        output[split.own_frames(), r] = after.astype(BF16).reshape(split.frames, cols, width)
        outputs.append(line.start(False, split.frames_view(output, r)))

    quarters = frame_count // 4
    for part in range(4):
        attend(part * quarters, (part + 1) * quarters)
        line.tick(2)
        if part >= 2 and part - 2 < chunks:
            finish_feed(part - 2)
    for r in range(2, chunks):
        finish_feed(r)
    key_copy = send(side_out, side_in, key_send, key_recv, place.sibling())
    for job in early:
        job.spread()
    line.tick(2)
    key_copy.wait()
    for j in range(2):
        wide_parts[1 + j] = (key_sums[j] + side_in[j].astype(F32)).astype(BF16)
    line.tick(2)
    scatters = []
    for r in range(chunks):
        spot = split.chunk(r)
        total = dot_tr(wide_parts[0, spot], query_full[0])
        for i in (1, 2):
            total = total + dot_tr(wide_parts[i, spot], query_full[i])
        partial[spot] = total.astype(BF16)
        scatters.append(scatter(partial, r, 0))
        line.tick(2)

    space_grads[0] = dot_outer(e1[...], o1[...]).astype(BF16)
    late[0].split()
    for i in range(3):
        narrow_parts[i] = dot_tr(wide_parts[i], spread[...]).astype(BF16)
        space_grads[1 + i] = dot_outer(h1[...], narrow_parts[i]).astype(BF16)
        late[1 + i].split()
        line.tick(2)
    for job in late:
        job.spread()
    gathers = []
    for r in range(chunks):
        kept = split.kept(r)
        line.finish(scatters[r])
        grad = split.total(partial, landing.at[r], r)
        x_own = frames[split.own_frames(), r].reshape(quarter, width).astype(F32)
        normed, inverse = norm_tile(x_own)
        tally[0:1] += jnp.sum(grad, 0, keepdims=True)
        tally[1:2] += jnp.sum(grad * normed, 0, keepdims=True)
        upstream = g1_own[kept] + norm_pull(normed, inverse, grad * vectors[1:2])
        frames_grad[split.own_frames(), r] = upstream.astype(BF16).reshape(
            split.frames, cols, width
        )
        gathers.append(line.start(False, split.frames_view(frames_grad, r)))

    tally_copy = send(tally, tally_side, tally_send.at[0], tally_recv.at[0], place.sibling())
    wait_all(word_copies)
    for j in range(2):
        total = dot_outer(words[0], word_parts[0, j, 0 : prompt.shape[0]])
        for step in range(1, clips):
            total = total + dot_outer(words[step], word_parts[step, j, 0 : prompt.shape[0]])
        prompt_out[j] = total
    mover.keep(prompt_out, outs[4])
    mover.keep(conditions, outs[6])
    tally_copy.wait()
    tally_side[...] = tally_side[...] + tally[...]
    peer_copies = [
        send(
            tally_side, tally_peers.at[step - 1], tally_send.at[step], tally_recv.at[step],
            place.over_tensor(step),
        )
        for step in range(1, sizes[TENSOR])
    ]
    for move in gathers:
        line.drain(move)
    for i, job in enumerate(early):
        job.finish(early_out.at[i])
    mover.keep(early_out, outs[2])
    wait_all(peer_copies)
    total = tally_side[...]
    for step in range(sizes[TENSOR] - 1):
        total = total + tally_peers[step]
    merged[place.n] = total
    base = sizes[TENSOR]
    far_copies = [
        send(
            merged.at[place.n], merged.at[place.n],
            tally_send.at[base + i], tally_recv.at[base + i], place.over_narrow(peer),
        )
        for i, peer in enumerate(far)
    ]
    for i, job in enumerate(late):
        job.finish(space_out.at[i])
    mover.keep(space_out, outs[3])
    for move in outputs:
        line.finish(move)
    mover.keep(output, outs[1])
    for move in gathers:
        line.finish(move)
    mover.keep(frames_grad, outs[0])
    wait_all(far_copies)
    mover.keep(merged, outs[5])
    for move in feed_scatters + outputs + scatters + gathers:
        line.release(move)
    mover.settle()


def space_call(sizes, small, acts, full, gradients):
    frames, spread, prompt, condition = acts[2], small[1], acts[8], small[5]
    frame_count, chunks, cols, width = frames.shape
    rows = frame_count * cols
    tokens = rows * chunks
    quarter = rows // sizes[TENSOR]
    head_width, padded = spread.shape
    full_rows = full.shape[1]
    parts = sizes[NARROW] * sizes[WIDE]
    block, word_block = width // parts, prompt.shape[1] // parts
    clips, peers = sizes[NARROW], sizes[TENSOR] - 1
    s = jax.ShapeDtypeStruct
    moves = 4 * chunks
    outs = [
        s(frames.shape, BF16), s(frames.shape, BF16),
        s((4, block, head_width), F32), s((4, block, head_width), F32),
        s((2, word_block, head_width), F32), s((clips, 16, width), F32),
        s((clips,) + condition.shape, F32),
    ]
    return pl.pallas_call(
        functools.partial(space_kernel, sizes),
        name="space",
        out_shape=outs,
        in_specs=[VM] * 6 + [ANY] * (len(acts) + 2),
        out_specs=[ANY] * len(outs),
        scratch_shapes=stage_scratch(list(acts) + outs)
        + [
            VMEM((3, full_rows, padded), BF16), VMEM((1, full_rows, padded), BF16),
            VMEM((tokens, padded), BF16),
            VMEM((3, tokens, padded), BF16),
            VMEM((3, tokens, head_width), BF16),
            VMEM((2, tokens, padded), F32),
            VMEM((2, tokens, padded), BF16), VMEM((2, tokens, padded), BF16),
            VMEM((4, width, head_width), BF16),
            VMEM((clips, prompt.shape[0], word_block), BF16),
            VMEM((clips, 2, LANES, head_width), BF16),
            VMEM((tokens, width), BF16),
            VMEM((2 * chunks, 4, 1, quarter, width), BF16),
            VMEM((16, width), F32), VMEM((16, width), F32), VMEM((peers, 16, width), F32),
            DMA((2,)), DMA(()), DMA(()),
            DMA((clips - 1, 3)), DMA((clips - 1, 3)),
            DMA((peers + clips,)), DMA((peers + clips,)),
            DMA((moves, 4, 1)), DMA((moves, 4, 1)),
        ]
        + reducer_scratch(sizes, 4, block, head_width)
        + reducer_scratch(sizes, 4, block, head_width),
        compiler_params=pltpu.CompilerParams(
            collective_id=4, has_side_effects=True, vmem_limit_bytes=61 << 20
        ),
    )(*small, *acts, full, gradients)


def fused_on_device(
    sizes,
    frames, cotangent, prompt, timestep, clip_lengths, text_lengths,
    modulation_weight, modulation_bias, space_query, space_key, space_value, space_out,
    time_gain, time_query, time_key, time_value, time_out, time_gate, cross_gain, cross_query,
    prompt_key, prompt_value, cross_out, feed_up, feed_down,
):
    frame_count, width = frames.shape[1], frames.shape[4]
    cols = frames.shape[2] * frames.shape[3] // CHUNKS
    head_width = space_query.shape[1]
    condition, spread = prepare(frames, timestep, head_width)
    lengths = jnp.broadcast_to(
        jnp.concatenate([clip_lengths, text_lengths]).astype(F32)[:, None], (2, LANES)
    )
    half_condition = lax.dynamic_slice_in_dim(
        condition, lax.axis_index(WIDE) * modulation_weight.shape[0], modulation_weight.shape[0]
    )
    params = jnp.concatenate([modulation_bias, time_gain, time_gate, cross_gain])[None]
    tiles = frames.reshape(frame_count, CHUNKS, cols, width)
    pulls = cotangent.reshape(frame_count, CHUNKS, cols, width)
    (
        h1, q1, side, o1, h2, q2, o2, h3, q3, kv3, o3, h4,
        a1_own, a2_own, x3_own, n2_own, n3_own, n4_own, inverses, full, up, down, vectors,
    ) = forward_call(
        sizes, tiles, jnp.broadcast_to(half_condition[None], (16, half_condition.shape[0])),
        params, lengths, spread, prompt[0],
        [
            weight.T
            for weight in (
                space_query, space_key, space_value, space_out, time_query, time_key,
                time_value, time_out, cross_query, cross_out, prompt_key, prompt_value,
            )
        ],
        [feed_up, feed_down], modulation_weight,
    )
    branch_part, e3, g3_own, up_grad, down_grad, mlp_sums = mlp_call(
        sizes, vectors, lengths, [h4, pulls, n4_own, inverses, up, down]
    )
    g1_own, e1, time_grads, word_grads, up_out, down_out, cross_grads, back_sums = back_call(
        sizes, cols, [vectors, lengths, spread],
        [e3, g3_own, n3_own, n2_own, inverses, a2_own, h3, q3, kv3, o3, h2, q2, o2],
        full, [up_grad, down_grad],
    )
    frames_grad, output, early_out, late_out, prompt_out, merged, conditions = space_call(
        sizes,
        [vectors, spread, lengths, mlp_sums, back_sums, condition.astype(F32)[None]],
        [e1, g1_own, tiles, a1_own, h1, q1, side, o1, prompt[0], word_grads, branch_part, x3_own,
         pulls],
        full, time_grads,
    )
    part = lax.axis_index(NARROW) * sizes[WIDE] + lax.axis_index(WIDE)
    block = width // (sizes[NARROW] * sizes[WIDE])
    slice_width = modulation_weight.shape[1]
    pulled = merged[:, :6].reshape(sizes[NARROW], 6 * width)
    own_pulled = lax.dynamic_slice_in_dim(
        pulled, lax.axis_index(TENSOR) * slice_width, slice_width, 1
    )
    own_condition = lax.dynamic_slice_in_dim(conditions[:, 0], part * block, block, 1)
    modulation_weight_grad = jnp.sum(own_condition[:, :, None] * own_pulled[:, None], 0)
    summed_rows = jnp.sum(merged, 0)
    bias_block = 6 * block
    modulation_bias_grad = lax.dynamic_slice_in_dim(
        summed_rows[:6].reshape(6 * width), part * bias_block, bias_block
    )
    cross_gain_grad, gate_rows, time_gain_grad = (
        lax.dynamic_slice_in_dim(summed_rows[i], part * block, block) for i in (6, 7, 8)
    )
    own_gate = jnp.tanh(lax.dynamic_slice_in_dim(time_gate, part * block, block))
    time_gate_grad = gate_rows * (1.0 - own_gate * own_gate)
    return (
        output.reshape(frames.shape), frames_grad.reshape(frames.shape),
        modulation_weight_grad, modulation_bias_grad,
        late_out[1], late_out[2], late_out[3], late_out[0],
        time_gain_grad, early_out[1], early_out[2], early_out[3], early_out[0], time_gate_grad,
        cross_gain_grad, cross_grads[1], prompt_out[0], prompt_out[1], cross_grads[0],
        up_out, down_out,
    )


CONTRACT_LAST = (((1,), (1,)), ((), ()))
CONTRACT_FIRST = (((0,), (0,)), ((), ()))


def matmul(left, right):
    return jnp.dot(left, right, preferred_element_type=jnp.float32)


def matmul_tr(left, right):
    return lax.dot_general(left, right, CONTRACT_LAST, preferred_element_type=jnp.float32)


def outer_sum(left, right):
    return lax.dot_general(left, right, CONTRACT_FIRST, preferred_element_type=jnp.float32)


def norm_rows(values):
    center = values - jnp.mean(values, -1, keepdims=True)
    inverse = lax.rsqrt(jnp.mean(center * center, -1, keepdims=True) + EPSILON)
    return (center * inverse, inverse)


def norm_back(normed, inverse, incoming):
    return inverse * (
        incoming
        - jnp.mean(incoming, -1, keepdims=True)
        - normed * jnp.mean(incoming * normed, -1, keepdims=True)
    )


def over_heads(partial_sum):
    return lax.psum(partial_sum.astype(jnp.bfloat16), TENSOR).astype(jnp.float32)


def attend_forward(queries, key_rows, values, allowed, pattern, score_scale):
    scores = jnp.where(
        allowed,
        jnp.einsum(pattern[0], queries, key_rows, preferred_element_type=jnp.float32) * score_scale,
        NEGATIVE,
    )
    row_max = jnp.max(scores, -1, keepdims=True)
    exponent = jnp.exp(scores - row_max)
    row_total = jnp.sum(exponent, -1, keepdims=True)
    attend = (exponent / row_total).astype(jnp.bfloat16)
    context = jnp.einsum(pattern[1], attend, values, preferred_element_type=jnp.float32)
    return (context.astype(jnp.bfloat16), row_max + jnp.log(row_total))


def attend_back(queries, key_rows, values, allowed, log_total, context_grad, pattern, score_scale):
    scores = jnp.where(
        allowed,
        jnp.einsum(pattern[0], queries, key_rows, preferred_element_type=jnp.float32) * score_scale,
        NEGATIVE,
    )
    attend = jnp.exp(scores - log_total)
    attend_grad = jnp.einsum(pattern[0], context_grad, values, preferred_element_type=jnp.float32)
    score_grad = (attend * (attend_grad - jnp.sum(attend * attend_grad, -1, keepdims=True))).astype(
        jnp.bfloat16
    )
    query_grad = (
        jnp.einsum(pattern[1], score_grad, key_rows, preferred_element_type=jnp.float32)
        * score_scale
    )
    key_grad = (
        jnp.einsum(pattern[2], score_grad, queries, preferred_element_type=jnp.float32)
        * score_scale
    )
    value_grad = jnp.einsum(
        pattern[2], attend.astype(jnp.bfloat16), context_grad, preferred_element_type=jnp.float32
    )
    return (query_grad, key_grad, value_grad)


def on_device(
    frames,
    cotangent,
    prompt,
    timestep,
    clip_lengths,
    text_lengths,
    modulation_weight,
    modulation_bias,
    space_query,
    space_key,
    space_value,
    space_out,
    time_gain,
    time_query,
    time_key,
    time_value,
    time_out,
    time_gate,
    cross_gain,
    cross_query,
    prompt_key,
    prompt_value,
    cross_out,
    feed_up,
    feed_down,
):
    frame_count = frames.shape[1]
    patch_count = frames.shape[2] * frames.shape[3]
    model_width = frames.shape[4]
    token_count = frame_count * patch_count
    score_scale = 1.0 / math.sqrt(HEAD_DIM)
    residual = frames.reshape(token_count, model_width).astype(jnp.float32)
    frame_live = jnp.arange(frame_count) < clip_lengths[0]
    token_live = jnp.repeat(frame_live, patch_count)[:, None]
    prompt_rows = prompt[0]
    word_live = jnp.arange(prompt_rows.shape[0]) < text_lengths[0]
    (
        modulation_weight,
        space_query,
        space_key,
        space_value,
        space_out,
        time_query,
        time_key,
        time_value,
        time_out,
        cross_query,
        prompt_key,
        prompt_value,
        cross_out,
        feed_up,
        feed_down,
    ) = (
        lax.all_gather(modulation_weight, WIDE, axis=0, tiled=True),
        lax.all_gather(space_query, WIDE, axis=0, tiled=True),
        lax.all_gather(space_key, WIDE, axis=0, tiled=True),
        lax.all_gather(space_value, WIDE, axis=0, tiled=True),
        lax.all_gather(space_out, WIDE, axis=0, tiled=True),
        lax.all_gather(time_query, WIDE, axis=0, tiled=True),
        lax.all_gather(time_key, WIDE, axis=0, tiled=True),
        lax.all_gather(time_value, WIDE, axis=0, tiled=True),
        lax.all_gather(time_out, WIDE, axis=0, tiled=True),
        lax.all_gather(cross_query, WIDE, axis=0, tiled=True),
        lax.all_gather(prompt_key, WIDE, axis=0, tiled=True),
        lax.all_gather(prompt_value, WIDE, axis=0, tiled=True),
        lax.all_gather(cross_out, WIDE, axis=0, tiled=True),
        lax.all_gather(feed_up, WIDE, axis=0, tiled=True),
        lax.all_gather(feed_down, WIDE, axis=0, tiled=True),
    )
    head_width = space_query.shape[1]
    head_count = head_width // HEAD_DIM
    split_heads = (frame_count, patch_count, head_count, HEAD_DIM)
    half_width = model_width // 2
    frequency = jnp.exp(-math.log(10000.0) * jnp.arange(half_width, dtype=jnp.float32) / half_width)
    angles = timestep[0].astype(jnp.float32) * frequency
    condition = jax.nn.silu(jnp.concatenate([jnp.cos(angles), jnp.sin(angles)])).astype(
        jnp.bfloat16
    )
    slice_width = modulation_weight.shape[1]
    slice_start = lax.axis_index(TENSOR) * slice_width
    own_modulation = matmul(condition[None, :], modulation_weight)[0] + lax.dynamic_slice_in_dim(
        modulation_bias, slice_start, slice_width
    )
    modulation = lax.all_gather(own_modulation, TENSOR, axis=0, tiled=True)
    shift_one, scale_one, gate_one, shift_two, scale_two, gate_two = jnp.split(modulation, 6)
    normed_one, inverse_one = norm_rows(residual)
    input_one = (normed_one * (1.0 + scale_one) + shift_one).astype(jnp.bfloat16)
    query_one = matmul(input_one, space_query).astype(jnp.bfloat16).reshape(split_heads)
    key_one = matmul(input_one, space_key).astype(jnp.bfloat16).reshape(split_heads)
    value_one = matmul(input_one, space_value).astype(jnp.bfloat16).reshape(split_heads)
    key_frame, value_frame = (
        lax.all_gather(key_one, WIDE, axis=1, tiled=True),
        lax.all_gather(value_one, WIDE, axis=1, tiled=True),
    )
    space_pattern = ("fphe,fkhe->fhpk", "fhpk,fkhe->fphe", "fhpk,fphe->fkhe")
    every_patch = jnp.ones((key_frame.shape[1],), jnp.bool_)
    context_one, log_one = attend_forward(
        query_one, key_frame, value_frame, every_patch, space_pattern, score_scale
    )
    context_one = context_one.reshape(token_count, head_width)
    branch_one = over_heads(matmul_tr(context_one, space_out))
    after_one = residual + gate_one * branch_one
    normed_two, inverse_two = norm_rows(after_one)
    input_two = (normed_two * time_gain).astype(jnp.bfloat16)
    query_two = matmul(input_two, time_query).astype(jnp.bfloat16).reshape(split_heads)
    key_two = matmul(input_two, time_key).astype(jnp.bfloat16).reshape(split_heads)
    value_two = matmul(input_two, time_value).astype(jnp.bfloat16).reshape(split_heads)
    time_pattern = ("fphe,gphe->phfg", "phfg,gphe->fphe", "phfg,fphe->gphe")
    context_two, log_two = attend_forward(
        query_two, key_two, value_two, frame_live, time_pattern, score_scale
    )
    context_two = context_two.reshape(token_count, head_width)
    branch_two = over_heads(matmul_tr(context_two, time_out))
    gate_time = jnp.tanh(time_gate)
    after_two = after_one + gate_time * branch_two
    normed_three, inverse_three = norm_rows(after_two)
    input_three = (normed_three * cross_gain).astype(jnp.bfloat16)
    query_three = (
        matmul(input_three, cross_query)
        .astype(jnp.bfloat16)
        .reshape(token_count, head_count, HEAD_DIM)
    )
    word_keys = (
        matmul(prompt_rows, prompt_key).astype(jnp.bfloat16).reshape(-1, head_count, HEAD_DIM)
    )
    word_values = (
        matmul(prompt_rows, prompt_value).astype(jnp.bfloat16).reshape(-1, head_count, HEAD_DIM)
    )
    cross_pattern = ("nhe,jhe->nhj", "nhj,jhe->nhe", "nhj,nhe->jhe")
    context_three, log_three = attend_forward(
        query_three, word_keys, word_values, word_live, cross_pattern, score_scale
    )
    context_three = context_three.reshape(token_count, head_width)
    branch_three = over_heads(matmul_tr(context_three, cross_out))
    after_three = after_two + branch_three
    normed_four, inverse_four = norm_rows(after_three)
    input_four = (normed_four * (1.0 + scale_two) + shift_two).astype(jnp.bfloat16)
    pre_act = matmul(input_four, feed_up)
    hidden, gelu_pull = jax.vjp(lambda inner: jax.nn.gelu(inner, approximate=True), pre_act)
    hidden = hidden.astype(jnp.bfloat16)
    branch_four = over_heads(matmul_tr(hidden, feed_down))
    after_four = after_three + gate_two * branch_four
    output = jnp.where(token_live, after_four, 0.0).astype(jnp.bfloat16).reshape(frames.shape)
    upstream = jnp.where(
        token_live, cotangent.reshape(token_count, model_width).astype(jnp.float32), 0.0
    )
    feed_grad = (gate_two * upstream).astype(jnp.bfloat16)
    gate_two_grad = jnp.sum(upstream * branch_four, 0)
    feed_down_grad = outer_sum(feed_grad, hidden)
    pre_grad = gelu_pull(matmul(feed_grad, feed_down))[0].astype(jnp.bfloat16)
    feed_up_grad = outer_sum(input_four, pre_grad)
    input_four_grad = over_heads(matmul_tr(pre_grad, feed_up))
    shift_two_grad = jnp.sum(input_four_grad, 0)
    scale_two_grad = jnp.sum(input_four_grad * normed_four, 0)
    upstream = upstream + norm_back(normed_four, inverse_four, input_four_grad * (1.0 + scale_two))
    cross_grad = upstream.astype(jnp.bfloat16)
    cross_out_grad = outer_sum(cross_grad, context_three)
    context_grad = (
        matmul(cross_grad, cross_out)
        .astype(jnp.bfloat16)
        .reshape(token_count, head_count, HEAD_DIM)
    )
    query_grad, key_grad, value_grad = attend_back(
        query_three,
        word_keys,
        word_values,
        word_live,
        log_three,
        context_grad,
        cross_pattern,
        score_scale,
    )
    query_grad = query_grad.astype(jnp.bfloat16).reshape(token_count, head_width)
    cross_query_grad = outer_sum(input_three, query_grad)
    word_key_grad = key_grad.astype(jnp.bfloat16).reshape(-1, head_width)
    word_value_grad = value_grad.astype(jnp.bfloat16).reshape(-1, head_width)
    prompt_key_grad = outer_sum(prompt_rows, word_key_grad)
    prompt_value_grad = outer_sum(prompt_rows, word_value_grad)
    input_three_grad = over_heads(matmul_tr(query_grad, cross_query))
    cross_gain_grad = jnp.sum(input_three_grad * normed_three, 0)
    upstream = upstream + norm_back(normed_three, inverse_three, input_three_grad * cross_gain)
    time_grad = (gate_time * upstream).astype(jnp.bfloat16)
    time_gate_grad = jnp.sum(upstream * branch_two, 0) * (1.0 - gate_time * gate_time)
    time_out_grad = outer_sum(time_grad, context_two)
    context_grad = matmul(time_grad, time_out).astype(jnp.bfloat16).reshape(split_heads)
    query_grad, key_grad, value_grad = attend_back(
        query_two, key_two, value_two, frame_live, log_two, context_grad, time_pattern, score_scale
    )
    query_grad = query_grad.astype(jnp.bfloat16).reshape(token_count, head_width)
    key_grad = key_grad.astype(jnp.bfloat16).reshape(token_count, head_width)
    value_grad = value_grad.astype(jnp.bfloat16).reshape(token_count, head_width)
    time_query_grad = outer_sum(input_two, query_grad)
    time_key_grad = outer_sum(input_two, key_grad)
    time_value_grad = outer_sum(input_two, value_grad)
    input_two_grad = over_heads(
        matmul_tr(query_grad, time_query)
        + matmul_tr(key_grad, time_key)
        + matmul_tr(value_grad, time_value)
    )
    time_gain_grad = jnp.sum(input_two_grad * normed_two, 0)
    upstream = upstream + norm_back(normed_two, inverse_two, input_two_grad * time_gain)
    space_grad = (gate_one * upstream).astype(jnp.bfloat16)
    gate_one_grad = jnp.sum(upstream * branch_one, 0)
    space_out_grad = outer_sum(space_grad, context_one)
    context_grad = matmul(space_grad, space_out).astype(jnp.bfloat16).reshape(split_heads)
    key_frame, value_frame = (
        lax.all_gather(key_one, WIDE, axis=1, tiled=True),
        lax.all_gather(value_one, WIDE, axis=1, tiled=True),
    )
    query_grad, key_grad, value_grad = attend_back(
        query_one,
        key_frame,
        value_frame,
        every_patch,
        log_one,
        context_grad,
        space_pattern,
        score_scale,
    )
    key_grad, value_grad = (
        lax.psum_scatter(
            key_grad.astype(jnp.bfloat16), WIDE, scatter_dimension=1, tiled=True
        ).astype(jnp.float32),
        lax.psum_scatter(
            value_grad.astype(jnp.bfloat16), WIDE, scatter_dimension=1, tiled=True
        ).astype(jnp.float32),
    )
    query_grad = query_grad.astype(jnp.bfloat16).reshape(token_count, head_width)
    key_grad = key_grad.astype(jnp.bfloat16).reshape(token_count, head_width)
    value_grad = value_grad.astype(jnp.bfloat16).reshape(token_count, head_width)
    space_query_grad = outer_sum(input_one, query_grad)
    space_key_grad = outer_sum(input_one, key_grad)
    space_value_grad = outer_sum(input_one, value_grad)
    input_one_grad = over_heads(
        matmul_tr(query_grad, space_query)
        + matmul_tr(key_grad, space_key)
        + matmul_tr(value_grad, space_value)
    )
    shift_one_grad = jnp.sum(input_one_grad, 0)
    scale_one_grad = jnp.sum(input_one_grad * normed_one, 0)
    upstream = upstream + norm_back(normed_one, inverse_one, input_one_grad * (1.0 + scale_one))
    frames_grad = upstream.astype(jnp.bfloat16).reshape(frames.shape)
    modulation_bias_grad = jnp.concatenate(
        [
            shift_one_grad,
            scale_one_grad,
            gate_one_grad,
            shift_two_grad,
            scale_two_grad,
            gate_two_grad,
        ]
    )
    own_grad = lax.dynamic_slice_in_dim(modulation_bias_grad, slice_start, slice_width)
    modulation_weight_grad = condition.astype(jnp.float32)[:, None] * own_grad[None, :]
    (
        modulation_weight_grad,
        modulation_bias_grad,
        space_query_grad,
        space_key_grad,
        space_value_grad,
        space_out_grad,
        time_gain_grad,
        time_query_grad,
        time_key_grad,
        time_value_grad,
        time_out_grad,
        time_gate_grad,
        cross_gain_grad,
        cross_query_grad,
        prompt_key_grad,
        prompt_value_grad,
        cross_out_grad,
        feed_up_grad,
        feed_down_grad,
    ) = (
        lax.psum_scatter(
            modulation_weight_grad, (NARROW, WIDE), scatter_dimension=0, tiled=True
        ),
        lax.psum_scatter(modulation_bias_grad, (NARROW, WIDE), scatter_dimension=0, tiled=True),
        lax.psum_scatter(space_query_grad, (NARROW, WIDE), scatter_dimension=0, tiled=True),
        lax.psum_scatter(space_key_grad, (NARROW, WIDE), scatter_dimension=0, tiled=True),
        lax.psum_scatter(space_value_grad, (NARROW, WIDE), scatter_dimension=0, tiled=True),
        lax.psum_scatter(space_out_grad, (NARROW, WIDE), scatter_dimension=0, tiled=True),
        lax.psum_scatter(time_gain_grad, (NARROW, WIDE), scatter_dimension=0, tiled=True),
        lax.psum_scatter(time_query_grad, (NARROW, WIDE), scatter_dimension=0, tiled=True),
        lax.psum_scatter(time_key_grad, (NARROW, WIDE), scatter_dimension=0, tiled=True),
        lax.psum_scatter(time_value_grad, (NARROW, WIDE), scatter_dimension=0, tiled=True),
        lax.psum_scatter(time_out_grad, (NARROW, WIDE), scatter_dimension=0, tiled=True),
        lax.psum_scatter(time_gate_grad, (NARROW, WIDE), scatter_dimension=0, tiled=True),
        lax.psum_scatter(cross_gain_grad, (NARROW, WIDE), scatter_dimension=0, tiled=True),
        lax.psum_scatter(cross_query_grad, (NARROW, WIDE), scatter_dimension=0, tiled=True),
        lax.psum_scatter(prompt_key_grad, (NARROW, WIDE), scatter_dimension=0, tiled=True),
        lax.psum_scatter(prompt_value_grad, (NARROW, WIDE), scatter_dimension=0, tiled=True),
        lax.psum_scatter(cross_out_grad, (NARROW, WIDE), scatter_dimension=0, tiled=True),
        lax.psum_scatter(feed_up_grad, (NARROW, WIDE), scatter_dimension=0, tiled=True),
        lax.psum_scatter(feed_down_grad, (NARROW, WIDE), scatter_dimension=0, tiled=True),
    )
    return (
        output,
        frames_grad,
        modulation_weight_grad,
        modulation_bias_grad,
        space_query_grad,
        space_key_grad,
        space_value_grad,
        space_out_grad,
        time_gain_grad,
        time_query_grad,
        time_key_grad,
        time_value_grad,
        time_out_grad,
        time_gate_grad,
        cross_gain_grad,
        cross_query_grad,
        prompt_key_grad,
        prompt_value_grad,
        cross_out_grad,
        feed_up_grad,
        feed_down_grad,
    )


WEIGHT = P(WIDE, TENSOR)
OWNED = P((NARROW, WIDE), TENSOR)
ROWS = P((NARROW, WIDE))
PATCHES = P(NARROW, None, WIDE, None, None)
CLIP = P(NARROW)
COPIED = P()


def fits(sizes):
    return sizes[WIDE] == 2 and sizes[TENSOR] == 4 and sizes[NARROW] == 4


def solution(mesh):
    sizes = {name: mesh.shape[name] for name in mesh.axis_names}
    return jax.shard_map(
        functools.partial(fused_on_device, sizes) if fits(sizes) else on_device,
        mesh=mesh,
        in_specs=(
            (PATCHES, PATCHES, P(NARROW, None, None), CLIP, CLIP, CLIP)
            + (WEIGHT, COPIED, WEIGHT, WEIGHT, WEIGHT, WEIGHT)
            + (COPIED, WEIGHT, WEIGHT, WEIGHT, WEIGHT, COPIED)
            + (COPIED, WEIGHT, WEIGHT, WEIGHT, WEIGHT, WEIGHT, WEIGHT)
        ),
        out_specs=(
            (PATCHES, PATCHES, OWNED, ROWS, OWNED, OWNED, OWNED, OWNED)
            + (ROWS, OWNED, OWNED, OWNED, OWNED, ROWS)
            + (ROWS, OWNED, OWNED, OWNED, OWNED, OWNED, OWNED)
        ),
        check_vma=False,
    )
```

```python
import functools
import math

import jax
import jax.numpy as jnp
import numpy as np
from jax import lax
from jax.experimental import pallas as pl
from jax.experimental.pallas import tpu as pltpu
from jax.sharding import PartitionSpec as P

HEAD_DIM = 72
LANES = 128
WHOLE = 256
CHUNKS = 4
EPSILON = 1e-06
NEGATIVE = -1e30
NARROW, WIDE, TENSOR = "narrow", "wide", "tensor"
COLS = "cols"
MESH_ID = pl.DeviceIdType.MESH
F32 = jnp.float32
BF16 = jnp.bfloat16
VMEM = pltpu.VMEM
VM = pl.BlockSpec(memory_space=pltpu.VMEM)
ANY = pl.BlockSpec(memory_space=pl.ANY)
DMA = pltpu.SemaphoreType.DMA


def dot(left, right):
    return jnp.dot(left, right, preferred_element_type=F32)


def dot_tr(left, right):
    return lax.dot_general(left, right, (((1,), (1,)), ((), ())), preferred_element_type=F32)


def dot_outer(left, right):
    return lax.dot_general(left, right, (((0,), (0,)), ((), ())), preferred_element_type=F32)


def norm_tile(values):
    center = values - jnp.mean(values, -1, keepdims=True)
    inverse = lax.rsqrt(jnp.mean(center * center, -1, keepdims=True) + EPSILON)
    return center * inverse, inverse


def norm_pull(normed, inverse, incoming):
    return inverse * (
        incoming
        - jnp.mean(incoming, -1, keepdims=True)
        - normed * jnp.mean(incoming * normed, -1, keepdims=True)
    )


def softmax_tile(scores):
    exponent = jnp.exp(scores - jnp.max(scores, -1, keepdims=True))
    return exponent / jnp.sum(exponent, -1, keepdims=True)


class Place:
    def __init__(self, sizes):
        self.sizes = sizes
        self.n = lax.axis_index(NARROW)
        self.w = lax.axis_index(WIDE)
        self.t = lax.axis_index(TENSOR)

    def tensor_peer(self, step):
        return lax.rem(self.t + step, self.sizes[TENSOR])

    def over_tensor(self, step):
        return (self.n, self.w, self.tensor_peer(step))

    def sibling(self):
        return (self.n, 1 - self.w, self.t)

    def over_narrow(self, peer):
        return (peer, self.w, self.t)


def greet(partners):
    barrier = pltpu.get_barrier_semaphore()
    for partner in partners:
        pl.semaphore_signal(barrier, inc=1, device_id=partner, device_id_type=MESH_ID)
    pl.semaphore_wait(barrier, len(partners))


def send(source, target, send_sem, recv_sem, partner):
    copy = pltpu.make_async_remote_copy(
        src_ref=source,
        dst_ref=target,
        send_sem=send_sem,
        recv_sem=recv_sem,
        device_id=partner,
        device_id_type=MESH_ID,
    )
    copy.start()
    return copy


class Transfer:
    def __init__(self, slot, scatter, view, landing, born):
        self.slot, self.scatter, self.view, self.landing = slot, scatter, view, landing
        self.step, self.born = 0, born


class Line:
    def __init__(self, place, send_sems, recv_sems, lag=2):
        self.lag = lag
        self.place, self.send_sems, self.recv_sems = place, send_sems, recv_sems
        self.granules = send_sems.shape[2]
        self.open, self.slots, self.clock = [], 0, 0

    def at(self, index, body):
        pl.when(self.place.t == index)(body)

    def hop(self, move, source, target, sent, received, g, peer):
        return pltpu.make_async_remote_copy(
            src_ref=source,
            dst_ref=target,
            send_sem=self.send_sems.at[move.slot, sent, g],
            recv_sem=self.recv_sems.at[move.slot, received, g],
            device_id=(self.place.n, self.place.w, peer),
            device_id_type=MESH_ID,
        )

    def reduce_hop(self, move, owner, lands, g, peer):
        return self.hop(
            move, move.view(owner, g), move.landing(lands, g), owner, lands, g, peer
        )

    def copy_hop(self, move, owner, sent, g, peer):
        block = move.view(owner, g)
        return self.hop(move, block, block, sent, owner, g, peer)

    def start(self, scatter, view, landing=None):
        move = Transfer(self.slots, scatter, view, landing, self.clock)
        self.slots += 1
        if scatter:
            plan = {
                0: [(3, 3, 1), (2, 2, 1), (1, 1, 1)],
                1: [(0, 0, 0)],
                2: [(3, 3, 3)],
                3: [(0, 0, 2), (1, 1, 2), (2, 2, 2)],
            }
            make = self.reduce_hop
        else:
            plan = {
                0: [(0, 0, 2), (0, 1, 1)],
                1: [(1, 0, 2), (1, 1, 0)],
                2: [(2, 0, 1), (2, 1, 3)],
                3: [(3, 0, 1), (3, 1, 2)],
            }
            make = self.copy_hop
        for device, hops in plan.items():

            def begin(hops=hops):
                for owner, index, peer in hops:
                    for g in range(self.granules):
                        make(move, owner, index, g, peer).start()

            self.at(device, begin)
        self.open.append(move)
        return move

    def pending_block(self, move, index, g):
        block = move.landing(index, g) if move.scatter else move.view(index, g)
        return self.hop(move, block, block, 0, index, g, 0)

    def relay(self, move, index, g, lands, sent, peer):
        self.pending_block(move, index, g).wait_recv()
        if move.scatter:
            block = move.landing(index, g)
            block[...] = (block[...].astype(F32) + move.view(index, g)[...].astype(F32)).astype(
                BF16
            )
            self.hop(move, block, move.landing(lands, g), index, lands, g, peer).start()
        else:
            self.copy_hop(move, index, sent, g, peer).start()

    def steps(self):
        return 2 * self.granules

    def advance(self, move):
        late, g = divmod(move.step, self.granules)
        move.step += 1
        if move.scatter:
            plan = {1: ((3, 2, 0, 3), (2, 3, 0, 2)), 2: ((0, 1, 0, 0), (1, 0, 0, 1))}
        else:
            plan = {1: ((2, 0, 2, 0), (3, 0, 3, 0)), 2: ((1, 0, 2, 3), (0, 0, 3, 3))}
        for device, pair in plan.items():
            index, lands, sent, peer = pair[late]

            def body(index=index, lands=lands, sent=sent, peer=peer):
                self.relay(move, index, g, lands, sent, peer)

            self.at(device, body)

    def tick(self, count=1, lag=None):
        self.clock += 1
        lag = self.lag if lag is None else lag
        for _ in range(count):
            for move in self.open:
                if move.step < self.steps() and move.born + lag <= self.clock:
                    self.advance(move)
                    break

    def drain(self, move):
        while move.step < self.steps():
            self.advance(move)

    def finish(self, move):
        while move.step < self.steps():
            self.advance(move)
            for other in self.open:
                if other is not move and other.step < self.steps() and not other.scatter:
                    self.advance(other)
                    break
        self.open.remove(move)
        if move.scatter:
            plan = {0: (0, 1), 1: (1, 0), 2: (2, 3), 3: (3, 2)}
        else:
            plan = {0: (1, 2, 3), 1: (0,), 2: (3,), 3: (2, 1, 0)}
        for device, blocks in plan.items():

            def body(blocks=blocks):
                for index in blocks:
                    for g in range(self.granules):
                        self.pending_block(move, index, g).wait_recv()

            self.at(device, body)

    def release(self, move):
        for device in range(4):
            if move.scatter:
                sent = [d for d in range(4) if d != device]
            else:
                sent = range(4) if device in (1, 2) else range(2)

            def body(sent=sent):
                for index in sent:
                    for g in range(self.granules):
                        block = move.view(0, g)
                        self.hop(move, block, block, index, 0, g, 0).wait_send()

            self.at(device, body)


class Mover:
    def __init__(self, sems):
        self.sems, self.used, self.loads, self.saves = sems, 0, {}, []

    def go(self, source, target):
        copy = pltpu.make_async_copy(source, target, self.sems.at[self.used])
        self.used += 1
        copy.start()
        return copy

    def load(self, sources, targets):
        for source, target in zip(sources, targets):
            self.loads[id(target)] = self.go(source, target)

    def need(self, *targets):
        for target in targets:
            copy = self.loads.pop(id(target), None)
            if copy is not None:
                copy.wait()

    def keep(self, source, target):
        self.saves.append(self.go(source, target))

    def settle(self):
        wait_all(self.saves)


def stage_scratch(shapes):
    return [VMEM(shape.shape, shape.dtype) for shape in shapes] + [DMA((len(shapes) + 5,))]


def wait_all(copies):
    for copy in copies:
        copy.wait()


class Split:
    def __init__(self, place, frame_count, chunks, cols, group=1):
        parts = place.sizes[TENSOR]
        self.frame_count, self.chunks, self.cols = frame_count, chunks, cols
        self.rows = frame_count * cols
        self.quarter = self.rows // parts
        self.place, self.group = place, group
        self.frames = frame_count // parts

    def chunk(self, r):
        return pl.ds(r * self.rows * self.group, self.rows * self.group)

    def kept(self, r):
        return pl.ds(r * self.quarter, self.quarter)

    def own(self, r):
        start = r * self.rows + self.place.t * self.quarter
        return pl.ds(pl.multiple_of(start, self.quarter), self.quarter)

    def own_frames(self):
        return pl.ds(self.place.t * self.frames, self.frames)

    def rows_view(self, ref, r):
        def view(s, g):
            start = (r * self.group + g) * self.rows + s * self.quarter
            return ref.at[pl.ds(start, self.quarter)]

        return view

    def frames_view(self, ref, r):
        def view(s, g):
            return ref.at[pl.ds(s * self.frames, self.frames), r * self.group + g]

        return view

    def landing_view(self, ref):
        def view(s, g):
            return ref.at[s, g]

        return view

    def total(self, partial, landing, r):
        t = self.place.t
        beside = t + 1 - 2 * lax.rem(t, 2)
        return (
            partial[self.own(r)].astype(F32)
            + landing[t, r % self.group].astype(F32)
            + landing[beside, r % self.group].astype(F32)
        )

    def spots(self, f):
        return [
            pl.ds(pl.multiple_of(r * self.rows + f * self.cols, self.cols), self.cols)
            for r in range(self.chunks)
        ]


def neighbours(place):
    steps = range(1, place.sizes[TENSOR])
    return [place.sibling()] + [place.over_tensor(step) for step in steps]


def write_group_mask(group_mask, lengths, cols):
    shape = group_mask.shape
    row_id = lax.broadcasted_iota(jnp.int32, shape, 0)
    col_id = lax.broadcasted_iota(jnp.int32, shape, 1)
    live = col_id.astype(F32) < lengths[0:1, 0:1] * cols
    same = lax.rem(row_id, cols) == lax.rem(col_id, cols)
    group_mask[...] = jnp.where(jnp.logical_and(same, live), 1.0, 0.0)


def live_words(lengths):
    return lax.broadcasted_iota(jnp.int32, (1, LANES), 1).astype(F32) < lengths[1:2]


def pad_heads(turned):
    rows, columns = turned.shape
    filler = jnp.zeros((LANES - HEAD_DIM, columns), F32)
    pieces = []
    for start in range(0, rows, HEAD_DIM):
        pieces += [turned[start : start + HEAD_DIM].astype(F32), filler]
    return jnp.concatenate(pieces, 0).T.astype(BF16)


def group_partners(place):
    wide, tensor = place.sizes[WIDE], place.sizes[TENSOR]
    return [
        (place.n, lax.rem(place.w + dw, wide), lax.rem(place.t + dt, tensor))
        for dw in range(wide)
        for dt in range(tensor)
        if dw or dt
    ]


def forward_kernel(
    sizes,
    frames,
    condition,
    params,
    lengths,
    spread,
    prompt,
    *refs,
):
    weights, feed, modulation_weight = refs[:12], refs[12:14], refs[14]
    kept_out, full_out, feed_out, vectors_out = refs[15:34], refs[34], refs[35:37], refs[37]
    (
        h1, q1, side, o1, h2, q2, o2, h3, q3, kv3, o3, h4,
        a1_own, a2_own, x3_own, n2_own, n3_own, n4_own, inverses,
    ) = kept_refs = refs[38:57]
    (
        save_sems, turned, turned_prompt, full, full_prompt, feed_full, modulation_full,
        mine, shared, flat, vectors,
        wide_context, partial, landing, residual, group_mask,
        local_sems, side_send, side_recv, share_send, share_recv, kv_send, kv_recv,
        ring_send, ring_recv,
    ) = refs[57:]
    mover = Mover(save_sems)

    def keep(*sources):
        for source in sources:
            for kept_ref, out in zip(kept_refs, kept_out):
                if kept_ref is source:
                    mover.keep(source, out)

    place = Place(sizes)
    frame_count, chunks, cols, width = frames.shape
    split = Split(place, frame_count, chunks, cols)
    rows, half = split.rows, split.quarter
    heads = spread.shape[1] // LANES
    scale = 1.0 / math.sqrt(HEAD_DIM)
    chain = Line(place, ring_send, ring_recv)
    order = (0, 1, 2, 3, 4, 5, 6, 7, 8, 9, 10, 11)
    loads = {}

    def begin(i):
        target = turned.at[i] if i < 10 else turned_prompt.at[i - 10]
        loads[i] = pltpu.make_async_copy(weights[i], target, local_sems.at[i])
        loads[i].start()

    for i in order[:4]:
        begin(i)
    modulation_load = pltpu.make_async_copy(modulation_weight, modulation_full, local_sems.at[14])
    modulation_load.start()
    for i in order[4:]:
        begin(i)
    feed_spots, feed_loads = [], []
    for i in range(2):
        feed_half = feed[i].shape[0]
        feed_spots.append(pl.ds(pl.multiple_of(place.w * feed_half, feed_half), feed_half))
        feed_loads.append(
            pltpu.make_async_copy(
                feed[i], feed_full.at[i, feed_spots[i]], local_sems.at[12 + i]
            )
        )
        feed_loads[i].start()
    partners = group_partners(place)
    greet(partners)
    modulation_load.wait()
    slice_width = modulation_weight.shape[1]
    mine[...] = jnp.zeros_like(mine)
    mine[:, 0:slice_width] = dot(condition[...], modulation_full[...])[0:8]
    shifted = pltpu.roll(mine[...], slice_width % LANES, 1)
    mine[...] = jnp.where(lax.rem(place.t, 2) == 1, shifted, mine[...])
    slot = place.w * sizes[TENSOR] + place.t
    shared[slot] = mine[0:1]
    share_copies = [
        send(shared.at[slot], shared.at[slot], share_send.at[i], share_recv.at[i], partner)
        for i, partner in enumerate(partners)
    ]
    pending = {}

    def turn(*which):
        for i in which:
            loads[i].wait()
            half_rows = weights[i].shape[1]
            spot = pl.ds(pl.multiple_of(place.w * half_rows, half_rows), half_rows)
            if i < 10:
                full[i, spot] = pad_heads(turned[i])
                target = full.at[i, spot]
            else:
                full_prompt[i - 10, spot] = turned_prompt[i - 10].T
                target = full_prompt.at[i - 10, spot]
            pending[i] = [
                send(target, target, side_send.at[i], side_recv.at[i], place.sibling())
            ]

    def ready(*which):
        for i in which:
            wait_all(pending.pop(i))

    turn(0, 1, 2)
    write_group_mask(group_mask, lengths, cols)
    wait_all(share_copies)
    flat[...] = params[:, 0 : flat.shape[1]]
    for slot in range(shared.shape[0]):
        start = slot % sizes[TENSOR] * slice_width // LANES * LANES
        flat[:, start : start + shared.shape[2]] += shared[slot]
    for j in range(6):
        row = flat[:, j * width : (j + 1) * width]
        vectors[j : j + 1] = 1.0 + row if j in (1, 4) else row
    for j in range(6, 9):
        row = params[:, j * width : (j + 1) * width]
        vectors[j : j + 1] = jnp.tanh(row) if j == 7 else row
    mover.keep(vectors, vectors_out)

    @pl.loop(0, frame_count)
    def _(f):
        for r in range(chunks):
            normed, _ = norm_tile(frames[f, r].astype(F32))
            h1[pl.ds(pl.multiple_of(r * rows + f * cols, cols), cols)] = (
                normed * vectors[1:2] + vectors[0:1]
            ).astype(BF16)

    keep(h1)

    def project(source, spot, weight, out, index):
        out[index, spot] = dot(source[spot], full[weight]).astype(BF16)

    ready(0, 1, 2)

    @pl.loop(0, 3)
    def _(i):
        for r in range(0, chunks * rows, WHOLE):
            project(h1, pl.ds(r, WHOLE), i, q1, i)

    kv_copies = [
        send(q1.at[1 + j], side.at[j], kv_send.at[j], kv_recv.at[j], place.sibling())
        for j in range(2)
    ]
    turn(3)
    wait_all(kv_copies)
    keep(q1, side)

    @pl.loop(0, frame_count)
    def _(f):
        spots = split.spots(f)
        queries = jnp.concatenate([q1[0, spot] for spot in spots], 0)
        keys = jnp.concatenate(
            [q1[1, spot] for spot in spots] + [side[0, spot] for spot in spots], 0
        )
        values = jnp.concatenate(
            [q1[2, spot] for spot in spots] + [side[1, spot] for spot in spots], 0
        )
        for h in range(heads):
            lanes = slice(h * LANES, (h + 1) * LANES)
            attend = softmax_tile(dot_tr(queries[:, lanes], keys[:, lanes]) * scale)
            context = dot(attend.astype(BF16), values[:, lanes]).astype(BF16)
            for r in range(chunks):
                wide_context[spots[r], lanes] = context[r * cols : (r + 1) * cols]

    sent = [None] * chunks

    def emit(r, out, weight, stage):
        spot = split.chunk(r)
        if sent[r] is not None:
            chain.release(sent[r])
        partial[spot] = dot_tr(wide_context[spot], full[weight]).astype(BF16)
        sent[r] = chain.start(
            True, split.rows_view(partial, r), split.landing_view(landing.at[stage * chunks + r])
        )
        out[spot] = dot_tr(wide_context[spot], spread[...]).astype(BF16)
        return sent[r]

    def branch(r, stage):
        return split.total(partial, landing.at[stage * chunks + r], r)

    def settle(scatters, body, target):
        gathers = []
        for r in range(chunks):
            chain.finish(scatters[r])
            body(r)
            gathers.append(chain.start(False, split.rows_view(target, r)))
            chain.tick(4, 3)
        return gathers

    ready(3)
    scatters = []
    for r in range(chunks):
        scatters.append(emit(r, o1, 3, 0))
        chain.tick(0)

    keep(o1)
    turn(4, 5, 6, 7)
    chain.tick(4)
    turn(10, 11)
    chain.tick(4)
    ready(10, 11)
    kv3[...] = jnp.zeros_like(kv3)
    for j in range(2):
        narrow = dot(prompt[...], full_prompt[j]).astype(BF16)
        kv3[j, 0 : prompt.shape[0]] = dot(narrow, spread[...]).astype(BF16)
        chain.tick(4)
    keep(kv3)

    def body_one(r):
        kept = split.kept(r)
        branch_one = branch(r, 0)
        a1_own[kept] = branch_one
        x_own = frames[split.own_frames(), r].reshape(half, width)
        after = x_own.astype(F32) + vectors[2:3] * branch_one
        normed, inverse = norm_tile(after)
        residual[kept] = after
        n2_own[kept] = normed
        inverses[0, kept] = jnp.broadcast_to(inverse, (half, LANES))
        h2[split.own(r)] = (normed * vectors[6:7]).astype(BF16)

    gathers = settle(scatters, body_one, h2)
    released = list(gathers)
    keep(a1_own, n2_own)
    turn(8, 9)
    feed_copies = []
    for i in range(2):
        feed_loads[i].wait()
        target = feed_full.at[i, feed_spots[i]]
        feed_copies.append(
            send(target, target, side_send.at[12 + i], side_recv.at[12 + i], place.sibling())
        )
    ready(4, 5, 6, 7)
    scatters = []
    for r in range(chunks):
        chain.finish(gathers[r])
        spot = split.chunk(r)
        for i in range(3):
            project(h2, spot, 4 + i, q2, i)
            chain.tick()
        for h in range(heads):
            lanes = slice(h * LANES, (h + 1) * LANES)
            scores = dot_tr(q2[0, spot, lanes], q2[1, spot, lanes]) * scale
            attend = softmax_tile(jnp.where(group_mask[...] > 0.5, scores, NEGATIVE))
            wide_context[spot, lanes] = dot(attend.astype(BF16), q2[2, spot, lanes]).astype(BF16)
        chain.tick()
        scatters.append(emit(r, o2, 7, 1))

    def body_two(r):
        kept = split.kept(r)
        branch_two = branch(r, 1)
        a2_own[kept] = branch_two
        after = residual[kept] + vectors[7:8] * branch_two
        normed, inverse = norm_tile(after)
        residual[kept] = after
        n3_own[kept] = normed
        inverses[1, kept] = jnp.broadcast_to(inverse, (half, LANES))
        h3[split.own(r)] = (normed * vectors[8:9]).astype(BF16)

    gathers = settle(scatters, body_two, h3)
    released += gathers
    keep(h2, q2, o2, a2_own, n3_own)
    ready(8, 9)
    mover.keep(full, full_out)
    scatters = []
    for r in range(chunks):
        chain.finish(gathers[r])
        spot = split.chunk(r)
        q3[spot] = dot(h3[spot], full[8]).astype(BF16)
        chain.tick()
        for h in range(heads):
            lanes = slice(h * LANES, (h + 1) * LANES)
            scores = dot_tr(q3[spot, lanes], kv3[0, :, lanes]) * scale
            attend = softmax_tile(jnp.where(live_words(lengths), scores, NEGATIVE))
            wide_context[spot, lanes] = dot(attend.astype(BF16), kv3[1, :, lanes]).astype(BF16)
        chain.tick()
        scatters.append(emit(r, o3, 9, 2))

    def body_three(r):
        kept = split.kept(r)
        after = residual[kept] + branch(r, 2)
        normed, inverse = norm_tile(after)
        x3_own[kept] = after
        n4_own[kept] = normed
        inverses[2, kept] = jnp.broadcast_to(inverse, (half, LANES))
        h4[split.own(r)] = (normed * vectors[4:5] + vectors[3:4]).astype(BF16)

    gathers = settle(scatters, body_three, h4)
    keep(h3, q3, o3, x3_own, n4_own, inverses)
    wait_all(feed_copies)
    for i in range(2):
        mover.keep(feed_full.at[i], feed_out[i])
    for move in gathers:
        chain.finish(move)
    keep(h4)
    for move in sent + released + gathers:
        chain.release(move)
    mover.settle()


def forward_call(
    sizes, frames, condition, params, lengths, spread, prompt, weights, feed,
    modulation_weight,
):
    frame_count, chunks, cols, width = frames.shape
    rows = frame_count * cols
    tokens = rows * chunks
    head_width, padded = spread.shape
    half = rows // sizes[TENSOR]
    kept = half * chunks
    full_rows = weights[0].shape[1] * sizes[WIDE]
    prompt_width = weights[10].shape[1] * sizes[WIDE]
    slice_width = modulation_weight.shape[1]
    group = sizes[WIDE] * sizes[TENSOR]
    placed = slice_width + slice_width % LANES
    moves = 6 * chunks
    s = jax.ShapeDtypeStruct
    wide_act, heads_act = s((tokens, width), BF16), s((tokens, head_width), BF16)
    triple, own = s((3, tokens, padded), BF16), s((kept, width), F32)
    outs = [
        wide_act, triple, s((2, tokens, padded), BF16), heads_act,
        wide_act, triple, heads_act,
        wide_act, s((tokens, padded), BF16), s((2, LANES, padded), BF16), heads_act,
        wide_act, own, own, own, own, own, own, s((3, kept, LANES), F32),
    ]
    return pl.pallas_call(
        functools.partial(forward_kernel, sizes),
        name="forward",
        out_shape=outs
        + [s((10, full_rows, padded), BF16)]
        + [s((ref.shape[0] * sizes[WIDE], ref.shape[1]), BF16) for ref in feed]
        + [s((16, width), F32)],
        in_specs=[VM] * 6 + [ANY] * 15,
        out_specs=[ANY] * (len(outs) + 4),
        scratch_shapes=stage_scratch(outs)
        + [
            VMEM((10,) + weights[0].shape, BF16), VMEM((2,) + weights[10].shape, BF16),
            VMEM((10, full_rows, padded), BF16),
            VMEM((2, prompt_width, head_width), BF16),
            VMEM((2, feed[0].shape[0] * sizes[WIDE], feed[0].shape[1]), BF16),
            VMEM(modulation_weight.shape, BF16),
            VMEM((8, placed), F32), VMEM((group, 1, placed), F32),
            VMEM((1, 6 * width), F32), VMEM((16, width), F32),
            VMEM((tokens, padded), BF16),
            VMEM((tokens, width), BF16),
            VMEM((3 * chunks, 4, 1, half, width), BF16),
            VMEM((kept, width), F32),
            VMEM((rows, rows), F32),
            DMA((15,)), DMA((14,)), DMA((14,)), DMA((group - 1,)), DMA((group - 1,)),
            DMA((2,)), DMA((2,)),
            DMA((moves, 4, 1)), DMA((moves, 4, 1)),
        ],
        compiler_params=pltpu.CompilerParams(
            collective_id=1, has_side_effects=True, vmem_limit_bytes=60 << 20
        ),
    )(
        frames, condition, params, lengths, spread, prompt, *weights, *feed,
        modulation_weight,
    )


def prepare(frames, timestep, head_width):
    width = frames.shape[4]
    half_width = width // 2
    frequency = jnp.exp(-math.log(10000.0) * jnp.arange(half_width, dtype=F32) / half_width)
    angles = timestep[0].astype(F32) * frequency
    condition = jax.nn.silu(jnp.concatenate([jnp.cos(angles), jnp.sin(angles)])).astype(BF16)
    heads = head_width // HEAD_DIM
    padded = np.arange(heads * LANES)
    source = np.where(
        padded % LANES < HEAD_DIM, padded // LANES * HEAD_DIM + padded % LANES, -1
    )
    spread = (np.arange(head_width)[:, None] == source[None]).astype(np.float32)
    return condition, jnp.asarray(spread, BF16)


def over_columns(width, tile, body):
    whole = width // tile

    @pl.loop(0, whole)
    def _(j):
        body(pl.ds(pl.multiple_of(j * tile, tile), tile))

    if width % tile:
        body(pl.ds(whole * tile, width % tile))


GELU_C = math.sqrt(2.0 / math.pi)


def live_rows(lengths, split):
    first = split.place.t * split.frames
    pieces = []
    for f in range(split.frames):
        live = (first + f).astype(F32) < lengths[0:1, 0:1]
        pieces.append(jnp.broadcast_to(jnp.where(live, 1.0, 0.0), (split.cols, 1)))
    return jnp.concatenate(pieces, 0)


def own_cotangent(cotangent, lengths, split, r):
    width = cotangent.shape[3]
    rows = cotangent[split.own_frames(), r].reshape(split.quarter, width)
    return rows.astype(F32) * live_rows(lengths, split)


def mlp_kernel(
    sizes,
    vectors, lengths, *refs,
):
    ins, outs = refs[:6], refs[6:12]
    h4, cotangent, n4_own, inverses, up, down = loaded = refs[12:18]
    branch_part, e3, g3_own, up_grad, down_grad, sums = made = refs[18:24]
    (
        move_sems, e4, hidden, pre_grad, partial, landing, ring_send, ring_recv,
    ) = refs[24:]
    place = Place(sizes)
    frame_count, chunks, cols, width = cotangent.shape
    group = landing.shape[2]
    split = Split(place, frame_count, chunks, cols, group)
    line = Line(place, ring_send, ring_recv)
    mover = Mover(move_sems)
    mover.load(
        [ins[i] for i in (1, 4, 5, 0, 2, 3)], [loaded[i] for i in (1, 4, 5, 0, 2, 3)]
    )
    greet(neighbours(place))
    mover.need(cotangent)

    @pl.loop(0, frame_count)
    def _(f):
        live = jnp.where(f.astype(F32) < lengths[0:1, 0:1], 1.0, 0.0)
        for r, spot in enumerate(split.spots(f)):
            e4[spot] = (
                vectors[5:6] * (cotangent[f, r].astype(F32) * live)
            ).astype(BF16)

    sums[...] = jnp.zeros_like(sums)
    mover.need(up, down, h4)
    scatters = []
    for r in range(chunks // group):
        spot = split.chunk(r)

        def act(lanes):
            pre = dot(h4[spot], up[:, lanes])
            grad = dot(e4[spot], down[:, lanes])
            inner = jnp.tanh(GELU_C * (pre + 0.044715 * pre * pre * pre))
            gate = 0.5 * (1.0 + inner)
            hidden[spot, lanes] = (pre * gate).astype(BF16)
            slope = gate + 0.5 * pre * (1.0 - inner * inner) * (
                GELU_C * (1.0 + 3.0 * 0.044715 * pre * pre)
            )
            pre_grad[spot, lanes] = (grad * slope).astype(BF16)

        over_columns(up.shape[1], 256, act)
        line.tick(1, 1)
        partial[spot] = dot_tr(pre_grad[spot], up[...]).astype(BF16)
        line.tick(1, 1)
        scatters.append(
            line.start(True, split.rows_view(partial, r), split.landing_view(landing.at[r]))
        )

    for r in range(chunks // group):
        spot = split.chunk(r)
        branch_part[spot] = dot_tr(hidden[spot], down[...]).astype(BF16)
        line.tick(1, 1)

    mover.keep(branch_part, outs[0])

    def down_tile(lanes):
        down_grad[:, lanes] = dot_outer(e4[...], hidden[:, lanes]).astype(BF16)

    def up_tile(lanes):
        up_grad[:, lanes] = dot_outer(h4[...], pre_grad[:, lanes]).astype(BF16)

    mover.need(n4_own, inverses)
    gathers = []
    for r in range(chunks // group):
        line.finish(scatters[r])
        for c in range(r * group, (r + 1) * group):
            kept = split.kept(c)
            grad = split.total(partial, landing.at[r], c)
            normed = n4_own[kept]
            sums[0:1] += jnp.sum(grad, 0, keepdims=True)
            sums[1:2] += jnp.sum(grad * normed, 0, keepdims=True)
            upstream = own_cotangent(cotangent, lengths, split, c) + norm_pull(
                normed, inverses[2, kept][:, 0:1], grad * vectors[4:5]
            )
            g3_own[kept] = upstream
            e3[split.own(c)] = upstream.astype(BF16)
        gathers.append(line.start(False, split.rows_view(e3, r)))
        if r == 0:
            over_columns(up.shape[1], 256, down_tile)
            line.tick(2, 1)

    mover.keep(g3_own, outs[2])
    mover.keep(sums, outs[5])
    mover.keep(down_grad, outs[4])
    over_columns(up.shape[1], 256, up_tile)
    mover.keep(up_grad, outs[3])
    for move in gathers:
        line.finish(move)
    mover.keep(e3, outs[1])
    for move in scatters + gathers:
        line.release(move)
    mover.settle()


def mlp_call(sizes, vectors, lengths, acts):
    frame_count, chunks, cols, width = acts[1].shape
    rows = frame_count * cols
    tokens = rows * chunks
    quarter = rows // sizes[TENSOR]
    hidden = acts[4].shape[1]
    s = jax.ShapeDtypeStruct
    group = max(1, chunks // 2)
    moves = 2 * chunks // group
    outs = [
        s((tokens, width), BF16), s((tokens, width), BF16), s((quarter * chunks, width), F32),
        s((width, hidden), BF16), s((width, hidden), BF16), s((8, width), F32),
    ]
    return pl.pallas_call(
        functools.partial(mlp_kernel, sizes),
        name="mlp",
        out_shape=outs,
        in_specs=[VM] * 2 + [ANY] * len(acts),
        out_specs=[ANY] * len(outs),
        scratch_shapes=stage_scratch(list(acts) + outs)
        + [
            VMEM((tokens, width), BF16), VMEM((tokens, hidden), BF16),
            VMEM((tokens, hidden), BF16),
            VMEM((tokens, width), BF16),
            VMEM((chunks // group, 4, group, quarter, width), BF16),
            DMA((moves, 4, group)), DMA((moves, 4, group)),
        ],
        compiler_params=pltpu.CompilerParams(
            collective_id=2, has_side_effects=True, vmem_limit_bytes=60 << 20
        ),
    )(vectors, lengths, *acts)


class Reducer:
    def __init__(self, place, source, mine, merged, received, sems):
        self.place, self.source = place, source
        self.mine, self.merged, self.received = mine, merged, received
        self.local, self.side_send, self.side_recv, self.far_send, self.far_recv = sems
        self.clips = place.sizes[NARROW]
        self.block = mine.shape[1]

    def rows(self, clip, core):
        start = (clip * self.place.sizes[WIDE] + core) * self.block
        return pl.ds(pl.multiple_of(start, self.block), self.block)

    def split(self):
        self.copies = []
        for clip in range(self.clips):
            local = pltpu.make_async_copy(
                self.source.at[self.rows(clip, self.place.w)],
                self.mine.at[clip],
                self.local.at[clip],
            )
            local.start()
            self.copies += [
                local,
                send(
                    self.source.at[self.rows(clip, 1 - self.place.w)],
                    self.merged.at[clip],
                    self.side_send.at[clip],
                    self.side_recv.at[clip],
                    self.place.sibling(),
                ),
            ]

    def spread(self):
        wait_all(self.copies)
        self.copies = []

        @pl.loop(0, self.clips)
        def _(clip):
            self.merged[clip] = (
                self.merged[clip].astype(F32) + self.mine[clip].astype(F32)
            ).astype(BF16)

        for step in (3, 1, 2) if self.clips == 4 else range(1, self.clips):
            peer = lax.rem(self.place.n + step, self.clips)
            self.copies.append(
                send(
                    self.merged.at[peer],
                    self.received.at[step - 1],
                    self.far_send.at[step - 1],
                    self.far_recv.at[step - 1],
                    self.place.over_narrow(peer),
                )
            )

    def finish(self, out):
        wait_all(self.copies)
        total = self.merged[self.place.n].astype(F32)
        for step in range(self.clips - 1):
            total = total + self.received[step].astype(F32)
        out[...] = total


def reducer_scratch(sizes, jobs, block, width):
    clips = sizes[NARROW]
    return [
        VMEM((jobs, clips, block, width), BF16),
        VMEM((jobs, clips, block, width), BF16),
        VMEM((jobs, clips - 1, block, width), BF16),
        DMA((jobs, clips)), DMA((jobs, clips)), DMA((jobs, clips)),
        DMA((jobs, clips - 1)), DMA((jobs, clips - 1)),
    ]


def reducers(place, sources, scratch):
    mine, merged, received, *sems = scratch
    return [
        Reducer(
            place, source, mine.at[i], merged.at[i], received.at[i], [sem.at[i] for sem in sems]
        )
        for i, source in enumerate(sources)
    ]


def all_partners(place):
    sizes = place.sizes
    return (
        [place.sibling()]
        + [place.over_tensor(step) for step in range(1, sizes[TENSOR])]
        + [
            place.over_narrow(lax.rem(place.n + step, sizes[NARROW]))
            for step in range(1, sizes[NARROW])
        ]
    )


def attention_pull(queries, keys, values, context_grad, mask, scale):
    scores = dot_tr(queries, keys) * scale
    if mask is not None:
        scores = jnp.where(mask, scores, NEGATIVE)
    attend = softmax_tile(scores)
    attend_grad = dot_tr(context_grad, values)
    score_grad = (
        attend * (attend_grad - jnp.sum(attend * attend_grad, -1, keepdims=True))
    ).astype(BF16)
    return (
        dot(score_grad, keys) * scale,
        dot_outer(score_grad, queries) * scale,
        dot_outer(attend.astype(BF16), context_grad),
    )


def back_kernel(
    sizes,
    vectors, lengths, spread, *refs,
):
    ins, full_in, gradients = refs[:13], refs[13], refs[14:16]
    outs = refs[16:24]
    (
        e3, g3_own, n3_own, n2_own, inverses, a2_own, h3, q3, kv3, o3, h2, q2, o2,
    ) = loaded = refs[24:37]
    g1_own, e1, time_grads, word_grads, up_out, down_out, cross_out, sums = refs[37:45]
    (
        move_sems, cross_full, time_full, wide_grad, wide_parts, narrow_parts, word_sums,
        word_side, e2, partial, landing, group_mask, cross_grads,
        full_sems, word_send, word_recv, ring_send, ring_recv,
    ) = refs[45:63]
    place = Place(sizes)
    tokens, width = e3.shape
    rows, cols = group_mask.shape[0], sizes[COLS]
    chunks = tokens // rows
    split = Split(place, rows // cols, chunks, cols)
    heads = spread.shape[1] // LANES
    scale = 1.0 / math.sqrt(HEAD_DIM)
    line = Line(place, ring_send, ring_recv, 3)
    mover = Mover(move_sems)
    weights = []
    for i, (source, target) in enumerate(
        ((full_in.at[pl.ds(8, 2)], cross_full), (full_in.at[pl.ds(4, 4)], time_full))
    ):
        weights.append(pltpu.make_async_copy(source, target, full_sems.at[i]))
    weights[0].start()
    first = (0, 7, 8)
    order = first + tuple(i for i in range(13) if i not in first)
    mover.load([ins[i] for i in order], [loaded[i] for i in order])
    weights[1].start()
    greet(all_partners(place))
    feed = reducers(place, gradients, refs[63:71])
    cross = reducers(place, [cross_grads.at[0], cross_grads.at[1]], refs[71:79])
    for job in feed:
        job.split()
    write_group_mask(group_mask, lengths, cols)
    sums[...] = jnp.zeros_like(sums)
    word_sums[...] = jnp.zeros_like(word_sums)

    def context_grad(source, spot, weight):
        wide_grad[spot] = dot(source[spot], weight).astype(BF16)

    def scatter(r, stage):
        return line.start(
            True,
            split.rows_view(partial, r),
            split.landing_view(landing.at[stage * chunks + r]),
        )

    weights[0].wait()
    mover.need(e3, q3, kv3)
    scatters = []
    for r in range(chunks):
        spot = split.chunk(r)
        context_grad(e3, spot, cross_full[1])
        line.tick()
        for h in range(heads):
            lanes = slice(h * LANES, (h + 1) * LANES)
            query_grad, key_grad, value_grad = attention_pull(
                q3[spot, lanes], kv3[0, :, lanes], kv3[1, :, lanes], wide_grad[spot, lanes],
                live_words(lengths), scale,
            )
            wide_parts[0, spot, lanes] = query_grad.astype(BF16)
            word_sums[0, :, lanes] += key_grad
            word_sums[1, :, lanes] += value_grad
        line.tick()
        partial[spot] = dot_tr(wide_parts[0, spot], cross_full[0]).astype(BF16)
        scatters.append(scatter(r, 0))
        narrow_parts[0, spot] = dot_tr(wide_parts[0, spot], spread[...]).astype(BF16)
    word_copy = send(word_sums, word_side, word_send, word_recv, place.sibling())
    mover.need(o3, h3)
    cross_grads[0] = dot_outer(e3[...], o3[...]).astype(BF16)
    line.tick(2)
    cross_grads[1] = dot_outer(h3[...], narrow_parts[0]).astype(BF16)
    line.tick(2)
    for job in cross:
        job.split()
    mover.need(*loaded)
    gathers = []
    for r in range(chunks):
        kept = split.kept(r)
        line.finish(scatters[r])
        grad = split.total(partial, landing.at[r], r)
        normed = n3_own[kept]
        sums[0:1] += jnp.sum(grad * normed, 0, keepdims=True)
        upstream = g3_own[kept] + norm_pull(
            normed, inverses[1, kept][:, 0:1], grad * vectors[8:9]
        )
        g1_own[kept] = upstream
        sums[1:2] += jnp.sum(upstream * a2_own[kept], 0, keepdims=True)
        e2[split.own(r)] = (vectors[7:8] * upstream).astype(BF16)
        gathers.append(line.start(False, split.rows_view(e2, r)))
        line.tick(4, 3)
        if r == 0:
            for job in feed:
                job.spread()
    for job in cross:
        job.spread()
    word_copy.wait()
    for j in range(2):
        word_grads[j] = dot_tr(
            (word_sums[j] + word_side[j]).astype(BF16), spread[...]
        ).astype(BF16)
    mover.keep(word_grads, outs[3])
    sent = scatters + gathers

    weights[1].wait()
    former, scatters = scatters, []
    for r in range(chunks):
        spot = split.chunk(r)
        line.finish(gathers[r])
        context_grad(e2, spot, time_full[3])
        line.tick()
        for h in range(heads):
            lanes = slice(h * LANES, (h + 1) * LANES)
            parts = attention_pull(
                q2[0, spot, lanes], q2[1, spot, lanes], q2[2, spot, lanes],
                wide_grad[spot, lanes], group_mask[...] > 0.5, scale,
            )
            for i in range(3):
                wide_parts[i, spot, lanes] = parts[i].astype(BF16)
            if h % 2:
                line.tick()
        total = None
        for i in range(3):
            part = dot_tr(wide_parts[i, spot], time_full[i])
            total = part if total is None else total + part
        line.tick()
        line.release(former[r])
        sent.remove(former[r])
        partial[spot] = total.astype(BF16)
        scatters.append(scatter(r, 1))
        for i in range(3):
            narrow_parts[i, spot] = dot_tr(wide_parts[i, spot], spread[...]).astype(BF16)
    sent += scatters
    time_grads[0] = dot_outer(e2[...], o2[...]).astype(BF16)
    line.tick(2)
    for i in range(3):
        time_grads[1 + i] = dot_outer(h2[...], narrow_parts[i]).astype(BF16)
        line.tick(1)
    mover.keep(time_grads, outs[2])

    gathers = []
    for r in range(chunks):
        kept = split.kept(r)
        line.finish(scatters[r])
        grad = split.total(partial, landing.at[chunks + r], r)
        normed = n2_own[kept]
        sums[2:3] += jnp.sum(grad * normed, 0, keepdims=True)
        upstream = g1_own[kept] + norm_pull(
            normed, inverses[0, kept][:, 0:1], grad * vectors[6:7]
        )
        g1_own[kept] = upstream
        e1[split.own(r)] = (vectors[2:3] * upstream).astype(BF16)
        gathers.append(line.start(False, split.rows_view(e1, r)))
        line.tick(4, 3)
    mover.keep(g1_own, outs[0])
    mover.keep(sums, outs[7])
    feed[0].finish(up_out)
    mover.keep(up_out, outs[4])
    line.drain(gathers[0])
    feed[1].finish(down_out)
    mover.keep(down_out, outs[5])
    for r in range(1, chunks):
        line.drain(gathers[r])
    cross[0].finish(cross_out.at[0])
    cross[1].finish(cross_out.at[1])
    mover.keep(cross_out, outs[6])
    for move in gathers:
        line.finish(move)
    mover.keep(e1, outs[1])
    for move in sent + gathers:
        line.release(move)
    mover.settle()


def back_call(sizes, cols, small, acts, full, gradients):
    spread = small[2]
    tokens, width = acts[0].shape
    rows = tokens // CHUNKS
    chunks = tokens // rows
    quarter = rows // sizes[TENSOR]
    head_width, padded = spread.shape
    full_rows = full.shape[1]
    hidden = gradients[0].shape[1]
    block = width // (sizes[NARROW] * sizes[WIDE])
    s = jax.ShapeDtypeStruct
    moves = 4 * chunks
    outs = [
        s((quarter * chunks, width), F32), s((tokens, width), BF16),
        s((4, width, head_width), BF16), s((2, LANES, head_width), BF16),
        s((block, hidden), F32), s((block, hidden), F32), s((2, block, head_width), F32),
        s((8, width), F32),
    ]
    return pl.pallas_call(
        functools.partial(back_kernel, {**sizes, COLS: cols}),
        name="back",
        out_shape=outs,
        in_specs=[VM] * 3 + [ANY] * (len(acts) + 3),
        out_specs=[ANY] * len(outs),
        scratch_shapes=stage_scratch(list(acts) + outs)
        + [
            VMEM((2, full_rows, padded), BF16), VMEM((4, full_rows, padded), BF16),
            VMEM((tokens, padded), BF16),
            VMEM((3, tokens, padded), BF16),
            VMEM((3, tokens, head_width), BF16),
            VMEM((2, LANES, padded), F32), VMEM((2, LANES, padded), F32),
            VMEM((tokens, width), BF16),
            VMEM((tokens, width), BF16),
            VMEM((2 * chunks, 4, 1, quarter, width), BF16),
            VMEM((rows, rows), F32),
            VMEM((2, width, head_width), BF16),
            DMA((2,)), DMA(()), DMA(()),
            DMA((moves, 4, 1)), DMA((moves, 4, 1)),
        ]
        + reducer_scratch(sizes, 2, block, hidden)
        + reducer_scratch(sizes, 2, block, head_width),
        compiler_params=pltpu.CompilerParams(
            collective_id=3, has_side_effects=True, vmem_limit_bytes=60 << 20
        ),
    )(*small, *acts, full, *gradients)


def space_kernel(
    sizes,
    vectors, spread, lengths, mlp_sums, back_sums, condition, *refs,
):
    ins, full_in, gradients, outs = refs[:13], refs[13], refs[14], refs[15:23]
    (
        e1, g1_own, frames, a1_own, h1, q1, side, o1, prompt, word_grads, branch_part, x3_own,
        cotangent,
    ) = loaded = refs[23:36]
    frames_grad, output, early_out, space_out, prompt_out, merged, conditions, grand = refs[36:44]
    (
        move_sems, query_full, out_full, wide_grad, wide_parts, narrow_parts, key_sums, side_out,
        side_in, space_grads, words, word_parts, partial, landing, tally, tally_side, tally_peers,
        full_sems, key_send, key_recv, word_send, word_recv,
        tally_send, tally_recv, ring_send, ring_recv,
    ) = refs[44:70]
    early_scratch, late_scratch = refs[70:78], refs[78:86]
    place = Place(sizes)
    clips = sizes[NARROW]
    frame_count, chunks, cols, width = frames.shape
    split = Split(place, frame_count, chunks, cols)
    quarter = split.quarter
    heads = spread.shape[1] // LANES
    scale = 1.0 / math.sqrt(HEAD_DIM)
    line = Line(place, ring_send, ring_recv)
    mover = Mover(move_sems)
    weights = [
        pltpu.make_async_copy(full_in.at[pl.ds(3, 1)], out_full, full_sems.at[0]),
        pltpu.make_async_copy(full_in.at[pl.ds(0, 3)], query_full, full_sems.at[1]),
    ]
    weights[0].start()
    first = (10, 8, 9, 0, 5, 6)
    order = first + tuple(i for i in range(13) if i not in first)
    mover.load([ins[i] for i in order], [loaded[i] for i in order])
    weights[1].start()
    greet(all_partners(place))
    mover.need(branch_part)

    def scatter(source, r, stage):
        return line.start(
            True,
            split.rows_view(source, r),
            split.landing_view(landing.at[stage * chunks + r]),
        )

    feed_scatters = [scatter(branch_part, r, 1) for r in range(chunks)]
    mover.need(prompt, word_grads)
    early = reducers(place, [gradients.at[i] for i in range(4)], early_scratch)
    late = reducers(place, [space_grads.at[i] for i in range(4)], late_scratch)
    for job in early:
        job.split()
    block = words.shape[2]
    far = [lax.rem(place.n + step, clips) for step in range(1, clips)]
    word_copies = []
    for i, peer in enumerate(far):
        lanes = pl.ds(pl.multiple_of((peer * sizes[WIDE] + place.w) * block, block), block)
        for j, (source, target) in enumerate(
            (
                (prompt.at[:, lanes], words.at[i + 1]),
                (word_grads, word_parts.at[i + 1]),
                (condition, conditions.at[place.n]),
            )
        ):
            word_copies.append(
                send(
                    source, target, word_send.at[i, j], word_recv.at[i, j],
                    place.over_narrow(peer),
                )
            )
    mine = pl.ds(pl.multiple_of((place.n * sizes[WIDE] + place.w) * block, block), block)
    words[0] = prompt[:, mine]
    word_parts[0] = word_grads[...]
    conditions[place.n] = condition[...]
    tally[...] = jnp.zeros_like(tally)
    tally[3:5] = mlp_sums[0:2]
    tally[6:7] = back_sums[0:1]
    tally[7:8] = back_sums[1:2] * (1.0 - vectors[7:8] * vectors[7:8])
    tally[8:9] = back_sums[2:3]

    weights[0].wait()
    mover.need(e1)
    for r in range(chunks):
        spot = split.chunk(r)
        wide_grad[spot] = dot(e1[spot], out_full[0]).astype(BF16)
        line.tick()

    mover.need(*loaded)
    weights[1].wait()
    tally[2:3] = jnp.sum(g1_own[...] * a1_own[...], 0, keepdims=True)

    def attend(first, stop):
        @pl.loop(first, stop)
        def _(f):
            spots = split.spots(f)
            queries = jnp.concatenate([q1[0, spot] for spot in spots], 0)
            grads = jnp.concatenate([wide_grad[spot] for spot in spots], 0)
            keys = jnp.concatenate(
                [q1[1, spot] for spot in spots] + [side[0, spot] for spot in spots], 0
            )
            values = jnp.concatenate(
                [q1[2, spot] for spot in spots] + [side[1, spot] for spot in spots], 0
            )
            for h in range(heads):
                lanes = slice(h * LANES, (h + 1) * LANES)
                parts = attention_pull(
                    queries[:, lanes], keys[:, lanes], values[:, lanes], grads[:, lanes],
                    None, scale,
                )
                for r in range(chunks):
                    here = slice(r * cols, (r + 1) * cols)
                    there = slice((chunks + r) * cols, (chunks + r + 1) * cols)
                    wide_parts[0, spots[r], lanes] = parts[0][here].astype(BF16)
                    for j in range(2):
                        key_sums[j, spots[r], lanes] = parts[1 + j][here]
                        side_out[j, spots[r], lanes] = parts[1 + j][there].astype(BF16)

    outputs = []

    def finish_feed(r):
        kept = split.kept(r)
        line.finish(feed_scatters[r])
        branch = split.total(branch_part, landing.at[chunks + r], r)
        tally[5:6] += jnp.sum(
            own_cotangent(cotangent, lengths, split, r) * branch, 0, keepdims=True
        )
        after = (x3_own[kept] + vectors[5:6] * branch) * live_rows(lengths, split)
        output[split.own_frames(), r] = after.astype(BF16).reshape(split.frames, cols, width)
        outputs.append(line.start(False, split.frames_view(output, r)))

    quarters = frame_count // 4
    for part in range(4):
        attend(part * quarters, (part + 1) * quarters)
        line.tick(2)
        if part >= 2 and part - 2 < chunks:
            finish_feed(part - 2)
    for r in range(2, chunks):
        finish_feed(r)
    key_copy = send(side_out, side_in, key_send, key_recv, place.sibling())
    for job in early:
        job.spread()
    line.tick(2)
    key_copy.wait()
    for j in range(2):
        wide_parts[1 + j] = (key_sums[j] + side_in[j].astype(F32)).astype(BF16)
    line.tick(2)
    scatters = []
    for r in range(chunks):
        spot = split.chunk(r)
        total = dot_tr(wide_parts[0, spot], query_full[0])
        for i in (1, 2):
            total = total + dot_tr(wide_parts[i, spot], query_full[i])
        partial[spot] = total.astype(BF16)
        scatters.append(scatter(partial, r, 0))
        line.tick(2)

    space_grads[0] = dot_outer(e1[...], o1[...]).astype(BF16)
    late[0].split()
    for i in range(3):
        narrow_parts[i] = dot_tr(wide_parts[i], spread[...]).astype(BF16)
        space_grads[1 + i] = dot_outer(h1[...], narrow_parts[i]).astype(BF16)
        late[1 + i].split()
        line.tick(2)
    for job in late:
        job.spread()
    gathers = []
    for r in range(chunks):
        kept = split.kept(r)
        line.finish(scatters[r])
        grad = split.total(partial, landing.at[r], r)
        x_own = frames[split.own_frames(), r].reshape(quarter, width).astype(F32)
        normed, inverse = norm_tile(x_own)
        tally[0:1] += jnp.sum(grad, 0, keepdims=True)
        tally[1:2] += jnp.sum(grad * normed, 0, keepdims=True)
        upstream = g1_own[kept] + norm_pull(normed, inverse, grad * vectors[1:2])
        frames_grad[split.own_frames(), r] = upstream.astype(BF16).reshape(
            split.frames, cols, width
        )
        gathers.append(line.start(False, split.frames_view(frames_grad, r)))

    tally_copy = send(tally, tally_side, tally_send.at[0], tally_recv.at[0], place.sibling())
    wait_all(word_copies)
    for j in range(2):
        total = dot_outer(words[0], word_parts[0, j, 0 : prompt.shape[0]])
        for step in range(1, clips):
            total = total + dot_outer(words[step], word_parts[step, j, 0 : prompt.shape[0]])
        prompt_out[j] = total
    mover.keep(prompt_out, outs[4])
    mover.keep(conditions, outs[6])
    tally_copy.wait()
    tally_side[...] = tally_side[...] + tally[...]
    peer_copies = [
        send(
            tally_side, tally_peers.at[step - 1], tally_send.at[step], tally_recv.at[step],
            place.over_tensor(step),
        )
        for step in range(1, sizes[TENSOR])
    ]
    for move in gathers:
        line.drain(move)
    for i, job in enumerate(early):
        job.finish(early_out.at[i])
    mover.keep(early_out, outs[2])
    wait_all(peer_copies)
    total = tally_side[...]
    for step in range(sizes[TENSOR] - 1):
        total = total + tally_peers[step]
    merged[place.n] = total
    base = sizes[TENSOR]
    far_copies = [
        send(
            merged.at[place.n], merged.at[place.n],
            tally_send.at[base + i], tally_recv.at[base + i], place.over_narrow(peer),
        )
        for i, peer in enumerate(far)
    ]
    for i, job in enumerate(late):
        job.finish(space_out.at[i])
    mover.keep(space_out, outs[3])
    for move in outputs:
        line.finish(move)
    mover.keep(output, outs[1])
    for move in gathers:
        line.finish(move)
    mover.keep(frames_grad, outs[0])
    wait_all(far_copies)
    mover.keep(merged, outs[5])
    total = merged[0]
    for clip in range(1, clips):
        total = total + merged[clip]
    grand[...] = total
    mover.keep(grand, outs[7])
    for move in feed_scatters + outputs + scatters + gathers:
        line.release(move)
    mover.settle()


def space_call(sizes, small, acts, full, gradients):
    frames, spread, prompt, condition = acts[2], small[1], acts[8], small[5]
    frame_count, chunks, cols, width = frames.shape
    rows = frame_count * cols
    tokens = rows * chunks
    quarter = rows // sizes[TENSOR]
    head_width, padded = spread.shape
    full_rows = full.shape[1]
    parts = sizes[NARROW] * sizes[WIDE]
    block, word_block = width // parts, prompt.shape[1] // parts
    clips, peers = sizes[NARROW], sizes[TENSOR] - 1
    s = jax.ShapeDtypeStruct
    moves = 4 * chunks
    outs = [
        s(frames.shape, BF16), s(frames.shape, BF16),
        s((4, block, head_width), F32), s((4, block, head_width), F32),
        s((2, word_block, head_width), F32), s((clips, 16, width), F32),
        s((clips,) + condition.shape, F32), s((16, width), F32),
    ]
    return pl.pallas_call(
        functools.partial(space_kernel, sizes),
        name="space",
        out_shape=outs,
        in_specs=[VM] * 6 + [ANY] * (len(acts) + 2),
        out_specs=[ANY] * len(outs),
        scratch_shapes=stage_scratch(list(acts) + outs)
        + [
            VMEM((3, full_rows, padded), BF16), VMEM((1, full_rows, padded), BF16),
            VMEM((tokens, padded), BF16),
            VMEM((3, tokens, padded), BF16),
            VMEM((3, tokens, head_width), BF16),
            VMEM((2, tokens, padded), F32),
            VMEM((2, tokens, padded), BF16), VMEM((2, tokens, padded), BF16),
            VMEM((4, width, head_width), BF16),
            VMEM((clips, prompt.shape[0], word_block), BF16),
            VMEM((clips, 2, LANES, head_width), BF16),
            VMEM((tokens, width), BF16),
            VMEM((2 * chunks, 4, 1, quarter, width), BF16),
            VMEM((16, width), F32), VMEM((16, width), F32), VMEM((peers, 16, width), F32),
            DMA((2,)), DMA(()), DMA(()),
            DMA((clips - 1, 3)), DMA((clips - 1, 3)),
            DMA((peers + clips,)), DMA((peers + clips,)),
            DMA((moves, 4, 1)), DMA((moves, 4, 1)),
        ]
        + reducer_scratch(sizes, 4, block, head_width)
        + reducer_scratch(sizes, 4, block, head_width),
        compiler_params=pltpu.CompilerParams(
            collective_id=4, has_side_effects=True, vmem_limit_bytes=61 << 20
        ),
    )(*small, *acts, full, gradients)


def fused_on_device(
    sizes,
    frames, cotangent, prompt, timestep, clip_lengths, text_lengths,
    modulation_weight, modulation_bias, space_query, space_key, space_value, space_out,
    time_gain, time_query, time_key, time_value, time_out, time_gate, cross_gain, cross_query,
    prompt_key, prompt_value, cross_out, feed_up, feed_down,
):
    frame_count, width = frames.shape[1], frames.shape[4]
    cols = frames.shape[2] * frames.shape[3] // CHUNKS
    head_width = space_query.shape[1]
    condition, spread = prepare(frames, timestep, head_width)
    lengths = jnp.broadcast_to(
        jnp.concatenate([clip_lengths, text_lengths]).astype(F32)[:, None], (2, LANES)
    )
    half_condition = lax.dynamic_slice_in_dim(
        condition, lax.axis_index(WIDE) * modulation_weight.shape[0], modulation_weight.shape[0]
    )
    params = jnp.concatenate([modulation_bias, time_gain, time_gate, cross_gain])[None]
    tiles = frames.reshape(frame_count, CHUNKS, cols, width)
    pulls = cotangent.reshape(frame_count, CHUNKS, cols, width)
    (
        h1, q1, side, o1, h2, q2, o2, h3, q3, kv3, o3, h4,
        a1_own, a2_own, x3_own, n2_own, n3_own, n4_own, inverses, full, up, down, vectors,
    ) = forward_call(
        sizes, tiles, jnp.broadcast_to(half_condition[None], (16, half_condition.shape[0])),
        params, lengths, spread, prompt[0],
        [
            weight.T
            for weight in (
                space_query, space_key, space_value, space_out, time_query, time_key,
                time_value, time_out, cross_query, cross_out, prompt_key, prompt_value,
            )
        ],
        [feed_up, feed_down], modulation_weight,
    )
    branch_part, e3, g3_own, up_grad, down_grad, mlp_sums = mlp_call(
        sizes, vectors, lengths, [h4, pulls, n4_own, inverses, up, down]
    )
    g1_own, e1, time_grads, word_grads, up_out, down_out, cross_grads, back_sums = back_call(
        sizes, cols, [vectors, lengths, spread],
        [e3, g3_own, n3_own, n2_own, inverses, a2_own, h3, q3, kv3, o3, h2, q2, o2],
        full, [up_grad, down_grad],
    )
    frames_grad, output, early_out, late_out, prompt_out, merged, conditions, grand = space_call(
        sizes,
        [vectors, spread, lengths, mlp_sums, back_sums, condition.astype(F32)[None]],
        [e1, g1_own, tiles, a1_own, h1, q1, side, o1, prompt[0], word_grads, branch_part, x3_own,
         pulls],
        full, time_grads,
    )
    part = lax.axis_index(NARROW) * sizes[WIDE] + lax.axis_index(WIDE)
    block = width // (sizes[NARROW] * sizes[WIDE])
    slice_width = modulation_weight.shape[1]
    pulled = merged[:, :6].reshape(sizes[NARROW], 6 * width)
    own_pulled = lax.dynamic_slice_in_dim(
        pulled, lax.axis_index(TENSOR) * slice_width, slice_width, 1
    )
    own_condition = lax.dynamic_slice_in_dim(conditions[:, 0], part * block, block, 1)
    modulation_weight_grad = jnp.sum(own_condition[:, :, None] * own_pulled[:, None], 0)
    bias_block = 6 * block
    modulation_bias_grad = lax.dynamic_slice_in_dim(
        grand[:6].reshape(6 * width), part * bias_block, bias_block
    )
    cross_gain_grad, time_gate_grad, time_gain_grad = lax.dynamic_slice(
        grand, (6, part * block), (3, block)
    )
    return (
        output.reshape(frames.shape), frames_grad.reshape(frames.shape),
        modulation_weight_grad, modulation_bias_grad,
        late_out[1], late_out[2], late_out[3], late_out[0],
        time_gain_grad, early_out[1], early_out[2], early_out[3], early_out[0], time_gate_grad,
        cross_gain_grad, cross_grads[1], prompt_out[0], prompt_out[1], cross_grads[0],
        up_out, down_out,
    )


CONTRACT_LAST = (((1,), (1,)), ((), ()))
CONTRACT_FIRST = (((0,), (0,)), ((), ()))


def matmul(left, right):
    return jnp.dot(left, right, preferred_element_type=jnp.float32)


def matmul_tr(left, right):
    return lax.dot_general(left, right, CONTRACT_LAST, preferred_element_type=jnp.float32)


def outer_sum(left, right):
    return lax.dot_general(left, right, CONTRACT_FIRST, preferred_element_type=jnp.float32)


def norm_rows(values):
    center = values - jnp.mean(values, -1, keepdims=True)
    inverse = lax.rsqrt(jnp.mean(center * center, -1, keepdims=True) + EPSILON)
    return (center * inverse, inverse)


def norm_back(normed, inverse, incoming):
    return inverse * (
        incoming
        - jnp.mean(incoming, -1, keepdims=True)
        - normed * jnp.mean(incoming * normed, -1, keepdims=True)
    )


def over_heads(partial_sum):
    return lax.psum(partial_sum.astype(jnp.bfloat16), TENSOR).astype(jnp.float32)


def attend_forward(queries, key_rows, values, allowed, pattern, score_scale):
    scores = jnp.where(
        allowed,
        jnp.einsum(pattern[0], queries, key_rows, preferred_element_type=jnp.float32) * score_scale,
        NEGATIVE,
    )
    row_max = jnp.max(scores, -1, keepdims=True)
    exponent = jnp.exp(scores - row_max)
    row_total = jnp.sum(exponent, -1, keepdims=True)
    attend = (exponent / row_total).astype(jnp.bfloat16)
    context = jnp.einsum(pattern[1], attend, values, preferred_element_type=jnp.float32)
    return (context.astype(jnp.bfloat16), row_max + jnp.log(row_total))


def attend_back(queries, key_rows, values, allowed, log_total, context_grad, pattern, score_scale):
    scores = jnp.where(
        allowed,
        jnp.einsum(pattern[0], queries, key_rows, preferred_element_type=jnp.float32) * score_scale,
        NEGATIVE,
    )
    attend = jnp.exp(scores - log_total)
    attend_grad = jnp.einsum(pattern[0], context_grad, values, preferred_element_type=jnp.float32)
    score_grad = (attend * (attend_grad - jnp.sum(attend * attend_grad, -1, keepdims=True))).astype(
        jnp.bfloat16
    )
    query_grad = (
        jnp.einsum(pattern[1], score_grad, key_rows, preferred_element_type=jnp.float32)
        * score_scale
    )
    key_grad = (
        jnp.einsum(pattern[2], score_grad, queries, preferred_element_type=jnp.float32)
        * score_scale
    )
    value_grad = jnp.einsum(
        pattern[2], attend.astype(jnp.bfloat16), context_grad, preferred_element_type=jnp.float32
    )
    return (query_grad, key_grad, value_grad)


def on_device(
    frames,
    cotangent,
    prompt,
    timestep,
    clip_lengths,
    text_lengths,
    modulation_weight,
    modulation_bias,
    space_query,
    space_key,
    space_value,
    space_out,
    time_gain,
    time_query,
    time_key,
    time_value,
    time_out,
    time_gate,
    cross_gain,
    cross_query,
    prompt_key,
    prompt_value,
    cross_out,
    feed_up,
    feed_down,
):
    frame_count = frames.shape[1]
    patch_count = frames.shape[2] * frames.shape[3]
    model_width = frames.shape[4]
    token_count = frame_count * patch_count
    score_scale = 1.0 / math.sqrt(HEAD_DIM)
    residual = frames.reshape(token_count, model_width).astype(jnp.float32)
    frame_live = jnp.arange(frame_count) < clip_lengths[0]
    token_live = jnp.repeat(frame_live, patch_count)[:, None]
    prompt_rows = prompt[0]
    word_live = jnp.arange(prompt_rows.shape[0]) < text_lengths[0]
    (
        modulation_weight,
        space_query,
        space_key,
        space_value,
        space_out,
        time_query,
        time_key,
        time_value,
        time_out,
        cross_query,
        prompt_key,
        prompt_value,
        cross_out,
        feed_up,
        feed_down,
    ) = (
        lax.all_gather(modulation_weight, WIDE, axis=0, tiled=True),
        lax.all_gather(space_query, WIDE, axis=0, tiled=True),
        lax.all_gather(space_key, WIDE, axis=0, tiled=True),
        lax.all_gather(space_value, WIDE, axis=0, tiled=True),
        lax.all_gather(space_out, WIDE, axis=0, tiled=True),
        lax.all_gather(time_query, WIDE, axis=0, tiled=True),
        lax.all_gather(time_key, WIDE, axis=0, tiled=True),
        lax.all_gather(time_value, WIDE, axis=0, tiled=True),
        lax.all_gather(time_out, WIDE, axis=0, tiled=True),
        lax.all_gather(cross_query, WIDE, axis=0, tiled=True),
        lax.all_gather(prompt_key, WIDE, axis=0, tiled=True),
        lax.all_gather(prompt_value, WIDE, axis=0, tiled=True),
        lax.all_gather(cross_out, WIDE, axis=0, tiled=True),
        lax.all_gather(feed_up, WIDE, axis=0, tiled=True),
        lax.all_gather(feed_down, WIDE, axis=0, tiled=True),
    )
    head_width = space_query.shape[1]
    head_count = head_width // HEAD_DIM
    split_heads = (frame_count, patch_count, head_count, HEAD_DIM)
    half_width = model_width // 2
    frequency = jnp.exp(-math.log(10000.0) * jnp.arange(half_width, dtype=jnp.float32) / half_width)
    angles = timestep[0].astype(jnp.float32) * frequency
    condition = jax.nn.silu(jnp.concatenate([jnp.cos(angles), jnp.sin(angles)])).astype(
        jnp.bfloat16
    )
    slice_width = modulation_weight.shape[1]
    slice_start = lax.axis_index(TENSOR) * slice_width
    own_modulation = matmul(condition[None, :], modulation_weight)[0] + lax.dynamic_slice_in_dim(
        modulation_bias, slice_start, slice_width
    )
    modulation = lax.all_gather(own_modulation, TENSOR, axis=0, tiled=True)
    shift_one, scale_one, gate_one, shift_two, scale_two, gate_two = jnp.split(modulation, 6)
    normed_one, inverse_one = norm_rows(residual)
    input_one = (normed_one * (1.0 + scale_one) + shift_one).astype(jnp.bfloat16)
    query_one = matmul(input_one, space_query).astype(jnp.bfloat16).reshape(split_heads)
    key_one = matmul(input_one, space_key).astype(jnp.bfloat16).reshape(split_heads)
    value_one = matmul(input_one, space_value).astype(jnp.bfloat16).reshape(split_heads)
    key_frame, value_frame = (
        lax.all_gather(key_one, WIDE, axis=1, tiled=True),
        lax.all_gather(value_one, WIDE, axis=1, tiled=True),
    )
    space_pattern = ("fphe,fkhe->fhpk", "fhpk,fkhe->fphe", "fhpk,fphe->fkhe")
    every_patch = jnp.ones((key_frame.shape[1],), jnp.bool_)
    context_one, log_one = attend_forward(
        query_one, key_frame, value_frame, every_patch, space_pattern, score_scale
    )
    context_one = context_one.reshape(token_count, head_width)
    branch_one = over_heads(matmul_tr(context_one, space_out))
    after_one = residual + gate_one * branch_one
    normed_two, inverse_two = norm_rows(after_one)
    input_two = (normed_two * time_gain).astype(jnp.bfloat16)
    query_two = matmul(input_two, time_query).astype(jnp.bfloat16).reshape(split_heads)
    key_two = matmul(input_two, time_key).astype(jnp.bfloat16).reshape(split_heads)
    value_two = matmul(input_two, time_value).astype(jnp.bfloat16).reshape(split_heads)
    time_pattern = ("fphe,gphe->phfg", "phfg,gphe->fphe", "phfg,fphe->gphe")
    context_two, log_two = attend_forward(
        query_two, key_two, value_two, frame_live, time_pattern, score_scale
    )
    context_two = context_two.reshape(token_count, head_width)
    branch_two = over_heads(matmul_tr(context_two, time_out))
    gate_time = jnp.tanh(time_gate)
    after_two = after_one + gate_time * branch_two
    normed_three, inverse_three = norm_rows(after_two)
    input_three = (normed_three * cross_gain).astype(jnp.bfloat16)
    query_three = (
        matmul(input_three, cross_query)
        .astype(jnp.bfloat16)
        .reshape(token_count, head_count, HEAD_DIM)
    )
    word_keys = (
        matmul(prompt_rows, prompt_key).astype(jnp.bfloat16).reshape(-1, head_count, HEAD_DIM)
    )
    word_values = (
        matmul(prompt_rows, prompt_value).astype(jnp.bfloat16).reshape(-1, head_count, HEAD_DIM)
    )
    cross_pattern = ("nhe,jhe->nhj", "nhj,jhe->nhe", "nhj,nhe->jhe")
    context_three, log_three = attend_forward(
        query_three, word_keys, word_values, word_live, cross_pattern, score_scale
    )
    context_three = context_three.reshape(token_count, head_width)
    branch_three = over_heads(matmul_tr(context_three, cross_out))
    after_three = after_two + branch_three
    normed_four, inverse_four = norm_rows(after_three)
    input_four = (normed_four * (1.0 + scale_two) + shift_two).astype(jnp.bfloat16)
    pre_act = matmul(input_four, feed_up)
    hidden, gelu_pull = jax.vjp(lambda inner: jax.nn.gelu(inner, approximate=True), pre_act)
    hidden = hidden.astype(jnp.bfloat16)
    branch_four = over_heads(matmul_tr(hidden, feed_down))
    after_four = after_three + gate_two * branch_four
    output = jnp.where(token_live, after_four, 0.0).astype(jnp.bfloat16).reshape(frames.shape)
    upstream = jnp.where(
        token_live, cotangent.reshape(token_count, model_width).astype(jnp.float32), 0.0
    )
    feed_grad = (gate_two * upstream).astype(jnp.bfloat16)
    gate_two_grad = jnp.sum(upstream * branch_four, 0)
    feed_down_grad = outer_sum(feed_grad, hidden)
    pre_grad = gelu_pull(matmul(feed_grad, feed_down))[0].astype(jnp.bfloat16)
    feed_up_grad = outer_sum(input_four, pre_grad)
    input_four_grad = over_heads(matmul_tr(pre_grad, feed_up))
    shift_two_grad = jnp.sum(input_four_grad, 0)
    scale_two_grad = jnp.sum(input_four_grad * normed_four, 0)
    upstream = upstream + norm_back(normed_four, inverse_four, input_four_grad * (1.0 + scale_two))
    cross_grad = upstream.astype(jnp.bfloat16)
    cross_out_grad = outer_sum(cross_grad, context_three)
    context_grad = (
        matmul(cross_grad, cross_out)
        .astype(jnp.bfloat16)
        .reshape(token_count, head_count, HEAD_DIM)
    )
    query_grad, key_grad, value_grad = attend_back(
        query_three,
        word_keys,
        word_values,
        word_live,
        log_three,
        context_grad,
        cross_pattern,
        score_scale,
    )
    query_grad = query_grad.astype(jnp.bfloat16).reshape(token_count, head_width)
    cross_query_grad = outer_sum(input_three, query_grad)
    word_key_grad = key_grad.astype(jnp.bfloat16).reshape(-1, head_width)
    word_value_grad = value_grad.astype(jnp.bfloat16).reshape(-1, head_width)
    prompt_key_grad = outer_sum(prompt_rows, word_key_grad)
    prompt_value_grad = outer_sum(prompt_rows, word_value_grad)
    input_three_grad = over_heads(matmul_tr(query_grad, cross_query))
    cross_gain_grad = jnp.sum(input_three_grad * normed_three, 0)
    upstream = upstream + norm_back(normed_three, inverse_three, input_three_grad * cross_gain)
    time_grad = (gate_time * upstream).astype(jnp.bfloat16)
    time_gate_grad = jnp.sum(upstream * branch_two, 0) * (1.0 - gate_time * gate_time)
    time_out_grad = outer_sum(time_grad, context_two)
    context_grad = matmul(time_grad, time_out).astype(jnp.bfloat16).reshape(split_heads)
    query_grad, key_grad, value_grad = attend_back(
        query_two, key_two, value_two, frame_live, log_two, context_grad, time_pattern, score_scale
    )
    query_grad = query_grad.astype(jnp.bfloat16).reshape(token_count, head_width)
    key_grad = key_grad.astype(jnp.bfloat16).reshape(token_count, head_width)
    value_grad = value_grad.astype(jnp.bfloat16).reshape(token_count, head_width)
    time_query_grad = outer_sum(input_two, query_grad)
    time_key_grad = outer_sum(input_two, key_grad)
    time_value_grad = outer_sum(input_two, value_grad)
    input_two_grad = over_heads(
        matmul_tr(query_grad, time_query)
        + matmul_tr(key_grad, time_key)
        + matmul_tr(value_grad, time_value)
    )
    time_gain_grad = jnp.sum(input_two_grad * normed_two, 0)
    upstream = upstream + norm_back(normed_two, inverse_two, input_two_grad * time_gain)
    space_grad = (gate_one * upstream).astype(jnp.bfloat16)
    gate_one_grad = jnp.sum(upstream * branch_one, 0)
    space_out_grad = outer_sum(space_grad, context_one)
    context_grad = matmul(space_grad, space_out).astype(jnp.bfloat16).reshape(split_heads)
    key_frame, value_frame = (
        lax.all_gather(key_one, WIDE, axis=1, tiled=True),
        lax.all_gather(value_one, WIDE, axis=1, tiled=True),
    )
    query_grad, key_grad, value_grad = attend_back(
        query_one,
        key_frame,
        value_frame,
        every_patch,
        log_one,
        context_grad,
        space_pattern,
        score_scale,
    )
    key_grad, value_grad = (
        lax.psum_scatter(
            key_grad.astype(jnp.bfloat16), WIDE, scatter_dimension=1, tiled=True
        ).astype(jnp.float32),
        lax.psum_scatter(
            value_grad.astype(jnp.bfloat16), WIDE, scatter_dimension=1, tiled=True
        ).astype(jnp.float32),
    )
    query_grad = query_grad.astype(jnp.bfloat16).reshape(token_count, head_width)
    key_grad = key_grad.astype(jnp.bfloat16).reshape(token_count, head_width)
    value_grad = value_grad.astype(jnp.bfloat16).reshape(token_count, head_width)
    space_query_grad = outer_sum(input_one, query_grad)
    space_key_grad = outer_sum(input_one, key_grad)
    space_value_grad = outer_sum(input_one, value_grad)
    input_one_grad = over_heads(
        matmul_tr(query_grad, space_query)
        + matmul_tr(key_grad, space_key)
        + matmul_tr(value_grad, space_value)
    )
    shift_one_grad = jnp.sum(input_one_grad, 0)
    scale_one_grad = jnp.sum(input_one_grad * normed_one, 0)
    upstream = upstream + norm_back(normed_one, inverse_one, input_one_grad * (1.0 + scale_one))
    frames_grad = upstream.astype(jnp.bfloat16).reshape(frames.shape)
    modulation_bias_grad = jnp.concatenate(
        [
            shift_one_grad,
            scale_one_grad,
            gate_one_grad,
            shift_two_grad,
            scale_two_grad,
            gate_two_grad,
        ]
    )
    own_grad = lax.dynamic_slice_in_dim(modulation_bias_grad, slice_start, slice_width)
    modulation_weight_grad = condition.astype(jnp.float32)[:, None] * own_grad[None, :]
    (
        modulation_weight_grad,
        modulation_bias_grad,
        space_query_grad,
        space_key_grad,
        space_value_grad,
        space_out_grad,
        time_gain_grad,
        time_query_grad,
        time_key_grad,
        time_value_grad,
        time_out_grad,
        time_gate_grad,
        cross_gain_grad,
        cross_query_grad,
        prompt_key_grad,
        prompt_value_grad,
        cross_out_grad,
        feed_up_grad,
        feed_down_grad,
    ) = (
        lax.psum_scatter(
            modulation_weight_grad, (NARROW, WIDE), scatter_dimension=0, tiled=True
        ),
        lax.psum_scatter(modulation_bias_grad, (NARROW, WIDE), scatter_dimension=0, tiled=True),
        lax.psum_scatter(space_query_grad, (NARROW, WIDE), scatter_dimension=0, tiled=True),
        lax.psum_scatter(space_key_grad, (NARROW, WIDE), scatter_dimension=0, tiled=True),
        lax.psum_scatter(space_value_grad, (NARROW, WIDE), scatter_dimension=0, tiled=True),
        lax.psum_scatter(space_out_grad, (NARROW, WIDE), scatter_dimension=0, tiled=True),
        lax.psum_scatter(time_gain_grad, (NARROW, WIDE), scatter_dimension=0, tiled=True),
        lax.psum_scatter(time_query_grad, (NARROW, WIDE), scatter_dimension=0, tiled=True),
        lax.psum_scatter(time_key_grad, (NARROW, WIDE), scatter_dimension=0, tiled=True),
        lax.psum_scatter(time_value_grad, (NARROW, WIDE), scatter_dimension=0, tiled=True),
        lax.psum_scatter(time_out_grad, (NARROW, WIDE), scatter_dimension=0, tiled=True),
        lax.psum_scatter(time_gate_grad, (NARROW, WIDE), scatter_dimension=0, tiled=True),
        lax.psum_scatter(cross_gain_grad, (NARROW, WIDE), scatter_dimension=0, tiled=True),
        lax.psum_scatter(cross_query_grad, (NARROW, WIDE), scatter_dimension=0, tiled=True),
        lax.psum_scatter(prompt_key_grad, (NARROW, WIDE), scatter_dimension=0, tiled=True),
        lax.psum_scatter(prompt_value_grad, (NARROW, WIDE), scatter_dimension=0, tiled=True),
        lax.psum_scatter(cross_out_grad, (NARROW, WIDE), scatter_dimension=0, tiled=True),
        lax.psum_scatter(feed_up_grad, (NARROW, WIDE), scatter_dimension=0, tiled=True),
        lax.psum_scatter(feed_down_grad, (NARROW, WIDE), scatter_dimension=0, tiled=True),
    )
    return (
        output,
        frames_grad,
        modulation_weight_grad,
        modulation_bias_grad,
        space_query_grad,
        space_key_grad,
        space_value_grad,
        space_out_grad,
        time_gain_grad,
        time_query_grad,
        time_key_grad,
        time_value_grad,
        time_out_grad,
        time_gate_grad,
        cross_gain_grad,
        cross_query_grad,
        prompt_key_grad,
        prompt_value_grad,
        cross_out_grad,
        feed_up_grad,
        feed_down_grad,
    )


WEIGHT = P(WIDE, TENSOR)
OWNED = P((NARROW, WIDE), TENSOR)
ROWS = P((NARROW, WIDE))
PATCHES = P(NARROW, None, WIDE, None, None)
CLIP = P(NARROW)
COPIED = P()


def fits(sizes):
    return sizes[WIDE] == 2 and sizes[TENSOR] == 4 and sizes[NARROW] == 4


def solution(mesh):
    sizes = {name: mesh.shape[name] for name in mesh.axis_names}
    return jax.shard_map(
        functools.partial(fused_on_device, sizes) if fits(sizes) else on_device,
        mesh=mesh,
        in_specs=(
            (PATCHES, PATCHES, P(NARROW, None, None), CLIP, CLIP, CLIP)
            + (WEIGHT, COPIED, WEIGHT, WEIGHT, WEIGHT, WEIGHT)
            + (COPIED, WEIGHT, WEIGHT, WEIGHT, WEIGHT, COPIED)
            + (COPIED, WEIGHT, WEIGHT, WEIGHT, WEIGHT, WEIGHT, WEIGHT)
        ),
        out_specs=(
            (PATCHES, PATCHES, OWNED, ROWS, OWNED, OWNED, OWNED, OWNED)
            + (ROWS, OWNED, OWNED, OWNED, OWNED, ROWS)
            + (ROWS, OWNED, OWNED, OWNED, OWNED, OWNED, OWNED)
        ),
        check_vma=False,
    )
```

```python
import functools
import math

import jax
import jax.numpy as jnp
import numpy as np
from jax import lax
from jax.experimental import pallas as pl
from jax.experimental.pallas import tpu as pltpu
from jax.sharding import PartitionSpec as P

HEAD_DIM = 72
LANES = 128
WHOLE = 256
CHUNKS = 4
EPSILON = 1e-06
NEGATIVE = -1e30
NARROW, WIDE, TENSOR = "narrow", "wide", "tensor"
COLS = "cols"
MESH_ID = pl.DeviceIdType.MESH
F32 = jnp.float32
BF16 = jnp.bfloat16
VMEM = pltpu.VMEM
VM = pl.BlockSpec(memory_space=pltpu.VMEM)
ANY = pl.BlockSpec(memory_space=pl.ANY)
DMA = pltpu.SemaphoreType.DMA


def dot(left, right):
    return jnp.dot(left, right, preferred_element_type=F32)


def dot_tr(left, right):
    return lax.dot_general(left, right, (((1,), (1,)), ((), ())), preferred_element_type=F32)


def dot_outer(left, right):
    return lax.dot_general(left, right, (((0,), (0,)), ((), ())), preferred_element_type=F32)


def norm_tile(values):
    center = values - jnp.mean(values, -1, keepdims=True)
    inverse = lax.rsqrt(jnp.mean(center * center, -1, keepdims=True) + EPSILON)
    return center * inverse, inverse


def norm_pull(normed, inverse, incoming):
    return inverse * (
        incoming
        - jnp.mean(incoming, -1, keepdims=True)
        - normed * jnp.mean(incoming * normed, -1, keepdims=True)
    )


def softmax_tile(scores):
    exponent = jnp.exp(scores - jnp.max(scores, -1, keepdims=True))
    return exponent / jnp.sum(exponent, -1, keepdims=True)


class Place:
    def __init__(self, sizes):
        self.sizes = sizes
        self.n = lax.axis_index(NARROW)
        self.w = lax.axis_index(WIDE)
        self.t = lax.axis_index(TENSOR)

    def tensor_peer(self, step):
        return lax.rem(self.t + step, self.sizes[TENSOR])

    def over_tensor(self, step):
        return (self.n, self.w, self.tensor_peer(step))

    def sibling(self):
        return (self.n, 1 - self.w, self.t)

    def over_narrow(self, peer):
        return (peer, self.w, self.t)


def greet(partners):
    barrier = pltpu.get_barrier_semaphore()
    for partner in partners:
        pl.semaphore_signal(barrier, inc=1, device_id=partner, device_id_type=MESH_ID)
    pl.semaphore_wait(barrier, len(partners))


def send(source, target, send_sem, recv_sem, partner):
    copy = pltpu.make_async_remote_copy(
        src_ref=source,
        dst_ref=target,
        send_sem=send_sem,
        recv_sem=recv_sem,
        device_id=partner,
        device_id_type=MESH_ID,
    )
    copy.start()
    return copy


class Transfer:
    def __init__(self, slot, scatter, view, landing, born):
        self.slot, self.scatter, self.view, self.landing = slot, scatter, view, landing
        self.step, self.born = 0, born


class Line:
    def __init__(self, place, send_sems, recv_sems, lag=2):
        self.lag = lag
        self.place, self.send_sems, self.recv_sems = place, send_sems, recv_sems
        self.granules = send_sems.shape[2]
        self.open, self.slots, self.clock = [], 0, 0

    def at(self, index, body):
        pl.when(self.place.t == index)(body)

    def hop(self, move, source, target, sent, received, g, peer):
        return pltpu.make_async_remote_copy(
            src_ref=source,
            dst_ref=target,
            send_sem=self.send_sems.at[move.slot, sent, g],
            recv_sem=self.recv_sems.at[move.slot, received, g],
            device_id=(self.place.n, self.place.w, peer),
            device_id_type=MESH_ID,
        )

    def reduce_hop(self, move, owner, lands, g, peer):
        return self.hop(
            move, move.view(owner, g), move.landing(lands, g), owner, lands, g, peer
        )

    def copy_hop(self, move, owner, sent, g, peer):
        block = move.view(owner, g)
        return self.hop(move, block, block, sent, owner, g, peer)

    def start(self, scatter, view, landing=None):
        move = Transfer(self.slots, scatter, view, landing, self.clock)
        self.slots += 1
        if scatter:
            plan = {
                0: [(3, 3, 1), (2, 2, 1), (1, 1, 1)],
                1: [(0, 0, 0)],
                2: [(3, 3, 3)],
                3: [(0, 0, 2), (1, 1, 2), (2, 2, 2)],
            }
            make = self.reduce_hop
        else:
            plan = {
                0: [(0, 0, 2), (0, 1, 1)],
                1: [(1, 0, 2), (1, 1, 0)],
                2: [(2, 0, 1), (2, 1, 3)],
                3: [(3, 0, 1), (3, 1, 2)],
            }
            make = self.copy_hop
        for device, hops in plan.items():

            def begin(hops=hops):
                for owner, index, peer in hops:
                    for g in range(self.granules):
                        make(move, owner, index, g, peer).start()

            self.at(device, begin)
        self.open.append(move)
        return move

    def pending_block(self, move, index, g):
        block = move.landing(index, g) if move.scatter else move.view(index, g)
        return self.hop(move, block, block, 0, index, g, 0)

    def relay(self, move, index, g, lands, sent, peer):
        self.pending_block(move, index, g).wait_recv()
        if move.scatter:
            block = move.landing(index, g)
            block[...] = (block[...].astype(F32) + move.view(index, g)[...].astype(F32)).astype(
                BF16
            )
            self.hop(move, block, move.landing(lands, g), index, lands, g, peer).start()
        else:
            self.copy_hop(move, index, sent, g, peer).start()

    def steps(self):
        return 2 * self.granules

    def advance(self, move):
        late, g = divmod(move.step, self.granules)
        move.step += 1
        if move.scatter:
            plan = {1: ((3, 2, 0, 3), (2, 3, 0, 2)), 2: ((0, 1, 0, 0), (1, 0, 0, 1))}
        else:
            plan = {1: ((2, 0, 2, 0), (3, 0, 3, 0)), 2: ((1, 0, 2, 3), (0, 0, 3, 3))}
        for device, pair in plan.items():
            index, lands, sent, peer = pair[late]

            def body(index=index, lands=lands, sent=sent, peer=peer):
                self.relay(move, index, g, lands, sent, peer)

            self.at(device, body)

    def tick(self, count=1, lag=None):
        self.clock += 1
        lag = self.lag if lag is None else lag
        for _ in range(count):
            for move in self.open:
                if move.step < self.steps() and move.born + lag <= self.clock:
                    self.advance(move)
                    break

    def drain(self, move):
        while move.step < self.steps():
            self.advance(move)

    def finish(self, move):
        while move.step < self.steps():
            self.advance(move)
            for other in self.open:
                if other is not move and other.step < self.steps() and not other.scatter:
                    self.advance(other)
                    break
        self.open.remove(move)
        if move.scatter:
            plan = {0: (0, 1), 1: (1, 0), 2: (2, 3), 3: (3, 2)}
        else:
            plan = {0: (1, 2, 3), 1: (0,), 2: (3,), 3: (2, 1, 0)}
        for device, blocks in plan.items():

            def body(blocks=blocks):
                for index in blocks:
                    for g in range(self.granules):
                        self.pending_block(move, index, g).wait_recv()

            self.at(device, body)

    def release(self, move):
        for device in range(4):
            if move.scatter:
                sent = [d for d in range(4) if d != device]
            else:
                sent = range(4) if device in (1, 2) else range(2)

            def body(sent=sent):
                for index in sent:
                    for g in range(self.granules):
                        block = move.view(0, g)
                        self.hop(move, block, block, index, 0, g, 0).wait_send()

            self.at(device, body)


class Mover:
    def __init__(self, sems):
        self.sems, self.used, self.loads, self.saves = sems, 0, {}, []

    def go(self, source, target):
        copy = pltpu.make_async_copy(source, target, self.sems.at[self.used])
        self.used += 1
        copy.start()
        return copy

    def load(self, sources, targets):
        for source, target in zip(sources, targets):
            self.loads[id(target)] = self.go(source, target)

    def need(self, *targets):
        for target in targets:
            copy = self.loads.pop(id(target), None)
            if copy is not None:
                copy.wait()

    def keep(self, source, target):
        self.saves.append(self.go(source, target))

    def settle(self):
        wait_all(self.saves)


def stage_scratch(shapes):
    return [VMEM(shape.shape, shape.dtype) for shape in shapes] + [DMA((len(shapes) + 5,))]


def wait_all(copies):
    for copy in copies:
        copy.wait()


class Split:
    def __init__(self, place, frame_count, chunks, cols, group=1):
        parts = place.sizes[TENSOR]
        self.frame_count, self.chunks, self.cols = frame_count, chunks, cols
        self.rows = frame_count * cols
        self.quarter = self.rows // parts
        self.place, self.group = place, group
        self.frames = frame_count // parts

    def chunk(self, r):
        return pl.ds(r * self.rows * self.group, self.rows * self.group)

    def kept(self, r):
        return pl.ds(r * self.quarter, self.quarter)

    def own(self, r):
        start = r * self.rows + self.place.t * self.quarter
        return pl.ds(pl.multiple_of(start, self.quarter), self.quarter)

    def own_frames(self):
        return pl.ds(self.place.t * self.frames, self.frames)

    def rows_view(self, ref, r):
        def view(s, g):
            start = (r * self.group + g) * self.rows + s * self.quarter
            return ref.at[pl.ds(start, self.quarter)]

        return view

    def frames_view(self, ref, r):
        def view(s, g):
            return ref.at[pl.ds(s * self.frames, self.frames), r * self.group + g]

        return view

    def landing_view(self, ref):
        def view(s, g):
            return ref.at[s, g]

        return view

    def total(self, partial, landing, r):
        t = self.place.t
        beside = t + 1 - 2 * lax.rem(t, 2)
        return (
            partial[self.own(r)].astype(F32)
            + landing[t, r % self.group].astype(F32)
            + landing[beside, r % self.group].astype(F32)
        )

    def spots(self, f):
        return [
            pl.ds(pl.multiple_of(r * self.rows + f * self.cols, self.cols), self.cols)
            for r in range(self.chunks)
        ]


def neighbours(place):
    steps = range(1, place.sizes[TENSOR])
    return [place.sibling()] + [place.over_tensor(step) for step in steps]


def write_group_mask(group_mask, lengths, cols):
    shape = group_mask.shape
    row_id = lax.broadcasted_iota(jnp.int32, shape, 0)
    col_id = lax.broadcasted_iota(jnp.int32, shape, 1)
    live = col_id.astype(F32) < lengths[0:1, 0:1] * cols
    same = lax.rem(row_id, cols) == lax.rem(col_id, cols)
    group_mask[...] = jnp.where(jnp.logical_and(same, live), 1.0, 0.0)


def live_words(lengths):
    return lax.broadcasted_iota(jnp.int32, (1, LANES), 1).astype(F32) < lengths[1:2]


def pad_heads(turned):
    rows, columns = turned.shape
    filler = jnp.zeros((LANES - HEAD_DIM, columns), F32)
    pieces = []
    for start in range(0, rows, HEAD_DIM):
        pieces += [turned[start : start + HEAD_DIM].astype(F32), filler]
    return jnp.concatenate(pieces, 0).T.astype(BF16)


def group_partners(place):
    wide, tensor = place.sizes[WIDE], place.sizes[TENSOR]
    return [
        (place.n, lax.rem(place.w + dw, wide), lax.rem(place.t + dt, tensor))
        for dw in range(wide)
        for dt in range(tensor)
        if dw or dt
    ]


def forward_kernel(
    sizes,
    frames,
    condition,
    params,
    lengths,
    spread,
    prompt,
    *refs,
):
    weights, feed, modulation_weight = refs[:12], refs[12:14], refs[14]
    kept_out, full_out, feed_out, vectors_out = refs[15:34], refs[34], refs[35:37], refs[37]
    (
        h1, q1, side, o1, h2, q2, o2, h3, q3, kv3, o3, h4,
        a1_own, a2_own, x3_own, n2_own, n3_own, n4_own, inverses,
    ) = kept_refs = refs[38:57]
    (
        save_sems, turned, turned_prompt, full, full_prompt, feed_full, modulation_full,
        mine, shared, flat, vectors,
        wide_context, partial, landing, residual, group_mask,
        local_sems, side_send, side_recv, share_send, share_recv, kv_send, kv_recv,
        ring_send, ring_recv,
    ) = refs[57:]
    mover = Mover(save_sems)

    def keep(*sources):
        for source in sources:
            for kept_ref, out in zip(kept_refs, kept_out):
                if kept_ref is source:
                    mover.keep(source, out)

    place = Place(sizes)
    frame_count, chunks, cols, width = frames.shape
    split = Split(place, frame_count, chunks, cols)
    rows, half = split.rows, split.quarter
    heads = spread.shape[1] // LANES
    scale = 1.0 / math.sqrt(HEAD_DIM)
    chain = Line(place, ring_send, ring_recv)
    order = (0, 1, 2, 3, 4, 5, 6, 7, 8, 9, 10, 11)
    loads = {}

    def begin(i):
        target = turned.at[i] if i < 10 else turned_prompt.at[i - 10]
        loads[i] = pltpu.make_async_copy(weights[i], target, local_sems.at[i])
        loads[i].start()

    for i in order[:4]:
        begin(i)
    modulation_load = pltpu.make_async_copy(modulation_weight, modulation_full, local_sems.at[14])
    modulation_load.start()
    for i in order[4:]:
        begin(i)
    feed_spots, feed_loads = [], []
    for i in range(2):
        feed_half = feed[i].shape[0]
        feed_spots.append(pl.ds(pl.multiple_of(place.w * feed_half, feed_half), feed_half))
        feed_loads.append(
            pltpu.make_async_copy(
                feed[i], feed_full.at[i, feed_spots[i]], local_sems.at[12 + i]
            )
        )
        feed_loads[i].start()
    partners = group_partners(place)
    greet(partners)
    modulation_load.wait()
    slice_width = modulation_weight.shape[1]
    mine[...] = jnp.zeros_like(mine)
    asked = jnp.broadcast_to(condition[...], (16, condition.shape[1])).astype(BF16)
    mine[:, 0:slice_width] = dot(asked, modulation_full[...])[0:8]
    shifted = pltpu.roll(mine[...], slice_width % LANES, 1)
    mine[...] = jnp.where(lax.rem(place.t, 2) == 1, shifted, mine[...])
    slot = place.w * sizes[TENSOR] + place.t
    shared[slot] = mine[0:1]
    share_copies = [
        send(shared.at[slot], shared.at[slot], share_send.at[i], share_recv.at[i], partner)
        for i, partner in enumerate(partners)
    ]
    pending = {}

    def turn(*which):
        for i in which:
            loads[i].wait()
            half_rows = weights[i].shape[1]
            spot = pl.ds(pl.multiple_of(place.w * half_rows, half_rows), half_rows)
            if i < 10:
                full[i, spot] = pad_heads(turned[i])
                target = full.at[i, spot]
            else:
                full_prompt[i - 10, spot] = turned_prompt[i - 10].T
                target = full_prompt.at[i - 10, spot]
            pending[i] = [
                send(target, target, side_send.at[i], side_recv.at[i], place.sibling())
            ]

    def ready(*which):
        for i in which:
            wait_all(pending.pop(i))

    turn(0, 1, 2)
    write_group_mask(group_mask, lengths, cols)
    wait_all(share_copies)
    flat[...] = params[:, 0 : flat.shape[1]]
    for slot in range(shared.shape[0]):
        start = slot % sizes[TENSOR] * slice_width // LANES * LANES
        flat[:, start : start + shared.shape[2]] += shared[slot]
    for j in range(6):
        row = flat[:, j * width : (j + 1) * width]
        vectors[j : j + 1] = 1.0 + row if j in (1, 4) else row
    for j in range(6, 9):
        row = params[:, j * width : (j + 1) * width]
        vectors[j : j + 1] = jnp.tanh(row) if j == 7 else row
    mover.keep(vectors, vectors_out)

    @pl.loop(0, frame_count)
    def _(f):
        for r in range(chunks):
            normed, _ = norm_tile(frames[f, r].astype(F32))
            h1[pl.ds(pl.multiple_of(r * rows + f * cols, cols), cols)] = (
                normed * vectors[1:2] + vectors[0:1]
            ).astype(BF16)

    keep(h1)

    def project(source, spot, weight, out, index):
        out[index, spot] = dot(source[spot], full[weight]).astype(BF16)

    ready(0, 1, 2)

    @pl.loop(0, 3)
    def _(i):
        for r in range(0, chunks * rows, WHOLE):
            project(h1, pl.ds(r, WHOLE), i, q1, i)

    kv_copies = [
        send(q1.at[1 + j], side.at[j], kv_send.at[j], kv_recv.at[j], place.sibling())
        for j in range(2)
    ]
    turn(3)
    wait_all(kv_copies)
    keep(q1, side)

    @pl.loop(0, frame_count)
    def _(f):
        spots = split.spots(f)
        queries = jnp.concatenate([q1[0, spot] for spot in spots], 0)
        keys = jnp.concatenate(
            [q1[1, spot] for spot in spots] + [side[0, spot] for spot in spots], 0
        )
        values = jnp.concatenate(
            [q1[2, spot] for spot in spots] + [side[1, spot] for spot in spots], 0
        )
        for h in range(heads):
            lanes = slice(h * LANES, (h + 1) * LANES)
            attend = softmax_tile(dot_tr(queries[:, lanes], keys[:, lanes]) * scale)
            context = dot(attend.astype(BF16), values[:, lanes]).astype(BF16)
            for r in range(chunks):
                wide_context[spots[r], lanes] = context[r * cols : (r + 1) * cols]

    sent = [None] * chunks

    def emit(r, out, weight, stage):
        spot = split.chunk(r)
        if sent[r] is not None:
            chain.release(sent[r])
        partial[spot] = dot_tr(wide_context[spot], full[weight]).astype(BF16)
        sent[r] = chain.start(
            True, split.rows_view(partial, r), split.landing_view(landing.at[stage * chunks + r])
        )
        out[spot] = dot_tr(wide_context[spot], spread[...]).astype(BF16)
        return sent[r]

    def branch(r, stage):
        return split.total(partial, landing.at[stage * chunks + r], r)

    def settle(scatters, body, target):
        gathers = []
        for r in range(chunks):
            chain.finish(scatters[r])
            body(r)
            gathers.append(chain.start(False, split.rows_view(target, r)))
            chain.tick(4, 3)
        return gathers

    ready(3)
    scatters = []
    for r in range(chunks):
        scatters.append(emit(r, o1, 3, 0))
        chain.tick(0)

    keep(o1)
    turn(4, 5, 6, 7)
    chain.tick(4)
    turn(10, 11)
    chain.tick(4)
    ready(10, 11)
    kv3[...] = jnp.zeros_like(kv3)
    for j in range(2):
        narrow = dot(prompt[...], full_prompt[j]).astype(BF16)
        kv3[j, 0 : prompt.shape[0]] = dot(narrow, spread[...]).astype(BF16)
        chain.tick(4)
    keep(kv3)

    def body_one(r):
        kept = split.kept(r)
        branch_one = branch(r, 0)
        a1_own[kept] = branch_one
        x_own = frames[split.own_frames(), r].reshape(half, width)
        after = x_own.astype(F32) + vectors[2:3] * branch_one
        normed, inverse = norm_tile(after)
        residual[kept] = after
        n2_own[kept] = normed
        inverses[0, kept] = jnp.broadcast_to(inverse, (half, LANES))
        h2[split.own(r)] = (normed * vectors[6:7]).astype(BF16)

    gathers = settle(scatters, body_one, h2)
    released = list(gathers)
    keep(a1_own, n2_own)
    turn(8, 9)
    feed_copies = []
    for i in range(2):
        feed_loads[i].wait()
        target = feed_full.at[i, feed_spots[i]]
        feed_copies.append(
            send(target, target, side_send.at[12 + i], side_recv.at[12 + i], place.sibling())
        )
    ready(4, 5, 6, 7)
    scatters = []
    for r in range(chunks):
        chain.finish(gathers[r])
        spot = split.chunk(r)
        for i in range(3):
            project(h2, spot, 4 + i, q2, i)
            chain.tick()
        for h in range(heads):
            lanes = slice(h * LANES, (h + 1) * LANES)
            scores = dot_tr(q2[0, spot, lanes], q2[1, spot, lanes]) * scale
            attend = softmax_tile(jnp.where(group_mask[...] > 0.5, scores, NEGATIVE))
            wide_context[spot, lanes] = dot(attend.astype(BF16), q2[2, spot, lanes]).astype(BF16)
        chain.tick()
        scatters.append(emit(r, o2, 7, 1))

    def body_two(r):
        kept = split.kept(r)
        branch_two = branch(r, 1)
        a2_own[kept] = branch_two
        after = residual[kept] + vectors[7:8] * branch_two
        normed, inverse = norm_tile(after)
        residual[kept] = after
        n3_own[kept] = normed
        inverses[1, kept] = jnp.broadcast_to(inverse, (half, LANES))
        h3[split.own(r)] = (normed * vectors[8:9]).astype(BF16)

    gathers = settle(scatters, body_two, h3)
    released += gathers
    keep(h2, q2, o2, a2_own, n3_own)
    ready(8, 9)
    mover.keep(full, full_out)
    scatters = []
    for r in range(chunks):
        chain.finish(gathers[r])
        spot = split.chunk(r)
        q3[spot] = dot(h3[spot], full[8]).astype(BF16)
        chain.tick()
        for h in range(heads):
            lanes = slice(h * LANES, (h + 1) * LANES)
            scores = dot_tr(q3[spot, lanes], kv3[0, :, lanes]) * scale
            attend = softmax_tile(jnp.where(live_words(lengths), scores, NEGATIVE))
            wide_context[spot, lanes] = dot(attend.astype(BF16), kv3[1, :, lanes]).astype(BF16)
        chain.tick()
        scatters.append(emit(r, o3, 9, 2))

    def body_three(r):
        kept = split.kept(r)
        after = residual[kept] + branch(r, 2)
        normed, inverse = norm_tile(after)
        x3_own[kept] = after
        n4_own[kept] = normed
        inverses[2, kept] = jnp.broadcast_to(inverse, (half, LANES))
        h4[split.own(r)] = (normed * vectors[4:5] + vectors[3:4]).astype(BF16)

    gathers = settle(scatters, body_three, h4)
    keep(h3, q3, o3, x3_own, n4_own, inverses)
    wait_all(feed_copies)
    for i in range(2):
        mover.keep(feed_full.at[i], feed_out[i])
    for move in gathers:
        chain.finish(move)
    keep(h4)
    for move in sent + released + gathers:
        chain.release(move)
    mover.settle()


def forward_call(
    sizes, frames, condition, params, lengths, spread, prompt, weights, feed,
    modulation_weight,
):
    frame_count, chunks, cols, width = frames.shape
    rows = frame_count * cols
    tokens = rows * chunks
    head_width, padded = spread.shape
    half = rows // sizes[TENSOR]
    kept = half * chunks
    full_rows = weights[0].shape[1] * sizes[WIDE]
    prompt_width = weights[10].shape[1] * sizes[WIDE]
    slice_width = modulation_weight.shape[1]
    group = sizes[WIDE] * sizes[TENSOR]
    placed = slice_width + slice_width % LANES
    moves = 6 * chunks
    s = jax.ShapeDtypeStruct
    wide_act, heads_act = s((tokens, width), BF16), s((tokens, head_width), BF16)
    triple, own = s((3, tokens, padded), BF16), s((kept, width), F32)
    outs = [
        wide_act, triple, s((2, tokens, padded), BF16), heads_act,
        wide_act, triple, heads_act,
        wide_act, s((tokens, padded), BF16), s((2, LANES, padded), BF16), heads_act,
        wide_act, own, own, own, own, own, own, s((3, kept, LANES), F32),
    ]
    return pl.pallas_call(
        functools.partial(forward_kernel, sizes),
        name="forward",
        out_shape=outs
        + [s((10, full_rows, padded), BF16)]
        + [s((ref.shape[0] * sizes[WIDE], ref.shape[1]), BF16) for ref in feed]
        + [s((16, width), F32)],
        in_specs=[VM] * 6 + [ANY] * 15,
        out_specs=[ANY] * (len(outs) + 4),
        scratch_shapes=stage_scratch(outs)
        + [
            VMEM((10,) + weights[0].shape, BF16), VMEM((2,) + weights[10].shape, BF16),
            VMEM((10, full_rows, padded), BF16),
            VMEM((2, prompt_width, head_width), BF16),
            VMEM((2, feed[0].shape[0] * sizes[WIDE], feed[0].shape[1]), BF16),
            VMEM(modulation_weight.shape, BF16),
            VMEM((8, placed), F32), VMEM((group, 1, placed), F32),
            VMEM((1, 6 * width), F32), VMEM((16, width), F32),
            VMEM((tokens, padded), BF16),
            VMEM((tokens, width), BF16),
            VMEM((3 * chunks, 4, 1, half, width), BF16),
            VMEM((kept, width), F32),
            VMEM((rows, rows), F32),
            DMA((15,)), DMA((14,)), DMA((14,)), DMA((group - 1,)), DMA((group - 1,)),
            DMA((2,)), DMA((2,)),
            DMA((moves, 4, 1)), DMA((moves, 4, 1)),
        ],
        compiler_params=pltpu.CompilerParams(
            collective_id=1, has_side_effects=True, vmem_limit_bytes=60 << 20
        ),
    )(
        frames, condition, params, lengths, spread, prompt, *weights, *feed,
        modulation_weight,
    )


def prepare(frames, timestep, head_width):
    width = frames.shape[4]
    half_width = width // 2
    frequency = jnp.exp(-math.log(10000.0) * jnp.arange(half_width, dtype=F32) / half_width)
    angles = timestep.astype(F32)[:, None] * frequency[None]
    condition = jax.nn.silu(jnp.concatenate([jnp.cos(angles), jnp.sin(angles)], 1)).astype(BF16)
    heads = head_width // HEAD_DIM
    padded = np.arange(heads * LANES)
    source = np.where(
        padded % LANES < HEAD_DIM, padded // LANES * HEAD_DIM + padded % LANES, -1
    )
    spread = (np.arange(head_width)[:, None] == source[None]).astype(np.float32)
    return condition, jnp.asarray(spread, BF16)


def over_columns(width, tile, body):
    whole = width // tile

    @pl.loop(0, whole)
    def _(j):
        body(pl.ds(pl.multiple_of(j * tile, tile), tile))

    if width % tile:
        body(pl.ds(whole * tile, width % tile))


GELU_C = math.sqrt(2.0 / math.pi)


def live_rows(lengths, split):
    first = split.place.t * split.frames
    pieces = []
    for f in range(split.frames):
        live = (first + f).astype(F32) < lengths[0:1, 0:1]
        pieces.append(jnp.broadcast_to(jnp.where(live, 1.0, 0.0), (split.cols, 1)))
    return jnp.concatenate(pieces, 0)


def own_cotangent(cotangent, lengths, split, r):
    width = cotangent.shape[3]
    rows = cotangent[split.own_frames(), r].reshape(split.quarter, width)
    return rows.astype(F32) * live_rows(lengths, split)


def mlp_kernel(
    sizes,
    vectors, lengths, *refs,
):
    ins, outs = refs[:6], refs[6:12]
    h4, cotangent, n4_own, inverses, up, down = loaded = refs[12:18]
    branch_part, e3, g3_own, up_grad, down_grad, sums = made = refs[18:24]
    (
        move_sems, e4, hidden, pre_grad, partial, landing, ring_send, ring_recv,
    ) = refs[24:]
    place = Place(sizes)
    frame_count, chunks, cols, width = cotangent.shape
    group = landing.shape[2]
    split = Split(place, frame_count, chunks, cols, group)
    line = Line(place, ring_send, ring_recv)
    mover = Mover(move_sems)
    mover.load(
        [ins[i] for i in (1, 4, 5, 0, 2, 3)], [loaded[i] for i in (1, 4, 5, 0, 2, 3)]
    )
    greet(neighbours(place))
    mover.need(cotangent)

    @pl.loop(0, frame_count)
    def _(f):
        live = jnp.where(f.astype(F32) < lengths[0:1, 0:1], 1.0, 0.0)
        for r, spot in enumerate(split.spots(f)):
            e4[spot] = (
                vectors[5:6] * (cotangent[f, r].astype(F32) * live)
            ).astype(BF16)

    sums[...] = jnp.zeros_like(sums)
    mover.need(up, down, h4)
    scatters = []
    for r in range(chunks // group):
        spot = split.chunk(r)

        def act(lanes):
            pre = dot(h4[spot], up[:, lanes])
            grad = dot(e4[spot], down[:, lanes])
            inner = jnp.tanh(GELU_C * (pre + 0.044715 * pre * pre * pre))
            gate = 0.5 * (1.0 + inner)
            hidden[spot, lanes] = (pre * gate).astype(BF16)
            slope = gate + 0.5 * pre * (1.0 - inner * inner) * (
                GELU_C * (1.0 + 3.0 * 0.044715 * pre * pre)
            )
            pre_grad[spot, lanes] = (grad * slope).astype(BF16)

        over_columns(up.shape[1], 256, act)
        line.tick(1, 1)
        partial[spot] = dot_tr(pre_grad[spot], up[...]).astype(BF16)
        line.tick(1, 1)
        scatters.append(
            line.start(True, split.rows_view(partial, r), split.landing_view(landing.at[r]))
        )

    for r in range(chunks // group):
        spot = split.chunk(r)
        branch_part[spot] = dot_tr(hidden[spot], down[...]).astype(BF16)
        line.tick(1, 1)

    mover.keep(branch_part, outs[0])

    def down_tile(lanes):
        down_grad[:, lanes] = dot_outer(e4[...], hidden[:, lanes]).astype(BF16)

    def up_tile(lanes):
        up_grad[:, lanes] = dot_outer(h4[...], pre_grad[:, lanes]).astype(BF16)

    mover.need(n4_own, inverses)
    gathers = []
    for r in range(chunks // group):
        line.finish(scatters[r])
        for c in range(r * group, (r + 1) * group):
            kept = split.kept(c)
            grad = split.total(partial, landing.at[r], c)
            normed = n4_own[kept]
            sums[0:1] += jnp.sum(grad, 0, keepdims=True)
            sums[1:2] += jnp.sum(grad * normed, 0, keepdims=True)
            upstream = own_cotangent(cotangent, lengths, split, c) + norm_pull(
                normed, inverses[2, kept][:, 0:1], grad * vectors[4:5]
            )
            g3_own[kept] = upstream
            e3[split.own(c)] = upstream.astype(BF16)
        gathers.append(line.start(False, split.rows_view(e3, r)))
        if r == 0:
            over_columns(up.shape[1], 256, down_tile)
            line.tick(2, 1)

    mover.keep(g3_own, outs[2])
    mover.keep(sums, outs[5])
    mover.keep(down_grad, outs[4])
    over_columns(up.shape[1], 256, up_tile)
    mover.keep(up_grad, outs[3])
    for move in gathers:
        line.finish(move)
    mover.keep(e3, outs[1])
    for move in scatters + gathers:
        line.release(move)
    mover.settle()


def mlp_call(sizes, vectors, lengths, acts):
    frame_count, chunks, cols, width = acts[1].shape
    rows = frame_count * cols
    tokens = rows * chunks
    quarter = rows // sizes[TENSOR]
    hidden = acts[4].shape[1]
    s = jax.ShapeDtypeStruct
    group = max(1, chunks // 2)
    moves = 2 * chunks // group
    outs = [
        s((tokens, width), BF16), s((tokens, width), BF16), s((quarter * chunks, width), F32),
        s((width, hidden), BF16), s((width, hidden), BF16), s((8, width), F32),
    ]
    return pl.pallas_call(
        functools.partial(mlp_kernel, sizes),
        name="mlp",
        out_shape=outs,
        in_specs=[VM] * 2 + [ANY] * len(acts),
        out_specs=[ANY] * len(outs),
        scratch_shapes=stage_scratch(list(acts) + outs)
        + [
            VMEM((tokens, width), BF16), VMEM((tokens, hidden), BF16),
            VMEM((tokens, hidden), BF16),
            VMEM((tokens, width), BF16),
            VMEM((chunks // group, 4, group, quarter, width), BF16),
            DMA((moves, 4, group)), DMA((moves, 4, group)),
        ],
        compiler_params=pltpu.CompilerParams(
            collective_id=2, has_side_effects=True, vmem_limit_bytes=60 << 20
        ),
    )(vectors, lengths, *acts)


class Reducer:
    def __init__(self, place, source, mine, merged, received, sems):
        self.place, self.source = place, source
        self.mine, self.merged, self.received = mine, merged, received
        self.local, self.side_send, self.side_recv, self.far_send, self.far_recv = sems
        self.clips = place.sizes[NARROW]
        self.block = mine.shape[1]

    def rows(self, clip, core):
        start = (clip * self.place.sizes[WIDE] + core) * self.block
        return pl.ds(pl.multiple_of(start, self.block), self.block)

    def split(self):
        self.copies = []
        for clip in range(self.clips):
            local = pltpu.make_async_copy(
                self.source.at[self.rows(clip, self.place.w)],
                self.mine.at[clip],
                self.local.at[clip],
            )
            local.start()
            self.copies += [
                local,
                send(
                    self.source.at[self.rows(clip, 1 - self.place.w)],
                    self.merged.at[clip],
                    self.side_send.at[clip],
                    self.side_recv.at[clip],
                    self.place.sibling(),
                ),
            ]

    def spread(self):
        wait_all(self.copies)
        self.copies = []

        @pl.loop(0, self.clips)
        def _(clip):
            self.merged[clip] = (
                self.merged[clip].astype(F32) + self.mine[clip].astype(F32)
            ).astype(BF16)

        for step in (3, 1, 2) if self.clips == 4 else range(1, self.clips):
            peer = lax.rem(self.place.n + step, self.clips)
            self.copies.append(
                send(
                    self.merged.at[peer],
                    self.received.at[step - 1],
                    self.far_send.at[step - 1],
                    self.far_recv.at[step - 1],
                    self.place.over_narrow(peer),
                )
            )

    def finish(self, out):
        wait_all(self.copies)
        total = self.merged[self.place.n].astype(F32)
        for step in range(self.clips - 1):
            total = total + self.received[step].astype(F32)
        out[...] = total


def reducer_scratch(sizes, jobs, block, width):
    clips = sizes[NARROW]
    return [
        VMEM((jobs, clips, block, width), BF16),
        VMEM((jobs, clips, block, width), BF16),
        VMEM((jobs, clips - 1, block, width), BF16),
        DMA((jobs, clips)), DMA((jobs, clips)), DMA((jobs, clips)),
        DMA((jobs, clips - 1)), DMA((jobs, clips - 1)),
    ]


def reducers(place, sources, scratch):
    mine, merged, received, *sems = scratch
    return [
        Reducer(
            place, source, mine.at[i], merged.at[i], received.at[i], [sem.at[i] for sem in sems]
        )
        for i, source in enumerate(sources)
    ]


def all_partners(place):
    sizes = place.sizes
    return (
        [place.sibling()]
        + [place.over_tensor(step) for step in range(1, sizes[TENSOR])]
        + [
            place.over_narrow(lax.rem(place.n + step, sizes[NARROW]))
            for step in range(1, sizes[NARROW])
        ]
    )


def attention_pull(queries, keys, values, context_grad, mask, scale):
    scores = dot_tr(queries, keys) * scale
    if mask is not None:
        scores = jnp.where(mask, scores, NEGATIVE)
    attend = softmax_tile(scores)
    attend_grad = dot_tr(context_grad, values)
    score_grad = (
        attend * (attend_grad - jnp.sum(attend * attend_grad, -1, keepdims=True))
    ).astype(BF16)
    return (
        dot(score_grad, keys) * scale,
        dot_outer(score_grad, queries) * scale,
        dot_outer(attend.astype(BF16), context_grad),
    )


def back_kernel(
    sizes,
    vectors, lengths, spread, *refs,
):
    ins, full_in, gradients = refs[:13], refs[13], refs[14:16]
    outs = refs[16:24]
    (
        e3, g3_own, n3_own, n2_own, inverses, a2_own, h3, q3, kv3, o3, h2, q2, o2,
    ) = loaded = refs[24:37]
    g1_own, e1, time_grads, word_grads, up_out, down_out, cross_out, sums = refs[37:45]
    (
        move_sems, cross_full, time_full, wide_grad, wide_parts, narrow_parts, word_sums,
        word_side, e2, partial, landing, group_mask, cross_grads,
        full_sems, word_send, word_recv, ring_send, ring_recv,
    ) = refs[45:63]
    place = Place(sizes)
    tokens, width = e3.shape
    rows, cols = group_mask.shape[0], sizes[COLS]
    chunks = tokens // rows
    split = Split(place, rows // cols, chunks, cols)
    heads = spread.shape[1] // LANES
    scale = 1.0 / math.sqrt(HEAD_DIM)
    line = Line(place, ring_send, ring_recv, 3)
    mover = Mover(move_sems)
    weights = []
    for i, (source, target) in enumerate(
        ((full_in.at[pl.ds(8, 2)], cross_full), (full_in.at[pl.ds(4, 4)], time_full))
    ):
        weights.append(pltpu.make_async_copy(source, target, full_sems.at[i]))
    weights[0].start()
    first = (0, 7, 8)
    order = first + tuple(i for i in range(13) if i not in first)
    mover.load([ins[i] for i in order], [loaded[i] for i in order])
    weights[1].start()
    greet(all_partners(place))
    feed = reducers(place, gradients, refs[63:71])
    cross = reducers(place, [cross_grads.at[0], cross_grads.at[1]], refs[71:79])
    for job in feed:
        job.split()
    write_group_mask(group_mask, lengths, cols)
    sums[...] = jnp.zeros_like(sums)
    word_sums[...] = jnp.zeros_like(word_sums)

    def context_grad(source, spot, weight):
        wide_grad[spot] = dot(source[spot], weight).astype(BF16)

    def scatter(r, stage):
        return line.start(
            True,
            split.rows_view(partial, r),
            split.landing_view(landing.at[stage * chunks + r]),
        )

    weights[0].wait()
    mover.need(e3, q3, kv3)
    scatters = []
    for r in range(chunks):
        spot = split.chunk(r)
        context_grad(e3, spot, cross_full[1])
        line.tick()
        for h in range(heads):
            lanes = slice(h * LANES, (h + 1) * LANES)
            query_grad, key_grad, value_grad = attention_pull(
                q3[spot, lanes], kv3[0, :, lanes], kv3[1, :, lanes], wide_grad[spot, lanes],
                live_words(lengths), scale,
            )
            wide_parts[0, spot, lanes] = query_grad.astype(BF16)
            word_sums[0, :, lanes] += key_grad
            word_sums[1, :, lanes] += value_grad
        line.tick()
        partial[spot] = dot_tr(wide_parts[0, spot], cross_full[0]).astype(BF16)
        scatters.append(scatter(r, 0))
        narrow_parts[0, spot] = dot_tr(wide_parts[0, spot], spread[...]).astype(BF16)
    word_copy = send(word_sums, word_side, word_send, word_recv, place.sibling())
    mover.need(o3, h3)
    cross_grads[0] = dot_outer(e3[...], o3[...]).astype(BF16)
    line.tick(2)
    cross_grads[1] = dot_outer(h3[...], narrow_parts[0]).astype(BF16)
    line.tick(2)
    for job in cross:
        job.split()
    mover.need(*loaded)
    gathers = []
    for r in range(chunks):
        kept = split.kept(r)
        line.finish(scatters[r])
        grad = split.total(partial, landing.at[r], r)
        normed = n3_own[kept]
        sums[0:1] += jnp.sum(grad * normed, 0, keepdims=True)
        upstream = g3_own[kept] + norm_pull(
            normed, inverses[1, kept][:, 0:1], grad * vectors[8:9]
        )
        g1_own[kept] = upstream
        sums[1:2] += jnp.sum(upstream * a2_own[kept], 0, keepdims=True)
        e2[split.own(r)] = (vectors[7:8] * upstream).astype(BF16)
        gathers.append(line.start(False, split.rows_view(e2, r)))
        line.tick(4, 3)
    for job in feed + cross:
        job.spread()
    word_copy.wait()
    for j in range(2):
        word_grads[j] = dot_tr(
            (word_sums[j] + word_side[j]).astype(BF16), spread[...]
        ).astype(BF16)
    mover.keep(word_grads, outs[3])
    sent = scatters + gathers

    weights[1].wait()
    former, scatters = scatters, []
    for r in range(chunks):
        spot = split.chunk(r)
        line.finish(gathers[r])
        context_grad(e2, spot, time_full[3])
        line.tick()
        for h in range(heads):
            lanes = slice(h * LANES, (h + 1) * LANES)
            parts = attention_pull(
                q2[0, spot, lanes], q2[1, spot, lanes], q2[2, spot, lanes],
                wide_grad[spot, lanes], group_mask[...] > 0.5, scale,
            )
            for i in range(3):
                wide_parts[i, spot, lanes] = parts[i].astype(BF16)
            if h % 2:
                line.tick()
        total = None
        for i in range(3):
            part = dot_tr(wide_parts[i, spot], time_full[i])
            total = part if total is None else total + part
        line.tick()
        line.release(former[r])
        sent.remove(former[r])
        partial[spot] = total.astype(BF16)
        scatters.append(scatter(r, 1))
        for i in range(3):
            narrow_parts[i, spot] = dot_tr(wide_parts[i, spot], spread[...]).astype(BF16)
    sent += scatters
    time_grads[0] = dot_outer(e2[...], o2[...]).astype(BF16)
    line.tick(2)
    for i in range(3):
        time_grads[1 + i] = dot_outer(h2[...], narrow_parts[i]).astype(BF16)
        line.tick(1)
    mover.keep(time_grads, outs[2])

    gathers = []
    for r in range(chunks):
        kept = split.kept(r)
        line.finish(scatters[r])
        grad = split.total(partial, landing.at[chunks + r], r)
        normed = n2_own[kept]
        sums[2:3] += jnp.sum(grad * normed, 0, keepdims=True)
        upstream = g1_own[kept] + norm_pull(
            normed, inverses[0, kept][:, 0:1], grad * vectors[6:7]
        )
        g1_own[kept] = upstream
        e1[split.own(r)] = (vectors[2:3] * upstream).astype(BF16)
        gathers.append(line.start(False, split.rows_view(e1, r)))
        line.tick(4, 3)
    mover.keep(g1_own, outs[0])
    mover.keep(sums, outs[7])
    feed[0].finish(up_out)
    mover.keep(up_out, outs[4])
    line.drain(gathers[0])
    feed[1].finish(down_out)
    mover.keep(down_out, outs[5])
    for r in range(1, chunks):
        line.drain(gathers[r])
    cross[0].finish(cross_out.at[0])
    cross[1].finish(cross_out.at[1])
    mover.keep(cross_out, outs[6])
    for move in gathers:
        line.finish(move)
    mover.keep(e1, outs[1])
    for move in sent + gathers:
        line.release(move)
    mover.settle()


def back_call(sizes, cols, small, acts, full, gradients):
    spread = small[2]
    tokens, width = acts[0].shape
    rows = tokens // CHUNKS
    chunks = tokens // rows
    quarter = rows // sizes[TENSOR]
    head_width, padded = spread.shape
    full_rows = full.shape[1]
    hidden = gradients[0].shape[1]
    block = width // (sizes[NARROW] * sizes[WIDE])
    s = jax.ShapeDtypeStruct
    moves = 4 * chunks
    outs = [
        s((quarter * chunks, width), F32), s((tokens, width), BF16),
        s((4, width, head_width), BF16), s((2, LANES, head_width), BF16),
        s((block, hidden), F32), s((block, hidden), F32), s((2, block, head_width), F32),
        s((8, width), F32),
    ]
    return pl.pallas_call(
        functools.partial(back_kernel, {**sizes, COLS: cols}),
        name="back",
        out_shape=outs,
        in_specs=[VM] * 3 + [ANY] * (len(acts) + 3),
        out_specs=[ANY] * len(outs),
        scratch_shapes=stage_scratch(list(acts) + outs)
        + [
            VMEM((2, full_rows, padded), BF16), VMEM((4, full_rows, padded), BF16),
            VMEM((tokens, padded), BF16),
            VMEM((3, tokens, padded), BF16),
            VMEM((3, tokens, head_width), BF16),
            VMEM((2, LANES, padded), F32), VMEM((2, LANES, padded), F32),
            VMEM((tokens, width), BF16),
            VMEM((tokens, width), BF16),
            VMEM((2 * chunks, 4, 1, quarter, width), BF16),
            VMEM((rows, rows), F32),
            VMEM((2, width, head_width), BF16),
            DMA((2,)), DMA(()), DMA(()),
            DMA((moves, 4, 1)), DMA((moves, 4, 1)),
        ]
        + reducer_scratch(sizes, 2, block, hidden)
        + reducer_scratch(sizes, 2, block, head_width),
        compiler_params=pltpu.CompilerParams(
            collective_id=3, has_side_effects=True, vmem_limit_bytes=60 << 20
        ),
    )(*small, *acts, full, *gradients)


def space_kernel(
    sizes,
    vectors, spread, lengths, mlp_sums, back_sums, condition, *refs,
):
    ins, full_in, gradients, outs = refs[:13], refs[13], refs[14], refs[15:23]
    (
        e1, g1_own, frames, a1_own, h1, q1, side, o1, prompt, word_grads, branch_part, x3_own,
        cotangent,
    ) = loaded = refs[23:36]
    frames_grad, output, early_out, space_out, prompt_out, merged, conditions, grand = refs[36:44]
    (
        move_sems, query_full, out_full, wide_grad, wide_parts, narrow_parts, key_sums, side_out,
        side_in, space_grads, words, word_parts, partial, landing, tally, tally_side, tally_peers,
        full_sems, key_send, key_recv, word_send, word_recv,
        tally_send, tally_recv, ring_send, ring_recv,
    ) = refs[44:70]
    early_scratch, late_scratch = refs[70:78], refs[78:86]
    place = Place(sizes)
    clips = sizes[NARROW]
    frame_count, chunks, cols, width = frames.shape
    split = Split(place, frame_count, chunks, cols)
    quarter = split.quarter
    heads = spread.shape[1] // LANES
    scale = 1.0 / math.sqrt(HEAD_DIM)
    line = Line(place, ring_send, ring_recv)
    mover = Mover(move_sems)
    weights = [
        pltpu.make_async_copy(full_in.at[pl.ds(3, 1)], out_full, full_sems.at[0]),
        pltpu.make_async_copy(full_in.at[pl.ds(0, 3)], query_full, full_sems.at[1]),
    ]
    weights[0].start()
    first = (10, 8, 9, 0, 5, 6)
    order = first + tuple(i for i in range(13) if i not in first)
    mover.load([ins[i] for i in order], [loaded[i] for i in order])
    weights[1].start()
    greet(all_partners(place))
    mover.need(branch_part)

    def scatter(source, r, stage):
        return line.start(
            True,
            split.rows_view(source, r),
            split.landing_view(landing.at[stage * chunks + r]),
        )

    feed_scatters = [scatter(branch_part, r, 1) for r in range(chunks)]
    mover.need(prompt, word_grads)
    early = reducers(place, [gradients.at[i] for i in range(4)], early_scratch)
    late = reducers(place, [space_grads.at[i] for i in range(4)], late_scratch)
    for job in early:
        job.split()
    block = words.shape[2]
    far = [lax.rem(place.n + step, clips) for step in range(1, clips)]
    word_copies = []
    for i, peer in enumerate(far):
        lanes = pl.ds(pl.multiple_of((peer * sizes[WIDE] + place.w) * block, block), block)
        for j, (source, target) in enumerate(
            (
                (prompt.at[:, lanes], words.at[i + 1]),
                (word_grads, word_parts.at[i + 1]),
                (condition, conditions.at[place.n]),
            )
        ):
            word_copies.append(
                send(
                    source, target, word_send.at[i, j], word_recv.at[i, j],
                    place.over_narrow(peer),
                )
            )
    mine = pl.ds(pl.multiple_of((place.n * sizes[WIDE] + place.w) * block, block), block)
    words[0] = prompt[:, mine]
    word_parts[0] = word_grads[...]
    conditions[place.n] = condition[...]
    tally[...] = jnp.zeros_like(tally)
    tally[3:5] = mlp_sums[0:2]
    tally[6:7] = back_sums[0:1]
    tally[7:8] = back_sums[1:2] * (1.0 - vectors[7:8] * vectors[7:8])
    tally[8:9] = back_sums[2:3]

    weights[0].wait()
    mover.need(e1)
    for r in range(chunks):
        spot = split.chunk(r)
        wide_grad[spot] = dot(e1[spot], out_full[0]).astype(BF16)
        line.tick()

    mover.need(*loaded)
    weights[1].wait()
    tally[2:3] = jnp.sum(g1_own[...] * a1_own[...], 0, keepdims=True)

    def attend(first, stop):
        @pl.loop(first, stop)
        def _(f):
            spots = split.spots(f)
            queries = jnp.concatenate([q1[0, spot] for spot in spots], 0)
            grads = jnp.concatenate([wide_grad[spot] for spot in spots], 0)
            keys = jnp.concatenate(
                [q1[1, spot] for spot in spots] + [side[0, spot] for spot in spots], 0
            )
            values = jnp.concatenate(
                [q1[2, spot] for spot in spots] + [side[1, spot] for spot in spots], 0
            )
            for h in range(heads):
                lanes = slice(h * LANES, (h + 1) * LANES)
                parts = attention_pull(
                    queries[:, lanes], keys[:, lanes], values[:, lanes], grads[:, lanes],
                    None, scale,
                )
                for r in range(chunks):
                    here = slice(r * cols, (r + 1) * cols)
                    there = slice((chunks + r) * cols, (chunks + r + 1) * cols)
                    wide_parts[0, spots[r], lanes] = parts[0][here].astype(BF16)
                    for j in range(2):
                        key_sums[j, spots[r], lanes] = parts[1 + j][here]
                        side_out[j, spots[r], lanes] = parts[1 + j][there].astype(BF16)

    outputs = []

    def finish_feed(r):
        kept = split.kept(r)
        line.finish(feed_scatters[r])
        branch = split.total(branch_part, landing.at[chunks + r], r)
        tally[5:6] += jnp.sum(
            own_cotangent(cotangent, lengths, split, r) * branch, 0, keepdims=True
        )
        after = (x3_own[kept] + vectors[5:6] * branch) * live_rows(lengths, split)
        output[split.own_frames(), r] = after.astype(BF16).reshape(split.frames, cols, width)
        outputs.append(line.start(False, split.frames_view(output, r)))

    quarters = frame_count // 4
    for part in range(4):
        attend(part * quarters, (part + 1) * quarters)
        line.tick(2)
        if part >= 2 and part - 2 < chunks:
            finish_feed(part - 2)
    for r in range(2, chunks):
        finish_feed(r)
    key_copy = send(side_out, side_in, key_send, key_recv, place.sibling())
    for job in early:
        job.spread()
    line.tick(2)
    key_copy.wait()
    for j in range(2):
        wide_parts[1 + j] = (key_sums[j] + side_in[j].astype(F32)).astype(BF16)
    line.tick(2)
    scatters = []
    for r in range(chunks):
        spot = split.chunk(r)
        total = dot_tr(wide_parts[0, spot], query_full[0])
        for i in (1, 2):
            total = total + dot_tr(wide_parts[i, spot], query_full[i])
        partial[spot] = total.astype(BF16)
        scatters.append(scatter(partial, r, 0))
        line.tick(2)

    space_grads[0] = dot_outer(e1[...], o1[...]).astype(BF16)
    late[0].split()
    for i in range(3):
        narrow_parts[i] = dot_tr(wide_parts[i], spread[...]).astype(BF16)
        space_grads[1 + i] = dot_outer(h1[...], narrow_parts[i]).astype(BF16)
        late[1 + i].split()
        line.tick(2)
    for job in late:
        job.spread()
    gathers = []
    for r in range(chunks):
        kept = split.kept(r)
        line.finish(scatters[r])
        grad = split.total(partial, landing.at[r], r)
        x_own = frames[split.own_frames(), r].reshape(quarter, width).astype(F32)
        normed, inverse = norm_tile(x_own)
        tally[0:1] += jnp.sum(grad, 0, keepdims=True)
        tally[1:2] += jnp.sum(grad * normed, 0, keepdims=True)
        upstream = g1_own[kept] + norm_pull(normed, inverse, grad * vectors[1:2])
        frames_grad[split.own_frames(), r] = upstream.astype(BF16).reshape(
            split.frames, cols, width
        )
        gathers.append(line.start(False, split.frames_view(frames_grad, r)))

    tally_copy = send(tally, tally_side, tally_send.at[0], tally_recv.at[0], place.sibling())
    wait_all(word_copies)
    for j in range(2):
        total = dot_outer(word_parts[0, j, 0 : prompt.shape[0]], words[0])
        for step in range(1, clips):
            total = total + dot_outer(word_parts[step, j, 0 : prompt.shape[0]], words[step])
        prompt_out[j] = total
    mover.keep(prompt_out, outs[4])
    mover.keep(conditions, outs[6])
    tally_copy.wait()
    tally_side[...] = tally_side[...] + tally[...]
    peer_copies = [
        send(
            tally_side, tally_peers.at[step - 1], tally_send.at[step], tally_recv.at[step],
            place.over_tensor(step),
        )
        for step in range(1, sizes[TENSOR])
    ]
    for move in gathers:
        line.drain(move)
    for i, job in enumerate(early):
        job.finish(early_out.at[i])
    mover.keep(early_out, outs[2])
    wait_all(peer_copies)
    total = tally_side[...]
    for step in range(sizes[TENSOR] - 1):
        total = total + tally_peers[step]
    merged[place.n] = total
    base = sizes[TENSOR]
    far_copies = [
        send(
            merged.at[place.n], merged.at[place.n],
            tally_send.at[base + i], tally_recv.at[base + i], place.over_narrow(peer),
        )
        for i, peer in enumerate(far)
    ]
    for i, job in enumerate(late):
        job.finish(space_out.at[i])
    mover.keep(space_out, outs[3])
    for move in outputs:
        line.finish(move)
    mover.keep(output, outs[1])
    for move in gathers:
        line.finish(move)
    mover.keep(frames_grad, outs[0])
    wait_all(far_copies)
    mover.keep(merged, outs[5])
    total = merged[0]
    for clip in range(1, clips):
        total = total + merged[clip]
    grand[...] = total
    mover.keep(grand, outs[7])
    for move in feed_scatters + outputs + scatters + gathers:
        line.release(move)
    mover.settle()


def space_call(sizes, small, acts, full, gradients):
    frames, spread, prompt, condition = acts[2], small[1], acts[8], small[5]
    frame_count, chunks, cols, width = frames.shape
    rows = frame_count * cols
    tokens = rows * chunks
    quarter = rows // sizes[TENSOR]
    head_width, padded = spread.shape
    full_rows = full.shape[1]
    parts = sizes[NARROW] * sizes[WIDE]
    block, word_block = width // parts, prompt.shape[1] // parts
    clips, peers = sizes[NARROW], sizes[TENSOR] - 1
    s = jax.ShapeDtypeStruct
    moves = 4 * chunks
    outs = [
        s(frames.shape, BF16), s(frames.shape, BF16),
        s((4, block, head_width), F32), s((4, block, head_width), F32),
        s((2, head_width, word_block), F32), s((clips, 16, width), F32),
        s((clips,) + condition.shape, F32), s((16, width), F32),
    ]
    return pl.pallas_call(
        functools.partial(space_kernel, sizes),
        name="space",
        out_shape=outs,
        in_specs=[VM] * 6 + [ANY] * (len(acts) + 2),
        out_specs=[ANY] * len(outs),
        scratch_shapes=stage_scratch(list(acts) + outs)
        + [
            VMEM((3, full_rows, padded), BF16), VMEM((1, full_rows, padded), BF16),
            VMEM((tokens, padded), BF16),
            VMEM((3, tokens, padded), BF16),
            VMEM((3, tokens, head_width), BF16),
            VMEM((2, tokens, padded), F32),
            VMEM((2, tokens, padded), BF16), VMEM((2, tokens, padded), BF16),
            VMEM((4, width, head_width), BF16),
            VMEM((clips, prompt.shape[0], word_block), BF16),
            VMEM((clips, 2, LANES, head_width), BF16),
            VMEM((tokens, width), BF16),
            VMEM((2 * chunks, 4, 1, quarter, width), BF16),
            VMEM((16, width), F32), VMEM((16, width), F32), VMEM((peers, 16, width), F32),
            DMA((2,)), DMA(()), DMA(()),
            DMA((clips - 1, 3)), DMA((clips - 1, 3)),
            DMA((peers + clips,)), DMA((peers + clips,)),
            DMA((moves, 4, 1)), DMA((moves, 4, 1)),
        ]
        + reducer_scratch(sizes, 4, block, head_width)
        + reducer_scratch(sizes, 4, block, head_width),
        compiler_params=pltpu.CompilerParams(
            collective_id=4, has_side_effects=True, vmem_limit_bytes=61 << 20
        ),
    )(*small, *acts, full, gradients)


def fused_on_device(
    sizes,
    frames, cotangent, prompt, timestep, clip_lengths, text_lengths,
    modulation_weight, modulation_bias, space_query, space_key, space_value, space_out,
    time_gain, time_query, time_key, time_value, time_out, time_gate, cross_gain, cross_query,
    prompt_key, prompt_value, cross_out, feed_up, feed_down,
):
    frame_count, width = frames.shape[1], frames.shape[4]
    cols = frames.shape[2] * frames.shape[3] // CHUNKS
    head_width = space_query.shape[1]
    condition, spread = prepare(frames, timestep, head_width)
    lengths = jnp.broadcast_to(
        jnp.concatenate([clip_lengths, text_lengths]).astype(F32)[:, None], (2, LANES)
    )
    half_condition = lax.dynamic_slice_in_dim(
        condition, lax.axis_index(WIDE) * modulation_weight.shape[0],
        modulation_weight.shape[0], 1,
    )
    params = jnp.concatenate(
        [row[None] for row in (modulation_bias, time_gain, time_gate, cross_gain)], 1
    )
    tiles = frames.reshape(frame_count, CHUNKS, cols, width)
    pulls = cotangent.reshape(frame_count, CHUNKS, cols, width)
    (
        h1, q1, side, o1, h2, q2, o2, h3, q3, kv3, o3, h4,
        a1_own, a2_own, x3_own, n2_own, n3_own, n4_own, inverses, full, up, down, vectors,
    ) = forward_call(
        sizes, tiles, half_condition.astype(F32),
        params, lengths, spread, prompt[0],
        [
            weight.T
            for weight in (
                space_query, space_key, space_value, space_out, time_query, time_key,
                time_value, time_out, cross_query, cross_out, prompt_key, prompt_value,
            )
        ],
        [feed_up, feed_down], modulation_weight,
    )
    branch_part, e3, g3_own, up_grad, down_grad, mlp_sums = mlp_call(
        sizes, vectors, lengths, [h4, pulls, n4_own, inverses, up, down]
    )
    g1_own, e1, time_grads, word_grads, up_out, down_out, cross_grads, back_sums = back_call(
        sizes, cols, [vectors, lengths, spread],
        [e3, g3_own, n3_own, n2_own, inverses, a2_own, h3, q3, kv3, o3, h2, q2, o2],
        full, [up_grad, down_grad],
    )
    frames_grad, output, early_out, late_out, prompt_out, merged, conditions, grand = space_call(
        sizes,
        [vectors, spread, lengths, mlp_sums, back_sums, condition.astype(F32)],
        [e1, g1_own, tiles, a1_own, h1, q1, side, o1, prompt[0], word_grads, branch_part, x3_own,
         pulls],
        full, time_grads,
    )
    part = lax.axis_index(NARROW) * sizes[WIDE] + lax.axis_index(WIDE)
    block = width // (sizes[NARROW] * sizes[WIDE])
    slice_width = modulation_weight.shape[1]
    pulled = merged[:, :6].reshape(sizes[NARROW], 6 * width)
    own_pulled = lax.dynamic_slice_in_dim(
        pulled, lax.axis_index(TENSOR) * slice_width, slice_width, 1
    )
    own_condition = lax.dynamic_slice_in_dim(conditions[:, 0], part * block, block, 1)
    modulation_weight_grad = jnp.sum(own_condition[:, :, None] * own_pulled[:, None], 0)
    bias_block = 6 * block
    modulation_bias_grad = lax.dynamic_slice_in_dim(
        grand[:6].reshape(6 * width), part * bias_block, bias_block
    )
    cross_gain_grad, time_gate_grad, time_gain_grad = lax.dynamic_slice(
        grand, (6, part * block), (3, block)
    )
    return (
        output.reshape(frames.shape), frames_grad.reshape(frames.shape),
        modulation_weight_grad, modulation_bias_grad,
        late_out[1], late_out[2], late_out[3], late_out[0],
        time_gain_grad, early_out[1], early_out[2], early_out[3], early_out[0], time_gate_grad,
        cross_gain_grad, cross_grads[1], prompt_out[0].T, prompt_out[1].T, cross_grads[0],
        up_out, down_out,
    )


CONTRACT_LAST = (((1,), (1,)), ((), ()))
CONTRACT_FIRST = (((0,), (0,)), ((), ()))


def matmul(left, right):
    return jnp.dot(left, right, preferred_element_type=jnp.float32)


def matmul_tr(left, right):
    return lax.dot_general(left, right, CONTRACT_LAST, preferred_element_type=jnp.float32)


def outer_sum(left, right):
    return lax.dot_general(left, right, CONTRACT_FIRST, preferred_element_type=jnp.float32)


def norm_rows(values):
    center = values - jnp.mean(values, -1, keepdims=True)
    inverse = lax.rsqrt(jnp.mean(center * center, -1, keepdims=True) + EPSILON)
    return (center * inverse, inverse)


def norm_back(normed, inverse, incoming):
    return inverse * (
        incoming
        - jnp.mean(incoming, -1, keepdims=True)
        - normed * jnp.mean(incoming * normed, -1, keepdims=True)
    )


def over_heads(partial_sum):
    return lax.psum(partial_sum.astype(jnp.bfloat16), TENSOR).astype(jnp.float32)


def attend_forward(queries, key_rows, values, allowed, pattern, score_scale):
    scores = jnp.where(
        allowed,
        jnp.einsum(pattern[0], queries, key_rows, preferred_element_type=jnp.float32) * score_scale,
        NEGATIVE,
    )
    row_max = jnp.max(scores, -1, keepdims=True)
    exponent = jnp.exp(scores - row_max)
    row_total = jnp.sum(exponent, -1, keepdims=True)
    attend = (exponent / row_total).astype(jnp.bfloat16)
    context = jnp.einsum(pattern[1], attend, values, preferred_element_type=jnp.float32)
    return (context.astype(jnp.bfloat16), row_max + jnp.log(row_total))


def attend_back(queries, key_rows, values, allowed, log_total, context_grad, pattern, score_scale):
    scores = jnp.where(
        allowed,
        jnp.einsum(pattern[0], queries, key_rows, preferred_element_type=jnp.float32) * score_scale,
        NEGATIVE,
    )
    attend = jnp.exp(scores - log_total)
    attend_grad = jnp.einsum(pattern[0], context_grad, values, preferred_element_type=jnp.float32)
    score_grad = (attend * (attend_grad - jnp.sum(attend * attend_grad, -1, keepdims=True))).astype(
        jnp.bfloat16
    )
    query_grad = (
        jnp.einsum(pattern[1], score_grad, key_rows, preferred_element_type=jnp.float32)
        * score_scale
    )
    key_grad = (
        jnp.einsum(pattern[2], score_grad, queries, preferred_element_type=jnp.float32)
        * score_scale
    )
    value_grad = jnp.einsum(
        pattern[2], attend.astype(jnp.bfloat16), context_grad, preferred_element_type=jnp.float32
    )
    return (query_grad, key_grad, value_grad)


def on_device(
    frames,
    cotangent,
    prompt,
    timestep,
    clip_lengths,
    text_lengths,
    modulation_weight,
    modulation_bias,
    space_query,
    space_key,
    space_value,
    space_out,
    time_gain,
    time_query,
    time_key,
    time_value,
    time_out,
    time_gate,
    cross_gain,
    cross_query,
    prompt_key,
    prompt_value,
    cross_out,
    feed_up,
    feed_down,
):
    frame_count = frames.shape[1]
    patch_count = frames.shape[2] * frames.shape[3]
    model_width = frames.shape[4]
    token_count = frame_count * patch_count
    score_scale = 1.0 / math.sqrt(HEAD_DIM)
    residual = frames.reshape(token_count, model_width).astype(jnp.float32)
    frame_live = jnp.arange(frame_count) < clip_lengths[0]
    token_live = jnp.repeat(frame_live, patch_count)[:, None]
    prompt_rows = prompt[0]
    word_live = jnp.arange(prompt_rows.shape[0]) < text_lengths[0]
    (
        modulation_weight,
        space_query,
        space_key,
        space_value,
        space_out,
        time_query,
        time_key,
        time_value,
        time_out,
        cross_query,
        prompt_key,
        prompt_value,
        cross_out,
        feed_up,
        feed_down,
    ) = (
        lax.all_gather(modulation_weight, WIDE, axis=0, tiled=True),
        lax.all_gather(space_query, WIDE, axis=0, tiled=True),
        lax.all_gather(space_key, WIDE, axis=0, tiled=True),
        lax.all_gather(space_value, WIDE, axis=0, tiled=True),
        lax.all_gather(space_out, WIDE, axis=0, tiled=True),
        lax.all_gather(time_query, WIDE, axis=0, tiled=True),
        lax.all_gather(time_key, WIDE, axis=0, tiled=True),
        lax.all_gather(time_value, WIDE, axis=0, tiled=True),
        lax.all_gather(time_out, WIDE, axis=0, tiled=True),
        lax.all_gather(cross_query, WIDE, axis=0, tiled=True),
        lax.all_gather(prompt_key, WIDE, axis=0, tiled=True),
        lax.all_gather(prompt_value, WIDE, axis=0, tiled=True),
        lax.all_gather(cross_out, WIDE, axis=0, tiled=True),
        lax.all_gather(feed_up, WIDE, axis=0, tiled=True),
        lax.all_gather(feed_down, WIDE, axis=0, tiled=True),
    )
    head_width = space_query.shape[1]
    head_count = head_width // HEAD_DIM
    split_heads = (frame_count, patch_count, head_count, HEAD_DIM)
    half_width = model_width // 2
    frequency = jnp.exp(-math.log(10000.0) * jnp.arange(half_width, dtype=jnp.float32) / half_width)
    angles = timestep[0].astype(jnp.float32) * frequency
    condition = jax.nn.silu(jnp.concatenate([jnp.cos(angles), jnp.sin(angles)])).astype(
        jnp.bfloat16
    )
    slice_width = modulation_weight.shape[1]
    slice_start = lax.axis_index(TENSOR) * slice_width
    own_modulation = matmul(condition[None, :], modulation_weight)[0] + lax.dynamic_slice_in_dim(
        modulation_bias, slice_start, slice_width
    )
    modulation = lax.all_gather(own_modulation, TENSOR, axis=0, tiled=True)
    shift_one, scale_one, gate_one, shift_two, scale_two, gate_two = jnp.split(modulation, 6)
    normed_one, inverse_one = norm_rows(residual)
    input_one = (normed_one * (1.0 + scale_one) + shift_one).astype(jnp.bfloat16)
    query_one = matmul(input_one, space_query).astype(jnp.bfloat16).reshape(split_heads)
    key_one = matmul(input_one, space_key).astype(jnp.bfloat16).reshape(split_heads)
    value_one = matmul(input_one, space_value).astype(jnp.bfloat16).reshape(split_heads)
    key_frame, value_frame = (
        lax.all_gather(key_one, WIDE, axis=1, tiled=True),
        lax.all_gather(value_one, WIDE, axis=1, tiled=True),
    )
    space_pattern = ("fphe,fkhe->fhpk", "fhpk,fkhe->fphe", "fhpk,fphe->fkhe")
    every_patch = jnp.ones((key_frame.shape[1],), jnp.bool_)
    context_one, log_one = attend_forward(
        query_one, key_frame, value_frame, every_patch, space_pattern, score_scale
    )
    context_one = context_one.reshape(token_count, head_width)
    branch_one = over_heads(matmul_tr(context_one, space_out))
    after_one = residual + gate_one * branch_one
    normed_two, inverse_two = norm_rows(after_one)
    input_two = (normed_two * time_gain).astype(jnp.bfloat16)
    query_two = matmul(input_two, time_query).astype(jnp.bfloat16).reshape(split_heads)
    key_two = matmul(input_two, time_key).astype(jnp.bfloat16).reshape(split_heads)
    value_two = matmul(input_two, time_value).astype(jnp.bfloat16).reshape(split_heads)
    time_pattern = ("fphe,gphe->phfg", "phfg,gphe->fphe", "phfg,fphe->gphe")
    context_two, log_two = attend_forward(
        query_two, key_two, value_two, frame_live, time_pattern, score_scale
    )
    context_two = context_two.reshape(token_count, head_width)
    branch_two = over_heads(matmul_tr(context_two, time_out))
    gate_time = jnp.tanh(time_gate)
    after_two = after_one + gate_time * branch_two
    normed_three, inverse_three = norm_rows(after_two)
    input_three = (normed_three * cross_gain).astype(jnp.bfloat16)
    query_three = (
        matmul(input_three, cross_query)
        .astype(jnp.bfloat16)
        .reshape(token_count, head_count, HEAD_DIM)
    )
    word_keys = (
        matmul(prompt_rows, prompt_key).astype(jnp.bfloat16).reshape(-1, head_count, HEAD_DIM)
    )
    word_values = (
        matmul(prompt_rows, prompt_value).astype(jnp.bfloat16).reshape(-1, head_count, HEAD_DIM)
    )
    cross_pattern = ("nhe,jhe->nhj", "nhj,jhe->nhe", "nhj,nhe->jhe")
    context_three, log_three = attend_forward(
        query_three, word_keys, word_values, word_live, cross_pattern, score_scale
    )
    context_three = context_three.reshape(token_count, head_width)
    branch_three = over_heads(matmul_tr(context_three, cross_out))
    after_three = after_two + branch_three
    normed_four, inverse_four = norm_rows(after_three)
    input_four = (normed_four * (1.0 + scale_two) + shift_two).astype(jnp.bfloat16)
    pre_act = matmul(input_four, feed_up)
    hidden, gelu_pull = jax.vjp(lambda inner: jax.nn.gelu(inner, approximate=True), pre_act)
    hidden = hidden.astype(jnp.bfloat16)
    branch_four = over_heads(matmul_tr(hidden, feed_down))
    after_four = after_three + gate_two * branch_four
    output = jnp.where(token_live, after_four, 0.0).astype(jnp.bfloat16).reshape(frames.shape)
    upstream = jnp.where(
        token_live, cotangent.reshape(token_count, model_width).astype(jnp.float32), 0.0
    )
    feed_grad = (gate_two * upstream).astype(jnp.bfloat16)
    gate_two_grad = jnp.sum(upstream * branch_four, 0)
    feed_down_grad = outer_sum(feed_grad, hidden)
    pre_grad = gelu_pull(matmul(feed_grad, feed_down))[0].astype(jnp.bfloat16)
    feed_up_grad = outer_sum(input_four, pre_grad)
    input_four_grad = over_heads(matmul_tr(pre_grad, feed_up))
    shift_two_grad = jnp.sum(input_four_grad, 0)
    scale_two_grad = jnp.sum(input_four_grad * normed_four, 0)
    upstream = upstream + norm_back(normed_four, inverse_four, input_four_grad * (1.0 + scale_two))
    cross_grad = upstream.astype(jnp.bfloat16)
    cross_out_grad = outer_sum(cross_grad, context_three)
    context_grad = (
        matmul(cross_grad, cross_out)
        .astype(jnp.bfloat16)
        .reshape(token_count, head_count, HEAD_DIM)
    )
    query_grad, key_grad, value_grad = attend_back(
        query_three,
        word_keys,
        word_values,
        word_live,
        log_three,
        context_grad,
        cross_pattern,
        score_scale,
    )
    query_grad = query_grad.astype(jnp.bfloat16).reshape(token_count, head_width)
    cross_query_grad = outer_sum(input_three, query_grad)
    word_key_grad = key_grad.astype(jnp.bfloat16).reshape(-1, head_width)
    word_value_grad = value_grad.astype(jnp.bfloat16).reshape(-1, head_width)
    prompt_key_grad = outer_sum(prompt_rows, word_key_grad)
    prompt_value_grad = outer_sum(prompt_rows, word_value_grad)
    input_three_grad = over_heads(matmul_tr(query_grad, cross_query))
    cross_gain_grad = jnp.sum(input_three_grad * normed_three, 0)
    upstream = upstream + norm_back(normed_three, inverse_three, input_three_grad * cross_gain)
    time_grad = (gate_time * upstream).astype(jnp.bfloat16)
    time_gate_grad = jnp.sum(upstream * branch_two, 0) * (1.0 - gate_time * gate_time)
    time_out_grad = outer_sum(time_grad, context_two)
    context_grad = matmul(time_grad, time_out).astype(jnp.bfloat16).reshape(split_heads)
    query_grad, key_grad, value_grad = attend_back(
        query_two, key_two, value_two, frame_live, log_two, context_grad, time_pattern, score_scale
    )
    query_grad = query_grad.astype(jnp.bfloat16).reshape(token_count, head_width)
    key_grad = key_grad.astype(jnp.bfloat16).reshape(token_count, head_width)
    value_grad = value_grad.astype(jnp.bfloat16).reshape(token_count, head_width)
    time_query_grad = outer_sum(input_two, query_grad)
    time_key_grad = outer_sum(input_two, key_grad)
    time_value_grad = outer_sum(input_two, value_grad)
    input_two_grad = over_heads(
        matmul_tr(query_grad, time_query)
        + matmul_tr(key_grad, time_key)
        + matmul_tr(value_grad, time_value)
    )
    time_gain_grad = jnp.sum(input_two_grad * normed_two, 0)
    upstream = upstream + norm_back(normed_two, inverse_two, input_two_grad * time_gain)
    space_grad = (gate_one * upstream).astype(jnp.bfloat16)
    gate_one_grad = jnp.sum(upstream * branch_one, 0)
    space_out_grad = outer_sum(space_grad, context_one)
    context_grad = matmul(space_grad, space_out).astype(jnp.bfloat16).reshape(split_heads)
    key_frame, value_frame = (
        lax.all_gather(key_one, WIDE, axis=1, tiled=True),
        lax.all_gather(value_one, WIDE, axis=1, tiled=True),
    )
    query_grad, key_grad, value_grad = attend_back(
        query_one,
        key_frame,
        value_frame,
        every_patch,
        log_one,
        context_grad,
        space_pattern,
        score_scale,
    )
    key_grad, value_grad = (
        lax.psum_scatter(
            key_grad.astype(jnp.bfloat16), WIDE, scatter_dimension=1, tiled=True
        ).astype(jnp.float32),
        lax.psum_scatter(
            value_grad.astype(jnp.bfloat16), WIDE, scatter_dimension=1, tiled=True
        ).astype(jnp.float32),
    )
    query_grad = query_grad.astype(jnp.bfloat16).reshape(token_count, head_width)
    key_grad = key_grad.astype(jnp.bfloat16).reshape(token_count, head_width)
    value_grad = value_grad.astype(jnp.bfloat16).reshape(token_count, head_width)
    space_query_grad = outer_sum(input_one, query_grad)
    space_key_grad = outer_sum(input_one, key_grad)
    space_value_grad = outer_sum(input_one, value_grad)
    input_one_grad = over_heads(
        matmul_tr(query_grad, space_query)
        + matmul_tr(key_grad, space_key)
        + matmul_tr(value_grad, space_value)
    )
    shift_one_grad = jnp.sum(input_one_grad, 0)
    scale_one_grad = jnp.sum(input_one_grad * normed_one, 0)
    upstream = upstream + norm_back(normed_one, inverse_one, input_one_grad * (1.0 + scale_one))
    frames_grad = upstream.astype(jnp.bfloat16).reshape(frames.shape)
    modulation_bias_grad = jnp.concatenate(
        [
            shift_one_grad,
            scale_one_grad,
            gate_one_grad,
            shift_two_grad,
            scale_two_grad,
            gate_two_grad,
        ]
    )
    own_grad = lax.dynamic_slice_in_dim(modulation_bias_grad, slice_start, slice_width)
    modulation_weight_grad = condition.astype(jnp.float32)[:, None] * own_grad[None, :]
    (
        modulation_weight_grad,
        modulation_bias_grad,
        space_query_grad,
        space_key_grad,
        space_value_grad,
        space_out_grad,
        time_gain_grad,
        time_query_grad,
        time_key_grad,
        time_value_grad,
        time_out_grad,
        time_gate_grad,
        cross_gain_grad,
        cross_query_grad,
        prompt_key_grad,
        prompt_value_grad,
        cross_out_grad,
        feed_up_grad,
        feed_down_grad,
    ) = (
        lax.psum_scatter(
            modulation_weight_grad, (NARROW, WIDE), scatter_dimension=0, tiled=True
        ),
        lax.psum_scatter(modulation_bias_grad, (NARROW, WIDE), scatter_dimension=0, tiled=True),
        lax.psum_scatter(space_query_grad, (NARROW, WIDE), scatter_dimension=0, tiled=True),
        lax.psum_scatter(space_key_grad, (NARROW, WIDE), scatter_dimension=0, tiled=True),
        lax.psum_scatter(space_value_grad, (NARROW, WIDE), scatter_dimension=0, tiled=True),
        lax.psum_scatter(space_out_grad, (NARROW, WIDE), scatter_dimension=0, tiled=True),
        lax.psum_scatter(time_gain_grad, (NARROW, WIDE), scatter_dimension=0, tiled=True),
        lax.psum_scatter(time_query_grad, (NARROW, WIDE), scatter_dimension=0, tiled=True),
        lax.psum_scatter(time_key_grad, (NARROW, WIDE), scatter_dimension=0, tiled=True),
        lax.psum_scatter(time_value_grad, (NARROW, WIDE), scatter_dimension=0, tiled=True),
        lax.psum_scatter(time_out_grad, (NARROW, WIDE), scatter_dimension=0, tiled=True),
        lax.psum_scatter(time_gate_grad, (NARROW, WIDE), scatter_dimension=0, tiled=True),
        lax.psum_scatter(cross_gain_grad, (NARROW, WIDE), scatter_dimension=0, tiled=True),
        lax.psum_scatter(cross_query_grad, (NARROW, WIDE), scatter_dimension=0, tiled=True),
        lax.psum_scatter(prompt_key_grad, (NARROW, WIDE), scatter_dimension=0, tiled=True),
        lax.psum_scatter(prompt_value_grad, (NARROW, WIDE), scatter_dimension=0, tiled=True),
        lax.psum_scatter(cross_out_grad, (NARROW, WIDE), scatter_dimension=0, tiled=True),
        lax.psum_scatter(feed_up_grad, (NARROW, WIDE), scatter_dimension=0, tiled=True),
        lax.psum_scatter(feed_down_grad, (NARROW, WIDE), scatter_dimension=0, tiled=True),
    )
    return (
        output,
        frames_grad,
        modulation_weight_grad,
        modulation_bias_grad,
        space_query_grad,
        space_key_grad,
        space_value_grad,
        space_out_grad,
        time_gain_grad,
        time_query_grad,
        time_key_grad,
        time_value_grad,
        time_out_grad,
        time_gate_grad,
        cross_gain_grad,
        cross_query_grad,
        prompt_key_grad,
        prompt_value_grad,
        cross_out_grad,
        feed_up_grad,
        feed_down_grad,
    )


WEIGHT = P(WIDE, TENSOR)
OWNED = P((NARROW, WIDE), TENSOR)
ROWS = P((NARROW, WIDE))
PATCHES = P(NARROW, None, WIDE, None, None)
CLIP = P(NARROW)
COPIED = P()


def fits(sizes):
    return sizes[WIDE] == 2 and sizes[TENSOR] == 4 and sizes[NARROW] == 4


def solution(mesh):
    sizes = {name: mesh.shape[name] for name in mesh.axis_names}
    return jax.shard_map(
        functools.partial(fused_on_device, sizes) if fits(sizes) else on_device,
        mesh=mesh,
        in_specs=(
            (PATCHES, PATCHES, P(NARROW, None, None), CLIP, CLIP, CLIP)
            + (WEIGHT, COPIED, WEIGHT, WEIGHT, WEIGHT, WEIGHT)
            + (COPIED, WEIGHT, WEIGHT, WEIGHT, WEIGHT, COPIED)
            + (COPIED, WEIGHT, WEIGHT, WEIGHT, WEIGHT, WEIGHT, WEIGHT)
        ),
        out_specs=(
            (PATCHES, PATCHES, OWNED, ROWS, OWNED, OWNED, OWNED, OWNED)
            + (ROWS, OWNED, OWNED, OWNED, OWNED, ROWS)
            + (ROWS, OWNED, OWNED, OWNED, OWNED, OWNED, OWNED)
        ),
        check_vma=False,
    )
```
